32 devices in a mesh: rep: 4 (over y, core), fsdp: 4 (over z), seq: 2 (over x).
Axes of the slice: x: 2, y: 2, z: 4, core: 2. Of those that a mesh axis runs over, the one named last changes fastest.
Arguments:
- tokens: bfloat16 [12288, 768], P(('rep', 'fsdp', 'seq')), may hold values from -6 to 6
- piece_starts: int32 [16, 2], P(('rep', 'fsdp')), may hold values from 0 to 512, as said below
- routes: int32 [12288, 2], P(('rep', 'fsdp', 'seq')), may hold values from 0 to 3, all different within a row; in each aligned block of 384 rows (0 to 383, 384 to 767, ...) at most 288 rows name the same one
- buckets: int32 [1535], replicated, may hold values from 0 to 31
- attn_q: bfloat16 [768, 768], P(('fsdp', 'seq')), may hold values from -0.21875 to 0.21875
- attn_k: bfloat16 [768, 768], P(('fsdp', 'seq')), may hold values from -0.21875 to 0.21875
- attn_v: bfloat16 [768, 768], P(('fsdp', 'seq')), may hold values from -0.21875 to 0.21875
- attn_o: bfloat16 [768, 768], P(('fsdp', 'seq')), may hold values from -0.875 to 0.875
- expert_in: bfloat16 [4, 768, 3072], P(None, ('fsdp', 'seq')), may hold values from -0.21875 to 0.21875
- expert_out: bfloat16 [4, 3072, 768], P(None, ('fsdp', 'seq')), may hold values from -0.109375 to 0.109375
- gain_attn: float32 [768], replicated, may hold values from 0.5 to 1.5
- gain_ffn: float32 [768], replicated, may hold values from 0.5 to 1.5
- rel_table: float32 [32, 12], replicated, may hold values from -4 to 4
- router: float32 [768, 4], replicated, may hold values from -0.15 to 0.15
- cotangent: bfloat16 [12288, 768], P(('rep', 'fsdp', 'seq')), may hold values from -6 to 6
Outputs:
- out_rows: bfloat16 [12288, 768], P(('rep', 'fsdp', 'seq'))
- tokens_grad: bfloat16 [12288, 768], P(('rep', 'fsdp', 'seq'))
- attn_q_grad: float32 [768, 768], P(('fsdp', 'seq'))
- attn_k_grad: float32 [768, 768], P(('fsdp', 'seq'))
- attn_v_grad: float32 [768, 768], P(('fsdp', 'seq'))
- attn_o_grad: float32 [768, 768], P(('fsdp', 'seq'))
- expert_in_grad: float32 [4, 768, 3072], P(None, ('fsdp', 'seq'))
- expert_out_grad: float32 [4, 3072, 768], P(None, ('fsdp', 'seq'))
- gain_attn_grad: float32 [768], replicated
- gain_ffn_grad: float32 [768], replicated
- rel_table_grad: float32 [32, 12], replicated
- router_grad: float32 [768, 4], replicated
The draws below stay inside these ranges and needn't reach their ends.
Inputs may be any that keep to these rules, and one draw needn't show every extreme that they name: `routes`: A token's two experts differ. In the rows of one device (aligned blocks of 384 tokens) no expert is named more than 288 times, a bound that some block reaches. `piece_starts`: each sequence has two picture pieces of 256 positions inside it; the first ends at or before position 256 and the second starts at or after it.
All inputs are finite; a program needn't handle non-finite values.
Results may differ from the reference program's by a relative error of at most 0.018.
Values may be sent and summed in bfloat16 or wider, within the bound.
A program may use at most 256 MiB of HBM per device.

```python
import math
import jax
import jax.numpy as jnp
import numpy as np
from jax import lax

D = 768
HEADS = 12
HEAD_DIM = 64
FF = 3072
EXPERTS = 4
NB = 32
PIECE = 256
TOK_DEV = 384
CAP = 288
LEN = 768
SEQS = 16
TOKENS = 12288
N_SEQ = 2


def draw_piece_starts(key, part):
    first_start = jax.random.randint(jax.random.fold_in(key, 11), (SEQS,), 0, LEN // 2 - 3 * PIECE // 2 + 1)
    second_start = jax.random.randint(jax.random.fold_in(key, 12), (SEQS,), LEN // 2 - PIECE // 2, LEN - PIECE + 1)
    seq_ids = jnp.arange(SEQS)
    first_start = jnp.where(seq_ids == 0, 0, first_start)
    second_start = jnp.where(seq_ids == 0, LEN - PIECE, second_start)
    return jnp.stack([first_start, second_start], 1).astype(jnp.int32)


def plant(result, rng, least, high):
    longest = result.shape.index(max(result.shape))
    spots = []
    for shift in (0, 1):
        where = [jax.random.randint(jax.random.fold_in(rng, axis), (), 0, length) for axis, length in enumerate(result.shape)]
        where[longest] = (where[longest] + shift) % result.shape[longest]
        spots.append(tuple(where))
    return result.at[spots[0]].set(least).at[spots[1]].set(high)


def levels(key, extent, cuts, least, top_value):
    loudness = 1.0
    for position, shards_of in cuts:
        draws = jax.random.uniform(jax.random.fold_in(jax.random.fold_in(key, 6), position), (shards_of,), jnp.float32, least / len(cuts), top_value / len(cuts))
        loudness = loudness * jnp.repeat(jnp.exp(draws), extent[position] // shards_of).reshape((-1,) + (1,) * (len(extent) - 1 - position))
    return loudness


def routed_block(key, own, number, rows, count, top, limit, lean):
    ranking = jax.random.permutation(key, count)
    packed, usual = shares(count, rows * top, limit, lean, True), shares(count, rows * top, limit, lean, False)
    places = jnp.arange(count)

    def named(tallies, turn):
        used = int((tallies > 0).sum())
        fixed = max(1, used // 4)
        moved = fixed + (places - fixed + turn * (used - fixed)) % max(1, count - fixed)
        return jnp.zeros((count,), jnp.int32).at[ranking[jnp.where(places < fixed, places, moved)]].set(jnp.asarray(tallies, jnp.int32))

    tallies = jnp.where(number % 4 == 0, named(packed, number // 4), named(usual, number - number // 4 - 1))
    mixed = jax.random.permutation(jax.random.fold_in(own, 3), count)
    giver, receiver = mixed[0:count // 2 * 2:2], mixed[1:count // 2 * 2:2]
    room = jnp.minimum(tallies[giver] - 1, limit - tallies[receiver]) // 2
    room = jnp.where((giver == ranking[0]) | (receiver == ranking[0]) | (tallies[receiver] == 0), 0, jnp.maximum(room, 0))
    moved = jax.random.randint(jax.random.fold_in(own, 4), (count // 2,), 0, 1 << 20) % (room + 1)
    tallies = tallies.at[giver].add(-moved).at[receiver].add(moved)
    members = jnp.searchsorted(jnp.cumsum(tallies), jnp.arange(rows * top), side="right").astype(jnp.int32)
    listing = members.reshape(top, rows).T
    listing = listing[jax.random.permutation(jax.random.fold_in(own, 1), rows)]
    turn = jax.random.randint(jax.random.fold_in(own, 2), (rows, 1), 0, top)
    return jnp.take_along_axis(listing, (jnp.arange(top)[None, :] + turn) % top, axis=1)


def shares(count, total, bound, skew, full):
    weights = [(1 << 20) // math.isqrt(standing ** skew) + 1 for standing in range(1, count + 1)]
    largest = bound if full else min(bound, max(-(-total // count), total * weights[0] // sum(weights)))
    least = 1 if total - largest >= count - 1 else 0
    holding, surplus = [largest] + [least] * (count - 1), total - largest - least * (count - 1)
    while surplus > 0:
        movable = [i for i in range(1, count) if holding[i] < largest] or [i for i in range(1, count) if holding[i] < bound]
        pool, remaining = sum([weights[i] for i in movable]), surplus
        for i in movable:
            more = min(bound - holding[i], max(1, remaining * weights[i] // pool), surplus)
            holding[i] = holding[i] + more
            surplus = surplus - more
    return np.array(holding)


def centred(stream_key, dims, deviation, most, cuts=(), held_as=jnp.bfloat16):
    result = jax.random.normal(stream_key, dims, jnp.float32) * deviation
    if len(cuts) > 0:
        result = levels(stream_key, dims, cuts, -0.22, 0.18) * result
    return jnp.clip(result, min=-most, max=most).astype(held_as)


def setup_inputs(seed: int = 0) -> dict:
    seeds = jax.random.split(jax.random.key(seed), 16)
    tokens = centred(seeds[0], (TOKENS, D), 1.0, 6.0, ((0, 32),))
    piece_starts = draw_piece_starts(jax.random.fold_in(seeds[15], 71), 0)
    routes_keys = jax.random.split(jax.random.fold_in(seeds[2], 1), TOKENS // TOK_DEV)
    routes_turns = jax.random.permutation(jax.random.fold_in(seeds[2], 3), TOKENS // TOK_DEV)
    routes = jax.vmap(lambda own, number: routed_block(jax.random.fold_in(seeds[2], 2), own, number, TOK_DEV, EXPERTS, 2, CAP, 1))(routes_keys, routes_turns).reshape((TOKENS, 2))
    buckets = plant(jax.random.randint(seeds[3], (2 * LEN - 1,), 0, NB), jax.random.fold_in(seeds[3], 1), 0, NB - 1).astype(jnp.int32)
    attn_q = centred(seeds[4], (D, D), D ** -0.5, 0.21875, ((0, 8),))
    attn_k = centred(seeds[5], (D, D), D ** -0.5, 0.21875, ((0, 8),))
    attn_v = centred(seeds[6], (D, D), D ** -0.5, 0.21875, ((0, 8),))
    attn_o = centred(seeds[7], (D, D), (D // 16) ** -0.5, 0.875, ((0, 8),))
    expert_in = centred(seeds[8], (EXPERTS, D, FF), D ** -0.5, 0.21875, ((1, 8),))
    expert_out = centred(seeds[9], (EXPERTS, FF, D), FF ** -0.5, 0.109375, ((1, 8),))
    gain_attn = jnp.clip(1.0 + 0.1 * jax.random.normal(seeds[10], (D,), jnp.float32), 0.5, 1.5)
    gain_ffn = jnp.clip(1.0 + 0.1 * jax.random.normal(seeds[11], (D,), jnp.float32), 0.5, 1.5)
    rel_table = centred(seeds[12], (NB, HEADS), 1.0, 4.0, (), jnp.float32)
    router = centred(seeds[13], (D, EXPERTS), 0.025, 0.15, (), jnp.float32)
    cotangent = centred(seeds[14], (TOKENS, D), 1.0, 6.0, ((0, 32),))
    return {"tokens": tokens, "piece_starts": piece_starts, "routes": routes, "buckets": buckets, "attn_q": attn_q, "attn_k": attn_k, "attn_v": attn_v, "attn_o": attn_o, "expert_in": expert_in, "expert_out": expert_out, "gain_attn": gain_attn, "gain_ffn": gain_ffn, "rel_table": rel_table, "router": router, "cotangent": cotangent}


@jax.custom_vjp
def low(v):
    return lax.optimization_barrier(v.astype(jnp.bfloat16)).astype(jnp.float32)

@jax.custom_vjp
def low_back(v):
    return v

def low_keep(v):
    return (low(v), None)

def low_pass(kept, grad):
    return (grad,)

def back_keep(v):
    return (v, None)

def back_low(kept, grad):
    return (low(grad),)
low.defvjp(low_keep, low_pass)
low_back.defvjp(back_keep, back_low)
epsilon = 1e-06
masked_out = -1e+30
highest = lax.Precision.HIGHEST

def mat_mul(a_mat, b_mat):
    return jnp.dot(a_mat, b_mat, precision=highest)

def norm_rows(values, gain_vec):
    return values * lax.rsqrt(lax.optimization_barrier(jnp.mean(values * values, -1, keepdims=True)) + epsilon) * gain_vec

def piece_labels(positions, starts):
    inside = (positions[:, None] >= starts[None, :]) & (positions[:, None] < starts[None, :] + PIECE)
    return jnp.where(jnp.any(inside, 1), lax.optimization_barrier(jnp.sum(jnp.where(inside, starts[None, :], 0), 1)), -1)

def gate_values(logits, route_ids):
    soft_probs = jax.nn.softmax(logits, -1)
    chosen = jnp.take_along_axis(soft_probs, route_ids, 1)
    return chosen / lax.optimization_barrier(jnp.sum(chosen, 1, keepdims=True))

def slot_index(route_ids, n_experts, capacity):
    flat_routes = route_ids.reshape(-1)
    expert_hot = (flat_routes[:, None] == jnp.arange(n_experts)[None, :]).astype(jnp.int32)
    before = jnp.cumsum(expert_hot, 0) - expert_hot
    return (flat_routes * capacity + lax.optimization_barrier(jnp.sum(before * expert_hot, 1))).astype(jnp.int32)

def sequence_layer(params, dist_bias, x_seq, starts, route_seq):
    w_query, w_key, w_value, w_output, w_in, w_out, g_attn, g_ffn, dist_table, w_router = params
    h_one = low(norm_rows(x_seq, g_attn))
    q_rows = low_back(low(mat_mul(h_one, w_query)))
    k_rows = low_back(low(mat_mul(h_one, w_key)))
    v_rows = low_back(low(mat_mul(h_one, w_value)))
    positions = jnp.arange(LEN)
    labels = piece_labels(positions, starts)
    allowed = (positions[None, :] <= positions[:, None]) | (labels[:, None] == labels[None, :]) & (labels[:, None] >= 0)
    offset = positions[None, :] - positions[:, None] + (LEN - 1)
    bias_full = jnp.transpose(dist_bias[offset], (2, 0, 1))
    q_heads = q_rows.reshape(LEN, HEADS, HEAD_DIM)
    k_heads = k_rows.reshape(LEN, HEADS, HEAD_DIM)
    v_heads = v_rows.reshape(LEN, HEADS, HEAD_DIM)
    raw_scores = jnp.einsum('qhd,khd->hqk', q_heads, k_heads, precision=highest) * 0.125 + bias_full
    scores = jnp.where(allowed[None], low_back(raw_scores), masked_out)
    soft_probs = low(jax.nn.softmax(scores, -1))
    att_rows = jnp.einsum('hqk,khd->qhd', soft_probs, v_heads, precision=highest).reshape(LEN, D)
    att_rows = low_back(low(att_rows))
    x_mid = x_seq + low_back(mat_mul(att_rows, w_output))
    h_two = low(norm_rows(x_mid, g_ffn))
    gate_vals = gate_values(mat_mul(h_two, w_router), route_seq)
    blocks_h = h_two.reshape(N_SEQ, TOK_DEV, D)
    blocks_r = route_seq.reshape(N_SEQ, TOK_DEV, 2)

    def expert_block(h_blk, r_blk):
        slot_flat = slot_index(r_blk, EXPERTS, CAP)
        dispatch = jnp.zeros((EXPERTS * CAP, D), jnp.float32).at[slot_flat].set(jnp.repeat(h_blk, 2, axis=0))
        dispatch = dispatch.reshape(EXPERTS, CAP, D)
        up_vals = low_back(jnp.einsum('ecd,edf->ecf', dispatch, w_in, precision=highest))
        act_low = low(jax.nn.gelu(up_vals, approximate=True))
        y_exp = jnp.einsum('ecf,efd->ecd', act_low, w_out, precision=highest)
        y_exp = low_back(low(y_exp)).reshape(EXPERTS * CAP, D)
        return y_exp[slot_flat].reshape(TOK_DEV, 2, D)
    picked = jax.vmap(expert_block)(blocks_h, blocks_r).reshape(LEN, 2, D)
    return x_mid + lax.optimization_barrier(jnp.sum(gate_vals[:, :, None] * picked, 1))

def reference(tokens, piece_starts, routes, buckets, attn_q, attn_k, attn_v, attn_o, expert_in, expert_out, gain_attn, gain_ffn, rel_table, router, cotangent):
    params = (attn_q.astype(jnp.float32), attn_k.astype(jnp.float32), attn_v.astype(jnp.float32), attn_o.astype(jnp.float32), expert_in.astype(jnp.float32), expert_out.astype(jnp.float32), gain_attn.astype(jnp.float32), gain_ffn.astype(jnp.float32), rel_table.astype(jnp.float32), router.astype(jnp.float32))
    bucket_hot = (buckets[:, None] == jnp.arange(NB)[None, :]).astype(jnp.float32)
    route_seqs = routes.reshape(SEQS, LEN, 2)

    def layer(x_all, weights):
        dist_bias = mat_mul(bucket_hot, weights[8])

        def one_sequence(pieces):
            return sequence_layer(weights, dist_bias, pieces[0], pieces[1], pieces[2])
        step_fn = jax.checkpoint(one_sequence)
        outputs = lax.map(step_fn, (x_all.reshape(SEQS, LEN, D), piece_starts, route_seqs))
        return outputs.reshape(TOKENS, D)
    out_rows, pull_back = jax.vjp(layer, tokens.astype(jnp.float32), params)
    x_grad, all_grads = pull_back(cotangent.astype(jnp.float32))
    return (out_rows.astype(jnp.bfloat16), x_grad.astype(jnp.bfloat16), all_grads[0], all_grads[1], all_grads[2], all_grads[3], all_grads[4], all_grads[5], all_grads[6], all_grads[7], all_grads[8], all_grads[9])
```

```python
import functools

import jax
import jax.numpy as jnp
from jax import lax
from jax.experimental import pallas as pl
from jax.experimental.pallas import tpu as pltpu
from jax.sharding import PartitionSpec as P

PIECE = 256
LANES = 128
epsilon = 1e-06
masked_out = -1e30
highest = lax.Precision.HIGHEST
f32 = jnp.float32
bf16 = jnp.bfloat16
VMEM_LIMIT = 58 * 1024 * 1024


def dot(a, b):
    return jnp.dot(a, b, preferred_element_type=f32)


def dot_t(a, b):
    return lax.dot_general(a, b, (((1,), (1,)), ((), ())), preferred_element_type=f32)


def t_dot(a, b):
    return lax.dot_general(a, b, (((0,), (0,)), ((), ())), preferred_element_type=f32)


def exact_dot(a, b):
    return jnp.dot(a, b, precision=highest, preferred_element_type=f32)


def exact_dot_t(a, b):
    return lax.dot_general(
        a, b, (((1,), (1,)), ((), ())), precision=highest, preferred_element_type=f32
    )


def inverse_rms(values):
    return lax.rsqrt(jnp.mean(values * values, -1, keepdims=True) + epsilon)


def norm_back(values, gain, grad):
    scale = inverse_rms(values)
    scaled = values * scale
    grad_gain = jnp.sum(grad * scaled, 0, keepdims=True)
    weighted = gain * grad
    grad_values = scale * weighted - (
        values * (scale * scale * scale) * jnp.mean(weighted * values, -1, keepdims=True)
    )
    return grad_values, grad_gain


def make_mask(place_ref, mask_ref):
    shape = mask_ref.shape
    pos_q = place_ref[0] + lax.broadcasted_iota(jnp.int32, shape, 0)
    pos_k = lax.broadcasted_iota(jnp.int32, shape, 1)
    allowed = pos_k <= pos_q
    for piece in range(2):
        start = place_ref[1 + piece]
        in_q = (pos_q >= start) & (pos_q < start + PIECE)
        in_k = (pos_k >= start) & (pos_k < start + PIECE)
        allowed = allowed | (in_q & in_k)
    mask_ref[...] = jnp.where(allowed, 0.0, masked_out)


def spread(row, block, width):
    return pltpu.roll(
        jnp.broadcast_to(row, (block, width)), width - (block - 1), 1, stride=1, stride_axis=0
    )


def gather_diagonals(sums):
    rows = sums.shape[0]
    while rows > 1:
        half = rows // 2
        sums = pltpu.roll(sums[:half], half, 1) + sums[half:]
        rows = half
    return sums


def chosen_experts(routes_ref, shape):
    lane = lax.broadcasted_iota(jnp.int32, shape, 1)
    return (lane == routes_ref[:, 0:1]) | (lane == routes_ref[:, 1:2])


def forward_kernel(
    n_experts,
    head_dim,
    place_ref,
    x_ref,
    gain_one_ref,
    gain_two_ref,
    wq_ref,
    wk_ref,
    wv_ref,
    wo_ref,
    dist_ref,
    routes_ref,
    router_ref,
    q_out,
    k_out,
    v_out,
    o_out,
    lse_out,
    x_mid_out,
    message_out,
    probs_out,
    h_out,
    total_ref,
    mask_ref,
    bias_ref,
):
    step = pl.program_id(0)
    rows = x_mid_out.shape[0]
    length, width = x_ref.shape
    own = pl.ds(pl.multiple_of(place_ref[0], rows), rows)

    @pl.when(step == 0)
    def _():
        values = x_ref[...].astype(f32)
        h_out[...] = (values * inverse_rms(values) * gain_one_ref[...]).astype(bf16)
        total_ref[...] = jnp.zeros_like(total_ref)
        make_mask(place_ref, mask_ref)

    h_all = h_out[...]
    q_low = dot(h_out[own, :], wq_ref[...]).astype(bf16) * (head_dim**-0.5)
    k_low = dot(h_all, wk_ref[...]).astype(bf16)
    v_low = dot(h_all, wv_ref[...]).astype(bf16)
    q_out[...] = q_low
    k_out[...] = k_low
    v_out[...] = v_low
    block = LANES
    span = dist_ref.shape[2]
    first_half = lax.broadcasted_iota(jnp.int32, (block, LANES), 1) < head_dim
    for head in range(2):
        bias_ref[head] = spread(dist_ref[0, head : head + 1, :], block, span)
    for b in range(rows // block):
        here = slice(b * block, (b + 1) * block)
        offset = pl.multiple_of(length - LANES - block * b - place_ref[0], LANES)
        halves = []
        tops = []
        for head in range(2):
            mine = first_half if head == 0 else ~first_half
            q_head = jnp.where(mine, q_low[here], jnp.zeros((), bf16))
            scores = dot_t(q_head, k_low)
            scores = scores + bias_ref[head, :, pl.ds(offset, length)] + mask_ref[here, :]
            top = jnp.max(scores, -1, keepdims=True)
            exp_scores = jnp.exp(scores - top)
            total = jnp.sum(exp_scores, -1, keepdims=True)
            probs = (exp_scores * (1.0 / total)).astype(bf16)
            halves.append(dot(probs, v_low))
            tops.append(top + jnp.log(total))
        o_out[here, :] = jnp.where(first_half, halves[0], halves[1]).astype(bf16)
        lse_out[here, :] = jnp.where(first_half, tops[0], tops[1])
    total_ref[...] += dot(o_out[...], wo_ref[...])

    @pl.when(step == pl.num_programs(0) - 1)
    def _():
        x_mid = x_ref[own, :].astype(f32) + total_ref[...]
        x_mid_out[...] = x_mid
        h_two = (x_mid * inverse_rms(x_mid) * gain_two_ref[...]).astype(bf16)
        message_out[:, :width] = h_two
        logits = exact_dot(h_two.astype(f32), router_ref[...])
        lane = lax.broadcasted_iota(jnp.int32, logits.shape, 1)
        logits = jnp.where(lane < n_experts, logits, masked_out)
        exp_logits = jnp.exp(logits - jnp.max(logits, -1, keepdims=True))
        probs = exp_logits / jnp.sum(exp_logits, -1, keepdims=True)
        probs_out[...] = probs
        chosen = jnp.where(chosen_experts(routes_ref, probs.shape), probs, 0.0)
        gate = chosen / jnp.sum(chosen, -1, keepdims=True)
        high = gate.astype(bf16)
        low = gate - high.astype(f32)
        message_out[:, width:] = (high.astype(f32) + pltpu.roll(low, n_experts, 1)).astype(bf16)


def attention_forward(
    place, x_all, gain_one, gain_two, weights, dist, routes, router, n_rows, n_experts, head_dim
):
    length, width = x_all.shape
    pairs = width // LANES
    span = dist.shape[2]
    whole = lambda shape: pl.BlockSpec(shape, lambda p, *_: (0,) * len(shape))
    columns = lambda rows: pl.BlockSpec((rows, LANES), lambda p, *_: (0, p))
    matrix = lambda i: pl.BlockSpec((None, width, LANES), lambda p, *_: (i, 0, p))
    out_shape = [
        jax.ShapeDtypeStruct((n_rows, width), bf16),
        jax.ShapeDtypeStruct((length, width), bf16),
        jax.ShapeDtypeStruct((length, width), bf16),
        jax.ShapeDtypeStruct((n_rows, width), bf16),
        jax.ShapeDtypeStruct((n_rows, width), f32),
        jax.ShapeDtypeStruct((n_rows, width), f32),
        jax.ShapeDtypeStruct((n_rows, width + LANES), bf16),
        jax.ShapeDtypeStruct((n_rows, LANES), f32),
        jax.ShapeDtypeStruct((length, width), bf16),
    ]
    return pl.pallas_call(
        functools.partial(forward_kernel, n_experts, head_dim),
        out_shape=out_shape,
        grid_spec=pltpu.PrefetchScalarGridSpec(
            num_scalar_prefetch=1,
            grid=(pairs,),
            in_specs=[
                whole((length, width)),
                whole((1, width)),
                whole((1, width)),
                matrix(0),
                matrix(1),
                matrix(2),
                pl.BlockSpec((None, LANES, width), lambda p, *_: (3, p, 0)),
                pl.BlockSpec((1, 2, span), lambda p, *_: (p, 0, 0)),
                whole((n_rows, 2)),
                whole((width, LANES)),
            ],
            out_specs=[
                columns(n_rows),
                columns(length),
                columns(length),
                columns(n_rows),
                columns(n_rows),
                whole((n_rows, width)),
                whole((n_rows, width + LANES)),
                whole((n_rows, LANES)),
                whole((length, width)),
            ],
            scratch_shapes=[
                pltpu.VMEM((n_rows, width), f32),
                pltpu.VMEM((n_rows, length), f32),
                pltpu.VMEM((2, LANES, span), f32),
            ],
        ),
        compiler_params=pltpu.CompilerParams(vmem_limit_bytes=VMEM_LIMIT),
        cost_estimate=pl.CostEstimate(
            flops=20_000_000_000, transcendentals=0, bytes_accessed=20_000_000
        ),
        name="attention_forward",
    )(place, x_all, gain_one, gain_two, weights, weights, weights, weights, dist, routes, router)


GELU_A = 0.7978845608028654
GELU_B = 0.044715 * GELU_A


def experts_kernel(
    n_experts,
    chunk,
    expert_ref,
    message_ref,
    dy_ref,
    w_in_ref,
    w_out_ref,
    out_ref,
    dh_ref,
    dw_in_ref,
    dw_out_ref,
    dw_in_acc,
    dw_out_acc,
):
    step = pl.program_id(0)
    width = dy_ref.shape[1]
    hidden = w_in_ref.shape[1]
    expert = expert_ref[0]

    @pl.when(step == 0)
    def _():
        dw_in_acc[...] = jnp.zeros_like(dw_in_acc)
        dw_out_acc[...] = jnp.zeros_like(dw_out_acc)

    h = message_ref[:, :width]
    extra = message_ref[:, width:].astype(f32)
    lane = lax.broadcasted_iota(jnp.int32, extra.shape, 1)
    mine = (lane == expert) | (lane == expert + n_experts)
    gate = jnp.sum(jnp.where(mine, extra, 0.0), -1, keepdims=True)
    dy = dy_ref[...]
    out_total = None
    dh_total = None
    dgate = None
    for start in range(0, hidden, chunk):
        part = slice(start, start + chunk)
        up = dot(h, w_in_ref[:, part])
        dact = dot_t(dy, w_out_ref[part, :])
        square = up * up
        tanh = jnp.tanh(up * (GELU_A + GELU_B * square))
        half = 0.5 * up
        more = 1.0 + tanh
        act = half * more
        slope = 0.5 * more + half * (1.0 - tanh * tanh) * (GELU_A + 3.0 * GELU_B * square)
        gated = (gate * act).astype(bf16)
        dgate_part = jnp.sum(act * dact, -1, keepdims=True)
        dup = (gate * dact * slope).astype(bf16)
        out_part = dot(gated, w_out_ref[part, :])
        dh_part = dot_t(dup, w_in_ref[:, part])
        out_total = out_part if out_total is None else out_total + out_part
        dh_total = dh_part if dh_total is None else dh_total + dh_part
        dgate = dgate_part if dgate is None else dgate + dgate_part
        dw_out_acc[part, :] += t_dot(gated, dy)
        dw_in_acc[:, part] += t_dot(h, dup)
    out_ref[...] = out_total.astype(bf16)
    dh_ref[:, :width] = dh_total.astype(bf16)
    high = dgate.astype(bf16).astype(f32)
    low = dgate - high
    dh_ref[:, width:] = jnp.where(
        lane == expert, high, jnp.where(lane == expert + n_experts, low, 0.0)
    ).astype(bf16)

    @pl.when(step == pl.num_programs(0) - 1)
    def _():
        dw_in_ref[...] = dw_in_acc[...].astype(bf16)
        dw_out_ref[...] = dw_out_acc[...].astype(bf16)


def experts(expert, message, dy, w_in, w_out, n_experts, block):
    tokens, width = dy.shape
    hidden = w_in.shape[1]
    whole = lambda shape: pl.BlockSpec(shape, lambda i, *_: (0,) * len(shape))
    rows = lambda columns: pl.BlockSpec((block, columns), lambda i, *_: (i, 0))
    return pl.pallas_call(
        functools.partial(experts_kernel, n_experts, 512),
        out_shape=[
            jax.ShapeDtypeStruct((tokens, width), bf16),
            jax.ShapeDtypeStruct((tokens, width + LANES), bf16),
            jax.ShapeDtypeStruct((width, hidden), bf16),
            jax.ShapeDtypeStruct((hidden, width), bf16),
        ],
        grid_spec=pltpu.PrefetchScalarGridSpec(
            num_scalar_prefetch=1,
            grid=(tokens // block,),
            in_specs=[
                rows(width + LANES),
                rows(width),
                whole((width, hidden)),
                whole((hidden, width)),
            ],
            out_specs=[
                rows(width),
                rows(width + LANES),
                whole((width, hidden)),
                whole((hidden, width)),
            ],
            scratch_shapes=[
                pltpu.VMEM((width, hidden), f32),
                pltpu.VMEM((hidden, width), f32),
            ],
        ),
        compiler_params=pltpu.CompilerParams(vmem_limit_bytes=VMEM_LIMIT),
        cost_estimate=pl.CostEstimate(
            flops=60_000_000_000, transcendentals=0, bytes_accessed=30_000_000
        ),
        name="experts",
    )(expert, message, dy, w_in, w_out)


def backward_kernel(
    n_experts,
    head_dim,
    place_ref,
    back_ref,
    dy_ref,
    x_mid_ref,
    message_ref,
    probs_ref,
    routes_ref,
    router_ref,
    gain_two_ref,
    h_ref,
    wq_ref,
    wk_ref,
    wv_ref,
    wo_ref,
    q_ref,
    k_ref,
    v_ref,
    o_ref,
    lse_ref,
    dist_ref,
    dwq_out,
    dwk_out,
    dwv_out,
    dwo_out,
    dh_own_out,
    dh_other_out,
    dx_mid_out,
    gain_out,
    router_out,
    ddist_out,
    da_ref,
    dh_all_ref,
    dh_mine_ref,
    mask_ref,
    bias_ref,
    dbias_ref,
    dq_ref,
):
    step = pl.program_id(0)
    rows, width = x_mid_ref.shape
    length = h_ref.shape[0]
    own = pl.ds(pl.multiple_of(place_ref[0], rows), rows)

    @pl.when(step == 0)
    def _():
        probs = probs_ref[...]
        chosen = chosen_experts(routes_ref, probs.shape)
        picked = jnp.where(chosen, probs, 0.0)
        total = jnp.sum(picked, -1, keepdims=True)
        gate = picked / total
        extra = back_ref[:, width:].astype(f32)
        dgate = extra + pltpu.roll(extra, LANES - n_experts, 1)
        dgate = jnp.where(chosen, dgate, 0.0)
        shared = jnp.sum(dgate * gate, -1, keepdims=True)
        dprobs = jnp.where(chosen, (dgate - shared) / total, 0.0)
        dlogits = probs * (dprobs - jnp.sum(probs * dprobs, -1, keepdims=True))
        h_two = message_ref[:, :width].astype(f32)
        router_out[...] = lax.dot_general(
            dlogits,
            h_two,
            (((0,), (0,)), ((), ())),
            precision=highest,
            preferred_element_type=f32,
        )
        dh_two = back_ref[:, :width].astype(f32) + exact_dot_t(dlogits, router_ref[...])
        dx, dgain = norm_back(x_mid_ref[...], gain_two_ref[...], dh_two)
        gain_out[...] = dgain
        dx_mid = dx + dy_ref[...].astype(f32)
        dx_mid_out[...] = dx_mid
        da_ref[...] = dx_mid.astype(bf16)
        dh_all_ref[...] = jnp.zeros_like(dh_all_ref)
        dh_mine_ref[...] = jnp.zeros_like(dh_mine_ref)
        make_mask(place_ref, mask_ref)

    da = da_ref[...]
    do = dot_t(da, wo_ref[...]).astype(bf16)
    dwo_out[...] = t_dot(o_ref[...], da).astype(bf16)
    block = LANES
    span = dist_ref.shape[2]
    first_half = lax.broadcasted_iota(jnp.int32, (block, LANES), 1) < head_dim
    zero = jnp.zeros((), bf16)
    k_low = k_ref[...]
    v_low = v_ref[...]
    dk = None
    dv = None
    for head in range(2):
        bias_ref[head] = spread(dist_ref[0, head : head + 1, :], block, span)
        dbias_ref[head] = jnp.zeros_like(dbias_ref[head])
    for b in range(rows // block):
        here = slice(b * block, (b + 1) * block)
        offset = pl.multiple_of(length - LANES - block * b - place_ref[0], LANES)
        halves = []
        for head in range(2):
            mine = first_half if head == 0 else ~first_half
            q_head = jnp.where(mine, q_ref[here, :], zero)
            do_head = jnp.where(mine, do[here], zero)
            scores = dot_t(q_head, k_low)
            scores = scores + bias_ref[head, :, pl.ds(offset, length)] + mask_ref[here, :]
            at = head * head_dim
            probs = jnp.exp(scores - lse_ref[here, at : at + 1])
            dprobs = dot_t(do_head, v_low)
            weighted = probs * dprobs
            ds = weighted - probs * jnp.sum(weighted, -1, keepdims=True)
            ds_low = ds.astype(bf16)
            dbias_ref[head, :, pl.ds(offset, length)] += ds
            halves.append(dot(ds_low, k_low))
            dk_part = t_dot(ds_low, q_head)
            dv_part = t_dot(probs.astype(bf16), do_head)
            dk = dk_part if dk is None else dk + dk_part
            dv = dv_part if dv is None else dv + dv_part
        dq_ref[here, :] = (
            jnp.where(first_half, halves[0], halves[1]) * (head_dim**-0.5)
        ).astype(bf16)
    for head in range(2):
        ddist_out[0, head : head + 1, :] = gather_diagonals(dbias_ref[head])
    dq = dq_ref[...]
    dk = dk.astype(bf16)
    dv = dv.astype(bf16)
    h_all = h_ref[...]
    dwq_out[...] = t_dot(h_ref[own, :], dq).astype(bf16)
    dwk_out[...] = t_dot(h_all, dk).astype(bf16)
    dwv_out[...] = t_dot(h_all, dv).astype(bf16)
    dh_all_ref[...] += dot_t(dk, wk_ref[...]) + dot_t(dv, wv_ref[...])
    dh_mine_ref[...] += dot_t(dq, wq_ref[...])

    @pl.when(step == pl.num_programs(0) - 1)
    def _():
        other = pl.ds(pl.multiple_of(length - rows - place_ref[0], rows), rows)
        dh_own_out[...] = dh_mine_ref[...] + dh_all_ref[own, :]
        dh_other_out[...] = dh_all_ref[other, :].astype(bf16)


def attention_backward(
    place,
    back,
    dy,
    x_mid,
    message,
    probs,
    routes,
    router,
    gain_two,
    h_all,
    weights,
    q,
    k,
    v,
    o,
    lse,
    dist,
    n_experts,
    head_dim,
):
    n_rows, width = x_mid.shape
    length = h_all.shape[0]
    pairs = width // LANES
    span = dist.shape[2]
    whole = lambda shape: pl.BlockSpec(shape, lambda p, *_: (0,) * len(shape))
    columns = lambda rows: pl.BlockSpec((rows, LANES), lambda p, *_: (0, p))
    matrix = lambda i: pl.BlockSpec((None, width, LANES), lambda p, *_: (i, 0, p))
    return pl.pallas_call(
        functools.partial(backward_kernel, n_experts, head_dim),
        out_shape=[
            jax.ShapeDtypeStruct((width, width), bf16),
            jax.ShapeDtypeStruct((width, width), bf16),
            jax.ShapeDtypeStruct((width, width), bf16),
            jax.ShapeDtypeStruct((width, width), bf16),
            jax.ShapeDtypeStruct((n_rows, width), f32),
            jax.ShapeDtypeStruct((n_rows, width), bf16),
            jax.ShapeDtypeStruct((n_rows, width), f32),
            jax.ShapeDtypeStruct((1, width), f32),
            jax.ShapeDtypeStruct((LANES, width), f32),
            jax.ShapeDtypeStruct((pairs, 2, span), f32),
        ],
        grid_spec=pltpu.PrefetchScalarGridSpec(
            num_scalar_prefetch=1,
            grid=(pairs,),
            in_specs=[
                whole((n_rows, width + LANES)),
                whole((n_rows, width)),
                whole((n_rows, width)),
                whole((n_rows, width + LANES)),
                whole((n_rows, LANES)),
                whole((n_rows, 2)),
                whole((width, LANES)),
                whole((1, width)),
                whole((length, width)),
                matrix(0),
                matrix(1),
                matrix(2),
                pl.BlockSpec((None, LANES, width), lambda p, *_: (3, p, 0)),
                columns(n_rows),
                columns(length),
                columns(length),
                columns(n_rows),
                columns(n_rows),
                pl.BlockSpec((1, 2, span), lambda p, *_: (p, 0, 0)),
            ],
            out_specs=[
                columns(width),
                columns(width),
                columns(width),
                pl.BlockSpec((LANES, width), lambda p, *_: (p, 0)),
                whole((n_rows, width)),
                whole((n_rows, width)),
                whole((n_rows, width)),
                whole((1, width)),
                whole((LANES, width)),
                pl.BlockSpec((1, 2, span), lambda p, *_: (p, 0, 0)),
            ],
            scratch_shapes=[
                pltpu.VMEM((n_rows, width), bf16),
                pltpu.VMEM((length, width), f32),
                pltpu.VMEM((n_rows, width), f32),
                pltpu.VMEM((n_rows, length), f32),
                pltpu.VMEM((2, LANES, span), f32),
                pltpu.VMEM((2, LANES, span), f32),
                pltpu.VMEM((n_rows, LANES), bf16),
            ],
        ),
        compiler_params=pltpu.CompilerParams(vmem_limit_bytes=VMEM_LIMIT),
        cost_estimate=pl.CostEstimate(
            flops=40_000_000_000, transcendentals=0, bytes_accessed=30_000_000
        ),
        name="attention_backward",
    )(
        place,
        back,
        dy,
        x_mid,
        message,
        probs,
        routes,
        router,
        gain_two,
        h_all,
        weights,
        weights,
        weights,
        weights,
        q,
        k,
        v,
        o,
        lse,
        dist,
    )


def per_device(
    tokens,
    piece_starts,
    routes,
    buckets,
    attn_q,
    attn_k,
    attn_v,
    attn_o,
    expert_in,
    expert_out,
    gain_attn,
    gain_ffn,
    rel_table,
    router,
    cotangent,
):
    n_rep, n_fsdp, n_seq = (lax.axis_size(a) for a in ("rep", "fsdp", "seq"))
    rep = lax.axis_index("rep")
    seq = lax.axis_index("seq")
    plane = ("rep", "seq")
    n_rows, width = tokens.shape
    n_buckets, n_heads = rel_table.shape
    head_dim = width // n_heads
    n_experts, part_in, hidden = expert_in.shape
    part_out = expert_out.shape[1]
    part_attn = attn_q.shape[0]
    length = n_rows * n_seq
    assert n_experts == n_rep == 4 and n_seq == 2 and 2 * head_dim == LANES
    pairs = n_heads // 2

    place = jnp.concatenate([(seq * n_rows)[None], piece_starts[0]]).astype(jnp.int32)
    pick = lambda array: lax.dynamic_index_in_dim(array, rep, 0, keepdims=False)
    attn_own = pick(jnp.stack([attn_q, attn_k, attn_v, attn_o]))
    attn_line = lax.all_gather(attn_own, "fsdp", axis=0, tiled=False)
    attn_all = lax.all_gather(attn_line, plane, axis=0, tiled=False)
    attn_all = attn_all.reshape(n_rep, n_seq, n_fsdp, part_attn, width)
    weights = attn_all.transpose(0, 2, 1, 3, 4).reshape(n_rep, width, width)
    x_all = lax.all_gather(tokens, "seq", axis=0, tiled=True)

    in_own = pick(expert_in).reshape(part_in, n_fsdp, n_seq, part_out)
    in_own = in_own.transpose(2, 0, 1, 3).reshape(n_seq, part_in, n_fsdp * part_out)
    in_pair = lax.all_to_all(in_own, "seq", split_axis=0, concat_axis=0, tiled=True)
    in_pair = in_pair.reshape(n_seq * part_in, n_fsdp * part_out)
    w_in = lax.all_gather(in_pair, "fsdp", axis=0, tiled=True)
    w_out = lax.all_gather(pick(expert_out), "fsdp", axis=0, tiled=True)
    dy_all = lax.all_gather(cotangent, plane, axis=0, tiled=True)

    match = (buckets[:, None] == jnp.arange(n_buckets, dtype=jnp.int32)[None, :]).astype(f32)
    dist = lax.dot_general(
        rel_table, match, (((0,), (1,)), ((), ())), precision=highest, preferred_element_type=f32
    )
    span = -(-dist.shape[1] // LANES) * LANES
    dist = jnp.pad(dist, ((0, 0), (0, span - dist.shape[1]))).reshape(pairs, 2, span)
    router_wide = jnp.pad(router, ((0, 0), (0, LANES - n_experts)))
    gain_one = gain_attn[None, :]
    gain_two = gain_ffn[None, :]

    q, k, v, o, lse, x_mid, message, probs, h_all = attention_forward(
        place,
        x_all,
        gain_one,
        gain_two,
        weights,
        dist,
        routes,
        router_wide,
        n_rows,
        n_experts,
        head_dim,
    )
    message_all = lax.all_gather(message, plane, axis=0, tiled=True)
    out_part, back_part, dw_in, dw_out = experts(
        rep[None].astype(jnp.int32), message_all, dy_all, w_in, w_out, n_experts, n_rows
    )
    back = lax.psum_scatter(back_part, plane, scatter_dimension=0, tiled=True)
    out_sum = lax.psum_scatter(out_part, plane, scatter_dimension=0, tiled=True)
    out_rows = (x_mid + out_sum.astype(f32)).astype(bf16)

    dwq, dwk, dwv, dwo, dh_own, dh_other, dx_mid, dgain_two, drouter, ddist = attention_backward(
        place,
        back,
        cotangent,
        x_mid,
        message,
        probs,
        routes,
        router_wide,
        gain_two,
        h_all,
        weights,
        q,
        k,
        v,
        o,
        lse,
        dist,
        n_experts,
        head_dim,
    )
    sum_out = lax.psum_scatter(dw_out, "fsdp", scatter_dimension=0, tiled=True)
    sum_in = lax.psum_scatter(dw_in, "fsdp", scatter_dimension=0, tiled=True)
    sum_in = sum_in.reshape(n_seq, part_in, n_fsdp * part_out)
    sum_in = lax.all_to_all(sum_in, "seq", split_axis=0, concat_axis=0, tiled=True)
    sum_in = sum_in.reshape(n_seq, part_in, n_fsdp, part_out).transpose(1, 2, 0, 3)
    sum_in = sum_in.reshape(part_in, hidden)
    grad_out = lax.all_gather(sum_out, "rep", axis=0, tiled=False).astype(f32)
    grad_in = lax.all_gather(sum_in, "rep", axis=0, tiled=False).astype(f32)

    swap = [(0, 1), (1, 0)]
    dh_one = dh_own + lax.ppermute(dh_other, "seq", swap).astype(f32)
    dx, dgain_one = norm_back(tokens.astype(f32), gain_one, dh_one)
    grad_tokens = (dx_mid + dx).astype(bf16)

    attn_grads = jnp.stack([dwq, dwk, dwv, dwo]).reshape(n_rep, n_fsdp, n_seq, part_attn, width)
    attn_grads = attn_grads.transpose(0, 2, 1, 3, 4).reshape(
        n_rep * n_seq * n_fsdp * part_attn, width
    )
    attn_sum = lax.psum_scatter(attn_grads, plane, scatter_dimension=0, tiled=True)
    attn_sum = lax.psum_scatter(attn_sum, "fsdp", scatter_dimension=0, tiled=True)
    attn_sum = lax.all_gather(attn_sum, "rep", axis=0, tiled=False).astype(f32)

    ddist = ddist.reshape(n_heads, span)[:, : buckets.shape[0]]
    table = lax.dot_general(
        match, ddist, (((0,), (1,)), ((), ())), precision=highest, preferred_element_type=f32
    )
    grad_one, grad_two, grad_table, grad_router = lax.psum(
        (dgain_one[0], dgain_two[0], table, drouter[:n_experts].T), ("rep", "fsdp", "seq")
    )
    return (
        out_rows,
        grad_tokens,
        attn_sum[0],
        attn_sum[1],
        attn_sum[2],
        attn_sum[3],
        grad_in,
        grad_out,
        grad_one,
        grad_two,
        grad_table,
        grad_router,
    )


def solution(mesh):
    rows = P(("rep", "fsdp", "seq"), None)
    owned = P(("fsdp", "seq"), None)
    expert = P(None, ("fsdp", "seq"), None)
    in_specs = (
        rows,
        P(("rep", "fsdp"), None),
        rows,
        P(),
        owned,
        owned,
        owned,
        owned,
        expert,
        expert,
        P(),
        P(),
        P(),
        P(),
        rows,
    )
    out_specs = (
        rows,
        rows,
        owned,
        owned,
        owned,
        owned,
        expert,
        expert,
        P(),
        P(),
        P(),
        P(),
    )
    return jax.shard_map(
        per_device, mesh=mesh, in_specs=in_specs, out_specs=out_specs, check_vma=False
    )
```

```python
import functools

import jax
import jax.numpy as jnp
from jax import lax
from jax.experimental import pallas as pl
from jax.experimental.pallas import tpu as pltpu
from jax.sharding import PartitionSpec as P

PIECE = 256
LANES = 128
epsilon = 1e-06
masked_out = -1e30
highest = lax.Precision.HIGHEST
f32 = jnp.float32
bf16 = jnp.bfloat16
VMEM_LIMIT = 58 * 1024 * 1024


def dot(a, b):
    return jnp.dot(a, b, preferred_element_type=f32)


def dot_t(a, b):
    return lax.dot_general(a, b, (((1,), (1,)), ((), ())), preferred_element_type=f32)


def t_dot(a, b):
    return lax.dot_general(a, b, (((0,), (0,)), ((), ())), preferred_element_type=f32)


def exact_dot(a, b):
    return jnp.dot(a, b, precision=highest, preferred_element_type=f32)


def exact_dot_t(a, b):
    return lax.dot_general(
        a, b, (((1,), (1,)), ((), ())), precision=highest, preferred_element_type=f32
    )


def inverse_rms(values):
    return lax.rsqrt(jnp.mean(values * values, -1, keepdims=True) + epsilon)


def norm_back(values, gain, grad):
    scale = inverse_rms(values)
    scaled = values * scale
    grad_gain = jnp.sum(grad * scaled, 0, keepdims=True)
    weighted = gain * grad
    grad_values = scale * weighted - (
        values * (scale * scale * scale) * jnp.mean(weighted * values, -1, keepdims=True)
    )
    return grad_values, grad_gain


def first_row(rows):
    return lax.axis_index("seq") * rows


def make_mask(place_ref, mask_ref):
    shape = mask_ref.shape
    pos_q = first_row(shape[0]) + lax.broadcasted_iota(jnp.int32, shape, 0)
    pos_k = lax.broadcasted_iota(jnp.int32, shape, 1)
    allowed = pos_k <= pos_q
    for piece in range(2):
        start = place_ref[piece]
        in_q = (pos_q >= start) & (pos_q < start + PIECE)
        in_k = (pos_k >= start) & (pos_k < start + PIECE)
        allowed = allowed | (in_q & in_k)
    mask_ref[...] = jnp.where(allowed, 0.0, masked_out)


def spread(row, block, width):
    return pltpu.roll(
        jnp.broadcast_to(row, (block, width)), width - (block - 1), 1, stride=1, stride_axis=0
    )


def gather_diagonals(sums):
    rows = sums.shape[0]
    while rows > 1:
        half = rows // 2
        sums = pltpu.roll(sums[:half], half, 1) + sums[half:]
        rows = half
    return sums


def chosen_experts(routes_ref, shape):
    lane = lax.broadcasted_iota(jnp.int32, shape, 1)
    return (lane == routes_ref[:, 0:1]) | (lane == routes_ref[:, 1:2])


MESH = pl.DeviceIdType.MESH


class Place:
    def __init__(self, n_fsdp):
        self.rep = lax.axis_index("rep")
        self.line = lax.axis_index("fsdp")
        self.seq = lax.axis_index("seq")
        self.n_fsdp = n_fsdp
        self.row = self.rep // 2
        self.core = self.rep % 2

    def mate(self):
        return (self.row * 2 + 1 - self.core, self.line, self.seq)

    def chip(self, rows, columns, core=None):
        core = self.core if core is None else core
        row = (self.row + rows) % 2
        return (row * 2 + core, self.line, (self.seq + columns) % 2)

    def along(self, steps):
        return (self.rep, (self.line + steps) % self.n_fsdp, self.seq)


def meet(partners):
    barrier = pltpu.get_barrier_semaphore()
    for partner in partners:
        pl.semaphore_signal(barrier, inc=1, device_id=partner, device_id_type=MESH)
    pl.semaphore_wait(barrier, len(partners))


class Wires:
    def __init__(self, send, recv):
        self.send, self.recv = send, recv
        self.names = {}

    def copy(self, name, source, target, device):
        index = self.names.setdefault(name, len(self.names))
        return pltpu.make_async_remote_copy(
            src_ref=source,
            dst_ref=target,
            send_sem=self.send.at[index],
            recv_sem=self.recv.at[index],
            device_id=device,
            device_id_type=MESH,
        )


class Planned:
    def __init__(self, plan, send, recv):
        self.plan, self.send, self.recv = plan, send, recv
        self.order = list(plan)

    def __getitem__(self, name):
        source, target, device = self.plan[name]
        index = self.order.index(name)
        return pltpu.make_async_remote_copy(
            src_ref=source,
            dst_ref=target,
            send_sem=self.send.at[index],
            recv_sem=self.recv.at[index],
            device_id=device,
            device_id_type=MESH,
        )


def gather_kernel(
    n_fsdp,
    attn_q,
    attn_k,
    attn_v,
    attn_o,
    tokens,
    expert_in,
    expert_out,
    weights,
    x_all,
    in_pair,
    w_out,
    send,
    recv,
    local,
):
    me = Place(n_fsdp)
    rep, line, seq = me.rep, me.line, me.seq
    far_row = (me.row + 1) % 2 * 2 + me.core
    mate, across, beside = me.mate(), me.chip(1, 0), me.chip(0, 1)
    part_out = expert_out.shape[1]
    wires = Wires(send, recv)
    meet([mate, across, beside, me.along(1), me.along(-1), me.along(2)])
    started = []

    def start(copy):
        copy.start()
        started.append(copy)
        return copy

    for i, matrix in enumerate((attn_q, attn_k, attn_v, attn_o)):

        @pl.when(rep == i)
        def _():
            own = pltpu.make_async_copy(matrix, weights.at[i, line, seq], local.at[n_fsdp])
            own.start()
            own.wait()

    mine = lambda z, r=rep, x=seq: weights.at[r, z, x]
    shifts = (0, 1, -1, 2)
    at = {0: line}
    z_copies = {}
    for shift in shifts[1:]:
        at[shift] = (line - shift) % n_fsdp
        z_copies[shift] = start(
            wires.copy(("z", shift), mine(line), mine(line), me.along(shift))
        )
    x_copies, y_copies, c_copies, far_copies = {}, {}, [], {}

    def spread_out(shift):
        z = at[shift]
        x_copies[shift] = start(wires.copy(("x", shift), mine(z), mine(z), beside))
        y_copies[shift] = start(wires.copy(("y", shift), mine(z), mine(z), across))
        c_copies.append(start(wires.copy(("c", shift), mine(z), mine(z), mate)))

    spread_out(0)
    x_own = pltpu.make_async_copy(tokens, x_all.at[seq], local.at[n_fsdp + 2])
    x_own.start()
    for shift in shifts[1:]:
        z_copies[shift].wait_recv()
        spread_out(shift)
    columns = lambda z, x: pl.ds(pl.multiple_of((z * 2 + x) * part_out, LANES), part_out)
    in_x, in_own = [], []
    for z in range(n_fsdp):
        here = pl.ds(z * part_out, part_out)
        copy = wires.copy(
            ("in", z),
            expert_in.at[rep, :, columns(z, 1 - seq)],
            in_pair.at[seq, :, here],
            beside,
        )
        in_x.append(start(copy))
        copy = pltpu.make_async_copy(
            expert_in.at[rep, :, columns(z, seq)], in_pair.at[seq, :, here], local.at[z]
        )
        copy.start()
        in_own.append(copy)
    out_own = pltpu.make_async_copy(expert_out.at[rep], w_out.at[line], local.at[n_fsdp + 1])
    out_own.start()
    out_copies = {}
    for shift in (1, -1):
        out_copies[shift] = start(
            wires.copy(("out", shift), expert_out.at[rep], w_out.at[line], me.along(shift))
        )
    token_copy = start(wires.copy("tokens", tokens, x_all.at[seq], beside))
    for shift in shifts:
        z = at[shift]
        x_copies[shift].wait_recv()
        near = mine(z, rep, 1 - seq)
        far_copies[shift] = start(wires.copy(("far", shift), near, near, across))
        c_copies.append(start(wires.copy(("cx", shift), near, near, mate)))
    for shift in shifts:
        z = at[shift]
        y_copies[shift].wait_recv()
        there = mine(z, far_row, seq)
        c_copies.append(start(wires.copy(("cy", shift), there, there, mate)))
    for shift in shifts:
        z = at[shift]
        far_copies[shift].wait_recv()
        there = mine(z, far_row, 1 - seq)
        c_copies.append(start(wires.copy(("cf", shift), there, there, mate)))
    half = part_out // 2
    relays = []
    for shift, rows in ((1, pl.ds(0, half)), (-1, pl.ds(half, half))):
        out_copies[shift].wait_recv()
        piece = w_out.at[(line - shift) % n_fsdp, rows]
        relays.append(start(wires.copy(("relay", shift), piece, piece, me.along(shift))))
    for copy in c_copies + relays + in_x + [token_copy]:
        copy.wait_recv()
    for copy in in_own + [out_own, x_own]:
        copy.wait()
    for copy in started:
        copy.wait_send()


def gather(attn, tokens, expert_in, expert_out, n_fsdp):
    part_attn, width = attn[0].shape
    n_rows = tokens.shape[0]
    n_experts, part_in, hidden = expert_in.shape
    part_out = expert_out.shape[1]
    anywhere = pl.BlockSpec(memory_space=pl.ANY)
    weights, x_all, in_pair, w_out = pl.pallas_call(
        functools.partial(gather_kernel, n_fsdp),
        out_shape=[
            jax.ShapeDtypeStruct((4, n_fsdp, 2, part_attn, width), bf16),
            jax.ShapeDtypeStruct((2, n_rows, width), bf16),
            jax.ShapeDtypeStruct((2, part_in, n_fsdp * part_out), bf16),
            jax.ShapeDtypeStruct((n_fsdp, part_out, width), bf16),
        ],
        in_specs=[anywhere] * 7,
        out_specs=[anywhere] * 4,
        scratch_shapes=[
            pltpu.SemaphoreType.DMA((48,)),
            pltpu.SemaphoreType.DMA((48,)),
            pltpu.SemaphoreType.DMA((8,)),
        ],
        compiler_params=pltpu.CompilerParams(collective_id=0, has_side_effects=True),
        name="gather_weights",
    )(*attn, tokens, expert_in, expert_out)
    return (
        weights.reshape(4, n_fsdp * 2 * part_attn, width),
        x_all.reshape(2 * n_rows, width),
        in_pair.reshape(2 * part_in, n_fsdp * part_out),
        w_out.reshape(n_fsdp * part_out, width),
    )


class Background:
    n_in, n_out = 2, 2

    def __init__(self, n_fsdp):
        self.n_fsdp = n_fsdp

    def out_shape(self, n_rows, width, pair_rows, columns):
        return [
            jax.ShapeDtypeStruct((8, n_rows, width), bf16),
            jax.ShapeDtypeStruct((self.n_fsdp, pair_rows, columns), bf16),
        ]

    scratch = (
        pltpu.SemaphoreType.DMA((16,)),
        pltpu.SemaphoreType.DMA((16,)),
        pltpu.SemaphoreType.DMA((2,)),
    )

    def run(self, step, before, ins, outs, scratch):
        dy, in_pair = ins
        dy_all, w_in = outs
        send, recv, local = scratch
        me = Place(self.n_fsdp)
        n_rows = dy.shape[0]
        half = n_rows // 2
        first, second = pl.ds(0, half), pl.ds(half, half)
        core = me.core
        own = 7 * (1 - core)
        mate, across, beside = me.mate(), me.chip(1, 0), me.chip(0, 1)
        slot = dy_all.at
        rows = w_in.shape[1] // 2
        parts = {1: pl.ds(0, rows), -1: pl.ds(rows, rows)}
        passed = {s: w_in.at[(me.line - s) % self.n_fsdp, parts[s]] for s in (1, -1)}
        plan = {
            "x": (dy, slot[1 + core], beside),
            "y": (dy, slot[3 + core], across),
            "c0": (dy, slot[own], mate),
            "c1": (slot[1 + core], slot[1 + core], mate),
            "c2": (slot[3 + core], slot[3 + core], mate),
            "c3": (slot[5 + core], slot[5 + core], mate),
            "xy": (slot[1 + core, first], slot[5 + core, first], across),
            "yx": (slot[3 + core, second], slot[5 + core, second], beside),
            ("z", 1): (in_pair, w_in.at[me.line], me.along(1)),
            ("z", -1): (in_pair, w_in.at[me.line], me.along(-1)),
            ("relay", 1): (passed[1], passed[1], me.along(1)),
            ("relay", -1): (passed[-1], passed[-1], me.along(-1)),
        }
        copies = Planned(plan, send, recv)
        if before:

            @pl.when(step == 0)
            def _():
                meet([mate, across, beside, me.along(1), me.along(-1)])
                for name in (("z", 1), ("z", -1), "x", "y", "c0"):
                    copies[name].start()
                pltpu.make_async_copy(dy, slot[own], local.at[0]).start()
                pltpu.make_async_copy(in_pair, w_in.at[me.line], local.at[1]).start()

            @pl.when(step == 3)
            def _():
                copies["x"].wait_recv()
                copies["xy"].start()
                copies["c1"].start()
                copies["y"].wait_recv()
                copies["yx"].start()
                copies["c2"].start()
                for shift in (1, -1):
                    copies["z", shift].wait_recv()
                    copies["relay", shift].start()

            return

        @pl.when(step == pl.num_programs(0) - 1)
        def _():
            copies["xy"].wait_recv()
            copies["yx"].wait_recv()
            copies["c3"].start()
            for shift in (1, -1):
                copies["relay", shift].wait_recv()
            for name in ("c0", "c1", "c2", "c3"):
                copies[name].wait_recv()
            pltpu.make_async_copy(dy, slot[own], local.at[0]).wait()
            pltpu.make_async_copy(in_pair, w_in.at[me.line], local.at[1]).wait()
            for name in plan:
                copies[name].wait_send()


def forward_kernel(
    background,
    n_experts,
    head_dim,
    place_ref,
    x_ref,
    gain_one_ref,
    gain_two_ref,
    wq_ref,
    wk_ref,
    wv_ref,
    wo_ref,
    dist_ref,
    routes_ref,
    router_ref,
    *refs,
):
    step = pl.program_id(0)
    n_in, n_out = (background.n_in, background.n_out) if background else (0, 0)
    behind_in, refs = refs[:n_in], refs[n_in:]
    q_out, k_out, v_out, o_out, lse_out, x_mid_out, message_out, probs_out, h_out = refs[:9]
    behind_out, refs = refs[9 : 9 + n_out], refs[9 + n_out :]
    total_ref, mask_ref, bias_ref = refs[:3]
    if background:
        background.run(step, True, behind_in, behind_out, refs[3:])
    rows = x_mid_out.shape[0]
    length, width = x_ref.shape
    own = pl.ds(pl.multiple_of(first_row(rows), rows), rows)

    @pl.when(step == 0)
    def _():
        values = x_ref[...].astype(f32)
        h_out[...] = (values * inverse_rms(values) * gain_one_ref[...]).astype(bf16)
        total_ref[...] = jnp.zeros_like(total_ref)
        make_mask(place_ref, mask_ref)

    h_all = h_out[...]
    q_low = dot(h_out[own, :], wq_ref[...]).astype(bf16) * (head_dim**-0.5)
    k_low = dot(h_all, wk_ref[...]).astype(bf16)
    v_low = dot(h_all, wv_ref[...]).astype(bf16)
    q_out[...] = q_low
    k_out[...] = k_low
    v_out[...] = v_low
    block = LANES
    span = dist_ref.shape[2]
    first_half = lax.broadcasted_iota(jnp.int32, (block, LANES), 1) < head_dim
    for head in range(2):
        bias_ref[head] = spread(dist_ref[0, head : head + 1, :], block, span)
    for b in range(rows // block):
        here = slice(b * block, (b + 1) * block)
        offset = pl.multiple_of(length - LANES - block * b - first_row(rows), LANES)
        halves = []
        tops = []
        for head in range(2):
            mine = first_half if head == 0 else ~first_half
            q_head = jnp.where(mine, q_low[here], jnp.zeros((), bf16))
            scores = dot_t(q_head, k_low)
            scores = scores + bias_ref[head, :, pl.ds(offset, length)] + mask_ref[here, :]
            top = jnp.max(scores, -1, keepdims=True)
            exp_scores = jnp.exp(scores - top)
            total = jnp.sum(exp_scores, -1, keepdims=True)
            probs = (exp_scores * (1.0 / total)).astype(bf16)
            halves.append(dot(probs, v_low))
            tops.append(top + jnp.log(total))
        o_out[here, :] = jnp.where(first_half, halves[0], halves[1]).astype(bf16)
        lse_out[here, :] = jnp.where(first_half, tops[0], tops[1])
    total_ref[...] += dot(o_out[...], wo_ref[...])

    @pl.when(step == pl.num_programs(0) - 1)
    def _():
        x_mid = x_ref[own, :].astype(f32) + total_ref[...]
        x_mid_out[...] = x_mid
        h_two = (x_mid * inverse_rms(x_mid) * gain_two_ref[...]).astype(bf16)
        message_out[:, :width] = h_two
        logits = exact_dot(h_two.astype(f32), router_ref[...])
        lane = lax.broadcasted_iota(jnp.int32, logits.shape, 1)
        logits = jnp.where(lane < n_experts, logits, masked_out)
        exp_logits = jnp.exp(logits - jnp.max(logits, -1, keepdims=True))
        probs = exp_logits / jnp.sum(exp_logits, -1, keepdims=True)
        probs_out[...] = probs
        chosen = jnp.where(chosen_experts(routes_ref, probs.shape), probs, 0.0)
        gate = chosen / jnp.sum(chosen, -1, keepdims=True)
        high = gate.astype(bf16)
        low = gate - high.astype(f32)
        message_out[:, width:] = (high.astype(f32) + pltpu.roll(low, n_experts, 1)).astype(bf16)

    if background:
        background.run(step, False, behind_in, behind_out, refs[3:])


def attention_forward(
    place,
    x_all,
    gain_one,
    gain_two,
    weights,
    dist,
    routes,
    router,
    n_rows,
    n_experts,
    head_dim,
    background=None,
    behind=(),
):
    length, width = x_all.shape
    pairs = width // LANES
    span = dist.shape[2]
    whole = lambda shape: pl.BlockSpec(shape, lambda p, *_: (0,) * len(shape))
    columns = lambda rows: pl.BlockSpec((rows, LANES), lambda p, *_: (0, p))
    matrix = lambda i: pl.BlockSpec((None, width, LANES), lambda p, *_: (i, 0, p))
    out_shape = [
        jax.ShapeDtypeStruct((n_rows, width), bf16),
        jax.ShapeDtypeStruct((length, width), bf16),
        jax.ShapeDtypeStruct((length, width), bf16),
        jax.ShapeDtypeStruct((n_rows, width), bf16),
        jax.ShapeDtypeStruct((n_rows, width), f32),
        jax.ShapeDtypeStruct((n_rows, width), f32),
        jax.ShapeDtypeStruct((n_rows, width + LANES), bf16),
        jax.ShapeDtypeStruct((n_rows, LANES), f32),
        jax.ShapeDtypeStruct((length, width), bf16),
    ]
    anywhere = pl.BlockSpec(memory_space=pl.ANY)
    params = {}
    if background:
        out_shape += background.out_shape(n_rows, width, *behind[1].shape)
        params = {"collective_id": 1, "has_side_effects": True}
    return pl.pallas_call(
        functools.partial(forward_kernel, background, n_experts, head_dim),
        out_shape=out_shape,
        grid_spec=pltpu.PrefetchScalarGridSpec(
            num_scalar_prefetch=1,
            grid=(pairs,),
            in_specs=[
                whole((length, width)),
                whole((1, width)),
                whole((1, width)),
                matrix(0),
                matrix(1),
                matrix(2),
                pl.BlockSpec((None, LANES, width), lambda p, *_: (3, p, 0)),
                pl.BlockSpec((1, 2, span), lambda p, *_: (p, 0, 0)),
                whole((n_rows, 2)),
                whole((width, LANES)),
            ]
            + [anywhere] * len(behind),
            out_specs=[
                columns(n_rows),
                columns(length),
                columns(length),
                columns(n_rows),
                columns(n_rows),
                whole((n_rows, width)),
                whole((n_rows, width + LANES)),
                whole((n_rows, LANES)),
                whole((length, width)),
            ]
            + [anywhere] * (background.n_out if background else 0),
            scratch_shapes=[
                pltpu.VMEM((n_rows, width), f32),
                pltpu.VMEM((n_rows, length), f32),
                pltpu.VMEM((2, LANES, span), f32),
            ]
            + list(background.scratch if background else ()),
        ),
        compiler_params=pltpu.CompilerParams(vmem_limit_bytes=VMEM_LIMIT, **params),
        cost_estimate=pl.CostEstimate(
            flops=20_000_000_000, transcendentals=0, bytes_accessed=20_000_000
        ),
        name="attention_forward",
    )(
        place,
        x_all,
        gain_one,
        gain_two,
        weights,
        weights,
        weights,
        weights,
        dist,
        routes,
        router,
        *behind,
    )


GELU_A = 0.7978845608028654
GELU_B = 0.044715 * GELU_A


def experts_kernel(
    n_experts,
    chunk,
    expert_ref,
    message_ref,
    dy_ref,
    w_in_ref,
    w_out_ref,
    out_ref,
    dh_ref,
    dw_in_ref,
    dw_out_ref,
    dw_in_acc,
    dw_out_acc,
):
    step = pl.program_id(0)
    width = dy_ref.shape[1]
    hidden = w_in_ref.shape[1]
    expert = expert_ref[0]

    @pl.when(step == 0)
    def _():
        dw_in_acc[...] = jnp.zeros_like(dw_in_acc)
        dw_out_acc[...] = jnp.zeros_like(dw_out_acc)

    h = message_ref[:, :width]
    extra = message_ref[:, width:].astype(f32)
    lane = lax.broadcasted_iota(jnp.int32, extra.shape, 1)
    mine = (lane == expert) | (lane == expert + n_experts)
    gate = jnp.sum(jnp.where(mine, extra, 0.0), -1, keepdims=True)
    dy = dy_ref[...]
    out_total = None
    dh_total = None
    dgate = None
    for start in range(0, hidden, chunk):
        part = slice(start, start + chunk)
        up = dot(h, w_in_ref[:, part])
        dact = dot_t(dy, w_out_ref[part, :])
        square = up * up
        tanh = jnp.tanh(up * (GELU_A + GELU_B * square))
        half = 0.5 * up
        more = 1.0 + tanh
        act = half * more
        slope = 0.5 * more + half * (1.0 - tanh * tanh) * (GELU_A + 3.0 * GELU_B * square)
        gated = (gate * act).astype(bf16)
        dgate_part = jnp.sum(act * dact, -1, keepdims=True)
        dup = (gate * dact * slope).astype(bf16)
        out_part = dot(gated, w_out_ref[part, :])
        dh_part = dot_t(dup, w_in_ref[:, part])
        out_total = out_part if out_total is None else out_total + out_part
        dh_total = dh_part if dh_total is None else dh_total + dh_part
        dgate = dgate_part if dgate is None else dgate + dgate_part
        dw_out_acc[part, :] += t_dot(gated, dy)
        dw_in_acc[:, part] += t_dot(h, dup)
    out_ref[...] = out_total.astype(bf16)
    dh_ref[:, :width] = dh_total.astype(bf16)
    high = dgate.astype(bf16).astype(f32)
    low = dgate - high
    dh_ref[:, width:] = jnp.where(
        lane == expert, high, jnp.where(lane == expert + n_experts, low, 0.0)
    ).astype(bf16)

    @pl.when(step == pl.num_programs(0) - 1)
    def _():
        dw_in_ref[...] = dw_in_acc[...].astype(bf16)
        dw_out_ref[...] = dw_out_acc[...].astype(bf16)


def experts(expert, message, dy, w_in, w_out, n_experts, block):
    tokens, width = dy.shape
    hidden = w_in.shape[1]
    whole = lambda shape: pl.BlockSpec(shape, lambda i, *_: (0,) * len(shape))
    rows = lambda columns: pl.BlockSpec((block, columns), lambda i, *_: (i, 0))
    return pl.pallas_call(
        functools.partial(experts_kernel, n_experts, 512),
        out_shape=[
            jax.ShapeDtypeStruct((tokens, width), bf16),
            jax.ShapeDtypeStruct((tokens, width + LANES), bf16),
            jax.ShapeDtypeStruct((width, hidden), bf16),
            jax.ShapeDtypeStruct((hidden, width), bf16),
        ],
        grid_spec=pltpu.PrefetchScalarGridSpec(
            num_scalar_prefetch=1,
            grid=(tokens // block,),
            in_specs=[
                rows(width + LANES),
                rows(width),
                whole((width, hidden)),
                whole((hidden, width)),
            ],
            out_specs=[
                rows(width),
                rows(width + LANES),
                whole((width, hidden)),
                whole((hidden, width)),
            ],
            scratch_shapes=[
                pltpu.VMEM((width, hidden), f32),
                pltpu.VMEM((hidden, width), f32),
            ],
        ),
        compiler_params=pltpu.CompilerParams(vmem_limit_bytes=VMEM_LIMIT),
        cost_estimate=pl.CostEstimate(
            flops=60_000_000_000, transcendentals=0, bytes_accessed=30_000_000
        ),
        name="experts",
    )(expert, message, dy, w_in, w_out)


def plane_slot(j):
    return (j + 1) // 2 % 4, (j + 1) % 2


def plane_experts_kernel(
    n_experts,
    chunk,
    n_fsdp,
    message_ref,
    dy_ref,
    w_in_ref,
    w_out_ref,
    back_ref,
    out_half,
    dw_in_ref,
    dw_out_ref,
    h_ref,
    part_ref,
    tx_ref,
    rx_ref,
    fin_ref,
    fin_out_ref,
    land_ref,
    dw_in_acc,
    dw_out_acc,
    send,
    recv,
    tx_sem,
    rx_sem,
    fin_sem,
    land_sem,
    local,
):
    step = pl.program_id(0)
    last = 7
    me = Place(n_fsdp)
    core = me.core
    rows, width = dy_ref.shape
    hidden = w_in_ref.shape[1]
    long = message_ref.shape[1]
    half = rows // 2
    first, second = pl.ds(0, half), pl.ds(half, half)
    mate, across, beside = me.mate(), me.chip(1, 0), me.chip(0, 1)
    own = 7 * (1 - core)
    slot = h_ref.at
    plan = {
        "x": (message_ref, slot[1 + core], beside),
        "y": (message_ref, slot[3 + core], across),
        "c0": (message_ref, slot[own], mate),
        "c1": (slot[1 + core], slot[1 + core], mate),
        "c2": (slot[3 + core], slot[3 + core], mate),
        "c3": (slot[5 + core], slot[5 + core], mate),
        "xy": (slot[1 + core, first], slot[5 + core, first], across),
        "yx": (slot[3 + core, second], slot[5 + core, second], beside),
    }
    copies = Planned(plan, send, recv)

    def to_mate(j):
        return pltpu.make_async_remote_copy(
            src_ref=tx_ref.at[j % 2],
            dst_ref=rx_ref.at[j],
            send_sem=tx_sem.at[j],
            recv_sem=rx_sem.at[j],
            device_id=mate,
            device_id_type=MESH,
        )

    def to_owner(j):
        q, k = plane_slot(j)
        return pltpu.make_async_remote_copy(
            src_ref=fin_ref.at[j % 2],
            dst_ref=land_ref.at[q, core],
            send_sem=fin_sem.at[j],
            recv_sem=land_sem.at[q, core],
            device_id=me.chip(q // 2, q % 2, k),
            device_id_type=MESH,
        )

    def keep_out(j):
        return pltpu.make_async_copy(fin_out_ref.at[j % 2], out_half.at[j], local.at[j])

    def stays(j):
        q, k = plane_slot(j)
        return (q == 0) & (k == core)

    def finish(j):
        to_mate(j).wait_recv()
        mine = part_ref.at[j % 2, pl.ds(core * half, half)]

        @pl.when(j >= 2)
        def _():
            keep_out(j - 2).wait()

        @pl.when((j >= 2) & ~stays(j - 2))
        def _():
            to_owner(j - 2).wait_send()

        fin_out_ref[j % 2] = (mine[:, long:] + rx_ref[j, :, long:].astype(f32)).astype(bf16)
        keep_out(j).start()
        fin_ref[j % 2] = (mine[:, :long] + rx_ref[j, :, :long].astype(f32)).astype(bf16)

        @pl.when(stays(j))
        def _():
            land_ref[0, core] = fin_ref[j % 2]

        @pl.when(~stays(j))
        def _():
            to_owner(j).start()

    @pl.when(step == 0)
    def _():
        meet([mate, across, beside, me.chip(1, 1), me.chip(1, 0, 1 - core), me.chip(0, 1, 1 - core), me.chip(1, 1, 1 - core)])
        copies["x"].start()
        copies["y"].start()
        copies["c0"].start()
        h_ref[own] = message_ref[...]
        dw_in_acc[...] = jnp.zeros_like(dw_in_acc)
        dw_out_acc[...] = jnp.zeros_like(dw_out_acc)
        copies["c0"].wait_recv()

    @pl.when(step == 1)
    def _():
        copies["x"].wait_recv()
        copies["c1"].start()
        copies["xy"].start()

    @pl.when(step == 2)
    def _():
        copies["y"].wait_recv()
        copies["c2"].start()
        copies["yx"].start()

    @pl.when(step == 4)
    def _():
        copies["xy"].wait_recv()
        copies["yx"].wait_recv()
        copies["c3"].start()

    for q in (1, 2, 3):

        @pl.when(step == 2 * q - core)
        def _():
            copies[f"c{q}"].wait_recv()

    expert = me.rep
    h = h_ref[step, :, :width]
    extra = h_ref[step, :, width:].astype(f32)
    lane = lax.broadcasted_iota(jnp.int32, extra.shape, 1)
    mine = (lane == expert) | (lane == expert + n_experts)
    gate = jnp.sum(jnp.where(mine, extra, 0.0), -1, keepdims=True)
    dy = dy_ref[...]
    dgate = None
    part = part_ref.at[step % 2]
    for start in range(0, hidden, chunk):
        piece = slice(start, start + chunk)
        up = dot(h, w_in_ref[:, piece])
        dact = dot_t(dy, w_out_ref[piece, :])
        square = up * up
        tanh = jnp.tanh(up * (GELU_A + GELU_B * square))
        halved = 0.5 * up
        more = 1.0 + tanh
        act = halved * more
        slope = 0.5 * more + halved * (1.0 - tanh * tanh) * (GELU_A + 3.0 * GELU_B * square)
        gated = (gate * act).astype(bf16)
        dgate_part = jnp.sum(act * dact, -1, keepdims=True)
        dup = (gate * dact * slope).astype(bf16)
        out_part = dot(gated, w_out_ref[piece, :])
        dh_part = dot_t(dup, w_in_ref[:, piece])
        if start == 0:
            part[:, long:] = out_part
            part[:, :width] = dh_part
        else:
            part[:, long:] += out_part
            part[:, :width] += dh_part
        dgate = dgate_part if dgate is None else dgate + dgate_part
        dw_out_acc[piece, :] += t_dot(gated, dy)
        dw_in_acc[:, piece] += t_dot(h, dup)
        if start == 0:

            @pl.when(step >= 1)
            def _():
                finish(step - 1)

    high = dgate.astype(bf16).astype(f32)
    low = dgate - high
    part[:, width:long] = jnp.where(
        lane == expert, high, jnp.where(lane == expert + n_experts, low, 0.0)
    )

    @pl.when(step >= 2)
    def _():
        to_mate(step - 2).wait_send()

    tx_ref[step % 2] = part_ref[step % 2, pl.ds((1 - core) * half, half)].astype(bf16)
    to_mate(step).start()

    @pl.when(step == last)
    def _():
        dw_in_ref[...] = dw_in_acc[...].astype(bf16)
        dw_out_ref[...] = dw_out_acc[...].astype(bf16)
        finish(last)
        to_mate(last - 1).wait_send()
        to_mate(last).wait_send()
        keep_out(last - 1).wait()
        keep_out(last).wait()
        to_owner(last - 1).wait_send()

        @pl.when(~stays(last))
        def _():
            to_owner(last).wait_send()

        for name in plan:
            copies[name].wait_send()
        for side in range(2):
            total = None
            for q in range(4):
                arrived = pltpu.make_async_remote_copy(
                    src_ref=fin_ref.at[0],
                    dst_ref=land_ref.at[q, side],
                    send_sem=fin_sem.at[0],
                    recv_sem=land_sem.at[q, side],
                    device_id=mate,
                    device_id_type=MESH,
                )
                if q == 0:

                    @pl.when(core != side)
                    def _():
                        arrived.wait_recv()

                else:
                    arrived.wait_recv()
                landed = land_ref[q, side].astype(f32)
                total = landed if total is None else total + landed
            back_ref[side * half : (side + 1) * half, :] = total


def plane_experts(message, dy_all, w_in, w_out, n_experts, n_fsdp):
    blocks, rows, width = dy_all.shape
    long = message.shape[1]
    hidden = w_in.shape[1]
    half = rows // 2
    once = pl.Buffered(1)
    whole = lambda shape: pl.BlockSpec(shape, lambda i: (0,) * len(shape), pipeline_mode=once)
    both = long + width
    dma = lambda *shape: pltpu.SemaphoreType.DMA(shape)
    return pl.pallas_call(
        functools.partial(plane_experts_kernel, n_experts, 512, n_fsdp),
        out_shape=[
            jax.ShapeDtypeStruct((rows, long), f32),
            jax.ShapeDtypeStruct((blocks, half, width), bf16),
            jax.ShapeDtypeStruct((width, hidden), bf16),
            jax.ShapeDtypeStruct((hidden, width), bf16),
        ],
        grid=(blocks,),
        in_specs=[
            whole((rows, long)),
            pl.BlockSpec((None, rows, width), lambda i: (i, 0, 0)),
            whole((width, hidden)),
            whole((hidden, width)),
        ],
        out_specs=[
            whole((rows, long)),
            pl.BlockSpec(memory_space=pl.ANY),
            whole((width, hidden)),
            whole((hidden, width)),
        ],
        scratch_shapes=[
            pltpu.VMEM((blocks, rows, long), bf16),
            pltpu.VMEM((2, rows, both), f32),
            pltpu.VMEM((2, half, both), bf16),
            pltpu.VMEM((blocks, half, both), bf16),
            pltpu.VMEM((2, half, long), bf16),
            pltpu.VMEM((2, half, width), bf16),
            pltpu.VMEM((4, 2, half, long), bf16),
            pltpu.VMEM((width, hidden), f32),
            pltpu.VMEM((hidden, width), f32),
            dma(8),
            dma(8),
            dma(8),
            dma(8),
            dma(8),
            dma(4, 2),
            dma(8),
        ],
        compiler_params=pltpu.CompilerParams(
            vmem_limit_bytes=VMEM_LIMIT, collective_id=2, has_side_effects=True
        ),
        cost_estimate=pl.CostEstimate(
            flops=60_000_000_000, transcendentals=0, bytes_accessed=30_000_000
        ),
        name="plane_experts",
    )(message, dy_all, w_in, w_out)


class LineSum:
    def __init__(self, me, whole, near, mid, far, mine, send, recv, local):
        self.me, self.whole, self.near, self.mid, self.far = me, whole, near, mid, far
        self.mine, self.local = mine, local
        rows = whole.shape[1]
        half = rows // 2
        self.parts = {1: slice(0, half), -1: slice(half, rows)}
        plan = {}
        for i, shift in enumerate((1, -1)):
            part = pl.ds(i * half, half)
            target = (me.line + 2) % me.n_fsdp
            plan["near", shift] = (whole.at[target, part], near.at[i], me.along(shift))
            plan["far", shift] = (mid.at[i], far.at[i], me.along(shift))
        self.copies = Planned(plan, send, recv)

    def loads(self):
        me = self.me
        for i, shift in enumerate((1, -1)):
            source = self.whole.at[(me.line + shift) % me.n_fsdp]
            yield pltpu.make_async_copy(source, self.mid.at[i], self.local.at[i])
        yield pltpu.make_async_copy(self.whole.at[me.line], self.mine, self.local.at[2])

    def start(self):
        for shift in (1, -1):
            self.copies["near", shift].start()
        for load in self.loads():
            load.start()

    def turn(self):
        for load in self.loads():
            load.wait()
        for i, shift in enumerate((1, -1)):
            self.copies["near", shift].wait_recv()
            part = self.parts[shift]
            total = self.mid[i, part, :].astype(f32) + self.near[i].astype(f32)
            self.mid[i, part, :] = total.astype(bf16)
            self.copies["far", shift].start()

    def total(self):
        for shift in (1, -1):
            self.copies["far", shift].wait_recv()
        total = self.mine[...].astype(f32) + self.far[0].astype(f32) + self.far[1].astype(f32)
        for shift in (1, -1):
            self.copies["near", shift].wait_send()
            self.copies["far", shift].wait_send()
        return total.astype(bf16)

    @staticmethod
    def scratch(rows, columns):
        return [
            pltpu.VMEM((2, rows // 2, columns), bf16),
            pltpu.VMEM((2, rows, columns), bf16),
            pltpu.VMEM((2, rows, columns), bf16),
            pltpu.VMEM((rows, columns), bf16),
            pltpu.SemaphoreType.DMA((4,)),
            pltpu.SemaphoreType.DMA((4,)),
            pltpu.SemaphoreType.DMA((3,)),
        ]


class BackgroundBack:
    n_in, n_out = 3, 2

    def __init__(self, n_fsdp):
        self.n_fsdp = n_fsdp

    def out_shape(self, out_half, dw_out, x_mid):
        return [
            jax.ShapeDtypeStruct(x_mid.shape, bf16),
            jax.ShapeDtypeStruct(dw_out.shape[1:], bf16),
        ]

    def scratch(self, out_half, dw_out, x_mid):
        half, width = out_half.shape[1:]
        return [
            pltpu.VMEM((4, 2, half, width), bf16),
            pltpu.SemaphoreType.DMA((8,)),
            pltpu.SemaphoreType.DMA((4, 2)),
        ] + LineSum.scratch(*dw_out.shape[1:])

    def run(self, step, before, ins, outs, scratch, x_mid):
        out_half, dw_out, _ = ins
        out_rows, sum_out = outs
        land, send, recv = scratch[:3]
        near, mid, far, mine, line_send, line_recv, line_local = scratch[3:]
        me = Place(self.n_fsdp)
        core = me.core
        half = out_half.shape[1]
        line = LineSum(me, dw_out, near, mid, far, mine, line_send, line_recv, line_local)

        def to_owner(j):
            q, k = plane_slot(j)
            return pltpu.make_async_remote_copy(
                src_ref=out_half.at[j],
                dst_ref=land.at[q, core],
                send_sem=send.at[j],
                recv_sem=recv.at[q, core],
                device_id=me.chip(q // 2, q % 2, k),
                device_id_type=MESH,
            )

        def stay(j):
            return pltpu.make_async_copy(out_half.at[j], land.at[0, core], send.at[j])

        if before:

            @pl.when(step == 0)
            def _():
                partners = [me.mate(), me.along(1), me.along(-1)]
                for q in (1, 2, 3):
                    for k in (0, 1):
                        partners.append(me.chip(q // 2, q % 2, (core + k) % 2))
                meet(partners)
                line.start()
                for j in range(8):
                    if j in (0, 7):

                        @pl.when(core == (j + 1) % 2)
                        def _():
                            stay(j).start()

                        @pl.when(core != (j + 1) % 2)
                        def _():
                            to_owner(j).start()

                    else:
                        to_owner(j).start()

            @pl.when(step == 2)
            def _():
                line.turn()

            return

        @pl.when(step == pl.num_programs(0) - 1)
        def _():
            for j in range(8):
                if j in (0, 7):

                    @pl.when(core == (j + 1) % 2)
                    def _():
                        stay(j).wait()

                    @pl.when(core != (j + 1) % 2)
                    def _():
                        to_owner(j).wait_send()

                else:
                    to_owner(j).wait_send()
            for side in range(2):
                here = slice(side * half, (side + 1) * half)
                total = x_mid[here, :]
                for q in range(4):
                    arrived = pltpu.make_async_remote_copy(
                        src_ref=out_half.at[0],
                        dst_ref=land.at[q, side],
                        send_sem=send.at[0],
                        recv_sem=recv.at[q, side],
                        device_id=me.mate(),
                        device_id_type=MESH,
                    )
                    if q == 0:

                        @pl.when(core != side)
                        def _():
                            arrived.wait_recv()

                    else:
                        arrived.wait_recv()
                    total = total + land[q, side].astype(f32)
                out_rows[here, :] = total.astype(bf16)
            sum_out[...] = line.total()


def backward_kernel(
    background,
    n_experts,
    head_dim,
    place_ref,
    back_ref,
    dy_ref,
    x_mid_ref,
    message_ref,
    probs_ref,
    routes_ref,
    router_ref,
    gain_two_ref,
    h_ref,
    wq_ref,
    wk_ref,
    wv_ref,
    wo_ref,
    q_ref,
    k_ref,
    v_ref,
    o_ref,
    lse_ref,
    dist_ref,
    *refs,
):
    step = pl.program_id(0)
    n_in, n_out = (background.n_in, background.n_out) if background else (0, 0)
    behind_in, refs = refs[:n_in], refs[n_in:]
    dwq_out, dwk_out, dwv_out, dwo_out, dh_own_out, dh_other_out = refs[:6]
    dx_mid_out, gain_out, router_out, ddist_out = refs[6:10]
    behind_out, refs = refs[10 : 10 + n_out], refs[10 + n_out :]
    da_ref, dh_all_ref, dh_mine_ref, mask_ref, bias_ref, dbias_ref, dq_ref = refs[:7]
    if background:
        background.run(step, True, behind_in, behind_out, refs[7:], x_mid_ref)
    rows, width = x_mid_ref.shape
    length = h_ref.shape[0]
    own = pl.ds(pl.multiple_of(first_row(rows), rows), rows)

    @pl.when(step == 0)
    def _():
        probs = probs_ref[...]
        chosen = chosen_experts(routes_ref, probs.shape)
        picked = jnp.where(chosen, probs, 0.0)
        total = jnp.sum(picked, -1, keepdims=True)
        gate = picked / total
        extra = back_ref[:, width:].astype(f32)
        dgate = extra + pltpu.roll(extra, LANES - n_experts, 1)
        dgate = jnp.where(chosen, dgate, 0.0)
        shared = jnp.sum(dgate * gate, -1, keepdims=True)
        dprobs = jnp.where(chosen, (dgate - shared) / total, 0.0)
        dlogits = probs * (dprobs - jnp.sum(probs * dprobs, -1, keepdims=True))
        h_two = message_ref[:, :width].astype(f32)
        router_out[...] = lax.dot_general(
            dlogits,
            h_two,
            (((0,), (0,)), ((), ())),
            precision=highest,
            preferred_element_type=f32,
        )
        dh_two = back_ref[:, :width].astype(f32) + exact_dot_t(dlogits, router_ref[...])
        dx, dgain = norm_back(x_mid_ref[...], gain_two_ref[...], dh_two)
        gain_out[...] = dgain
        dx_mid = dx + dy_ref[...].astype(f32)
        dx_mid_out[...] = dx_mid
        da_ref[...] = dx_mid.astype(bf16)
        dh_all_ref[...] = jnp.zeros_like(dh_all_ref)
        dh_mine_ref[...] = jnp.zeros_like(dh_mine_ref)
        make_mask(place_ref, mask_ref)

    da = da_ref[...]
    do = dot_t(da, wo_ref[...]).astype(bf16)
    dwo_out[...] = t_dot(o_ref[...], da).astype(bf16)
    block = LANES
    span = dist_ref.shape[2]
    first_half = lax.broadcasted_iota(jnp.int32, (block, LANES), 1) < head_dim
    zero = jnp.zeros((), bf16)
    k_low = k_ref[...]
    v_low = v_ref[...]
    dk = None
    dv = None
    for head in range(2):
        bias_ref[head] = spread(dist_ref[0, head : head + 1, :], block, span)
        dbias_ref[head] = jnp.zeros_like(dbias_ref[head])
    for b in range(rows // block):
        here = slice(b * block, (b + 1) * block)
        offset = pl.multiple_of(length - LANES - block * b - first_row(rows), LANES)
        halves = []
        for head in range(2):
            mine = first_half if head == 0 else ~first_half
            q_head = jnp.where(mine, q_ref[here, :], zero)
            do_head = jnp.where(mine, do[here], zero)
            scores = dot_t(q_head, k_low)
            scores = scores + bias_ref[head, :, pl.ds(offset, length)] + mask_ref[here, :]
            at = head * head_dim
            probs = jnp.exp(scores - lse_ref[here, at : at + 1])
            dprobs = dot_t(do_head, v_low)
            weighted = probs * dprobs
            ds = weighted - probs * jnp.sum(weighted, -1, keepdims=True)
            ds_low = ds.astype(bf16)
            dbias_ref[head, :, pl.ds(offset, length)] += ds
            halves.append(dot(ds_low, k_low))
            dk_part = t_dot(ds_low, q_head)
            dv_part = t_dot(probs.astype(bf16), do_head)
            dk = dk_part if dk is None else dk + dk_part
            dv = dv_part if dv is None else dv + dv_part
        dq_ref[here, :] = (
            jnp.where(first_half, halves[0], halves[1]) * (head_dim**-0.5)
        ).astype(bf16)
    for head in range(2):
        ddist_out[0, head : head + 1, :] = gather_diagonals(dbias_ref[head])
    dq = dq_ref[...]
    dk = dk.astype(bf16)
    dv = dv.astype(bf16)
    h_all = h_ref[...]
    dwq_out[...] = t_dot(h_ref[own, :], dq).astype(bf16)
    dwk_out[...] = t_dot(h_all, dk).astype(bf16)
    dwv_out[...] = t_dot(h_all, dv).astype(bf16)
    dh_all_ref[...] += dot_t(dk, wk_ref[...]) + dot_t(dv, wv_ref[...])
    dh_mine_ref[...] += dot_t(dq, wq_ref[...])

    @pl.when(step == pl.num_programs(0) - 1)
    def _():
        other = pl.ds(pl.multiple_of(length - rows - first_row(rows), rows), rows)
        dh_own_out[...] = dh_mine_ref[...] + dh_all_ref[own, :]
        dh_other_out[...] = dh_all_ref[other, :].astype(bf16)

    if background:
        background.run(step, False, behind_in, behind_out, refs[7:], x_mid_ref)


def attention_backward(
    place,
    back,
    dy,
    x_mid,
    message,
    probs,
    routes,
    router,
    gain_two,
    h_all,
    weights,
    q,
    k,
    v,
    o,
    lse,
    dist,
    n_experts,
    head_dim,
    background=None,
    behind=(),
):
    n_rows, width = x_mid.shape
    length = h_all.shape[0]
    pairs = width // LANES
    span = dist.shape[2]
    more_shapes, more_scratch, params = [], [], {}
    if background:
        more_shapes = background.out_shape(*behind)
        more_scratch = background.scratch(*behind)
        params = {"collective_id": 3, "has_side_effects": True}
    anywhere = pl.BlockSpec(memory_space=pl.ANY)
    whole = lambda shape: pl.BlockSpec(shape, lambda p, *_: (0,) * len(shape))
    columns = lambda rows: pl.BlockSpec((rows, LANES), lambda p, *_: (0, p))
    matrix = lambda i: pl.BlockSpec((None, width, LANES), lambda p, *_: (i, 0, p))
    return pl.pallas_call(
        functools.partial(backward_kernel, background, n_experts, head_dim),
        out_shape=[
            jax.ShapeDtypeStruct((width, width), bf16),
            jax.ShapeDtypeStruct((width, width), bf16),
            jax.ShapeDtypeStruct((width, width), bf16),
            jax.ShapeDtypeStruct((width, width), bf16),
            jax.ShapeDtypeStruct((n_rows, width), f32),
            jax.ShapeDtypeStruct((n_rows, width), bf16),
            jax.ShapeDtypeStruct((n_rows, width), f32),
            jax.ShapeDtypeStruct((1, width), f32),
            jax.ShapeDtypeStruct((LANES, width), f32),
            jax.ShapeDtypeStruct((pairs, 2, span), f32),
        ]
        + more_shapes,
        grid_spec=pltpu.PrefetchScalarGridSpec(
            num_scalar_prefetch=1,
            grid=(pairs,),
            in_specs=[
                whole((n_rows, width + LANES)),
                whole((n_rows, width)),
                whole((n_rows, width)),
                whole((n_rows, width + LANES)),
                whole((n_rows, LANES)),
                whole((n_rows, 2)),
                whole((width, LANES)),
                whole((1, width)),
                whole((length, width)),
                matrix(0),
                matrix(1),
                matrix(2),
                pl.BlockSpec((None, LANES, width), lambda p, *_: (3, p, 0)),
                columns(n_rows),
                columns(length),
                columns(length),
                columns(n_rows),
                columns(n_rows),
                pl.BlockSpec((1, 2, span), lambda p, *_: (p, 0, 0)),
            ]
            + [anywhere] * len(behind),
            out_specs=[
                columns(width),
                columns(width),
                columns(width),
                pl.BlockSpec((LANES, width), lambda p, *_: (p, 0)),
                whole((n_rows, width)),
                whole((n_rows, width)),
                whole((n_rows, width)),
                whole((1, width)),
                whole((LANES, width)),
                pl.BlockSpec((1, 2, span), lambda p, *_: (p, 0, 0)),
            ]
            + [whole(s.shape) for s in more_shapes],
            scratch_shapes=[
                pltpu.VMEM((n_rows, width), bf16),
                pltpu.VMEM((length, width), f32),
                pltpu.VMEM((n_rows, width), f32),
                pltpu.VMEM((n_rows, length), f32),
                pltpu.VMEM((2, LANES, span), f32),
                pltpu.VMEM((2, LANES, span), f32),
                pltpu.VMEM((n_rows, LANES), bf16),
            ]
            + more_scratch,
        ),
        compiler_params=pltpu.CompilerParams(vmem_limit_bytes=VMEM_LIMIT, **params),
        cost_estimate=pl.CostEstimate(
            flops=40_000_000_000, transcendentals=0, bytes_accessed=30_000_000
        ),
        name="attention_backward",
    )(
        place,
        back,
        dy,
        x_mid,
        message,
        probs,
        routes,
        router,
        gain_two,
        h_all,
        weights,
        weights,
        weights,
        weights,
        q,
        k,
        v,
        o,
        lse,
        dist,
        *behind,
    )


def finish_kernel(
    n_fsdp,
    n_experts,
    n_heads,
    dwq,
    dwk,
    dwv,
    dwo,
    sum_out,
    dw_in,
    dh_other,
    dh_own_ref,
    dx_mid_ref,
    tokens_ref,
    gain_one_ref,
    dgain_two_ref,
    drouter_ref,
    ddist_ref,
    match_ref,
    attn_out,
    grad_in,
    grad_out,
    tokens_out,
    small_ref,
    mine_ref,
    rx_ref,
    land_ref,
    line_ref,
    line_land,
    dh_land,
    in_ref,
    small_land,
    near,
    mid,
    far,
    own_ref,
    line_send,
    line_recv,
    line_local,
    send,
    recv,
    local,
):
    me = Place(n_fsdp)
    rep, line, seq, core, row = me.rep, me.line, me.seq, me.core, me.row
    mate, across, beside, corner = me.mate(), me.chip(1, 0), me.chip(0, 1), me.chip(1, 1)
    far_row = (row + 1) % 2
    far_rep = far_row * 2 + core
    pieces = dw_in.shape[0]
    part_out = grad_out.shape[1]
    part_in = grad_in.shape[1]
    columns = lambda z, x: pl.ds(pl.multiple_of((z * 2 + x) * part_out, LANES), part_out)
    flip = lambda place: place + 1 - 2 * (place % 2)
    hop = lambda place: (rep, place, seq)
    cube = [mate, across, beside, hop(flip(line)), hop((line + 2) % n_fsdp)]
    plan = {
        "pair0": (None, rx_ref.at[0], mate),
        "pair1": (None, rx_ref.at[1], mate),
        "dh": (dh_other, dh_land, beside),
        "out_c": (sum_out, grad_out.at[rep], mate),
        "out_y": (sum_out, grad_out.at[rep], across),
        "out_f": (grad_out.at[far_rep], grad_out.at[far_rep], mate),
        "to_y": (mine_ref.at[far_row, :, seq], land_ref.at[1], across),
        "to_xy": (mine_ref.at[far_row, :, 1 - seq], land_ref.at[2], corner),
        "to_x": (mine_ref.at[row, :, 1 - seq], land_ref.at[0], beside),
        "attn_c": (attn_out.at[rep], attn_out.at[rep], mate),
        "attn_y": (attn_out.at[rep], attn_out.at[rep], across),
        "attn_f": (attn_out.at[far_rep], attn_out.at[far_rep], mate),
        "in_c": (grad_in.at[rep], grad_in.at[rep], mate),
        "in_y": (grad_in.at[rep], grad_in.at[rep], across),
        "in_f": (grad_in.at[far_rep], grad_in.at[far_rep], mate),
    }
    for i, shift in enumerate((1, -1, 2)):
        target = (line + shift) % n_fsdp
        plan["line", i] = (line_ref.at[target], line_land.at[i], me.along(shift))
    for z in range(n_fsdp):
        plan["in_x", z] = (
            in_ref.at[1 - seq, :, pl.ds(z * part_out, part_out)],
            grad_in.at[rep, :, columns(z, seq)],
            beside,
        )
    for i, partner in enumerate(cube):
        plan["small", i] = (small_ref, small_land.at[i], partner)
    copies = Planned(plan, send, recv)
    adds = LineSum(me, dw_in, near, mid, far, own_ref, line_send, line_recv, line_local)
    matrices = (dwq, dwk, dwv, dwo)

    def pair(side, i):
        plan[f"pair{i}"] = (matrices[2 * i + 1 - side], rx_ref.at[i], mate)
        return copies[f"pair{i}"]

    keep = lambda side, i: pltpu.make_async_copy(
        matrices[2 * i + side], mine_ref.at[i], local.at[i]
    )
    own_out = lambda: pltpu.make_async_copy(sum_out, grad_out.at[rep], local.at[2])

    meet([mate, across, beside, corner, me.along(1), me.along(-1), me.along(2)])
    for side in (0, 1):

        @pl.when(core == side)
        def _():
            for i in (0, 1):
                pair(side, i).start()
                keep(side, i).start()

    adds.start()
    copies["dh"].start()
    copies["out_y"].start()
    copies["out_c"].start()
    own_out().start()
    for i in (0, 1):
        keep(0, i).wait()
        pair(0, i).wait_recv()
    for i in (0, 1):
        total = mine_ref[i].astype(f32) + rx_ref[i].astype(f32)
        mine_ref[i] = total.astype(bf16)
    copies["to_y"].start()
    copies["to_x"].start()
    copies["to_xy"].start()
    small_ref[...] = jnp.zeros_like(small_ref)
    small_ref[1:2, :] = dgain_two_ref[...]
    small_ref[2 : 2 + n_experts, :] = drouter_ref[:n_experts, :]
    small_ref[8 : 8 + n_heads, :LANES] = exact_dot_t(ddist_ref[...], match_ref[...])
    adds.turn()
    copies["dh"].wait_recv()
    dh_one = dh_own_ref[...] + dh_land[...].astype(f32)
    dx, dgain_one = norm_back(tokens_ref[...].astype(f32), gain_one_ref[...], dh_one)
    tokens_out[...] = (dx_mid_ref[...] + dx).astype(bf16)
    small_ref[0:1, :] = dgain_one
    copies["out_y"].wait_recv()
    copies["out_f"].start()
    for i in range(len(cube)):
        copies["small", i].start()
        copies["small", i].wait_recv()
        copies["small", i].wait_send()
        small_ref[...] = small_ref[...] + small_land[i]
    copies["to_x"].wait_recv()
    copies["to_y"].wait_recv()
    copies["to_xy"].wait_recv()
    for z in range(n_fsdp):
        total = mine_ref[row, z, seq].astype(f32)
        for i in range(3):
            total = total + land_ref[i, z].astype(f32)
        line_ref[z] = total.astype(bf16)
    for i in range(3):
        copies["line", i].start()
    in_ref[...] = adds.total().reshape(in_ref.shape)
    for z in range(n_fsdp):
        copies["in_x", z].start()
    kept = []
    for z in range(n_fsdp):
        source = in_ref.at[seq, :, pl.ds(z * part_out, part_out)]
        target = grad_in.at[rep, :, columns(z, seq)]
        kept.append(pltpu.make_async_copy(source, target, local.at[4 + z]))
        kept[-1].start()
    total = line_ref[line].astype(f32)
    for i in range(3):
        copies["line", i].wait_recv()
        total = total + line_land[i].astype(f32)
    line_land[3] = total.astype(bf16)
    own_attn = pltpu.make_async_copy(line_land.at[3], attn_out.at[rep], local.at[3])
    own_attn.start()
    own_attn.wait()
    copies["attn_y"].start()
    copies["attn_c"].start()
    for copy in kept:
        copy.wait()
    for z in range(n_fsdp):
        copies["in_x", z].wait_recv()
    copies["in_y"].start()
    copies["in_c"].start()
    copies["attn_y"].wait_recv()
    copies["attn_f"].start()
    copies["in_y"].wait_recv()
    copies["in_f"].start()
    own_out().wait()
    for name in ("out_c", "out_f", "attn_c", "attn_f", "in_c", "in_f"):
        copies[name].wait_recv()
    for name in plan:
        if name[0] != "small":
            copies[name].wait_send()


def finish(
    attn_grads,
    sum_out,
    dw_in,
    dh_other,
    dh_own,
    dx_mid,
    tokens,
    gain_one,
    dgain_two,
    drouter,
    ddist,
    match,
    n_fsdp,
    n_experts,
    part_in,
    hidden,
):
    n_rows, width = tokens.shape
    n_heads = ddist.shape[0]
    part_attn = width // (2 * n_fsdp)
    part_out = sum_out.shape[0]
    pair_rows, columns = dw_in.shape[1:]
    anywhere = pl.BlockSpec(memory_space=pl.ANY)
    inside = pl.BlockSpec(memory_space=pltpu.VMEM)
    dma = lambda n: pltpu.SemaphoreType.DMA((n,))
    split = (n_fsdp, 2, part_attn, width)
    attn_grads = [g.reshape(split) for g in attn_grads]
    return pl.pallas_call(
        functools.partial(finish_kernel, n_fsdp, n_experts, n_heads),
        out_shape=[
            jax.ShapeDtypeStruct((4, part_attn, width), bf16),
            jax.ShapeDtypeStruct((n_experts, part_in, hidden), bf16),
            jax.ShapeDtypeStruct((n_experts, part_out, width), bf16),
            jax.ShapeDtypeStruct((n_rows, width), bf16),
            jax.ShapeDtypeStruct((24, width), f32),
        ],
        in_specs=[anywhere] * 7 + [inside] * 8,
        out_specs=[anywhere] * 3 + [inside] * 2,
        scratch_shapes=[
            pltpu.VMEM((2,) + split, bf16),
            pltpu.VMEM((2,) + split, bf16),
            pltpu.VMEM((3, n_fsdp, part_attn, width), bf16),
            pltpu.VMEM((n_fsdp, part_attn, width), bf16),
            pltpu.VMEM((4, part_attn, width), bf16),
            pltpu.VMEM((n_rows, width), bf16),
            pltpu.VMEM((2, part_in, columns), bf16),
            pltpu.VMEM((5, 24, width), f32),
        ]
        + LineSum.scratch(pair_rows, columns)
        + [dma(32), dma(32), dma(12)],
        compiler_params=pltpu.CompilerParams(
            vmem_limit_bytes=VMEM_LIMIT, collective_id=4, has_side_effects=True
        ),
        name="finish_gradients",
    )(
        *attn_grads,
        sum_out,
        dw_in,
        dh_other,
        dh_own,
        dx_mid,
        tokens,
        gain_one,
        dgain_two,
        drouter,
        ddist,
        match,
    )


def per_device(
    tokens,
    piece_starts,
    routes,
    buckets,
    attn_q,
    attn_k,
    attn_v,
    attn_o,
    expert_in,
    expert_out,
    gain_attn,
    gain_ffn,
    rel_table,
    router,
    cotangent,
):
    n_rep, n_fsdp, n_seq = (lax.axis_size(a) for a in ("rep", "fsdp", "seq"))
    rep = lax.axis_index("rep")
    seq = lax.axis_index("seq")
    plane = ("rep", "seq")
    n_rows, width = tokens.shape
    n_buckets, n_heads = rel_table.shape
    head_dim = width // n_heads
    n_experts, part_in, hidden = expert_in.shape
    part_out = expert_out.shape[1]
    part_attn = attn_q.shape[0]
    length = n_rows * n_seq
    assert n_experts == n_rep == 4 and n_seq == 2 and 2 * head_dim == LANES
    pairs = n_heads // 2

    place = piece_starts[0]
    near = n_fsdp == 4 and part_attn % 16 == 0
    pick = lambda array: lax.dynamic_index_in_dim(array, rep, 0, keepdims=False)
    if near:
        weights, x_all, in_pair, w_out = gather(
            (attn_q, attn_k, attn_v, attn_o), tokens, expert_in, expert_out, n_fsdp
        )
    else:
        attn_own = pick(jnp.stack([attn_q, attn_k, attn_v, attn_o]))
        attn_line = lax.all_gather(attn_own, "fsdp", axis=0, tiled=False)
        attn_all = lax.all_gather(attn_line, plane, axis=0, tiled=False)
        attn_all = attn_all.reshape(n_rep, n_seq, n_fsdp, part_attn, width)
        weights = attn_all.transpose(0, 2, 1, 3, 4).reshape(n_rep, width, width)
        x_all = lax.all_gather(tokens, "seq", axis=0, tiled=True)
        in_own = pick(expert_in).reshape(part_in, n_fsdp, n_seq, part_out)
        in_own = in_own.transpose(2, 0, 1, 3).reshape(n_seq, part_in, n_fsdp * part_out)
        in_pair = lax.all_to_all(in_own, "seq", split_axis=0, concat_axis=0, tiled=True)
        in_pair = in_pair.reshape(n_seq * part_in, n_fsdp * part_out)
        w_in = lax.all_gather(in_pair, "fsdp", axis=0, tiled=True)
        w_out = lax.all_gather(pick(expert_out), "fsdp", axis=0, tiled=True)
        dy_all = lax.all_gather(cotangent, plane, axis=0, tiled=True)

    match = (buckets[:, None] == jnp.arange(n_buckets, dtype=jnp.int32)[None, :]).astype(f32)
    dist = lax.dot_general(
        rel_table, match, (((0,), (1,)), ((), ())), precision=highest, preferred_element_type=f32
    )
    span = -(-dist.shape[1] // LANES) * LANES
    dist = jnp.pad(dist, ((0, 0), (0, span - dist.shape[1]))).reshape(pairs, 2, span)
    router_wide = jnp.pad(router, ((0, 0), (0, LANES - n_experts)))
    gain_one = gain_attn[None, :]
    gain_two = gain_ffn[None, :]

    q, k, v, o, lse, x_mid, message, probs, h_all, *gathered = attention_forward(
        place,
        x_all,
        gain_one,
        gain_two,
        weights,
        dist,
        routes,
        router_wide,
        n_rows,
        n_experts,
        head_dim,
        Background(n_fsdp) if near else None,
        (cotangent, in_pair) if near else (),
    )
    if near:
        dy_all = gathered[0]
        w_in = gathered[1].reshape(width, n_fsdp * part_out)
    behind = ()
    if near:
        back, out_half, dw_in, dw_out = plane_experts(
            message, dy_all, w_in, w_out, n_experts, n_fsdp
        )
        behind = (out_half, dw_out.reshape(n_fsdp, part_out, width), x_mid)
    else:
        message_all = lax.all_gather(message, plane, axis=0, tiled=True)
        out_part, back_part, dw_in, dw_out = experts(
            rep[None].astype(jnp.int32), message_all, dy_all, w_in, w_out, n_experts, n_rows
        )
        back = lax.psum_scatter(back_part, plane, scatter_dimension=0, tiled=True)
        out_sum = lax.psum_scatter(out_part, plane, scatter_dimension=0, tiled=True)
        out_rows = (x_mid + out_sum.astype(f32)).astype(bf16)

    grads = attention_backward(
        place,
        back,
        cotangent,
        x_mid,
        message,
        probs,
        routes,
        router_wide,
        gain_two,
        h_all,
        weights,
        q,
        k,
        v,
        o,
        lse,
        dist,
        n_experts,
        head_dim,
        BackgroundBack(n_fsdp) if near else None,
        behind,
    )
    dwq, dwk, dwv, dwo, dh_own, dh_other, dx_mid, dgain_two, drouter, ddist = grads[:10]
    if near:
        out_rows, sum_out = grads[10:]
        match_wide = jnp.pad(match.T, ((0, LANES - n_buckets), (0, span - match.shape[0])))
        attn_sum, grad_in, grad_out, grad_tokens, small = finish(
            (dwq, dwk, dwv, dwo),
            sum_out,
            dw_in.reshape(n_fsdp, n_seq * part_in, n_fsdp * part_out),
            dh_other,
            dh_own,
            dx_mid,
            tokens,
            gain_one,
            dgain_two,
            drouter,
            ddist.reshape(n_heads, span),
            match_wide,
            n_fsdp,
            n_experts,
            part_in,
            hidden,
        )
        grad_one, grad_two = small[0], small[1]
        grad_router = small[2 : 2 + n_experts].T
        grad_table = small[8 : 8 + n_heads, :n_buckets].T
    else:
        sum_out = lax.psum_scatter(dw_out, "fsdp", scatter_dimension=0, tiled=True)
        sum_in = lax.psum_scatter(dw_in, "fsdp", scatter_dimension=0, tiled=True)
        sum_in = sum_in.reshape(n_seq, part_in, n_fsdp * part_out)
        sum_in = lax.all_to_all(sum_in, "seq", split_axis=0, concat_axis=0, tiled=True)
        sum_in = sum_in.reshape(n_seq, part_in, n_fsdp, part_out).transpose(1, 2, 0, 3)
        sum_in = sum_in.reshape(part_in, hidden)
        grad_out = lax.all_gather(sum_out, "rep", axis=0, tiled=False)
        grad_in = lax.all_gather(sum_in, "rep", axis=0, tiled=False)
        swap = [(0, 1), (1, 0)]
        dh_one = dh_own + lax.ppermute(dh_other, "seq", swap).astype(f32)
        dx, dgain_one = norm_back(tokens.astype(f32), gain_one, dh_one)
        grad_tokens = (dx_mid + dx).astype(bf16)
        attn_grads = jnp.stack([dwq, dwk, dwv, dwo])
        attn_grads = attn_grads.reshape(n_rep, n_fsdp, n_seq, part_attn, width)
        attn_grads = attn_grads.transpose(0, 2, 1, 3, 4)
        attn_grads = attn_grads.reshape(n_rep * n_seq * n_fsdp * part_attn, width)
        attn_sum = lax.psum_scatter(attn_grads, plane, scatter_dimension=0, tiled=True)
        attn_sum = lax.psum_scatter(attn_sum, "fsdp", scatter_dimension=0, tiled=True)
        attn_sum = lax.all_gather(attn_sum, "rep", axis=0, tiled=False)
        ddist = ddist.reshape(n_heads, span)[:, : buckets.shape[0]]
        table = lax.dot_general(
            match,
            ddist,
            (((0,), (1,)), ((), ())),
            precision=highest,
            preferred_element_type=f32,
        )
        grad_one, grad_two, grad_table, grad_router = lax.psum(
            (dgain_one[0], dgain_two[0], table, drouter[:n_experts].T), ("rep", "fsdp", "seq")
        )
    attn_sum = attn_sum.astype(f32)
    return (
        out_rows,
        grad_tokens,
        attn_sum[0],
        attn_sum[1],
        attn_sum[2],
        attn_sum[3],
        grad_in.astype(f32),
        grad_out.astype(f32),
        grad_one,
        grad_two,
        grad_table,
        grad_router,
    )


def solution(mesh):
    rows = P(("rep", "fsdp", "seq"), None)
    owned = P(("fsdp", "seq"), None)
    expert = P(None, ("fsdp", "seq"), None)
    in_specs = (
        rows,
        P(("rep", "fsdp"), None),
        rows,
        P(),
        owned,
        owned,
        owned,
        owned,
        expert,
        expert,
        P(),
        P(),
        P(),
        P(),
        rows,
    )
    out_specs = (
        rows,
        rows,
        owned,
        owned,
        owned,
        owned,
        expert,
        expert,
        P(),
        P(),
        P(),
        P(),
    )
    return jax.shard_map(
        per_device, mesh=mesh, in_specs=in_specs, out_specs=out_specs, check_vma=False
    )
```

```python
import functools

import jax
import jax.numpy as jnp
from jax import lax
from jax.experimental import pallas as pl
from jax.experimental.pallas import tpu as pltpu
from jax.sharding import PartitionSpec as P

PIECE = 256
LANES = 128
epsilon = 1e-06
masked_out = -1e30
highest = lax.Precision.HIGHEST
f32 = jnp.float32
bf16 = jnp.bfloat16
VMEM_LIMIT = 58 * 1024 * 1024


def dot(a, b):
    return jnp.dot(a, b, preferred_element_type=f32)


def dot_t(a, b):
    return lax.dot_general(a, b, (((1,), (1,)), ((), ())), preferred_element_type=f32)


def t_dot(a, b):
    return lax.dot_general(a, b, (((0,), (0,)), ((), ())), preferred_element_type=f32)


def exact_dot(a, b):
    return jnp.dot(a, b, precision=highest, preferred_element_type=f32)


def exact_dot_t(a, b):
    return lax.dot_general(
        a, b, (((1,), (1,)), ((), ())), precision=highest, preferred_element_type=f32
    )


def inverse_rms(values):
    return lax.rsqrt(jnp.mean(values * values, -1, keepdims=True) + epsilon)


def norm_back(values, gain, grad):
    scale = inverse_rms(values)
    scaled = values * scale
    grad_gain = jnp.sum(grad * scaled, 0, keepdims=True)
    weighted = gain * grad
    grad_values = scale * weighted - (
        values * (scale * scale * scale) * jnp.mean(weighted * values, -1, keepdims=True)
    )
    return grad_values, grad_gain


def first_row(rows):
    return lax.axis_index("seq") * rows


def make_mask(place_ref, mask_ref):
    shape = mask_ref.shape
    pos_q = first_row(shape[0]) + lax.broadcasted_iota(jnp.int32, shape, 0)
    pos_k = lax.broadcasted_iota(jnp.int32, shape, 1)
    allowed = pos_k <= pos_q
    for piece in range(2):
        start = place_ref[piece]
        in_q = (pos_q >= start) & (pos_q < start + PIECE)
        in_k = (pos_k >= start) & (pos_k < start + PIECE)
        allowed = allowed | (in_q & in_k)
    mask_ref[...] = jnp.where(allowed, 0.0, masked_out)


def spread(row, block, width):
    return pltpu.roll(
        jnp.broadcast_to(row, (block, width)), width - (block - 1), 1, stride=1, stride_axis=0
    )


def gather_diagonals(sums):
    rows = sums.shape[0]
    while rows > 1:
        half = rows // 2
        sums = pltpu.roll(sums[:half], half, 1) + sums[half:]
        rows = half
    return sums


def chosen_experts(pack_ref, shape):
    lane = lax.broadcasted_iota(jnp.int32, shape, 1).astype(f32)
    routes = pack_ref[24:32, : shape[0]].T
    return (lane == routes[:, 0:1]) | (lane == routes[:, 1:2])


def pack_small(router, gain_attn, gain_ffn, buckets, rel_table, routes, span):
    def rows(array, count):
        array = array.astype(f32)
        return jnp.pad(array, ((0, count - array.shape[0]), (0, span - array.shape[1])))

    return jnp.concatenate(
        [
            rows(router.T, 4),
            rows(gain_attn[None, :], 1),
            rows(gain_ffn[None, :], 1),
            rows(buckets[None, :], 2),
            rows(rel_table.T, 16),
            rows(routes.T, 8),
        ]
    )


def router_rows(pack_ref, n_experts, width):
    first = pack_ref[0:8, :width]
    row = lax.broadcasted_iota(jnp.int32, first.shape, 0)
    first = jnp.where(row < n_experts, first, 0.0)
    return jnp.concatenate([first, jnp.zeros((LANES - 8, width), f32)])


def bucket_match(pack_ref):
    shape = (LANES, pack_ref.shape[1])
    bucket = lax.broadcasted_iota(jnp.int32, shape, 0).astype(f32)
    return (bucket == pack_ref[6:7, :]).astype(f32)


def distances(pack_ref):
    return exact_dot(pack_ref[8:24, :LANES], bucket_match(pack_ref))


MESH = pl.DeviceIdType.MESH


class Place:
    def __init__(self, n_fsdp):
        self.rep = lax.axis_index("rep")
        self.line = lax.axis_index("fsdp")
        self.seq = lax.axis_index("seq")
        self.n_fsdp = n_fsdp
        self.row = self.rep // 2
        self.core = self.rep % 2

    def mate(self):
        return (self.row * 2 + 1 - self.core, self.line, self.seq)

    def chip(self, rows, columns, core=None):
        core = self.core if core is None else core
        row = (self.row + rows) % 2
        return (row * 2 + core, self.line, (self.seq + columns) % 2)

    def along(self, steps):
        return (self.rep, (self.line + steps) % self.n_fsdp, self.seq)


def meet(partners):
    barrier = pltpu.get_barrier_semaphore()
    for partner in partners:
        pl.semaphore_signal(barrier, inc=1, device_id=partner, device_id_type=MESH)
    pl.semaphore_wait(barrier, len(partners))


class Wires:
    def __init__(self, send, recv):
        self.send, self.recv = send, recv
        self.names = {}

    def copy(self, name, source, target, device):
        index = self.names.setdefault(name, len(self.names))
        return pltpu.make_async_remote_copy(
            src_ref=source,
            dst_ref=target,
            send_sem=self.send.at[index],
            recv_sem=self.recv.at[index],
            device_id=device,
            device_id_type=MESH,
        )


class Planned:
    def __init__(self, plan, send, recv):
        self.plan, self.send, self.recv = plan, send, recv
        self.order = list(plan)

    def __getitem__(self, name):
        source, target, device = self.plan[name]
        index = self.order.index(name)
        return pltpu.make_async_remote_copy(
            src_ref=source,
            dst_ref=target,
            send_sem=self.send.at[index],
            recv_sem=self.recv.at[index],
            device_id=device,
            device_id_type=MESH,
        )


def gather_kernel(
    n_fsdp,
    part_out,
    attn_q,
    attn_k,
    attn_v,
    attn_o,
    tokens,
    expert_in,
    weights,
    x_all,
    w_in,
    attn_held,
    tokens_held,
    in_held,
    send,
    recv,
    local,
):
    me = Place(n_fsdp)
    rep, line, seq = me.rep, me.line, me.seq
    far_row = (me.row + 1) % 2 * 2 + me.core
    mate, across, beside = me.mate(), me.chip(1, 0), me.chip(0, 1)
    part_in = expert_in.shape[1]
    wires = Wires(send, recv)
    meet([mate, across, beside, me.along(1), me.along(-1), me.along(2)])
    started = []

    def start(copy):
        copy.start()
        started.append(copy)
        return copy

    for i, matrix in enumerate((attn_q, attn_k, attn_v, attn_o)):

        @pl.when(rep == i)
        def _():
            own = pltpu.make_async_copy(matrix, attn_held, local.at[0])
            own.start()
            own.wait()

    mine = lambda z, r=rep, x=seq: weights.at[r, z, x]
    shifts = (0, 1, -1, 2)
    at = {0: line}
    z_copies = {}
    for shift in shifts[1:]:
        at[shift] = (line - shift) % n_fsdp
        z_copies[shift] = start(
            wires.copy(("z", shift), attn_held, mine(line), me.along(shift))
        )
    x_copies, y_copies, c_copies, far_copies = {}, {}, [], {}

    def spread_out(shift):
        z = at[shift]
        source = mine(z) if shift else attn_held
        x_copies[shift] = start(wires.copy(("x", shift), source, mine(z), beside))
        y_copies[shift] = start(wires.copy(("y", shift), source, mine(z), across))
        c_copies.append(start(wires.copy(("c", shift), source, mine(z), mate)))

    spread_out(0)
    columns = lambda z, x: pl.ds(pl.multiple_of((z * 2 + x) * part_out, LANES), part_out)
    rows = lambda x: pl.ds(pl.multiple_of(x * part_in, part_in), part_in)
    in_x, in_own = [], []
    for z in range(n_fsdp):
        here = pl.ds(z * part_out, part_out)
        target = w_in.at[line, rows(seq), here]
        in_x.append(
            start(wires.copy(("in", z), expert_in.at[rep, :, columns(z, 1 - seq)], target, beside))
        )
        copy = pltpu.make_async_copy(
            expert_in.at[rep, :, columns(z, seq)], in_held.at[:, here], local.at[1 + z]
        )
        copy.start()
        in_own.append(copy)
    own_attn = pltpu.make_async_copy(attn_held, mine(line), local.at[0])
    own_attn.start()
    x_own = Bounce(tokens, tokens_held, x_all.at[seq], local.at[pl.ds(n_fsdp + 1, 2)])
    x_own.start()
    for copy in in_own:
        copy.wait()
    own_in = pltpu.make_async_copy(in_held, w_in.at[line, rows(seq)], local.at[n_fsdp + 3])
    own_in.start()
    x_own.turn()
    for shift in shifts[1:]:
        z_copies[shift].wait_recv()
        spread_out(shift)
    for copy in in_x:
        copy.wait_recv()
    own_in.wait()
    in_copies = [
        start(wires.copy(("line", shift), w_in.at[line], w_in.at[line], me.along(shift)))
        for shift in (1, -1)
    ]
    token_copy = start(wires.copy("tokens", tokens, x_all.at[seq], beside))
    for shift in shifts:
        z = at[shift]
        x_copies[shift].wait_recv()
        near = mine(z, rep, 1 - seq)
        far_copies[shift] = start(wires.copy(("far", shift), near, near, across))
        c_copies.append(start(wires.copy(("cx", shift), near, near, mate)))
    for shift in shifts:
        z = at[shift]
        y_copies[shift].wait_recv()
        there = mine(z, far_row, seq)
        c_copies.append(start(wires.copy(("cy", shift), there, there, mate)))
    for shift in shifts:
        z = at[shift]
        far_copies[shift].wait_recv()
        there = mine(z, far_row, 1 - seq)
        c_copies.append(start(wires.copy(("cf", shift), there, there, mate)))
    for copy in c_copies + in_copies + [token_copy]:
        copy.wait_recv()
    x_own.wait()
    own_attn.wait()
    for copy in started:
        copy.wait_send()


def gather(attn, tokens, expert_in, part_out, n_fsdp):
    part_attn, width = attn[0].shape
    n_rows = tokens.shape[0]
    n_experts, part_in, hidden = expert_in.shape
    anywhere = pl.BlockSpec(memory_space=pl.ANY)
    weights, x_all, w_in = pl.pallas_call(
        functools.partial(gather_kernel, n_fsdp, part_out),
        out_shape=[
            jax.ShapeDtypeStruct((4, n_fsdp, 2, part_attn, width), bf16),
            jax.ShapeDtypeStruct((2, n_rows, width), bf16),
            jax.ShapeDtypeStruct((n_fsdp, 2 * part_in, n_fsdp * part_out), bf16),
        ],
        in_specs=[anywhere] * 6,
        out_specs=[anywhere] * 3,
        scratch_shapes=[
            pltpu.VMEM((part_attn, width), bf16),
            pltpu.VMEM((n_rows, width), bf16),
            pltpu.VMEM((part_in, n_fsdp * part_out), bf16),
            pltpu.SemaphoreType.DMA((48,)),
            pltpu.SemaphoreType.DMA((48,)),
            pltpu.SemaphoreType.DMA((8,)),
        ],
        compiler_params=pltpu.CompilerParams(collective_id=0, has_side_effects=True),
        name="gather_weights",
    )(*attn, tokens, expert_in)
    return (
        weights.reshape(4, n_fsdp * 2 * part_attn, width),
        x_all.reshape(2 * n_rows, width),
        w_in,
    )


class Bounce:
    def __init__(self, source, held, target, sems):
        self.load = lambda: pltpu.make_async_copy(source, held, sems.at[0])
        self.store = lambda: pltpu.make_async_copy(held, target, sems.at[1])

    def start(self):
        self.load().start()

    def turn(self):
        self.load().wait()
        self.store().start()

    def wait(self):
        self.store().wait()


def relay_plan(me, pieces):
    rows = pieces.shape[1] // 2
    plan = {}
    for i, shift in enumerate((1, -1)):
        piece = pieces.at[(me.line - shift) % me.n_fsdp, pl.ds(i * rows, rows)]
        plan["relay", shift] = (piece, piece, me.along(shift))
    return plan


class Background:
    n_in, n_out = 3, 3

    def __init__(self, n_fsdp):
        self.n_fsdp = n_fsdp

    def out_shape(self, dy, w_in, expert_out):
        return [
            jax.ShapeDtypeStruct((8,) + dy.shape, bf16),
            jax.ShapeDtypeStruct(w_in.shape, bf16),
            jax.ShapeDtypeStruct((self.n_fsdp,) + expert_out.shape[1:], bf16),
        ]

    def scratch(self, dy, w_in, expert_out):
        return [
            pltpu.SemaphoreType.DMA((16,)),
            pltpu.SemaphoreType.DMA((16,)),
            pltpu.SemaphoreType.DMA((4,)),
            pltpu.VMEM(dy.shape, bf16),
            pltpu.VMEM(expert_out.shape[1:], bf16),
        ]

    def run(self, step, before, ins, outs, scratch):
        dy, _, expert_out = ins
        dy_all, w_in, w_out = outs
        send, recv, local, dy_held, out_held = scratch
        me = Place(self.n_fsdp)
        half = dy.shape[0] // 2
        first, second = pl.ds(0, half), pl.ds(half, half)
        core = me.core
        own = 7 * (1 - core)
        mate, across, beside = me.mate(), me.chip(1, 0), me.chip(0, 1)
        slot = dy_all.at
        plan = {
            "x": (dy, slot[1 + core], beside),
            "y": (dy, slot[3 + core], across),
            "c0": (dy, slot[own], mate),
            "c1": (slot[1 + core], slot[1 + core], mate),
            "c2": (slot[3 + core], slot[3 + core], mate),
            "c3": (slot[5 + core], slot[5 + core], mate),
            "xy": (slot[1 + core, first], slot[5 + core, first], across),
            "yx": (slot[3 + core, second], slot[5 + core, second], beside),
            ("z", 1): (expert_out.at[me.rep], w_out.at[me.line], me.along(1)),
            ("z", -1): (expert_out.at[me.rep], w_out.at[me.line], me.along(-1)),
        } | relay_plan(me, w_in)
        copies = Planned(plan, send, recv)
        own_dy = Bounce(dy, dy_held, slot[own], local.at[pl.ds(0, 2)])
        own_out = Bounce(expert_out.at[me.rep], out_held, w_out.at[me.line], local.at[pl.ds(2, 2)])
        if before:

            @pl.when(step == 0)
            def _():
                meet([mate, across, beside, me.along(1), me.along(-1)])
                for name in (("relay", 1), ("relay", -1), ("z", 1), ("z", -1), "x", "y", "c0"):
                    copies[name].start()
                own_dy.start()
                own_out.start()

            @pl.when(step == 3)
            def _():
                own_dy.turn()
                own_out.turn()
                copies["x"].wait_recv()
                copies["xy"].start()
                copies["c1"].start()
                copies["y"].wait_recv()
                copies["yx"].start()
                copies["c2"].start()

            return

        @pl.when(step == pl.num_programs(0) - 1)
        def _():
            copies["xy"].wait_recv()
            copies["yx"].wait_recv()
            copies["c3"].start()
            for name in plan:
                if name not in ("x", "y", "xy", "yx"):
                    copies[name].wait_recv()
            own_dy.wait()
            own_out.wait()
            for name in plan:
                copies[name].wait_send()


def forward_kernel(
    background,
    n_experts,
    head_dim,
    place_ref,
    x_ref,
    wq_ref,
    wk_ref,
    wv_ref,
    wo_ref,
    pack_ref,
    *refs,
):
    step = pl.program_id(0)
    n_in, n_out = (background.n_in, background.n_out) if background else (0, 0)
    behind_in, refs = refs[:n_in], refs[n_in:]
    q_out, k_out, v_out, o_out, lse_out, x_mid_out, message_out, probs_out, h_out = refs[:9]
    behind_out, refs = refs[9 : 9 + n_out], refs[9 + n_out :]
    total_ref, mask_ref, bias_ref, dist_ref = refs[:4]
    if background:
        background.run(step, True, behind_in, behind_out, refs[4:])
    rows = x_mid_out.shape[0]
    length, width = x_ref.shape
    own = pl.ds(pl.multiple_of(first_row(rows), rows), rows)

    @pl.when(step == 0)
    def _():
        values = x_ref[...].astype(f32)
        gain_one = pack_ref[4:5, :width]
        h_out[...] = (values * inverse_rms(values) * gain_one).astype(bf16)
        dist_ref[...] = distances(pack_ref)
        total_ref[...] = jnp.zeros_like(total_ref)
        make_mask(place_ref, mask_ref)

    h_all = h_out[...]
    q_low = dot(h_out[own, :], wq_ref[...]).astype(bf16) * (head_dim**-0.5)
    k_low = dot(h_all, wk_ref[...]).astype(bf16)
    v_low = dot(h_all, wv_ref[...]).astype(bf16)
    q_out[...] = q_low
    k_out[...] = k_low
    v_out[...] = v_low
    block = LANES
    span = pack_ref.shape[1]
    first_half = lax.broadcasted_iota(jnp.int32, (block, LANES), 1) < head_dim
    for head in range(2):
        bias_ref[head] = spread(dist_ref[pl.ds(2 * step + head, 1), :], block, span)
    for b in range(rows // block):
        here = slice(b * block, (b + 1) * block)
        offset = pl.multiple_of(length - LANES - block * b - first_row(rows), LANES)
        halves = []
        tops = []
        for head in range(2):
            mine = first_half if head == 0 else ~first_half
            q_head = jnp.where(mine, q_low[here], jnp.zeros((), bf16))
            scores = dot_t(q_head, k_low)
            scores = scores + bias_ref[head, :, pl.ds(offset, length)] + mask_ref[here, :]
            top = jnp.max(scores, -1, keepdims=True)
            exp_scores = jnp.exp(scores - top)
            total = jnp.sum(exp_scores, -1, keepdims=True)
            probs = (exp_scores * (1.0 / total)).astype(bf16)
            halves.append(dot(probs, v_low))
            tops.append(top + jnp.log(total))
        o_out[here, :] = jnp.where(first_half, halves[0], halves[1]).astype(bf16)
        lse_out[here, :] = jnp.where(first_half, tops[0], tops[1])
    total_ref[...] += dot(o_out[...], wo_ref[...])

    @pl.when(step == pl.num_programs(0) - 1)
    def _():
        x_mid = x_ref[own, :].astype(f32) + total_ref[...]
        x_mid_out[...] = x_mid
        h_two = (x_mid * inverse_rms(x_mid) * pack_ref[5:6, :width]).astype(bf16)
        message_out[:, :width] = h_two
        logits = exact_dot_t(h_two.astype(f32), router_rows(pack_ref, n_experts, width))
        lane = lax.broadcasted_iota(jnp.int32, logits.shape, 1)
        logits = jnp.where(lane < n_experts, logits, masked_out)
        exp_logits = jnp.exp(logits - jnp.max(logits, -1, keepdims=True))
        probs = exp_logits / jnp.sum(exp_logits, -1, keepdims=True)
        probs_out[...] = probs
        chosen = jnp.where(chosen_experts(pack_ref, probs.shape), probs, 0.0)
        gate = chosen / jnp.sum(chosen, -1, keepdims=True)
        high = gate.astype(bf16)
        low = gate - high.astype(f32)
        message_out[:, width:] = (high.astype(f32) + pltpu.roll(low, n_experts, 1)).astype(bf16)

    if background:
        background.run(step, False, behind_in, behind_out, refs[4:])


def attention_forward(
    place,
    x_all,
    weights,
    pack,
    n_rows,
    n_experts,
    head_dim,
    background=None,
    behind=(),
):
    length, width = x_all.shape
    pairs = width // LANES
    span = pack.shape[1]
    whole = lambda shape: pl.BlockSpec(shape, lambda p, *_: (0,) * len(shape))
    columns = lambda rows: pl.BlockSpec((rows, LANES), lambda p, *_: (0, p))
    matrix = lambda i: pl.BlockSpec((None, width, LANES), lambda p, *_: (i, 0, p))
    out_shape = [
        jax.ShapeDtypeStruct((n_rows, width), bf16),
        jax.ShapeDtypeStruct((length, width), bf16),
        jax.ShapeDtypeStruct((length, width), bf16),
        jax.ShapeDtypeStruct((n_rows, width), bf16),
        jax.ShapeDtypeStruct((n_rows, width), f32),
        jax.ShapeDtypeStruct((n_rows, width), f32),
        jax.ShapeDtypeStruct((n_rows, width + LANES), bf16),
        jax.ShapeDtypeStruct((n_rows, LANES), f32),
        jax.ShapeDtypeStruct((length, width), bf16),
    ]
    anywhere = pl.BlockSpec(memory_space=pl.ANY)
    params, aliases = {}, {}
    if background:
        out_shape += background.out_shape(*behind)
        params = {"collective_id": 1, "has_side_effects": True}
        aliases = {8: 10}
    return pl.pallas_call(
        functools.partial(forward_kernel, background, n_experts, head_dim),
        out_shape=out_shape,
        grid_spec=pltpu.PrefetchScalarGridSpec(
            num_scalar_prefetch=1,
            grid=(pairs,),
            in_specs=[
                whole((length, width)),
                matrix(0),
                matrix(1),
                matrix(2),
                pl.BlockSpec((None, LANES, width), lambda p, *_: (3, p, 0)),
                whole(pack.shape),
            ]
            + [anywhere] * len(behind),
            out_specs=[
                columns(n_rows),
                columns(length),
                columns(length),
                columns(n_rows),
                columns(n_rows),
                whole((n_rows, width)),
                whole((n_rows, width + LANES)),
                whole((n_rows, LANES)),
                whole((length, width)),
            ]
            + [anywhere] * (background.n_out if background else 0),
            scratch_shapes=[
                pltpu.VMEM((n_rows, width), f32),
                pltpu.VMEM((n_rows, length), f32),
                pltpu.VMEM((2, LANES, span), f32),
                pltpu.VMEM((16, span), f32),
            ]
            + (background.scratch(*behind) if background else []),
        ),
        input_output_aliases=aliases,
        compiler_params=pltpu.CompilerParams(vmem_limit_bytes=VMEM_LIMIT, **params),
        cost_estimate=pl.CostEstimate(
            flops=20_000_000_000, transcendentals=0, bytes_accessed=20_000_000
        ),
        name="attention_forward",
    )(
        place,
        x_all,
        weights,
        weights,
        weights,
        weights,
        pack,
        *behind,
    )


GELU_A = 0.7978845608028654
GELU_B = 0.044715 * GELU_A


def experts_kernel(
    n_experts,
    chunk,
    expert_ref,
    message_ref,
    dy_ref,
    w_in_ref,
    w_out_ref,
    out_ref,
    dh_ref,
    dw_in_ref,
    dw_out_ref,
    dw_in_acc,
    dw_out_acc,
):
    step = pl.program_id(0)
    width = dy_ref.shape[1]
    hidden = w_in_ref.shape[1]
    expert = expert_ref[0]

    @pl.when(step == 0)
    def _():
        dw_in_acc[...] = jnp.zeros_like(dw_in_acc)
        dw_out_acc[...] = jnp.zeros_like(dw_out_acc)

    h = message_ref[:, :width]
    extra = message_ref[:, width:].astype(f32)
    lane = lax.broadcasted_iota(jnp.int32, extra.shape, 1)
    mine = (lane == expert) | (lane == expert + n_experts)
    gate = jnp.sum(jnp.where(mine, extra, 0.0), -1, keepdims=True)
    dy = dy_ref[...]
    out_total = None
    dh_total = None
    dgate = None
    for start in range(0, hidden, chunk):
        part = slice(start, start + chunk)
        up = dot(h, w_in_ref[:, part])
        dact = dot_t(dy, w_out_ref[part, :])
        square = up * up
        tanh = jnp.tanh(up * (GELU_A + GELU_B * square))
        half = 0.5 * up
        more = 1.0 + tanh
        act = half * more
        slope = 0.5 * more + half * (1.0 - tanh * tanh) * (GELU_A + 3.0 * GELU_B * square)
        gated = (gate * act).astype(bf16)
        dgate_part = jnp.sum(act * dact, -1, keepdims=True)
        dup = (gate * dact * slope).astype(bf16)
        out_part = dot(gated, w_out_ref[part, :])
        dh_part = dot_t(dup, w_in_ref[:, part])
        out_total = out_part if out_total is None else out_total + out_part
        dh_total = dh_part if dh_total is None else dh_total + dh_part
        dgate = dgate_part if dgate is None else dgate + dgate_part
        dw_out_acc[part, :] += t_dot(gated, dy)
        dw_in_acc[:, part] += t_dot(h, dup)
    out_ref[...] = out_total.astype(bf16)
    dh_ref[:, :width] = dh_total.astype(bf16)
    high = dgate.astype(bf16).astype(f32)
    low = dgate - high
    dh_ref[:, width:] = jnp.where(
        lane == expert, high, jnp.where(lane == expert + n_experts, low, 0.0)
    ).astype(bf16)

    @pl.when(step == pl.num_programs(0) - 1)
    def _():
        dw_in_ref[...] = dw_in_acc[...].astype(bf16)
        dw_out_ref[...] = dw_out_acc[...].astype(bf16)


def experts(expert, message, dy, w_in, w_out, n_experts, block):
    tokens, width = dy.shape
    hidden = w_in.shape[1]
    whole = lambda shape: pl.BlockSpec(shape, lambda i, *_: (0,) * len(shape))
    rows = lambda columns: pl.BlockSpec((block, columns), lambda i, *_: (i, 0))
    return pl.pallas_call(
        functools.partial(experts_kernel, n_experts, 512),
        out_shape=[
            jax.ShapeDtypeStruct((tokens, width), bf16),
            jax.ShapeDtypeStruct((tokens, width + LANES), bf16),
            jax.ShapeDtypeStruct((width, hidden), bf16),
            jax.ShapeDtypeStruct((hidden, width), bf16),
        ],
        grid_spec=pltpu.PrefetchScalarGridSpec(
            num_scalar_prefetch=1,
            grid=(tokens // block,),
            in_specs=[
                rows(width + LANES),
                rows(width),
                whole((width, hidden)),
                whole((hidden, width)),
            ],
            out_specs=[
                rows(width),
                rows(width + LANES),
                whole((width, hidden)),
                whole((hidden, width)),
            ],
            scratch_shapes=[
                pltpu.VMEM((width, hidden), f32),
                pltpu.VMEM((hidden, width), f32),
            ],
        ),
        compiler_params=pltpu.CompilerParams(vmem_limit_bytes=VMEM_LIMIT),
        cost_estimate=pl.CostEstimate(
            flops=60_000_000_000, transcendentals=0, bytes_accessed=30_000_000
        ),
        name="experts",
    )(expert, message, dy, w_in, w_out)


def plane_slot(j):
    return (j + 1) // 2 % 4, (j + 1) % 2


def experts_up_kernel(
    n_experts,
    chunk,
    n_fsdp,
    message_ref,
    dy_ref,
    w_in_ref,
    _,
    h_out,
    act_out,
    slope_out,
    dw_out_ref,
    w_out,
    h_ref,
    dw_out_acc,
    send,
    recv,
):
    step = pl.program_id(0)
    last = pl.num_programs(0) - 1
    me = Place(n_fsdp)
    core = me.core
    rows, width = dy_ref.shape
    hidden = w_in_ref.shape[1]
    half = rows // 2
    first, second = pl.ds(0, half), pl.ds(half, half)
    mate, across, beside = me.mate(), me.chip(1, 0), me.chip(0, 1)
    own = 7 * (1 - core)
    slot = h_ref.at
    plan = {
        "x": (message_ref, slot[1 + core], beside),
        "y": (message_ref, slot[3 + core], across),
        "c0": (message_ref, slot[own], mate),
        "c1": (slot[1 + core], slot[1 + core], mate),
        "c2": (slot[3 + core], slot[3 + core], mate),
        "c3": (slot[5 + core], slot[5 + core], mate),
        "xy": (slot[1 + core, first], slot[5 + core, first], across),
        "yx": (slot[3 + core, second], slot[5 + core, second], beside),
    } | relay_plan(me, w_out)
    copies = Planned(plan, send, recv)

    @pl.when(step == 0)
    def _():
        meet([mate, across, beside, me.along(1), me.along(-1)])
        for name in ("c0", "x", "y", ("relay", 1), ("relay", -1)):
            copies[name].start()
        h_ref[own] = message_ref[...]
        dw_out_acc[...] = jnp.zeros_like(dw_out_acc)

    @pl.when(step == 2)
    def _():
        copies["x"].wait_recv()
        copies["c1"].start()
        copies["xy"].start()
        copies["y"].wait_recv()
        copies["c2"].start()
        copies["yx"].start()

    @pl.when(step == 6)
    def _():
        copies["xy"].wait_recv()
        copies["yx"].wait_recv()
        copies["c3"].start()

    for q in range(4):

        @pl.when(step == 2 * q + 1 - core)
        def _():
            copies[f"c{q}"].wait_recv()

    now = (step + 7) % 8
    expert = me.rep
    h_out[...] = h_ref[now]
    h = h_ref[now, :, :width]
    extra = h_ref[now, :, width:].astype(f32)
    lane = lax.broadcasted_iota(jnp.int32, extra.shape, 1)
    mine = (lane == expert) | (lane == expert + n_experts)
    gate = jnp.sum(jnp.where(mine, extra, 0.0), -1, keepdims=True)
    dy = dy_ref[...]
    for start in range(0, hidden, chunk):
        piece = slice(start, start + chunk)
        up = dot(h, w_in_ref[:, piece])
        square = up * up
        tanh = jnp.tanh(up * (GELU_A + GELU_B * square))
        halved = 0.5 * up
        more = 1.0 + tanh
        act = (halved * more).astype(bf16)
        slope = 0.5 * more + halved * (1.0 - tanh * tanh) * (GELU_A + 3.0 * GELU_B * square)
        act_out[:, piece] = act
        slope_out[:, piece] = slope.astype(bf16)
        gated = (gate * act.astype(f32)).astype(bf16)
        dw_out_acc[piece, :] += t_dot(gated, dy)

    @pl.when(step == last)
    def _():
        dw_out_ref[...] = dw_out_acc[...].astype(bf16)
        for shift in (1, -1):
            copies["relay", shift].wait_recv()
        for name in plan:
            copies[name].wait_send()


def experts_up(message, dy_all, w_in, w_out, n_experts, n_fsdp):
    blocks, rows, width = dy_all.shape
    long = message.shape[1]
    hidden = w_in.shape[1]
    once = pl.Buffered(1)
    whole = lambda shape: pl.BlockSpec(shape, lambda i: (0,) * len(shape), pipeline_mode=once)
    turn = lambda columns: pl.BlockSpec((None, rows, columns), lambda i: ((i + 7) % 8, 0, 0))
    anywhere = pl.BlockSpec(memory_space=pl.ANY)
    dma = lambda *shape: pltpu.SemaphoreType.DMA(shape)
    return pl.pallas_call(
        functools.partial(experts_up_kernel, n_experts, hidden, n_fsdp),
        out_shape=[
            jax.ShapeDtypeStruct((blocks, rows, long), bf16),
            jax.ShapeDtypeStruct((blocks, rows, hidden), bf16),
            jax.ShapeDtypeStruct((blocks, rows, hidden), bf16),
            jax.ShapeDtypeStruct((hidden, width), bf16),
            jax.ShapeDtypeStruct(w_out.shape, bf16),
        ],
        grid=(blocks,),
        in_specs=[whole((rows, long)), turn(width), whole((width, hidden)), anywhere],
        out_specs=[turn(long), turn(hidden), turn(hidden), whole((hidden, width)), anywhere],
        scratch_shapes=[
            pltpu.VMEM((blocks, rows, long), bf16),
            pltpu.VMEM((hidden, width), f32),
            dma(12),
            dma(12),
        ],
        input_output_aliases={3: 4},
        compiler_params=pltpu.CompilerParams(
            vmem_limit_bytes=VMEM_LIMIT, collective_id=2, has_side_effects=True
        ),
        cost_estimate=pl.CostEstimate(
            flops=20_000_000_000, transcendentals=0, bytes_accessed=30_000_000
        ),
        name="experts_up",
    )(message, dy_all, w_in, w_out)


def experts_down_kernel(
    n_experts,
    chunk,
    n_fsdp,
    message_ref,
    dy_ref,
    act_ref,
    slope_ref,
    w_in_ref,
    w_out_ref,
    dw_out,
    back_ref,
    out_half,
    dw_in_ref,
    sum_out,
    part_ref,
    tx_ref,
    rx_ref,
    fin_ref,
    fin_out_ref,
    land_ref,
    dw_in_acc,
    tx_send,
    tx_recv,
    fin_sem,
    land_sem,
    local,
    near,
    mid,
    far,
    own_ref,
    line_send,
    line_recv,
    line_local,
):
    step = pl.program_id(0)
    last = 7
    me = Place(n_fsdp)
    core = me.core
    rows, width = dy_ref.shape
    hidden = w_in_ref.shape[1]
    long = message_ref.shape[1]
    half = rows // 2
    mate = me.mate()
    adds = LineSum(me, dw_out, near, mid, far, own_ref, line_send, line_recv, line_local)

    def to_mate(j):
        return pltpu.make_async_remote_copy(
            src_ref=tx_ref.at[j % 2],
            dst_ref=rx_ref.at[j],
            send_sem=tx_send.at[j],
            recv_sem=tx_recv.at[j],
            device_id=mate,
            device_id_type=MESH,
        )

    def to_owner(j):
        q, k = plane_slot(j)
        return pltpu.make_async_remote_copy(
            src_ref=fin_ref.at[j % 2],
            dst_ref=land_ref.at[q, core],
            send_sem=fin_sem.at[j],
            recv_sem=land_sem.at[q, core],
            device_id=me.chip(q // 2, q % 2, k),
            device_id_type=MESH,
        )

    def keep_out(j):
        return pltpu.make_async_copy(fin_out_ref.at[j % 2], out_half.at[j], local.at[j])

    def stays(j):
        q, k = plane_slot(j)
        return (q == 0) & (k == core)

    def finish_block(j):
        to_mate(j).wait_recv()
        mine = part_ref.at[j % 2, pl.ds(core * half, half)]

        @pl.when(j >= 2)
        def _():
            keep_out(j - 2).wait()

        @pl.when((j >= 2) & ~stays(j - 2))
        def _():
            to_owner(j - 2).wait_send()

        fin_ref[j % 2] = (mine[:, :long] + rx_ref[j, :, :long].astype(f32)).astype(bf16)

        @pl.when(stays(j))
        def _():
            land_ref[0, core] = fin_ref[j % 2]

        @pl.when(~stays(j))
        def _():
            to_owner(j).start()

        fin_out_ref[j % 2] = (mine[:, long:] + rx_ref[j, :, long:].astype(f32)).astype(bf16)
        keep_out(j).start()

    @pl.when(step == 0)
    def _():
        partners = [mate, me.along(1), me.along(-1)]
        for q in (1, 2, 3):
            for k in (0, 1):
                partners.append(me.chip(q // 2, q % 2, (core + k) % 2))
        meet(partners)
        adds.start()
        dw_in_acc[...] = jnp.zeros_like(dw_in_acc)

    @pl.when(step == 3)
    def _():
        adds.turn()

    expert = me.rep
    h_turned = message_ref[:, :width].T
    extra = message_ref[:, width:].astype(f32)
    lane = lax.broadcasted_iota(jnp.int32, extra.shape, 1)
    mine = (lane == expert) | (lane == expert + n_experts)
    gate = jnp.sum(jnp.where(mine, extra, 0.0), -1, keepdims=True)
    dy = dy_ref[...]
    dgate = None
    part = part_ref.at[step % 2]
    for start in range(0, hidden, chunk):
        piece = slice(start, start + chunk)
        act = act_ref[:, piece].astype(f32)
        dact = dot_t(dy, w_out_ref[piece, :])
        gated = (gate * act).astype(bf16)
        dgate_part = jnp.sum(act * dact, -1, keepdims=True)
        dup = (gate * dact * slope_ref[:, piece].astype(f32)).astype(bf16)
        out_part = dot(gated, w_out_ref[piece, :])
        dh_part = dot_t(dup, w_in_ref[:, piece])
        if start == 0:
            part[:, long:] = out_part
            part[:, :width] = dh_part
        else:
            part[:, long:] += out_part
            part[:, :width] += dh_part
        dgate = dgate_part if dgate is None else dgate + dgate_part
        dw_in_acc[:, piece] += dot(h_turned, dup)
        if start == 0:

            @pl.when(step >= 1)
            def _():
                finish_block(step - 1)

    high = dgate.astype(bf16).astype(f32)
    low = dgate - high
    part[:, width:long] = jnp.where(
        lane == expert, high, jnp.where(lane == expert + n_experts, low, 0.0)
    )

    @pl.when(step >= 2)
    def _():
        to_mate(step - 2).wait_send()

    tx_ref[step % 2] = part_ref[step % 2, pl.ds((1 - core) * half, half)].astype(bf16)
    to_mate(step).start()

    @pl.when(step == last)
    def _():
        dw_in_ref[...] = dw_in_acc[...].astype(bf16)
        finish_block(last)
        sum_out[...] = adds.total()
        to_mate(last - 1).wait_send()
        to_mate(last).wait_send()
        keep_out(last - 1).wait()
        keep_out(last).wait()
        to_owner(last - 1).wait_send()

        @pl.when(~stays(last))
        def _():
            to_owner(last).wait_send()

        for side in range(2):
            total = None
            for q in range(4):
                arrived = pltpu.make_async_remote_copy(
                    src_ref=fin_ref.at[0],
                    dst_ref=land_ref.at[q, side],
                    send_sem=fin_sem.at[0],
                    recv_sem=land_sem.at[q, side],
                    device_id=mate,
                    device_id_type=MESH,
                )
                if q == 0:

                    @pl.when(core != side)
                    def _():
                        arrived.wait_recv()

                else:
                    arrived.wait_recv()
                landed = land_ref[q, side].astype(f32)
                total = landed if total is None else total + landed
            back_ref[side * half : (side + 1) * half, :] = total


def experts_down(message_all, dy_all, act, slope, w_in, w_out, dw_out, n_experts, n_fsdp):
    blocks, rows, width = dy_all.shape
    long = message_all.shape[2]
    hidden = w_in.shape[1]
    half = rows // 2
    once = pl.Buffered(1)
    whole = lambda shape: pl.BlockSpec(shape, lambda i: (0,) * len(shape), pipeline_mode=once)
    block = lambda columns: pl.BlockSpec((None, rows, columns), lambda i: (i, 0, 0))
    anywhere = pl.BlockSpec(memory_space=pl.ANY)
    both = long + width
    dma = lambda *shape: pltpu.SemaphoreType.DMA(shape)
    return pl.pallas_call(
        functools.partial(experts_down_kernel, n_experts, 512, n_fsdp),
        out_shape=[
            jax.ShapeDtypeStruct((rows, long), f32),
            jax.ShapeDtypeStruct((blocks, half, width), bf16),
            jax.ShapeDtypeStruct((width, hidden), bf16),
            jax.ShapeDtypeStruct(dw_out.shape[1:], bf16),
        ],
        grid=(blocks,),
        in_specs=[
            block(long),
            block(width),
            block(hidden),
            block(hidden),
            whole((width, hidden)),
            whole((hidden, width)),
            anywhere,
        ],
        out_specs=[
            whole((rows, long)),
            anywhere,
            whole((width, hidden)),
            whole(dw_out.shape[1:]),
        ],
        scratch_shapes=[
            pltpu.VMEM((2, rows, both), f32),
            pltpu.VMEM((2, half, both), bf16),
            pltpu.VMEM((blocks, half, both), bf16),
            pltpu.VMEM((2, half, long), bf16),
            pltpu.VMEM((2, half, width), bf16),
            pltpu.VMEM((4, 2, half, long), bf16),
            pltpu.VMEM((width, hidden), f32),
            dma(8),
            dma(8),
            dma(8),
            dma(4, 2),
            dma(8),
        ]
        + LineSum.scratch(*dw_out.shape[1:]),
        compiler_params=pltpu.CompilerParams(
            vmem_limit_bytes=VMEM_LIMIT, collective_id=3, has_side_effects=True
        ),
        cost_estimate=pl.CostEstimate(
            flops=40_000_000_000, transcendentals=0, bytes_accessed=40_000_000
        ),
        name="experts_down",
    )(message_all, dy_all, act, slope, w_in, w_out, dw_out)


class LineSum:
    def __init__(self, me, whole, near, mid, far, mine, send, recv, local):
        self.me, self.whole, self.near, self.mid, self.far = me, whole, near, mid, far
        self.mine, self.local = mine, local
        rows = whole.shape[1]
        half = rows // 2
        self.parts = {1: slice(0, half), -1: slice(half, rows)}
        plan = {}
        for i, shift in enumerate((1, -1)):
            part = pl.ds(i * half, half)
            target = (me.line + 2) % me.n_fsdp
            plan["near", shift] = (whole.at[target, part], near.at[i], me.along(shift))
            plan["far", shift] = (mid.at[i], far.at[i], me.along(shift))
        self.copies = Planned(plan, send, recv)

    def loads(self):
        me = self.me
        for i, shift in enumerate((1, -1)):
            source = self.whole.at[(me.line + shift) % me.n_fsdp]
            yield pltpu.make_async_copy(source, self.mid.at[i], self.local.at[i])
        yield pltpu.make_async_copy(self.whole.at[me.line], self.mine, self.local.at[2])

    def start(self):
        for shift in (1, -1):
            self.copies["near", shift].start()
        for load in self.loads():
            load.start()

    def turn(self):
        for load in self.loads():
            load.wait()
        for i, shift in enumerate((1, -1)):
            self.copies["near", shift].wait_recv()
            part = self.parts[shift]
            total = self.mid[i, part, :].astype(f32) + self.near[i].astype(f32)
            self.mid[i, part, :] = total.astype(bf16)
            self.copies["far", shift].start()

    def total(self):
        for shift in (1, -1):
            self.copies["far", shift].wait_recv()
        total = self.mine[...].astype(f32) + self.far[0].astype(f32) + self.far[1].astype(f32)
        for shift in (1, -1):
            self.copies["near", shift].wait_send()
            self.copies["far", shift].wait_send()
        return total.astype(bf16)

    @staticmethod
    def scratch(rows, columns):
        return [
            pltpu.VMEM((2, rows // 2, columns), bf16),
            pltpu.VMEM((2, rows, columns), bf16),
            pltpu.VMEM((2, rows, columns), bf16),
            pltpu.VMEM((rows, columns), bf16),
            pltpu.SemaphoreType.DMA((4,)),
            pltpu.SemaphoreType.DMA((4,)),
            pltpu.SemaphoreType.DMA((3,)),
        ]


class BackgroundBack:
    n_in, n_out = 2, 2

    def __init__(self, n_fsdp):
        self.n_fsdp = n_fsdp

    def out_shape(self, out_half, dw_in):
        half, width = out_half.shape[1:]
        return [
            jax.ShapeDtypeStruct((2 * half, width), bf16),
            jax.ShapeDtypeStruct(dw_in.shape[1:], bf16),
        ]

    def out_specs(self, shapes):
        whole = lambda shape: pl.BlockSpec(shape, lambda p, *_: (0,) * len(shape))
        return [whole(s.shape) for s in shapes]

    def scratch(self, out_half, dw_in):
        half, width = out_half.shape[1:]
        return [
            pltpu.VMEM((4, 2, half, width), bf16),
            pltpu.SemaphoreType.DMA((8,)),
            pltpu.SemaphoreType.DMA((4, 2)),
        ] + LineSum.scratch(*dw_in.shape[1:])

    def run(self, step, before, ins, outs, scratch, x_mid):
        out_half, dw_in = ins
        out_rows, sum_in = outs
        land, send, recv = scratch[:3]
        near, mid, far, mine, line_send, line_recv, line_local = scratch[3:]
        me = Place(self.n_fsdp)
        core = me.core
        half = out_half.shape[1]
        line = LineSum(me, dw_in, near, mid, far, mine, line_send, line_recv, line_local)

        def to_owner(j):
            q, k = plane_slot(j)
            return pltpu.make_async_remote_copy(
                src_ref=out_half.at[j],
                dst_ref=land.at[q, core],
                send_sem=send.at[j],
                recv_sem=recv.at[q, core],
                device_id=me.chip(q // 2, q % 2, k),
                device_id_type=MESH,
            )

        def stay(j):
            return pltpu.make_async_copy(out_half.at[j], land.at[0, core], send.at[j])

        if before:

            @pl.when(step == 0)
            def _():
                partners = [me.mate(), me.along(1), me.along(-1)]
                for q in (1, 2, 3):
                    for k in (0, 1):
                        partners.append(me.chip(q // 2, q % 2, (core + k) % 2))
                meet(partners)
                line.start()
                for j in range(8):
                    if j in (0, 7):

                        @pl.when(core == (j + 1) % 2)
                        def _():
                            stay(j).start()

                        @pl.when(core != (j + 1) % 2)
                        def _():
                            to_owner(j).start()

                    else:
                        to_owner(j).start()

            @pl.when(step == 2)
            def _():
                line.turn()

            return

        @pl.when(step == pl.num_programs(0) - 1)
        def _():
            for j in range(8):
                if j in (0, 7):

                    @pl.when(core == (j + 1) % 2)
                    def _():
                        stay(j).wait()

                    @pl.when(core != (j + 1) % 2)
                    def _():
                        to_owner(j).wait_send()

                else:
                    to_owner(j).wait_send()
            for side in range(2):
                here = slice(side * half, (side + 1) * half)
                total = x_mid[here, :]
                for q in range(4):
                    arrived = pltpu.make_async_remote_copy(
                        src_ref=out_half.at[0],
                        dst_ref=land.at[q, side],
                        send_sem=send.at[0],
                        recv_sem=recv.at[q, side],
                        device_id=me.mate(),
                        device_id_type=MESH,
                    )
                    if q == 0:

                        @pl.when(core != side)
                        def _():
                            arrived.wait_recv()

                    else:
                        arrived.wait_recv()
                    total = total + land[q, side].astype(f32)
                out_rows[here, :] = total.astype(bf16)
            sum_in[...] = line.total()


def backward_kernel(
    background,
    n_experts,
    head_dim,
    place_ref,
    back_ref,
    dy_ref,
    x_mid_ref,
    message_ref,
    probs_ref,
    pack_ref,
    h_ref,
    wq_ref,
    wk_ref,
    wv_ref,
    wo_ref,
    q_ref,
    k_ref,
    v_ref,
    o_ref,
    lse_ref,
    *refs,
):
    step = pl.program_id(0)
    n_in, n_out = (background.n_in, background.n_out) if background else (0, 0)
    behind_in, refs = refs[:n_in], refs[n_in:]
    dwq_out, dwk_out, dwv_out, dwo_out, dh_own_out, dh_other_out = refs[:6]
    dx_mid_out, gain_out, router_out, ddist_out = refs[6:10]
    behind_out, refs = refs[10 : 10 + n_out], refs[10 + n_out :]
    da_ref, dh_all_ref, dh_mine_ref, mask_ref, bias_ref, dbias_ref, dq_ref, dist_ref = refs[:8]
    if background:
        background.run(step, True, behind_in, behind_out, refs[8:], x_mid_ref)
    rows, width = x_mid_ref.shape
    length = h_ref.shape[0]
    own = pl.ds(pl.multiple_of(first_row(rows), rows), rows)

    @pl.when(step == 0)
    def _():
        probs = probs_ref[...]
        chosen = chosen_experts(pack_ref, probs.shape)
        picked = jnp.where(chosen, probs, 0.0)
        total = jnp.sum(picked, -1, keepdims=True)
        gate = picked / total
        extra = back_ref[:, width:].astype(f32)
        dgate = extra + pltpu.roll(extra, LANES - n_experts, 1)
        dgate = jnp.where(chosen, dgate, 0.0)
        shared = jnp.sum(dgate * gate, -1, keepdims=True)
        dprobs = jnp.where(chosen, (dgate - shared) / total, 0.0)
        dlogits = probs * (dprobs - jnp.sum(probs * dprobs, -1, keepdims=True))
        h_two = message_ref[:, :width].astype(f32)
        router_out[...] = lax.dot_general(
            dlogits,
            h_two,
            (((0,), (0,)), ((), ())),
            precision=highest,
            preferred_element_type=f32,
        )
        dh_two = back_ref[:, :width].astype(f32) + exact_dot(
            dlogits, router_rows(pack_ref, n_experts, width)
        )
        dx, dgain = norm_back(x_mid_ref[...], pack_ref[5:6, :width], dh_two)
        gain_out[...] = dgain
        dx_mid = dx + dy_ref[...].astype(f32)
        dx_mid_out[...] = dx_mid
        da_ref[...] = dx_mid.astype(bf16)
        dh_all_ref[...] = jnp.zeros_like(dh_all_ref)
        dh_mine_ref[...] = jnp.zeros_like(dh_mine_ref)
        ddist_out[...] = jnp.zeros_like(ddist_out)
        dist_ref[...] = distances(pack_ref)
        make_mask(place_ref, mask_ref)

    da = da_ref[...]
    do = dot_t(da, wo_ref[...]).astype(bf16)
    dwo_out[...] = t_dot(o_ref[...], da).astype(bf16)
    block = LANES
    span = pack_ref.shape[1]
    first_half = lax.broadcasted_iota(jnp.int32, (block, LANES), 1) < head_dim
    zero = jnp.zeros((), bf16)
    k_low = k_ref[...]
    v_low = v_ref[...]
    dk = None
    dv = None
    for head in range(2):
        bias_ref[head] = spread(dist_ref[pl.ds(2 * step + head, 1), :], block, span)
        dbias_ref[head] = jnp.zeros_like(dbias_ref[head])
    for b in range(rows // block):
        here = slice(b * block, (b + 1) * block)
        offset = pl.multiple_of(length - LANES - block * b - first_row(rows), LANES)
        halves = []
        for head in range(2):
            mine = first_half if head == 0 else ~first_half
            q_head = jnp.where(mine, q_ref[here, :], zero)
            do_head = jnp.where(mine, do[here], zero)
            scores = dot_t(q_head, k_low)
            scores = scores + bias_ref[head, :, pl.ds(offset, length)] + mask_ref[here, :]
            at = head * head_dim
            probs = jnp.exp(scores - lse_ref[here, at : at + 1])
            dprobs = dot_t(do_head, v_low)
            weighted = probs * dprobs
            ds = weighted - probs * jnp.sum(weighted, -1, keepdims=True)
            ds_low = ds.astype(bf16)
            dbias_ref[head, :, pl.ds(offset, length)] += ds
            halves.append(dot(ds_low, k_low))
            dk_part = t_dot(ds_low, q_head)
            dv_part = t_dot(probs.astype(bf16), do_head)
            dk = dk_part if dk is None else dk + dk_part
            dv = dv_part if dv is None else dv + dv_part
        dq_ref[here, :] = (
            jnp.where(first_half, halves[0], halves[1]) * (head_dim**-0.5)
        ).astype(bf16)
    for head in range(2):
        ddist_out[pl.ds(2 * step + head, 1), :] = gather_diagonals(dbias_ref[head])
    dq = dq_ref[...]
    dk = dk.astype(bf16)
    dv = dv.astype(bf16)
    h_all = h_ref[...]
    dwq_out[...] = t_dot(h_ref[own, :], dq).astype(bf16)
    dwk_out[...] = t_dot(h_all, dk).astype(bf16)
    dwv_out[...] = t_dot(h_all, dv).astype(bf16)
    dh_all_ref[...] += dot_t(dk, wk_ref[...]) + dot_t(dv, wv_ref[...])
    dh_mine_ref[...] += dot_t(dq, wq_ref[...])

    @pl.when(step == pl.num_programs(0) - 1)
    def _():
        other = pl.ds(pl.multiple_of(length - rows - first_row(rows), rows), rows)
        dh_own_out[...] = dh_mine_ref[...] + dh_all_ref[own, :]
        dh_other_out[...] = dh_all_ref[other, :].astype(bf16)

    if background:
        background.run(step, False, behind_in, behind_out, refs[8:], x_mid_ref)


def attention_backward(
    place,
    back,
    dy,
    x_mid,
    message,
    probs,
    pack,
    h_all,
    weights,
    q,
    k,
    v,
    o,
    lse,
    n_experts,
    head_dim,
    background=None,
    behind=(),
):
    n_rows, width = x_mid.shape
    length = h_all.shape[0]
    pairs = width // LANES
    span = pack.shape[1]
    more_shapes, more_scratch, params = [], [], {}
    if background:
        more_shapes = background.out_shape(*behind)
        more_scratch = background.scratch(*behind)
        params = {"collective_id": 4, "has_side_effects": True}
    anywhere = pl.BlockSpec(memory_space=pl.ANY)
    whole = lambda shape: pl.BlockSpec(shape, lambda p, *_: (0,) * len(shape))
    columns = lambda rows: pl.BlockSpec((rows, LANES), lambda p, *_: (0, p))
    matrix = lambda i: pl.BlockSpec((None, width, LANES), lambda p, *_: (i, 0, p))
    return pl.pallas_call(
        functools.partial(backward_kernel, background, n_experts, head_dim),
        out_shape=[
            jax.ShapeDtypeStruct((width, width), bf16),
            jax.ShapeDtypeStruct((width, width), bf16),
            jax.ShapeDtypeStruct((width, width), bf16),
            jax.ShapeDtypeStruct((width, width), bf16),
            jax.ShapeDtypeStruct((n_rows, width), f32),
            jax.ShapeDtypeStruct((n_rows, width), bf16),
            jax.ShapeDtypeStruct((n_rows, width), f32),
            jax.ShapeDtypeStruct((1, width), f32),
            jax.ShapeDtypeStruct((LANES, width), f32),
            jax.ShapeDtypeStruct((16, span), f32),
        ]
        + more_shapes,
        grid_spec=pltpu.PrefetchScalarGridSpec(
            num_scalar_prefetch=1,
            grid=(pairs,),
            in_specs=[
                whole((n_rows, width + LANES)),
                whole((n_rows, width)),
                whole((n_rows, width)),
                whole((n_rows, width + LANES)),
                whole((n_rows, LANES)),
                whole(pack.shape),
                whole((length, width)),
                matrix(0),
                matrix(1),
                matrix(2),
                pl.BlockSpec((None, LANES, width), lambda p, *_: (3, p, 0)),
                columns(n_rows),
                columns(length),
                columns(length),
                columns(n_rows),
                columns(n_rows),
            ]
            + [anywhere] * len(behind),
            out_specs=[
                columns(width),
                columns(width),
                columns(width),
                pl.BlockSpec((LANES, width), lambda p, *_: (p, 0)),
                whole((n_rows, width)),
                whole((n_rows, width)),
                whole((n_rows, width)),
                whole((1, width)),
                whole((LANES, width)),
                whole((16, span)),
            ]
            + (background.out_specs(more_shapes) if background else []),
            scratch_shapes=[
                pltpu.VMEM((n_rows, width), bf16),
                pltpu.VMEM((length, width), f32),
                pltpu.VMEM((n_rows, width), f32),
                pltpu.VMEM((n_rows, length), f32),
                pltpu.VMEM((2, LANES, span), f32),
                pltpu.VMEM((2, LANES, span), f32),
                pltpu.VMEM((n_rows, LANES), bf16),
                pltpu.VMEM((16, span), f32),
            ]
            + more_scratch,
        ),
        compiler_params=pltpu.CompilerParams(vmem_limit_bytes=VMEM_LIMIT, **params),
        cost_estimate=pl.CostEstimate(
            flops=40_000_000_000, transcendentals=0, bytes_accessed=30_000_000
        ),
        name="attention_backward",
    )(
        place,
        back,
        dy,
        x_mid,
        message,
        probs,
        pack,
        h_all,
        weights,
        weights,
        weights,
        weights,
        q,
        k,
        v,
        o,
        lse,
        *behind,
    )


def finish_kernel(
    n_fsdp,
    n_experts,
    n_heads,
    dwq,
    dwk,
    dwv,
    dwo,
    sum_in,
    sum_out,
    dh_other,
    dh_own_ref,
    dx_mid_ref,
    tokens_ref,
    pack_ref,
    dgain_two_ref,
    drouter_ref,
    ddist_ref,
    attn_out,
    grad_in,
    grad_out,
    tokens_out,
    small_out,
    mine_ref,
    rx_ref,
    land_ref,
    line_ref,
    line_land,
    dh_land,
    small_plane,
    small_line,
    in_held,
    out_held,
    send,
    recv,
    local,
):
    me = Place(n_fsdp)
    rep, line, seq, core, row = me.rep, me.line, me.seq, me.core, me.row
    width = tokens_ref.shape[1]
    mate, across, beside, corner = me.mate(), me.chip(1, 0), me.chip(0, 1), me.chip(1, 1)
    far_row = (row + 1) % 2
    far_rep = far_row * 2 + core
    part_out = sum_out.shape[0]
    columns = lambda z, x: pl.ds(pl.multiple_of((z * 2 + x) * part_out, LANES), part_out)
    here = rep * 2 + seq
    peers = [mate, across, beside, corner]
    peers += [me.chip(1, 0, 1 - core), me.chip(0, 1, 1 - core), me.chip(1, 1, 1 - core)]
    shifts = (1, -1, 2)
    plan = {
        "pair0": (None, rx_ref.at[0], mate),
        "pair1": (None, rx_ref.at[1], mate),
        "dh": (dh_other, dh_land, beside),
        "out_c": (sum_out, grad_out.at[rep], mate),
        "out_y": (sum_out, grad_out.at[rep], across),
        "out_f": (grad_out.at[far_rep], grad_out.at[far_rep], mate),
        "to_y": (mine_ref.at[far_row, :, seq], land_ref.at[1], across),
        "to_xy": (mine_ref.at[far_row, :, 1 - seq], land_ref.at[2], corner),
        "to_x": (mine_ref.at[row, :, 1 - seq], land_ref.at[0], beside),
        "attn_c": (line_land.at[3], attn_out.at[rep], mate),
        "attn_y": (line_land.at[3], attn_out.at[rep], across),
        "attn_f": (attn_out.at[far_rep], attn_out.at[far_rep], mate),
        "in_c": (grad_in.at[rep], grad_in.at[rep], mate),
        "in_y": (grad_in.at[rep], grad_in.at[rep], across),
        "in_f": (grad_in.at[far_rep], grad_in.at[far_rep], mate),
    }
    for i, shift in enumerate(shifts):
        target = (line + shift) % n_fsdp
        plan["line", i] = (line_ref.at[target], line_land.at[i], me.along(shift))
        plan["small_z", i] = (small_line.at[line], small_line.at[line], me.along(shift))
    for z in range(n_fsdp):
        plan["in_x", z] = (
            sum_in.at[1 - seq, :, pl.ds(z * part_out, part_out)],
            grad_in.at[rep, :, columns(z, seq)],
            beside,
        )
    for i, peer in enumerate(peers):
        plan["small", i] = (small_plane.at[here], small_plane.at[here], peer)
    copies = Planned(plan, send, recv)
    matrices = (dwq, dwk, dwv, dwo)

    def pair(side, i):
        plan[f"pair{i}"] = (matrices[2 * i + 1 - side], rx_ref.at[i], mate)
        return copies[f"pair{i}"]

    keep = lambda side, i: pltpu.make_async_copy(
        matrices[2 * i + side], mine_ref.at[i], local.at[i]
    )

    meet(peers + [me.along(shift) for shift in shifts])
    for side in (0, 1):

        @pl.when(core == side)
        def _():
            for i in (0, 1):
                pair(side, i).start()
                keep(side, i).start()

    for z in range(n_fsdp):
        copies["in_x", z].start()
    copies["out_y"].start()
    own_in = pltpu.make_async_copy(sum_in.at[seq], in_held, local.at[2])
    own_in.start()
    own_out = Bounce(sum_out, out_held, grad_out.at[rep], local.at[pl.ds(8, 2)])
    own_out.start()
    for i in (0, 1):
        keep(0, i).wait()
        pair(0, i).wait_recv()
    for i, names in ((far_row, ("to_y", "to_xy")), (row, ("to_x",))):
        total = mine_ref[i].astype(f32) + rx_ref[i].astype(f32)
        mine_ref[i] = total.astype(bf16)
        for name in names:
            copies[name].start()
    copies["out_c"].start()
    own_out.turn()
    own_in.wait()
    kept = []
    for z in range(n_fsdp):
        source = in_held.at[:, pl.ds(z * part_out, part_out)]
        target = grad_in.at[rep, :, columns(z, seq)]
        kept.append(pltpu.make_async_copy(source, target, local.at[4 + z]))
        kept[-1].start()
    table = exact_dot_t(ddist_ref[...], bucket_match(pack_ref))
    small = small_plane.at[here]
    small[...] = jnp.zeros_like(small_out)
    small[1:2, :] = dgain_two_ref[...]
    small[2 : 2 + n_experts, :] = drouter_ref[:n_experts, :]
    for head in range(n_heads):
        at = head % 6 * LANES
        small[6 + head // 6, at : at + LANES] = table[head]
    for copy in kept:
        copy.wait()
    for z in range(n_fsdp):
        copies["in_x", z].wait_recv()
    copies["in_c"].start()
    copies["out_y"].wait_recv()
    copies["out_f"].start()
    copies["to_x"].wait_recv()
    copies["dh"].start()
    copies["to_y"].wait_recv()
    copies["in_y"].start()
    copies["to_xy"].wait_recv()
    for z in range(n_fsdp):
        total = mine_ref[row, z, seq].astype(f32)
        for i in range(3):
            total = total + land_ref[i, z].astype(f32)
        line_ref[z] = total.astype(bf16)
    for i in range(3):
        copies["line", i].start()
    copies["dh"].wait_recv()
    dh_one = dh_own_ref[...] + dh_land[...].astype(f32)
    gain_one = pack_ref[4:5, :width]
    dx, dgain_one = norm_back(tokens_ref[...].astype(f32), gain_one, dh_one)
    small[0:1, :] = dgain_one
    for i in range(len(peers)):
        copies["small", i].start()
    tokens_out[...] = (dx_mid_ref[...] + dx).astype(bf16)
    total = line_ref[line].astype(f32)
    for i in range(3):
        copies["line", i].wait_recv()
        total = total + line_land[i].astype(f32)
    line_land[3] = total.astype(bf16)
    copies["attn_y"].start()
    copies["attn_c"].start()
    own_attn = pltpu.make_async_copy(line_land.at[3], attn_out.at[rep], local.at[3])
    own_attn.start()
    for i in range(len(peers)):
        copies["small", i].wait_recv()
    total = small_plane[0]
    for i in range(1, 8):
        total = total + small_plane[i]
    small_line[line] = total
    for i in range(3):
        copies["small_z", i].start()
    copies["in_y"].wait_recv()
    copies["in_f"].start()
    copies["attn_y"].wait_recv()
    copies["attn_f"].start()
    for i in range(3):
        copies["small_z", i].wait_recv()
    total = small_line[0]
    for i in range(1, n_fsdp):
        total = total + small_line[i]
    small_out[...] = total
    own_attn.wait()
    own_out.wait()
    for name in ("attn_c", "attn_f", "in_c", "in_f", "out_c", "out_f"):
        copies[name].wait_recv()
    for name in plan:
        copies[name].wait_send()


def finish(
    attn_grads,
    sum_in,
    sum_out,
    dh_other,
    dh_own,
    dx_mid,
    tokens,
    pack,
    dgain_two,
    drouter,
    ddist,
    n_fsdp,
    n_experts,
    n_heads,
    hidden,
):
    n_rows, width = tokens.shape
    part_attn = width // (2 * n_fsdp)
    part_in = sum_in.shape[1]
    anywhere = pl.BlockSpec(memory_space=pl.ANY)
    inside = pl.BlockSpec(memory_space=pltpu.VMEM)
    dma = lambda n: pltpu.SemaphoreType.DMA((n,))
    split = (n_fsdp, 2, part_attn, width)
    attn_grads = [g.reshape(split) for g in attn_grads]
    return pl.pallas_call(
        functools.partial(finish_kernel, n_fsdp, n_experts, n_heads),
        out_shape=[
            jax.ShapeDtypeStruct((4, part_attn, width), bf16),
            jax.ShapeDtypeStruct((n_experts, part_in, hidden), bf16),
            jax.ShapeDtypeStruct((n_experts,) + sum_out.shape, bf16),
            jax.ShapeDtypeStruct((n_rows, width), bf16),
            jax.ShapeDtypeStruct((8, width), f32),
        ],
        in_specs=[anywhere] * 7 + [inside] * 7,
        out_specs=[anywhere] * 3 + [inside] * 2,
        scratch_shapes=[
            pltpu.VMEM((2,) + split, bf16),
            pltpu.VMEM((2,) + split, bf16),
            pltpu.VMEM((3, n_fsdp, part_attn, width), bf16),
            pltpu.VMEM((n_fsdp, part_attn, width), bf16),
            pltpu.VMEM((4, part_attn, width), bf16),
            pltpu.VMEM((n_rows, width), bf16),
            pltpu.VMEM((8, 8, width), f32),
            pltpu.VMEM((n_fsdp, 8, width), f32),
            pltpu.VMEM(sum_in.shape[1:], bf16),
            pltpu.VMEM(sum_out.shape, bf16),
            dma(40),
            dma(40),
            dma(12),
        ],
        compiler_params=pltpu.CompilerParams(
            vmem_limit_bytes=VMEM_LIMIT, collective_id=5, has_side_effects=True
        ),
        name="finish_gradients",
    )(
        *attn_grads,
        sum_in,
        sum_out,
        dh_other,
        dh_own,
        dx_mid,
        tokens,
        pack,
        dgain_two,
        drouter,
        ddist,
    )


def widen_kernel(
    n_experts, n_heads, n_buckets, attn, grad_in, grad_out, small, q, k, v, o, win, wout, *rest
):
    step = pl.program_id(0)
    for i, target in enumerate((q, k, v, o)):

        @pl.when(step == i)
        def _():
            target[...] = attn[...].astype(f32)

    win[...] = grad_in[...].astype(f32)
    wout[...] = grad_out[...].astype(f32)
    gain_one, gain_two, table, router = rest

    @pl.when(step == 0)
    def _():
        gain_one[...] = small[0:1, :]
        gain_two[...] = small[1:2, :]
        router[...] = small[2 : 2 + n_experts, :]
        for head in range(n_heads):
            at = head % 6 * LANES
            table[head : head + 1, :] = small[
                6 + head // 6 : 7 + head // 6, at : at + n_buckets
            ]


def widen(attn, grad_in, grad_out, small, n_heads, n_buckets):
    n_experts = grad_in.shape[0]
    width = small.shape[1]
    own = lambda a: pl.BlockSpec((None,) + a.shape[1:], lambda i: (i, 0, 0))
    whole = lambda shape: pl.BlockSpec(shape, lambda i: (0,) * len(shape))
    small_shapes = [(1, width), (1, width), (n_heads, n_buckets), (n_experts, width)]
    wide = [attn.shape[1:]] * 4
    return pl.pallas_call(
        functools.partial(widen_kernel, n_experts, n_heads, n_buckets),
        out_shape=[jax.ShapeDtypeStruct(shape, f32) for shape in wide]
        + [jax.ShapeDtypeStruct(a.shape, f32) for a in (grad_in, grad_out)]
        + [jax.ShapeDtypeStruct(shape, f32) for shape in small_shapes],
        grid=(n_experts,),
        in_specs=[own(attn), own(grad_in), own(grad_out), whole(small.shape)],
        out_specs=[whole(shape) for shape in wide]
        + [own(grad_in), own(grad_out)]
        + [whole(shape) for shape in small_shapes],
        compiler_params=pltpu.CompilerParams(vmem_limit_bytes=VMEM_LIMIT),
        name="widen",
    )(attn, grad_in, grad_out, small)


def per_device(
    tokens,
    piece_starts,
    routes,
    buckets,
    attn_q,
    attn_k,
    attn_v,
    attn_o,
    expert_in,
    expert_out,
    gain_attn,
    gain_ffn,
    rel_table,
    router,
    cotangent,
):
    n_rep, n_fsdp, n_seq = (lax.axis_size(a) for a in ("rep", "fsdp", "seq"))
    rep = lax.axis_index("rep")
    seq = lax.axis_index("seq")
    plane = ("rep", "seq")
    n_rows, width = tokens.shape
    n_buckets, n_heads = rel_table.shape
    head_dim = width // n_heads
    n_experts, part_in, hidden = expert_in.shape
    part_out = expert_out.shape[1]
    part_attn = attn_q.shape[0]
    length = n_rows * n_seq
    assert n_experts == n_rep == 4 and n_seq == 2 and 2 * head_dim == LANES
    pairs = n_heads // 2

    place = piece_starts[0]
    near = n_fsdp == 4 and part_attn % 16 == 0
    pick = lambda array: lax.dynamic_index_in_dim(array, rep, 0, keepdims=False)
    if near:
        weights, x_all, w_in = gather(
            (attn_q, attn_k, attn_v, attn_o), tokens, expert_in, part_out, n_fsdp
        )
    else:
        attn_own = pick(jnp.stack([attn_q, attn_k, attn_v, attn_o]))
        attn_line = lax.all_gather(attn_own, "fsdp", axis=0, tiled=False)
        attn_all = lax.all_gather(attn_line, plane, axis=0, tiled=False)
        attn_all = attn_all.reshape(n_rep, n_seq, n_fsdp, part_attn, width)
        weights = attn_all.transpose(0, 2, 1, 3, 4).reshape(n_rep, width, width)
        x_all = lax.all_gather(tokens, "seq", axis=0, tiled=True)
        in_own = pick(expert_in).reshape(part_in, n_fsdp, n_seq, part_out)
        in_own = in_own.transpose(2, 0, 1, 3).reshape(n_seq, part_in, n_fsdp * part_out)
        in_pair = lax.all_to_all(in_own, "seq", split_axis=0, concat_axis=0, tiled=True)
        in_pair = in_pair.reshape(n_seq * part_in, n_fsdp * part_out)
        w_in = lax.all_gather(in_pair, "fsdp", axis=0, tiled=True)
        w_out = lax.all_gather(pick(expert_out), "fsdp", axis=0, tiled=True)
        dy_all = lax.all_gather(cotangent, plane, axis=0, tiled=True)

    span = -(-buckets.shape[0] // LANES) * LANES
    pack = pack_small(router, gain_attn, gain_ffn, buckets, rel_table, routes, span)

    q, k, v, o, lse, x_mid, message, probs, h_all, *gathered = attention_forward(
        place,
        x_all,
        weights,
        pack,
        n_rows,
        n_experts,
        head_dim,
        Background(n_fsdp) if near else None,
        (cotangent, w_in, expert_out) if near else (),
    )
    behind = ()
    if near:
        dy_all, w_in, w_out = gathered
        w_in = w_in.reshape(width, n_fsdp * part_out)
        message_all, act, slope, dw_out, w_out = experts_up(
            message, dy_all, w_in, w_out, n_experts, n_fsdp
        )
        back, out_half, dw_in, sum_out = experts_down(
            message_all,
            dy_all,
            act,
            slope,
            w_in,
            w_out.reshape(n_fsdp * part_out, width),
            dw_out.reshape(n_fsdp, part_out, width),
            n_experts,
            n_fsdp,
        )
        behind = (out_half, dw_in.reshape(n_fsdp, n_seq * part_in, n_fsdp * part_out))
    else:
        message_all = lax.all_gather(message, plane, axis=0, tiled=True)
        out_part, back_part, dw_in, dw_out = experts(
            rep[None].astype(jnp.int32), message_all, dy_all, w_in, w_out, n_experts, n_rows
        )
        back = lax.psum_scatter(back_part, plane, scatter_dimension=0, tiled=True)
        out_sum = lax.psum_scatter(out_part, plane, scatter_dimension=0, tiled=True)
        out_rows = (x_mid + out_sum.astype(f32)).astype(bf16)

    grads = attention_backward(
        place,
        back,
        cotangent,
        x_mid,
        message,
        probs,
        pack,
        h_all,
        weights,
        q,
        k,
        v,
        o,
        lse,
        n_experts,
        head_dim,
        BackgroundBack(n_fsdp) if near else None,
        behind,
    )
    dwq, dwk, dwv, dwo, dh_own, dh_other, dx_mid, dgain_two, drouter, ddist = grads[:10]
    if near:
        out_rows, sum_in = grads[10:]
        attn_sum, grad_in, grad_out, grad_tokens, small = finish(
            (dwq, dwk, dwv, dwo),
            sum_in.reshape(n_seq, part_in, n_fsdp * part_out),
            sum_out,
            dh_other,
            dh_own,
            dx_mid,
            tokens,
            pack,
            dgain_two,
            drouter,
            ddist,
            n_fsdp,
            n_experts,
            n_heads,
            hidden,
        )
        *wide, grad_one, grad_two, grad_table, grad_router = widen(
            attn_sum, grad_in, grad_out, small, n_heads, n_buckets
        )
        return (
            out_rows,
            grad_tokens,
            *wide,
            grad_one[0],
            grad_two[0],
            grad_table.T,
            grad_router.T,
        )
    sum_out = lax.psum_scatter(dw_out, "fsdp", scatter_dimension=0, tiled=True)
    sum_in = lax.psum_scatter(dw_in, "fsdp", scatter_dimension=0, tiled=True)
    sum_in = sum_in.reshape(n_seq, part_in, n_fsdp * part_out)
    sum_in = lax.all_to_all(sum_in, "seq", split_axis=0, concat_axis=0, tiled=True)
    sum_in = sum_in.reshape(n_seq, part_in, n_fsdp, part_out).transpose(1, 2, 0, 3)
    sum_in = sum_in.reshape(part_in, hidden)
    grad_out = lax.all_gather(sum_out, "rep", axis=0, tiled=False)
    grad_in = lax.all_gather(sum_in, "rep", axis=0, tiled=False)
    swap = [(0, 1), (1, 0)]
    dh_one = dh_own + lax.ppermute(dh_other, "seq", swap).astype(f32)
    dx, dgain_one = norm_back(tokens.astype(f32), gain_attn[None, :], dh_one)
    grad_tokens = (dx_mid + dx).astype(bf16)
    attn_grads = jnp.stack([dwq, dwk, dwv, dwo])
    attn_grads = attn_grads.reshape(n_rep, n_fsdp, n_seq, part_attn, width)
    attn_grads = attn_grads.transpose(0, 2, 1, 3, 4)
    attn_grads = attn_grads.reshape(n_rep * n_seq * n_fsdp * part_attn, width)
    attn_sum = lax.psum_scatter(attn_grads, plane, scatter_dimension=0, tiled=True)
    attn_sum = lax.psum_scatter(attn_sum, "fsdp", scatter_dimension=0, tiled=True)
    attn_sum = lax.all_gather(attn_sum, "rep", axis=0, tiled=False)
    ddist = ddist[:n_heads, : buckets.shape[0]]
    match = (buckets[:, None] == jnp.arange(n_buckets)[None, :]).astype(f32)
    table = lax.dot_general(
        match,
        ddist,
        (((0,), (1,)), ((), ())),
        precision=highest,
        preferred_element_type=f32,
    )
    grad_one, grad_two, grad_table, grad_router = lax.psum(
        (dgain_one[0], dgain_two[0], table, drouter[:n_experts].T), ("rep", "fsdp", "seq")
    )
    attn_sum = attn_sum.astype(f32)
    return (
        out_rows,
        grad_tokens,
        attn_sum[0],
        attn_sum[1],
        attn_sum[2],
        attn_sum[3],
        grad_in.astype(f32),
        grad_out.astype(f32),
        grad_one,
        grad_two,
        grad_table,
        grad_router,
    )


def solution(mesh):
    rows = P(("rep", "fsdp", "seq"), None)
    owned = P(("fsdp", "seq"), None)
    expert = P(None, ("fsdp", "seq"), None)
    in_specs = (
        rows,
        P(("rep", "fsdp"), None),
        rows,
        P(),
        owned,
        owned,
        owned,
        owned,
        expert,
        expert,
        P(),
        P(),
        P(),
        P(),
        rows,
    )
    out_specs = (
        rows,
        rows,
        owned,
        owned,
        owned,
        owned,
        expert,
        expert,
        P(),
        P(),
        P(),
        P(),
    )
    return jax.shard_map(
        per_device, mesh=mesh, in_specs=in_specs, out_specs=out_specs, check_vma=False
    )
```

```python
import functools

import jax
import jax.numpy as jnp
from jax import lax
from jax.experimental import pallas as pl
from jax.experimental.pallas import tpu as pltpu
from jax.sharding import PartitionSpec as P

PIECE = 256
LANES = 128
epsilon = 1e-06
masked_out = -1e30
highest = lax.Precision.HIGHEST
f32 = jnp.float32
bf16 = jnp.bfloat16
VMEM_LIMIT = 58 * 1024 * 1024


def dot(a, b):
    return jnp.dot(a, b, preferred_element_type=f32)


def dot_t(a, b):
    return lax.dot_general(a, b, (((1,), (1,)), ((), ())), preferred_element_type=f32)


def t_dot(a, b):
    return lax.dot_general(a, b, (((0,), (0,)), ((), ())), preferred_element_type=f32)


def exact_dot(a, b):
    return jnp.dot(a, b, precision=highest, preferred_element_type=f32)


def exact_dot_t(a, b):
    return lax.dot_general(
        a, b, (((1,), (1,)), ((), ())), precision=highest, preferred_element_type=f32
    )


def inverse_rms(values):
    return lax.rsqrt(jnp.mean(values * values, -1, keepdims=True) + epsilon)


def norm_back(values, gain, grad):
    scale = inverse_rms(values)
    scaled = values * scale
    grad_gain = jnp.sum(grad * scaled, 0, keepdims=True)
    weighted = gain * grad
    grad_values = scale * weighted - (
        values * (scale * scale * scale) * jnp.mean(weighted * values, -1, keepdims=True)
    )
    return grad_values, grad_gain


def first_row(rows):
    return lax.axis_index("seq") * rows


def make_mask(place_ref, mask_ref):
    shape = mask_ref.shape
    pos_q = first_row(shape[0]) + lax.broadcasted_iota(jnp.int32, shape, 0)
    pos_k = lax.broadcasted_iota(jnp.int32, shape, 1)
    allowed = pos_k <= pos_q
    for piece in range(2):
        start = place_ref[piece]
        in_q = (pos_q >= start) & (pos_q < start + PIECE)
        in_k = (pos_k >= start) & (pos_k < start + PIECE)
        allowed = allowed | (in_q & in_k)
    mask_ref[...] = jnp.where(allowed, 0.0, masked_out)


def spread(row, block, width):
    return pltpu.roll(
        jnp.broadcast_to(row, (block, width)), width - (block - 1), 1, stride=1, stride_axis=0
    )


def gather_diagonals(sums):
    rows = sums.shape[0]
    while rows > 1:
        half = rows // 2
        sums = pltpu.roll(sums[:half], half, 1) + sums[half:]
        rows = half
    return sums


def chosen_experts(pack_ref, shape):
    lane = lax.broadcasted_iota(jnp.int32, shape, 1).astype(f32)
    routes = pack_ref[24:32, : shape[0]].T
    return (lane == routes[:, 0:1]) | (lane == routes[:, 1:2])


def pack_small(router, gain_attn, gain_ffn, buckets, rel_table, routes, span):
    def rows(array, count):
        array = array.astype(f32)
        return jnp.pad(array, ((0, count - array.shape[0]), (0, span - array.shape[1])))

    return jnp.concatenate(
        [
            rows(router.T, 4),
            rows(gain_attn[None, :], 1),
            rows(gain_ffn[None, :], 1),
            rows(buckets[None, :], 2),
            rows(rel_table.T, 16),
            rows(routes.T, 8),
        ]
    )


def router_rows(pack_ref, n_experts, width):
    first = pack_ref[0:8, :width]
    row = lax.broadcasted_iota(jnp.int32, first.shape, 0)
    first = jnp.where(row < n_experts, first, 0.0)
    return jnp.concatenate([first, jnp.zeros((LANES - 8, width), f32)])


def bucket_match(pack_ref):
    shape = (LANES, pack_ref.shape[1])
    bucket = lax.broadcasted_iota(jnp.int32, shape, 0).astype(f32)
    return (bucket == pack_ref[6:7, :]).astype(f32)


def distances(pack_ref):
    return exact_dot(pack_ref[8:24, :LANES], bucket_match(pack_ref))


MESH = pl.DeviceIdType.MESH


class Place:
    def __init__(self, n_fsdp):
        self.rep = lax.axis_index("rep")
        self.line = lax.axis_index("fsdp")
        self.seq = lax.axis_index("seq")
        self.n_fsdp = n_fsdp
        self.row = self.rep // 2
        self.core = self.rep % 2

    def mate(self):
        return (self.row * 2 + 1 - self.core, self.line, self.seq)

    def chip(self, rows, columns, core=None):
        core = self.core if core is None else core
        row = (self.row + rows) % 2
        return (row * 2 + core, self.line, (self.seq + columns) % 2)

    def along(self, steps):
        return (self.rep, (self.line + steps) % self.n_fsdp, self.seq)


def meet(partners):
    barrier = pltpu.get_barrier_semaphore()
    for partner in partners:
        pl.semaphore_signal(barrier, inc=1, device_id=partner, device_id_type=MESH)
    pl.semaphore_wait(barrier, len(partners))


class Wires:
    def __init__(self, send, recv):
        self.send, self.recv = send, recv
        self.names = {}

    def copy(self, name, source, target, device):
        index = self.names.setdefault(name, len(self.names))
        return pltpu.make_async_remote_copy(
            src_ref=source,
            dst_ref=target,
            send_sem=self.send.at[index],
            recv_sem=self.recv.at[index],
            device_id=device,
            device_id_type=MESH,
        )


class Planned:
    def __init__(self, plan, send, recv):
        self.plan, self.send, self.recv = plan, send, recv
        self.order = list(plan)

    def __getitem__(self, name):
        source, target, device = self.plan[name]
        index = self.order.index(name)
        return pltpu.make_async_remote_copy(
            src_ref=source,
            dst_ref=target,
            send_sem=self.send.at[index],
            recv_sem=self.recv.at[index],
            device_id=device,
            device_id_type=MESH,
        )


def gather_kernel(
    n_fsdp,
    part_out,
    attn_q,
    attn_k,
    attn_v,
    attn_o,
    tokens,
    expert_in,
    router,
    gain_attn,
    gain_ffn,
    buckets,
    rel_table,
    routes,
    weights,
    x_all,
    w_in,
    pack,
    attn_held,
    tokens_held,
    in_held,
    send,
    recv,
    local,
):
    me = Place(n_fsdp)
    rep, line, seq = me.rep, me.line, me.seq
    far_row = (me.row + 1) % 2 * 2 + me.core
    mate, across, beside = me.mate(), me.chip(1, 0), me.chip(0, 1)
    part_in = expert_in.shape[1]
    wires = Wires(send, recv)
    meet([mate, across, beside, me.along(1), me.along(-1), me.along(2)])
    started = []

    def start(copy):
        copy.start()
        started.append(copy)
        return copy

    for i, matrix in enumerate((attn_q, attn_k, attn_v, attn_o)):

        @pl.when(rep == i)
        def _():
            own = pltpu.make_async_copy(matrix, attn_held, local.at[0])
            own.start()
            own.wait()

    mine = lambda z, r=rep, x=seq: weights.at[r, z, x]
    shifts = (0, 1, -1, 2)
    at = {0: line}
    z_copies = {}
    for shift in shifts[1:]:
        at[shift] = (line - shift) % n_fsdp
        z_copies[shift] = start(
            wires.copy(("z", shift), attn_held, mine(line), me.along(shift))
        )
    x_copies, y_copies, c_copies, far_copies = {}, {}, [], {}

    def spread_out(shift):
        z = at[shift]
        source = mine(z) if shift else attn_held
        x_copies[shift] = start(wires.copy(("x", shift), source, mine(z), beside))
        y_copies[shift] = start(wires.copy(("y", shift), source, mine(z), across))
        c_copies.append(start(wires.copy(("c", shift), source, mine(z), mate)))

    spread_out(0)
    columns = lambda z, x: pl.ds(pl.multiple_of((z * 2 + x) * part_out, LANES), part_out)
    rows = lambda x: pl.ds(pl.multiple_of(x * part_in, part_in), part_in)
    in_x, in_own = [], []
    for z in range(n_fsdp):
        here = pl.ds(z * part_out, part_out)
        target = w_in.at[line, rows(seq), here]
        in_x.append(
            start(wires.copy(("in", z), expert_in.at[rep, :, columns(z, 1 - seq)], target, beside))
        )
        copy = pltpu.make_async_copy(
            expert_in.at[rep, :, columns(z, seq)], in_held.at[:, here], local.at[1 + z]
        )
        copy.start()
        in_own.append(copy)
    own_attn = pltpu.make_async_copy(attn_held, mine(line), local.at[0])
    own_attn.start()
    x_own = Bounce(tokens, tokens_held, x_all.at[seq], local.at[pl.ds(n_fsdp + 1, 2)])
    x_own.start()
    for copy in in_own:
        copy.wait()
    own_in = pltpu.make_async_copy(in_held, w_in.at[line, rows(seq)], local.at[n_fsdp + 3])
    own_in.start()
    x_own.turn()
    pack[...] = jnp.zeros_like(pack)
    pack[0 : router.shape[0], : router.shape[1]] = router[...]
    pack[4, : gain_attn.shape[0]] = gain_attn[...]
    pack[5, : gain_ffn.shape[0]] = gain_ffn[...]
    pack[6, : buckets.shape[0]] = buckets[...].astype(f32)
    pack[8 : 8 + rel_table.shape[0], : rel_table.shape[1]] = rel_table[...]
    pack[24:26, : routes.shape[1]] = routes[...].astype(f32)
    for shift in shifts[1:]:
        z_copies[shift].wait_recv()
        spread_out(shift)
    for copy in in_x:
        copy.wait_recv()
    own_in.wait()
    in_copies = []
    for i, shift in enumerate((1, -1)):
        half = w_in.at[line, pl.ds(i * part_in, part_in)]
        in_copies.append(start(wires.copy(("line", shift), half, half, me.along(shift))))
    token_copy = start(wires.copy("tokens", tokens, x_all.at[seq], beside))
    for shift in shifts:
        z = at[shift]
        x_copies[shift].wait_recv()
        near = mine(z, rep, 1 - seq)
        far_copies[shift] = start(wires.copy(("far", shift), near, near, across))
        c_copies.append(start(wires.copy(("cx", shift), near, near, mate)))
    for shift in shifts:
        z = at[shift]
        y_copies[shift].wait_recv()
        there = mine(z, far_row, seq)
        c_copies.append(start(wires.copy(("cy", shift), there, there, mate)))
    for shift in shifts:
        z = at[shift]
        far_copies[shift].wait_recv()
        there = mine(z, far_row, 1 - seq)
        c_copies.append(start(wires.copy(("cf", shift), there, there, mate)))
    for copy in c_copies + in_copies + [token_copy]:
        copy.wait_recv()
    x_own.wait()
    own_attn.wait()
    for copy in started:
        copy.wait_send()


def gather(attn, tokens, expert_in, part_out, n_fsdp, small, span):
    part_attn, width = attn[0].shape
    n_rows = tokens.shape[0]
    n_experts, part_in, hidden = expert_in.shape
    anywhere = pl.BlockSpec(memory_space=pl.ANY)
    inside = pl.BlockSpec(memory_space=pltpu.VMEM)
    weights, x_all, w_in, pack = pl.pallas_call(
        functools.partial(gather_kernel, n_fsdp, part_out),
        out_shape=[
            jax.ShapeDtypeStruct((4, n_fsdp, 2, part_attn, width), bf16),
            jax.ShapeDtypeStruct((2, n_rows, width), bf16),
            jax.ShapeDtypeStruct((n_fsdp, 2 * part_in, n_fsdp * part_out), bf16),
            jax.ShapeDtypeStruct((32, span), f32),
        ],
        in_specs=[anywhere] * 6 + [inside] * 6,
        out_specs=[anywhere] * 3 + [inside],
        scratch_shapes=[
            pltpu.VMEM((part_attn, width), bf16),
            pltpu.VMEM((n_rows, width), bf16),
            pltpu.VMEM((part_in, n_fsdp * part_out), bf16),
            pltpu.SemaphoreType.DMA((48,)),
            pltpu.SemaphoreType.DMA((48,)),
            pltpu.SemaphoreType.DMA((8,)),
        ],
        compiler_params=pltpu.CompilerParams(collective_id=0, has_side_effects=True),
        name="gather_weights",
    )(*attn, tokens, expert_in, *small)
    return (
        weights.reshape(4, n_fsdp * 2 * part_attn, width),
        x_all.reshape(2 * n_rows, width),
        w_in,
        pack,
    )


class Bounce:
    def __init__(self, source, held, target, sems):
        self.load = lambda: pltpu.make_async_copy(source, held, sems.at[0])
        self.store = lambda: pltpu.make_async_copy(held, target, sems.at[1])

    def start(self):
        self.load().start()

    def turn(self):
        self.load().wait()
        self.store().start()

    def wait(self):
        self.store().wait()


def line_plan(me, own, pieces):
    rows = pieces.shape[1] // 2
    plan = {}
    for i, shift in enumerate((1, -1)):
        first, rest = pl.ds(i * rows, rows), pl.ds((1 - i) * rows, rows)
        target = pieces.at[me.line]
        piece = pieces.at[(me.line - shift) % me.n_fsdp, first]
        plan["first", shift] = (own.at[first], target.at[first], me.along(shift))
        plan["rest", shift] = (own.at[rest], target.at[rest], me.along(shift))
        plan["relay", shift] = (piece, piece, me.along(shift))
    return plan


class Background:
    n_in, n_out = 2, 2

    def __init__(self, n_fsdp):
        self.n_fsdp = n_fsdp

    def out_shape(self, dy, w_in):
        return [
            jax.ShapeDtypeStruct((8,) + dy.shape, bf16),
            jax.ShapeDtypeStruct(w_in.shape, bf16),
        ]

    def scratch(self, dy, w_in):
        return [
            pltpu.SemaphoreType.DMA((16,)),
            pltpu.SemaphoreType.DMA((16,)),
            pltpu.SemaphoreType.DMA((2,)),
            pltpu.VMEM(dy.shape, bf16),
        ]

    def run(self, step, before, ins, outs, scratch):
        dy, _ = ins
        dy_all, w_in = outs
        send, recv, local, dy_held = scratch
        me = Place(self.n_fsdp)
        half = dy.shape[0] // 2
        first, second = pl.ds(0, half), pl.ds(half, half)
        core = me.core
        own = 7 * (1 - core)
        mate, across, beside = me.mate(), me.chip(1, 0), me.chip(0, 1)
        slot = dy_all.at
        plan = {
            "x": (dy, slot[1 + core], beside),
            "y": (dy, slot[3 + core], across),
            "c0": (dy, slot[own], mate),
            "c1": (slot[1 + core], slot[1 + core], mate),
            "c2": (slot[3 + core], slot[3 + core], mate),
            "c3": (slot[5 + core], slot[5 + core], mate),
            "xy": (slot[1 + core, first], slot[5 + core, first], across),
            "yx": (slot[3 + core, second], slot[5 + core, second], beside),
        }
        line = line_plan(me, w_in.at[me.line], w_in)
        plan |= {name: line[name] for name in line if name[0] != "first"}
        copies = Planned(plan, send, recv)
        own_dy = Bounce(dy, dy_held, slot[own], local.at[pl.ds(0, 2)])
        if before:

            @pl.when(step == 0)
            def _():
                meet([mate, across, beside, me.along(1), me.along(-1)])
                for name in line:
                    if name[0] != "first":
                        copies[name].start()
                for name in ("x", "y", "c0"):
                    copies[name].start()
                own_dy.start()

            @pl.when(step == 3)
            def _():
                own_dy.turn()
                copies["x"].wait_recv()
                copies["xy"].start()
                copies["c1"].start()
                copies["y"].wait_recv()
                copies["yx"].start()
                copies["c2"].start()

            return

        @pl.when(step == pl.num_programs(0) - 1)
        def _():
            copies["xy"].wait_recv()
            copies["yx"].wait_recv()
            copies["c3"].start()
            for name in plan:
                if name not in ("x", "y", "xy", "yx"):
                    copies[name].wait_recv()
            own_dy.wait()
            for name in plan:
                copies[name].wait_send()


def forward_kernel(
    background,
    n_experts,
    head_dim,
    place_ref,
    x_ref,
    wq_ref,
    wk_ref,
    wv_ref,
    wo_ref,
    pack_ref,
    *refs,
):
    step = pl.program_id(0)
    n_in, n_out = (background.n_in, background.n_out) if background else (0, 0)
    behind_in, refs = refs[:n_in], refs[n_in:]
    q_out, k_out, v_out, o_out, lse_out, x_mid_out, message_out, probs_out, h_out = refs[:9]
    behind_out, refs = refs[9 : 9 + n_out], refs[9 + n_out :]
    total_ref, mask_ref, bias_ref, dist_ref = refs[:4]
    if background:
        background.run(step, True, behind_in, behind_out, refs[4:])
    rows = x_mid_out.shape[0]
    length, width = x_ref.shape
    own = pl.ds(pl.multiple_of(first_row(rows), rows), rows)

    @pl.when(step == 0)
    def _():
        values = x_ref[...].astype(f32)
        gain_one = pack_ref[4:5, :width]
        h_out[...] = (values * inverse_rms(values) * gain_one).astype(bf16)
        dist_ref[...] = distances(pack_ref)
        total_ref[...] = jnp.zeros_like(total_ref)
        make_mask(place_ref, mask_ref)

    h_all = h_out[...]
    q_low = dot(h_out[own, :], wq_ref[...]).astype(bf16) * (head_dim**-0.5)
    k_low = dot(h_all, wk_ref[...]).astype(bf16)
    v_low = dot(h_all, wv_ref[...]).astype(bf16)
    q_out[...] = q_low
    k_out[...] = k_low
    v_out[...] = v_low
    block = LANES
    span = pack_ref.shape[1]
    first_half = lax.broadcasted_iota(jnp.int32, (block, LANES), 1) < head_dim
    for head in range(2):
        bias_ref[head] = spread(dist_ref[pl.ds(2 * step + head, 1), :], block, span)
    for b in range(rows // block):
        here = slice(b * block, (b + 1) * block)
        offset = pl.multiple_of(length - LANES - block * b - first_row(rows), LANES)
        halves = []
        tops = []
        for head in range(2):
            mine = first_half if head == 0 else ~first_half
            q_head = jnp.where(mine, q_low[here], jnp.zeros((), bf16))
            scores = dot_t(q_head, k_low)
            scores = scores + bias_ref[head, :, pl.ds(offset, length)] + mask_ref[here, :]
            top = jnp.max(scores, -1, keepdims=True)
            exp_scores = jnp.exp(scores - top)
            total = jnp.sum(exp_scores, -1, keepdims=True)
            probs = (exp_scores * (1.0 / total)).astype(bf16)
            halves.append(dot(probs, v_low))
            tops.append(top + jnp.log(total))
        o_out[here, :] = jnp.where(first_half, halves[0], halves[1]).astype(bf16)
        lse_out[here, :] = jnp.where(first_half, tops[0], tops[1])
    total_ref[...] += dot(o_out[...], wo_ref[...])

    @pl.when(step == pl.num_programs(0) - 1)
    def _():
        x_mid = x_ref[own, :].astype(f32) + total_ref[...]
        x_mid_out[...] = x_mid
        h_two = (x_mid * inverse_rms(x_mid) * pack_ref[5:6, :width]).astype(bf16)
        message_out[:, :width] = h_two
        logits = exact_dot_t(h_two.astype(f32), router_rows(pack_ref, n_experts, width))
        lane = lax.broadcasted_iota(jnp.int32, logits.shape, 1)
        logits = jnp.where(lane < n_experts, logits, masked_out)
        exp_logits = jnp.exp(logits - jnp.max(logits, -1, keepdims=True))
        probs = exp_logits / jnp.sum(exp_logits, -1, keepdims=True)
        probs_out[...] = probs
        chosen = jnp.where(chosen_experts(pack_ref, probs.shape), probs, 0.0)
        gate = chosen / jnp.sum(chosen, -1, keepdims=True)
        high = gate.astype(bf16)
        low = gate - high.astype(f32)
        message_out[:, width:] = (high.astype(f32) + pltpu.roll(low, n_experts, 1)).astype(bf16)

    if background:
        background.run(step, False, behind_in, behind_out, refs[4:])


def attention_forward(
    place,
    x_all,
    weights,
    pack,
    n_rows,
    n_experts,
    head_dim,
    background=None,
    behind=(),
):
    length, width = x_all.shape
    pairs = width // LANES
    span = pack.shape[1]
    whole = lambda shape: pl.BlockSpec(shape, lambda p, *_: (0,) * len(shape))
    columns = lambda rows: pl.BlockSpec((rows, LANES), lambda p, *_: (0, p))
    matrix = lambda i: pl.BlockSpec((None, width, LANES), lambda p, *_: (i, 0, p))
    out_shape = [
        jax.ShapeDtypeStruct((n_rows, width), bf16),
        jax.ShapeDtypeStruct((length, width), bf16),
        jax.ShapeDtypeStruct((length, width), bf16),
        jax.ShapeDtypeStruct((n_rows, width), bf16),
        jax.ShapeDtypeStruct((n_rows, width), f32),
        jax.ShapeDtypeStruct((n_rows, width), f32),
        jax.ShapeDtypeStruct((n_rows, width + LANES), bf16),
        jax.ShapeDtypeStruct((n_rows, LANES), f32),
        jax.ShapeDtypeStruct((length, width), bf16),
    ]
    anywhere = pl.BlockSpec(memory_space=pl.ANY)
    params, aliases = {}, {}
    if background:
        out_shape += background.out_shape(*behind)
        params = {"collective_id": 1, "has_side_effects": True}
        aliases = {8: 10}
    return pl.pallas_call(
        functools.partial(forward_kernel, background, n_experts, head_dim),
        out_shape=out_shape,
        grid_spec=pltpu.PrefetchScalarGridSpec(
            num_scalar_prefetch=1,
            grid=(pairs,),
            in_specs=[
                whole((length, width)),
                matrix(0),
                matrix(1),
                matrix(2),
                pl.BlockSpec((None, LANES, width), lambda p, *_: (3, p, 0)),
                whole(pack.shape),
            ]
            + [anywhere] * len(behind),
            out_specs=[
                columns(n_rows),
                columns(length),
                columns(length),
                columns(n_rows),
                columns(n_rows),
                whole((n_rows, width)),
                whole((n_rows, width + LANES)),
                whole((n_rows, LANES)),
                whole((length, width)),
            ]
            + [anywhere] * (background.n_out if background else 0),
            scratch_shapes=[
                pltpu.VMEM((n_rows, width), f32),
                pltpu.VMEM((n_rows, length), f32),
                pltpu.VMEM((2, LANES, span), f32),
                pltpu.VMEM((16, span), f32),
            ]
            + (background.scratch(*behind) if background else []),
        ),
        input_output_aliases=aliases,
        compiler_params=pltpu.CompilerParams(vmem_limit_bytes=VMEM_LIMIT, **params),
        cost_estimate=pl.CostEstimate(
            flops=20_000_000_000, transcendentals=0, bytes_accessed=20_000_000
        ),
        name="attention_forward",
    )(
        place,
        x_all,
        weights,
        weights,
        weights,
        weights,
        pack,
        *behind,
    )


GELU_A = 0.7978845608028654
GELU_B = 0.044715 * GELU_A


def experts_kernel(
    n_experts,
    chunk,
    expert_ref,
    message_ref,
    dy_ref,
    w_in_ref,
    w_out_ref,
    out_ref,
    dh_ref,
    dw_in_ref,
    dw_out_ref,
    dw_in_acc,
    dw_out_acc,
):
    step = pl.program_id(0)
    width = dy_ref.shape[1]
    hidden = w_in_ref.shape[1]
    expert = expert_ref[0]

    @pl.when(step == 0)
    def _():
        dw_in_acc[...] = jnp.zeros_like(dw_in_acc)
        dw_out_acc[...] = jnp.zeros_like(dw_out_acc)

    h = message_ref[:, :width]
    extra = message_ref[:, width:].astype(f32)
    lane = lax.broadcasted_iota(jnp.int32, extra.shape, 1)
    mine = (lane == expert) | (lane == expert + n_experts)
    gate = jnp.sum(jnp.where(mine, extra, 0.0), -1, keepdims=True)
    dy = dy_ref[...]
    out_total = None
    dh_total = None
    dgate = None
    for start in range(0, hidden, chunk):
        part = slice(start, start + chunk)
        up = dot(h, w_in_ref[:, part])
        dact = dot_t(dy, w_out_ref[part, :])
        square = up * up
        tanh = jnp.tanh(up * (GELU_A + GELU_B * square))
        half = 0.5 * up
        more = 1.0 + tanh
        act = half * more
        slope = 0.5 * more + half * (1.0 - tanh * tanh) * (GELU_A + 3.0 * GELU_B * square)
        gated = (gate * act).astype(bf16)
        dgate_part = jnp.sum(act * dact, -1, keepdims=True)
        dup = (gate * dact * slope).astype(bf16)
        out_part = dot(gated, w_out_ref[part, :])
        dh_part = dot_t(dup, w_in_ref[:, part])
        out_total = out_part if out_total is None else out_total + out_part
        dh_total = dh_part if dh_total is None else dh_total + dh_part
        dgate = dgate_part if dgate is None else dgate + dgate_part
        dw_out_acc[part, :] += t_dot(gated, dy)
        dw_in_acc[:, part] += t_dot(h, dup)
    out_ref[...] = out_total.astype(bf16)
    dh_ref[:, :width] = dh_total.astype(bf16)
    high = dgate.astype(bf16).astype(f32)
    low = dgate - high
    dh_ref[:, width:] = jnp.where(
        lane == expert, high, jnp.where(lane == expert + n_experts, low, 0.0)
    ).astype(bf16)

    @pl.when(step == pl.num_programs(0) - 1)
    def _():
        dw_in_ref[...] = dw_in_acc[...].astype(bf16)
        dw_out_ref[...] = dw_out_acc[...].astype(bf16)


def experts(expert, message, dy, w_in, w_out, n_experts, block):
    tokens, width = dy.shape
    hidden = w_in.shape[1]
    whole = lambda shape: pl.BlockSpec(shape, lambda i, *_: (0,) * len(shape))
    rows = lambda columns: pl.BlockSpec((block, columns), lambda i, *_: (i, 0))
    return pl.pallas_call(
        functools.partial(experts_kernel, n_experts, 512),
        out_shape=[
            jax.ShapeDtypeStruct((tokens, width), bf16),
            jax.ShapeDtypeStruct((tokens, width + LANES), bf16),
            jax.ShapeDtypeStruct((width, hidden), bf16),
            jax.ShapeDtypeStruct((hidden, width), bf16),
        ],
        grid_spec=pltpu.PrefetchScalarGridSpec(
            num_scalar_prefetch=1,
            grid=(tokens // block,),
            in_specs=[
                rows(width + LANES),
                rows(width),
                whole((width, hidden)),
                whole((hidden, width)),
            ],
            out_specs=[
                rows(width),
                rows(width + LANES),
                whole((width, hidden)),
                whole((hidden, width)),
            ],
            scratch_shapes=[
                pltpu.VMEM((width, hidden), f32),
                pltpu.VMEM((hidden, width), f32),
            ],
        ),
        compiler_params=pltpu.CompilerParams(vmem_limit_bytes=VMEM_LIMIT),
        cost_estimate=pl.CostEstimate(
            flops=60_000_000_000, transcendentals=0, bytes_accessed=30_000_000
        ),
        name="experts",
    )(expert, message, dy, w_in, w_out)


def plane_slot(j):
    return (j + 1) // 2 % 4, (j + 1) % 2


def down_order(step):
    inner = (step % 7 + 6) // 7
    return step + inner * ((step + 3) % 6 + 1 - step)


def experts_up_kernel(
    n_experts,
    chunk,
    n_fsdp,
    message_ref,
    dy_ref,
    w_in_ref,
    expert_out,
    h_out,
    act_out,
    slope_out,
    dw_out_ref,
    w_out,
    h_ref,
    dw_out_acc,
    out_held,
    send,
    recv,
    local,
):
    step = pl.program_id(0)
    last = pl.num_programs(0) - 1
    me = Place(n_fsdp)
    core = me.core
    rows, width = dy_ref.shape
    hidden = w_in_ref.shape[1]
    half = rows // 2
    first, second = pl.ds(0, half), pl.ds(half, half)
    mate, across, beside = me.mate(), me.chip(1, 0), me.chip(0, 1)
    own = 7 * (1 - core)
    slot = h_ref.at
    plan = {
        "x": (message_ref, slot[1 + core], beside),
        "y": (message_ref, slot[3 + core], across),
        "c0": (message_ref, slot[own], mate),
        "c1": (slot[1 + core], slot[1 + core], mate),
        "c2": (slot[3 + core], slot[3 + core], mate),
        "c3": (slot[5 + core], slot[5 + core], mate),
        "xy": (slot[1 + core, first], slot[5 + core, first], across),
        "yx": (slot[3 + core, second], slot[5 + core, second], beside),
    } | line_plan(me, expert_out.at[me.rep], w_out)
    copies = Planned(plan, send, recv)
    own_out = Bounce(expert_out.at[me.rep], out_held, w_out.at[me.line], local)

    @pl.when(step == 0)
    def _():
        meet([mate, across, beside, me.along(1), me.along(-1)])
        for name in ("c0", "x", "y", ("first", 1), ("first", -1)):
            copies[name].start()
        own_out.start()
        h_ref[own] = message_ref[...]
        dw_out_acc[...] = jnp.zeros_like(dw_out_acc)

    @pl.when(step == 1)
    def _():
        own_out.turn()
        for shift in (1, -1):
            copies["rest", shift].start()

    @pl.when(step == 2)
    def _():
        for shift in (1, -1):
            copies["first", shift].wait_recv()
            copies["relay", shift].start()
        copies["x"].wait_recv()
        copies["c1"].start()
        copies["xy"].start()
        copies["y"].wait_recv()
        copies["c2"].start()
        copies["yx"].start()

    @pl.when(step == 6)
    def _():
        copies["xy"].wait_recv()
        copies["yx"].wait_recv()
        copies["c3"].start()

    for q in range(4):

        @pl.when(step == 2 * q + 1 - core)
        def _():
            copies[f"c{q}"].wait_recv()

    now = (step + 7) % 8
    expert = me.rep
    h_out[...] = h_ref[now]
    h = h_ref[now, :, :width]
    extra = h_ref[now, :, width:].astype(f32)
    lane = lax.broadcasted_iota(jnp.int32, extra.shape, 1)
    mine = (lane == expert) | (lane == expert + n_experts)
    gate = jnp.sum(jnp.where(mine, extra, 0.0), -1, keepdims=True)
    dy = dy_ref[...]
    for start in range(0, hidden, chunk):
        piece = slice(start, start + chunk)
        up = dot(h, w_in_ref[:, piece])
        square = up * up
        tanh = jnp.tanh(up * (GELU_A + GELU_B * square))
        halved = 0.5 * up
        more = 1.0 + tanh
        act = (halved * more).astype(bf16)
        slope = 0.5 * more + halved * (1.0 - tanh * tanh) * (GELU_A + 3.0 * GELU_B * square)
        act_out[:, piece] = act
        slope_out[:, piece] = slope.astype(bf16)
        gated = (gate * act.astype(f32)).astype(bf16)
        dw_out_acc[piece, :] += t_dot(gated, dy)

    @pl.when(step == last)
    def _():
        dw_out_ref[...] = dw_out_acc[...].astype(bf16)
        own_out.wait()
        for shift in (1, -1):
            copies["rest", shift].wait_recv()
            copies["relay", shift].wait_recv()
        for name in plan:
            copies[name].wait_send()


def experts_up(message, dy_all, w_in, expert_out, n_experts, n_fsdp):
    blocks, rows, width = dy_all.shape
    long = message.shape[1]
    hidden = w_in.shape[1]
    once = pl.Buffered(1)
    whole = lambda shape: pl.BlockSpec(shape, lambda i: (0,) * len(shape), pipeline_mode=once)
    turn = lambda columns: pl.BlockSpec((None, rows, columns), lambda i: ((i + 7) % 8, 0, 0))
    anywhere = pl.BlockSpec(memory_space=pl.ANY)
    dma = lambda *shape: pltpu.SemaphoreType.DMA(shape)
    return pl.pallas_call(
        functools.partial(experts_up_kernel, n_experts, hidden, n_fsdp),
        out_shape=[
            jax.ShapeDtypeStruct((blocks, rows, long), bf16),
            jax.ShapeDtypeStruct((blocks, rows, hidden), bf16),
            jax.ShapeDtypeStruct((blocks, rows, hidden), bf16),
            jax.ShapeDtypeStruct((hidden, width), bf16),
            jax.ShapeDtypeStruct((n_fsdp,) + expert_out.shape[1:], bf16),
        ],
        grid=(blocks,),
        in_specs=[whole((rows, long)), turn(width), whole((width, hidden)), anywhere],
        out_specs=[turn(long), turn(hidden), turn(hidden), whole((hidden, width)), anywhere],
        scratch_shapes=[
            pltpu.VMEM((blocks, rows, long), bf16),
            pltpu.VMEM((hidden, width), f32),
            pltpu.VMEM(expert_out.shape[1:], bf16),
            dma(16),
            dma(16),
            dma(2),
        ],
        compiler_params=pltpu.CompilerParams(
            vmem_limit_bytes=VMEM_LIMIT, collective_id=2, has_side_effects=True
        ),
        cost_estimate=pl.CostEstimate(
            flops=20_000_000_000, transcendentals=0, bytes_accessed=30_000_000
        ),
        name="experts_up",
    )(message, dy_all, w_in, expert_out)


def experts_down_kernel(
    n_experts,
    chunk,
    n_fsdp,
    message_ref,
    dy_ref,
    act_ref,
    slope_ref,
    w_in_ref,
    w_out_ref,
    dw_out,
    back_ref,
    out_half,
    dw_in_ref,
    sum_out,
    part_ref,
    tx_ref,
    rx_ref,
    fin_ref,
    fin_out_ref,
    land_ref,
    dw_in_acc,
    tx_send,
    tx_recv,
    fin_sem,
    land_sem,
    local,
    near,
    mid,
    far,
    own_ref,
    line_send,
    line_recv,
    line_local,
):
    step = pl.program_id(0)
    last = 7
    me = Place(n_fsdp)
    core = me.core
    rows, width = dy_ref.shape
    hidden = w_in_ref.shape[1]
    long = message_ref.shape[1]
    half = rows // 2
    mate = me.mate()
    adds = LineSum(me, dw_out, near, mid, far, own_ref, line_send, line_recv, line_local)

    def to_mate(j):
        return pltpu.make_async_remote_copy(
            src_ref=tx_ref.at[j % 2],
            dst_ref=rx_ref.at[j],
            send_sem=tx_send.at[j],
            recv_sem=tx_recv.at[j],
            device_id=mate,
            device_id_type=MESH,
        )

    def to_owner(j):
        q, k = plane_slot(down_order(j))
        return pltpu.make_async_remote_copy(
            src_ref=fin_ref.at[j % 2],
            dst_ref=land_ref.at[q, core],
            send_sem=fin_sem.at[j],
            recv_sem=land_sem.at[q, core],
            device_id=me.chip(q // 2, q % 2, k),
            device_id_type=MESH,
        )

    def keep_out(j):
        return pltpu.make_async_copy(fin_out_ref.at[j % 2], out_half.at[down_order(j)], local.at[j])

    def stays(j):
        q, k = plane_slot(down_order(j))
        return (q == 0) & (k == core)

    def finish_block(j):
        to_mate(j).wait_recv()
        mine = part_ref.at[j % 2, pl.ds(core * half, half)]

        @pl.when(j >= 2)
        def _():
            keep_out(j - 2).wait()

        @pl.when((j >= 2) & ~stays(j - 2))
        def _():
            to_owner(j - 2).wait_send()

        fin_ref[j % 2] = (mine[:, :long] + rx_ref[j, :, :long].astype(f32)).astype(bf16)

        @pl.when(stays(j))
        def _():
            land_ref[0, core] = fin_ref[j % 2]

        @pl.when(~stays(j))
        def _():
            to_owner(j).start()

        fin_out_ref[j % 2] = (mine[:, long:] + rx_ref[j, :, long:].astype(f32)).astype(bf16)
        keep_out(j).start()

    @pl.when(step == 0)
    def _():
        partners = [mate, me.along(1), me.along(-1)]
        for q in (1, 2, 3):
            for k in (0, 1):
                partners.append(me.chip(q // 2, q % 2, (core + k) % 2))
        meet(partners)
        adds.start()
        dw_in_acc[...] = jnp.zeros_like(dw_in_acc)

    @pl.when(step == 3)
    def _():
        adds.turn()

    expert = me.rep
    h_turned = message_ref[:, :width].T
    extra = message_ref[:, width:].astype(f32)
    lane = lax.broadcasted_iota(jnp.int32, extra.shape, 1)
    mine = (lane == expert) | (lane == expert + n_experts)
    gate = jnp.sum(jnp.where(mine, extra, 0.0), -1, keepdims=True)
    dy = dy_ref[...]
    dgate = None
    part = part_ref.at[step % 2]
    for start in range(0, hidden, chunk):
        piece = slice(start, start + chunk)
        act = act_ref[:, piece].astype(f32)
        dact = dot_t(dy, w_out_ref[piece, :])
        gated = (gate * act).astype(bf16)
        dgate_part = jnp.sum(act * dact, -1, keepdims=True)
        dup = (gate * dact * slope_ref[:, piece].astype(f32)).astype(bf16)
        out_part = dot(gated, w_out_ref[piece, :])
        dh_part = dot_t(dup, w_in_ref[:, piece])
        if start == 0:
            part[:, long:] = out_part
            part[:, :width] = dh_part
        else:
            part[:, long:] += out_part
            part[:, :width] += dh_part
        dgate = dgate_part if dgate is None else dgate + dgate_part
        dw_in_acc[:, piece] += dot(h_turned, dup)
        if start == chunk:

            @pl.when(step >= 1)
            def _():
                finish_block(step - 1)

    high = dgate.astype(bf16).astype(f32)
    low = dgate - high
    part[:, width:long] = jnp.where(
        lane == expert, high, jnp.where(lane == expert + n_experts, low, 0.0)
    )

    @pl.when(step >= 2)
    def _():
        to_mate(step - 2).wait_send()

    tx_ref[step % 2] = part_ref[step % 2, pl.ds((1 - core) * half, half)].astype(bf16)
    to_mate(step).start()

    @pl.when(step == last)
    def _():
        dw_in_ref[...] = dw_in_acc[...].astype(bf16)
        finish_block(last)
        sum_out[...] = adds.total()
        to_mate(last - 1).wait_send()
        to_mate(last).wait_send()
        keep_out(last - 1).wait()
        keep_out(last).wait()
        to_owner(last - 1).wait_send()

        @pl.when(~stays(last))
        def _():
            to_owner(last).wait_send()

        for side in range(2):
            total = None
            for q in range(4):
                arrived = pltpu.make_async_remote_copy(
                    src_ref=fin_ref.at[0],
                    dst_ref=land_ref.at[q, side],
                    send_sem=fin_sem.at[0],
                    recv_sem=land_sem.at[q, side],
                    device_id=mate,
                    device_id_type=MESH,
                )
                if q == 0:

                    @pl.when(core != side)
                    def _():
                        arrived.wait_recv()

                else:
                    arrived.wait_recv()
                landed = land_ref[q, side].astype(f32)
                total = landed if total is None else total + landed
            back_ref[side * half : (side + 1) * half, :] = total


def experts_down(message_all, dy_all, act, slope, w_in, w_out, dw_out, n_experts, n_fsdp):
    blocks, rows, width = dy_all.shape
    long = message_all.shape[2]
    hidden = w_in.shape[1]
    half = rows // 2
    once = pl.Buffered(1)
    whole = lambda shape: pl.BlockSpec(shape, lambda i: (0,) * len(shape), pipeline_mode=once)
    block = lambda columns: pl.BlockSpec(
        (None, rows, columns), lambda i: (down_order(i), 0, 0)
    )
    anywhere = pl.BlockSpec(memory_space=pl.ANY)
    both = long + width
    dma = lambda *shape: pltpu.SemaphoreType.DMA(shape)
    return pl.pallas_call(
        functools.partial(experts_down_kernel, n_experts, 512, n_fsdp),
        out_shape=[
            jax.ShapeDtypeStruct((rows, long), f32),
            jax.ShapeDtypeStruct((blocks, half, width), bf16),
            jax.ShapeDtypeStruct((width, hidden), bf16),
            jax.ShapeDtypeStruct(dw_out.shape[1:], bf16),
        ],
        grid=(blocks,),
        in_specs=[
            block(long),
            block(width),
            block(hidden),
            block(hidden),
            whole((width, hidden)),
            whole((hidden, width)),
            anywhere,
        ],
        out_specs=[
            whole((rows, long)),
            anywhere,
            whole((width, hidden)),
            whole(dw_out.shape[1:]),
        ],
        scratch_shapes=[
            pltpu.VMEM((2, rows, both), f32),
            pltpu.VMEM((2, half, both), bf16),
            pltpu.VMEM((blocks, half, both), bf16),
            pltpu.VMEM((2, half, long), bf16),
            pltpu.VMEM((2, half, width), bf16),
            pltpu.VMEM((4, 2, half, long), bf16),
            pltpu.VMEM((width, hidden), f32),
            dma(8),
            dma(8),
            dma(8),
            dma(4, 2),
            dma(8),
        ]
        + LineSum.scratch(*dw_out.shape[1:]),
        compiler_params=pltpu.CompilerParams(
            vmem_limit_bytes=VMEM_LIMIT, collective_id=3, has_side_effects=True
        ),
        cost_estimate=pl.CostEstimate(
            flops=40_000_000_000, transcendentals=0, bytes_accessed=40_000_000
        ),
        name="experts_down",
    )(message_all, dy_all, act, slope, w_in, w_out, dw_out)


class LineSum:
    def __init__(self, me, whole, near, mid, far, mine, send, recv, local):
        self.me, self.whole, self.near, self.mid, self.far = me, whole, near, mid, far
        self.mine, self.local = mine, local
        rows = whole.shape[1]
        half = rows // 2
        self.parts = {1: slice(0, half), -1: slice(half, rows)}
        plan = {}
        for i, shift in enumerate((1, -1)):
            part = pl.ds(i * half, half)
            target = (me.line + 2) % me.n_fsdp
            plan["near", shift] = (whole.at[target, part], near.at[i], me.along(shift))
            plan["far", shift] = (mid.at[i], far.at[i], me.along(shift))
        self.copies = Planned(plan, send, recv)

    def loads(self):
        me = self.me
        for i, shift in enumerate((1, -1)):
            source = self.whole.at[(me.line + shift) % me.n_fsdp]
            yield pltpu.make_async_copy(source, self.mid.at[i], self.local.at[i])
        yield pltpu.make_async_copy(self.whole.at[me.line], self.mine, self.local.at[2])

    def start(self):
        for shift in (1, -1):
            self.copies["near", shift].start()
        for load in self.loads():
            load.start()

    def turn(self):
        for load in self.loads():
            load.wait()
        for i, shift in enumerate((1, -1)):
            self.copies["near", shift].wait_recv()
            part = self.parts[shift]
            total = self.mid[i, part, :].astype(f32) + self.near[i].astype(f32)
            self.mid[i, part, :] = total.astype(bf16)
            self.copies["far", shift].start()

    def total(self):
        for shift in (1, -1):
            self.copies["far", shift].wait_recv()
        total = self.mine[...].astype(f32) + self.far[0].astype(f32) + self.far[1].astype(f32)
        for shift in (1, -1):
            self.copies["near", shift].wait_send()
            self.copies["far", shift].wait_send()
        return total.astype(bf16)

    @staticmethod
    def scratch(rows, columns):
        return [
            pltpu.VMEM((2, rows // 2, columns), bf16),
            pltpu.VMEM((2, rows, columns), bf16),
            pltpu.VMEM((2, rows, columns), bf16),
            pltpu.VMEM((rows, columns), bf16),
            pltpu.SemaphoreType.DMA((4,)),
            pltpu.SemaphoreType.DMA((4,)),
            pltpu.SemaphoreType.DMA((3,)),
        ]


class BackgroundBack:
    n_in, n_out = 2, 3

    def __init__(self, n_fsdp):
        self.n_fsdp = n_fsdp

    def out_shape(self, out_half, dw_in):
        half, width = out_half.shape[1:]
        return [
            jax.ShapeDtypeStruct((2 * half, width), bf16),
            jax.ShapeDtypeStruct(dw_in.shape[1:], bf16),
            jax.ShapeDtypeStruct((self.n_fsdp, width // (2 * self.n_fsdp), width), bf16),
        ]

    def out_specs(self, shapes):
        whole = lambda shape: pl.BlockSpec(shape, lambda p, *_: (0,) * len(shape))
        return [whole(s.shape) for s in shapes]

    def scratch(self, out_half, dw_in):
        half, width = out_half.shape[1:]
        pairs = width // LANES
        return [
            pltpu.VMEM((4, 2, half, width), bf16),
            pltpu.SemaphoreType.DMA((8,)),
            pltpu.SemaphoreType.DMA((4, 2)),
            pltpu.VMEM((2, 4) + self.split(width), bf16),
            pltpu.VMEM((pairs, 2) + self.split(width), bf16),
            pltpu.VMEM((pairs, 2) + self.split(width), bf16),
            pltpu.VMEM((pairs, 3, self.n_fsdp) + self.split(width)[2:], bf16),
            pltpu.SemaphoreType.DMA((pairs, 2)),
            pltpu.SemaphoreType.DMA((pairs, 2)),
            pltpu.SemaphoreType.DMA((pairs, 3)),
            pltpu.SemaphoreType.DMA((pairs, 3)),
        ] + LineSum.scratch(*dw_in.shape[1:])

    def split(self, width):
        return (self.n_fsdp, 2, width // (2 * self.n_fsdp), LANES)

    def to_mate(self, pair, i, scratch):
        me = Place(self.n_fsdp)
        own, given = scratch[3:5]
        send, recv = scratch[7:9]
        return pltpu.make_async_remote_copy(
            src_ref=own.at[pair % 2, 2 * i + 1 - me.core],
            dst_ref=given.at[pair, i],
            send_sem=send.at[pair, i],
            recv_sem=recv.at[pair, i],
            device_id=me.mate(),
            device_id_type=MESH,
        )

    def to_chip(self, pair, i, scratch):
        me = Place(self.n_fsdp)
        added, landed = scratch[5:7]
        send, recv = scratch[9:11]
        rows, columns = ((0, 1), (1, 0), (1, 1))[i]
        row, column = (me.row + rows) % 2, (me.seq + columns) % 2
        return pltpu.make_async_remote_copy(
            src_ref=added.at[pair, row, :, column],
            dst_ref=landed.at[pair, i],
            send_sem=send.at[pair, i],
            recv_sem=recv.at[pair, i],
            device_id=me.chip(rows, columns),
            device_id_type=MESH,
        )

    def give(self, pair, grads, scratch):
        own = scratch[3]

        @pl.when(pair >= 2)
        def _():
            for i in (0, 1):
                self.to_mate(pair - 2, i, scratch).wait_send()

        for i, grad in enumerate(grads):
            own[pair % 2, i] = grad.reshape(own.shape[2:])
        for i in (0, 1):
            self.to_mate(pair, i, scratch).start()

    def collect(self, pair, scratch):
        core = Place(self.n_fsdp).core
        own, given, added = scratch[3:6]
        for i in (0, 1):
            self.to_mate(pair, i, scratch).wait_recv()
            total = own[pair % 2, 2 * i + core].astype(f32) + given[pair, i].astype(f32)
            added[pair, i] = total.astype(bf16)
        for i in range(3):
            self.to_chip(pair, i, scratch).start()

    def collect_before(self, pair, scratch):
        @pl.when(pair >= 1)
        def _():
            self.collect(pair - 1, scratch)

    def run(self, step, before, ins, outs, scratch, x_mid):
        out_half, dw_in = ins
        out_rows, sum_in, plane_sum = outs
        land, send, recv = scratch[:3]
        near, mid, far, mine, line_send, line_recv, line_local = scratch[11:]
        me = Place(self.n_fsdp)
        core = me.core
        half = out_half.shape[1]
        line = LineSum(me, dw_in, near, mid, far, mine, line_send, line_recv, line_local)

        def to_owner(j):
            q, k = plane_slot(j)
            return pltpu.make_async_remote_copy(
                src_ref=out_half.at[j],
                dst_ref=land.at[q, core],
                send_sem=send.at[j],
                recv_sem=recv.at[q, core],
                device_id=me.chip(q // 2, q % 2, k),
                device_id_type=MESH,
            )

        def stay(j):
            return pltpu.make_async_copy(out_half.at[j], land.at[0, core], send.at[j])

        if before:

            @pl.when(step == 0)
            def _():
                partners = [me.mate(), me.along(1), me.along(-1)]
                for q in (1, 2, 3):
                    for k in (0, 1):
                        partners.append(me.chip(q // 2, q % 2, (core + k) % 2))
                meet(partners)
                line.start()
                for j in range(8):
                    if j in (0, 7):

                        @pl.when(core == (j + 1) % 2)
                        def _():
                            stay(j).start()

                        @pl.when(core != (j + 1) % 2)
                        def _():
                            to_owner(j).start()

                    else:
                        to_owner(j).start()

            @pl.when(step == 2)
            def _():
                line.turn()

            return

        @pl.when(step == pl.num_programs(0) - 1)
        def _():
            added, landed = scratch[5:7]
            pairs = landed.shape[0]
            self.collect(pairs - 1, scratch)
            sum_in[...] = line.total()
            for j in range(8):
                if j in (0, 7):

                    @pl.when(core == (j + 1) % 2)
                    def _():
                        stay(j).wait()

                    @pl.when(core != (j + 1) % 2)
                    def _():
                        to_owner(j).wait_send()

                else:
                    to_owner(j).wait_send()
            for side in range(2):
                here = slice(side * half, (side + 1) * half)
                total = x_mid[here, :]
                for q in range(4):
                    arrived = pltpu.make_async_remote_copy(
                        src_ref=out_half.at[0],
                        dst_ref=land.at[q, side],
                        send_sem=send.at[0],
                        recv_sem=recv.at[q, side],
                        device_id=me.mate(),
                        device_id_type=MESH,
                    )
                    if q == 0:

                        @pl.when(core != side)
                        def _():
                            arrived.wait_recv()

                    else:
                        arrived.wait_recv()
                    total = total + land[q, side].astype(f32)
                out_rows[here, :] = total.astype(bf16)
            for pair in (pairs - 2, pairs - 1):
                for i in (0, 1):
                    self.to_mate(pair, i, scratch).wait_send()
            for pair in range(pairs):
                total = added[pair, me.row, :, me.seq].astype(f32)
                for i in range(3):
                    self.to_chip(pair, i, scratch).wait_recv()
                    total = total + landed[pair, i].astype(f32)
                plane_sum[:, :, pair * LANES : (pair + 1) * LANES] = total.astype(bf16)
            for pair in range(pairs):
                for i in range(3):
                    self.to_chip(pair, i, scratch).wait_send()


def backward_kernel(
    background,
    n_experts,
    head_dim,
    place_ref,
    back_ref,
    dy_ref,
    x_mid_ref,
    message_ref,
    probs_ref,
    pack_ref,
    h_ref,
    wq_ref,
    wk_ref,
    wv_ref,
    wo_ref,
    q_ref,
    k_ref,
    v_ref,
    o_ref,
    lse_ref,
    *refs,
):
    step = pl.program_id(0)
    n_in, n_out = (background.n_in, background.n_out) if background else (0, 0)
    behind_in, refs = refs[:n_in], refs[n_in:]
    n_grads = 0 if background else 4
    grad_outs, refs = refs[:n_grads], refs[n_grads:]
    dh_own_out, dh_other_out, dx_mid_out, gain_out, router_out, ddist_out = refs[:6]
    behind_out, refs = refs[6 : 6 + n_out], refs[6 + n_out :]
    da_ref, dh_all_ref, dh_mine_ref, mask_ref, bias_ref, dbias_ref, dq_ref, dist_ref = refs[:8]
    if background:
        background.run(step, True, behind_in, behind_out, refs[8:], x_mid_ref)
    rows, width = x_mid_ref.shape
    length = h_ref.shape[0]
    own = pl.ds(pl.multiple_of(first_row(rows), rows), rows)

    @pl.when(step == 0)
    def _():
        probs = probs_ref[...]
        chosen = chosen_experts(pack_ref, probs.shape)
        picked = jnp.where(chosen, probs, 0.0)
        total = jnp.sum(picked, -1, keepdims=True)
        gate = picked / total
        extra = back_ref[:, width:].astype(f32)
        dgate = extra + pltpu.roll(extra, LANES - n_experts, 1)
        dgate = jnp.where(chosen, dgate, 0.0)
        shared = jnp.sum(dgate * gate, -1, keepdims=True)
        dprobs = jnp.where(chosen, (dgate - shared) / total, 0.0)
        dlogits = probs * (dprobs - jnp.sum(probs * dprobs, -1, keepdims=True))
        h_two = message_ref[:, :width].astype(f32)
        router_out[...] = lax.dot_general(
            dlogits,
            h_two,
            (((0,), (0,)), ((), ())),
            precision=highest,
            preferred_element_type=f32,
        )
        dh_two = back_ref[:, :width].astype(f32) + exact_dot(
            dlogits, router_rows(pack_ref, n_experts, width)
        )
        dx, dgain = norm_back(x_mid_ref[...], pack_ref[5:6, :width], dh_two)
        gain_out[...] = dgain
        dx_mid = dx + dy_ref[...].astype(f32)
        dx_mid_out[...] = dx_mid
        da_ref[...] = dx_mid.astype(bf16)
        dh_all_ref[...] = jnp.zeros_like(dh_all_ref)
        dh_mine_ref[...] = jnp.zeros_like(dh_mine_ref)
        ddist_out[...] = jnp.zeros_like(ddist_out)
        dist_ref[...] = distances(pack_ref)
        make_mask(place_ref, mask_ref)

    da = da_ref[...]
    do = dot_t(da, wo_ref[...]).astype(bf16)
    block = LANES
    span = pack_ref.shape[1]
    first_half = lax.broadcasted_iota(jnp.int32, (block, LANES), 1) < head_dim
    zero = jnp.zeros((), bf16)
    k_low = k_ref[...]
    v_low = v_ref[...]
    dk = None
    dv = None
    for head in range(2):
        bias_ref[head] = spread(dist_ref[pl.ds(2 * step + head, 1), :], block, span)
        dbias_ref[head] = jnp.zeros_like(dbias_ref[head])
    for b in range(rows // block):
        here = slice(b * block, (b + 1) * block)
        offset = pl.multiple_of(length - LANES - block * b - first_row(rows), LANES)
        halves = []
        for head in range(2):
            mine = first_half if head == 0 else ~first_half
            q_head = jnp.where(mine, q_ref[here, :], zero)
            do_head = jnp.where(mine, do[here], zero)
            scores = dot_t(q_head, k_low)
            scores = scores + bias_ref[head, :, pl.ds(offset, length)] + mask_ref[here, :]
            at = head * head_dim
            probs = jnp.exp(scores - lse_ref[here, at : at + 1])
            dprobs = dot_t(do_head, v_low)
            weighted = probs * dprobs
            ds = weighted - probs * jnp.sum(weighted, -1, keepdims=True)
            ds_low = ds.astype(bf16)
            dbias_ref[head, :, pl.ds(offset, length)] += ds
            halves.append(dot(ds_low, k_low))
            dk_part = t_dot(ds_low, q_head)
            dv_part = t_dot(probs.astype(bf16), do_head)
            dk = dk_part if dk is None else dk + dk_part
            dv = dv_part if dv is None else dv + dv_part
        dq_ref[here, :] = (
            jnp.where(first_half, halves[0], halves[1]) * (head_dim**-0.5)
        ).astype(bf16)
    for head in range(2):
        ddist_out[pl.ds(2 * step + head, 1), :] = gather_diagonals(dbias_ref[head])
    dq = dq_ref[...]
    dk = dk.astype(bf16)
    dv = dv.astype(bf16)
    h_all = h_ref[...]
    da_columns = da_ref[:, pl.ds(pl.multiple_of(step * LANES, LANES), LANES)]
    if background:
        background.collect_before(step, refs[8:])
    factors = ((h_ref[own, :], dq), (h_all, dk), (h_all, dv), (o_ref[...], da_columns))
    grads = [t_dot(left, right).astype(bf16) for left, right in factors]
    if background:
        background.give(step, grads, refs[8:])
    else:
        for target, grad in zip(grad_outs, grads):
            target[...] = grad
    dh_all_ref[...] += dot_t(dk, wk_ref[...]) + dot_t(dv, wv_ref[...])
    dh_mine_ref[...] += dot_t(dq, wq_ref[...])

    @pl.when(step == pl.num_programs(0) - 1)
    def _():
        other = pl.ds(pl.multiple_of(length - rows - first_row(rows), rows), rows)
        dh_own_out[...] = dh_mine_ref[...] + dh_all_ref[own, :]
        dh_other_out[...] = dh_all_ref[other, :].astype(bf16)

    if background:
        background.run(step, False, behind_in, behind_out, refs[8:], x_mid_ref)


def attention_backward(
    place,
    back,
    dy,
    x_mid,
    message,
    probs,
    pack,
    h_all,
    weights,
    q,
    k,
    v,
    o,
    lse,
    n_experts,
    head_dim,
    background=None,
    behind=(),
):
    n_rows, width = x_mid.shape
    length = h_all.shape[0]
    pairs = width // LANES
    span = pack.shape[1]
    more_shapes, more_scratch, params = [], [], {}
    n_grads = 0 if background else 4
    if background:
        more_shapes = background.out_shape(*behind)
        more_scratch = background.scratch(*behind)
        params = {"collective_id": 4, "has_side_effects": True}
    anywhere = pl.BlockSpec(memory_space=pl.ANY)
    whole = lambda shape: pl.BlockSpec(shape, lambda p, *_: (0,) * len(shape))
    columns = lambda rows: pl.BlockSpec((rows, LANES), lambda p, *_: (0, p))
    matrix = lambda i: pl.BlockSpec((None, width, LANES), lambda p, *_: (i, 0, p))
    return pl.pallas_call(
        functools.partial(backward_kernel, background, n_experts, head_dim),
        out_shape=[jax.ShapeDtypeStruct((width, width), bf16)] * n_grads
        + [
            jax.ShapeDtypeStruct((n_rows, width), f32),
            jax.ShapeDtypeStruct((n_rows, width), bf16),
            jax.ShapeDtypeStruct((n_rows, width), f32),
            jax.ShapeDtypeStruct((1, width), f32),
            jax.ShapeDtypeStruct((LANES, width), f32),
            jax.ShapeDtypeStruct((16, span), f32),
        ]
        + more_shapes,
        grid_spec=pltpu.PrefetchScalarGridSpec(
            num_scalar_prefetch=1,
            grid=(pairs,),
            in_specs=[
                whole((n_rows, width + LANES)),
                whole((n_rows, width)),
                whole((n_rows, width)),
                whole((n_rows, width + LANES)),
                whole((n_rows, LANES)),
                whole(pack.shape),
                whole((length, width)),
                matrix(0),
                matrix(1),
                matrix(2),
                pl.BlockSpec((None, LANES, width), lambda p, *_: (3, p, 0)),
                columns(n_rows),
                columns(length),
                columns(length),
                whole((n_rows, width)),
                columns(n_rows),
            ]
            + [anywhere] * len(behind),
            out_specs=[columns(width)] * n_grads
            + [
                whole((n_rows, width)),
                whole((n_rows, width)),
                whole((n_rows, width)),
                whole((1, width)),
                whole((LANES, width)),
                whole((16, span)),
            ]
            + (background.out_specs(more_shapes) if background else []),
            scratch_shapes=[
                pltpu.VMEM((n_rows, width), bf16),
                pltpu.VMEM((length, width), f32),
                pltpu.VMEM((n_rows, width), f32),
                pltpu.VMEM((n_rows, length), f32),
                pltpu.VMEM((2, LANES, span), f32),
                pltpu.VMEM((2, LANES, span), f32),
                pltpu.VMEM((n_rows, LANES), bf16),
                pltpu.VMEM((16, span), f32),
            ]
            + more_scratch,
        ),
        compiler_params=pltpu.CompilerParams(vmem_limit_bytes=VMEM_LIMIT, **params),
        cost_estimate=pl.CostEstimate(
            flops=40_000_000_000, transcendentals=0, bytes_accessed=30_000_000
        ),
        name="attention_backward",
    )(
        place,
        back,
        dy,
        x_mid,
        message,
        probs,
        pack,
        h_all,
        weights,
        weights,
        weights,
        weights,
        q,
        k,
        v,
        o,
        lse,
        *behind,
    )


def finish_kernel(
    n_fsdp,
    n_experts,
    n_heads,
    sum_in,
    sum_out,
    dh_other,
    line_ref,
    dh_own_ref,
    dx_mid_ref,
    tokens_ref,
    pack_ref,
    dgain_two_ref,
    drouter_ref,
    ddist_ref,
    attn_out,
    grad_in,
    grad_out,
    tokens_out,
    small_out,
    line_land,
    dh_land,
    small_plane,
    small_line,
    in_held,
    out_held,
    send,
    recv,
    local,
):
    me = Place(n_fsdp)
    rep, line, seq, core, row = me.rep, me.line, me.seq, me.core, me.row
    width = tokens_ref.shape[1]
    mate, across, beside, corner = me.mate(), me.chip(1, 0), me.chip(0, 1), me.chip(1, 1)
    far_row = (row + 1) % 2
    far_rep = far_row * 2 + core
    part_out = sum_out.shape[0]
    columns = lambda z, x: pl.ds(pl.multiple_of((z * 2 + x) * part_out, LANES), part_out)
    here = rep * 2 + seq
    peers = [mate, across, beside, corner]
    peers += [me.chip(1, 0, 1 - core), me.chip(0, 1, 1 - core), me.chip(1, 1, 1 - core)]
    shifts = (1, -1, 2)
    plan = {
        "dh": (dh_other, dh_land, beside),
        "out_c": (sum_out, grad_out.at[rep], mate),
        "out_y": (sum_out, grad_out.at[rep], across),
        "out_f": (grad_out.at[far_rep], grad_out.at[far_rep], mate),
        "attn_c": (line_land.at[3], attn_out.at[rep], mate),
        "attn_y": (line_land.at[3], attn_out.at[rep], across),
        "attn_f": (attn_out.at[far_rep], attn_out.at[far_rep], mate),
        "in_c": (grad_in.at[rep], grad_in.at[rep], mate),
        "in_y": (grad_in.at[rep], grad_in.at[rep], across),
        "in_f": (grad_in.at[far_rep], grad_in.at[far_rep], mate),
    }
    for i, shift in enumerate(shifts):
        target = (line + shift) % n_fsdp
        plan["line", i] = (line_ref.at[target], line_land.at[i], me.along(shift))
        plan["small_z", i] = (small_line.at[line], small_line.at[line], me.along(shift))
    for z in range(n_fsdp):
        plan["in_x", z] = (
            sum_in.at[1 - seq, :, pl.ds(z * part_out, part_out)],
            grad_in.at[rep, :, columns(z, seq)],
            beside,
        )
    for i, peer in enumerate(peers):
        plan["small", i] = (small_plane.at[here], small_plane.at[here], peer)
    copies = Planned(plan, send, recv)
    meet(peers + [me.along(shift) for shift in shifts])
    for i in range(3):
        copies["line", i].start()
    for z in range(n_fsdp):
        copies["in_x", z].start()
    copies["out_y"].start()
    copies["dh"].start()
    copies["out_c"].start()
    own_in = pltpu.make_async_copy(sum_in.at[seq], in_held, local.at[2])
    own_in.start()
    own_out = Bounce(sum_out, out_held, grad_out.at[rep], local.at[pl.ds(8, 2)])
    own_out.start()
    own_in.wait()
    kept = []
    for z in range(n_fsdp):
        source = in_held.at[:, pl.ds(z * part_out, part_out)]
        target = grad_in.at[rep, :, columns(z, seq)]
        kept.append(pltpu.make_async_copy(source, target, local.at[4 + z]))
        kept[-1].start()
    own_out.turn()
    table = exact_dot_t(ddist_ref[...], bucket_match(pack_ref))
    small = small_plane.at[here]
    small[...] = jnp.zeros_like(small_out)
    small[1:2, :] = dgain_two_ref[...]
    small[2 : 2 + n_experts, :] = drouter_ref[:n_experts, :]
    for head in range(n_heads):
        at = head % 6 * LANES
        small[6 + head // 6, at : at + LANES] = table[head]
    for copy in kept:
        copy.wait()
    for z in range(n_fsdp):
        copies["in_x", z].wait_recv()
    copies["in_y"].start()
    copies["in_c"].start()
    total = line_ref[line].astype(f32)
    for i in range(3):
        copies["line", i].wait_recv()
        total = total + line_land[i].astype(f32)
    line_land[3] = total.astype(bf16)
    copies["attn_y"].start()
    copies["attn_c"].start()
    own_attn = pltpu.make_async_copy(line_land.at[3], attn_out.at[rep], local.at[3])
    own_attn.start()
    copies["out_y"].wait_recv()
    copies["out_f"].start()
    copies["dh"].wait_recv()
    dh_one = dh_own_ref[...] + dh_land[...].astype(f32)
    gain_one = pack_ref[4:5, :width]
    dx, dgain_one = norm_back(tokens_ref[...].astype(f32), gain_one, dh_one)
    small[0:1, :] = dgain_one
    for i in range(len(peers)):
        copies["small", i].start()
    tokens_out[...] = (dx_mid_ref[...] + dx).astype(bf16)
    copies["attn_y"].wait_recv()
    copies["attn_f"].start()
    for i in range(len(peers)):
        copies["small", i].wait_recv()
    total = small_plane[0]
    for i in range(1, 8):
        total = total + small_plane[i]
    small_line[line] = total
    for i in range(3):
        copies["small_z", i].start()
    copies["in_y"].wait_recv()
    copies["in_f"].start()
    for i in range(3):
        copies["small_z", i].wait_recv()
    total = small_line[0]
    for i in range(1, n_fsdp):
        total = total + small_line[i]
    small_out[...] = total
    own_attn.wait()
    own_out.wait()
    for name in ("attn_c", "attn_f", "in_c", "in_f", "out_c", "out_f"):
        copies[name].wait_recv()
    for name in plan:
        copies[name].wait_send()


def finish(
    plane_sum,
    sum_in,
    sum_out,
    dh_other,
    dh_own,
    dx_mid,
    tokens,
    pack,
    dgain_two,
    drouter,
    ddist,
    n_fsdp,
    n_experts,
    n_heads,
    hidden,
):
    n_rows, width = tokens.shape
    part_attn = plane_sum.shape[1]
    part_in = sum_in.shape[1]
    anywhere = pl.BlockSpec(memory_space=pl.ANY)
    inside = pl.BlockSpec(memory_space=pltpu.VMEM)
    dma = lambda n: pltpu.SemaphoreType.DMA((n,))
    return pl.pallas_call(
        functools.partial(finish_kernel, n_fsdp, n_experts, n_heads),
        out_shape=[
            jax.ShapeDtypeStruct((4, part_attn, width), bf16),
            jax.ShapeDtypeStruct((n_experts, part_in, hidden), bf16),
            jax.ShapeDtypeStruct((n_experts,) + sum_out.shape, bf16),
            jax.ShapeDtypeStruct((n_rows, width), bf16),
            jax.ShapeDtypeStruct((8, width), f32),
        ],
        in_specs=[anywhere] * 3 + [inside] * 8,
        out_specs=[anywhere] * 3 + [inside] * 2,
        scratch_shapes=[
            pltpu.VMEM((4, part_attn, width), bf16),
            pltpu.VMEM((n_rows, width), bf16),
            pltpu.VMEM((8, 8, width), f32),
            pltpu.VMEM((n_fsdp, 8, width), f32),
            pltpu.VMEM(sum_in.shape[1:], bf16),
            pltpu.VMEM(sum_out.shape, bf16),
            dma(40),
            dma(40),
            dma(12),
        ],
        compiler_params=pltpu.CompilerParams(
            vmem_limit_bytes=VMEM_LIMIT, collective_id=5, has_side_effects=True
        ),
        name="finish_gradients",
    )(
        sum_in,
        sum_out,
        dh_other,
        plane_sum,
        dh_own,
        dx_mid,
        tokens,
        pack,
        dgain_two,
        drouter,
        ddist,
    )


def widen_kernel(
    n_experts, n_heads, n_buckets, attn, grad_in, grad_out, small, q, k, v, o, win, wout, *rest
):
    step = pl.program_id(0)
    for i, target in enumerate((q, k, v, o)):

        @pl.when(step == i)
        def _():
            target[...] = attn[...].astype(f32)

    win[...] = grad_in[...].astype(f32)
    wout[...] = grad_out[...].astype(f32)
    gain_one, gain_two, table, router = rest

    @pl.when(step == 0)
    def _():
        gain_one[...] = small[0, :]
        gain_two[...] = small[1, :]
        router[...] = small[2 : 2 + n_experts, :]
        for head in range(n_heads):
            at = head % 6 * LANES
            table[head : head + 1, :] = small[
                6 + head // 6 : 7 + head // 6, at : at + n_buckets
            ]


def widen(attn, grad_in, grad_out, small, n_heads, n_buckets):
    n_experts = grad_in.shape[0]
    width = small.shape[1]
    own = lambda a: pl.BlockSpec((None,) + a.shape[1:], lambda i: (i, 0, 0))
    whole = lambda shape: pl.BlockSpec(shape, lambda i: (0,) * len(shape))
    small_shapes = [(width,), (width,), (n_heads, n_buckets), (n_experts, width)]
    wide = [attn.shape[1:]] * 4
    return pl.pallas_call(
        functools.partial(widen_kernel, n_experts, n_heads, n_buckets),
        out_shape=[jax.ShapeDtypeStruct(shape, f32) for shape in wide]
        + [jax.ShapeDtypeStruct(a.shape, f32) for a in (grad_in, grad_out)]
        + [jax.ShapeDtypeStruct(shape, f32) for shape in small_shapes],
        grid=(n_experts,),
        in_specs=[own(attn), own(grad_in), own(grad_out), whole(small.shape)],
        out_specs=[whole(shape) for shape in wide]
        + [own(grad_in), own(grad_out)]
        + [whole(shape) for shape in small_shapes],
        compiler_params=pltpu.CompilerParams(vmem_limit_bytes=VMEM_LIMIT),
        name="widen",
    )(attn, grad_in, grad_out, small)


def per_device(
    tokens,
    piece_starts,
    routes,
    buckets,
    attn_q,
    attn_k,
    attn_v,
    attn_o,
    expert_in,
    expert_out,
    gain_attn,
    gain_ffn,
    rel_table,
    router,
    cotangent,
):
    n_rep, n_fsdp, n_seq = (lax.axis_size(a) for a in ("rep", "fsdp", "seq"))
    rep = lax.axis_index("rep")
    seq = lax.axis_index("seq")
    plane = ("rep", "seq")
    n_rows, width = tokens.shape
    n_buckets, n_heads = rel_table.shape
    head_dim = width // n_heads
    n_experts, part_in, hidden = expert_in.shape
    part_out = expert_out.shape[1]
    part_attn = attn_q.shape[0]
    length = n_rows * n_seq
    assert n_experts == n_rep == 4 and n_seq == 2 and 2 * head_dim == LANES
    pairs = n_heads // 2

    place = piece_starts[0]
    near = n_fsdp == 4 and part_attn % 16 == 0
    pick = lambda array: lax.dynamic_index_in_dim(array, rep, 0, keepdims=False)
    span = -(-buckets.shape[0] // LANES) * LANES
    if near:
        weights, x_all, w_in, pack = gather(
            (attn_q, attn_k, attn_v, attn_o),
            tokens,
            expert_in,
            part_out,
            n_fsdp,
            (router.T, gain_attn, gain_ffn, buckets, rel_table.T, routes.T),
            span,
        )
    else:
        attn_own = pick(jnp.stack([attn_q, attn_k, attn_v, attn_o]))
        attn_line = lax.all_gather(attn_own, "fsdp", axis=0, tiled=False)
        attn_all = lax.all_gather(attn_line, plane, axis=0, tiled=False)
        attn_all = attn_all.reshape(n_rep, n_seq, n_fsdp, part_attn, width)
        weights = attn_all.transpose(0, 2, 1, 3, 4).reshape(n_rep, width, width)
        x_all = lax.all_gather(tokens, "seq", axis=0, tiled=True)
        in_own = pick(expert_in).reshape(part_in, n_fsdp, n_seq, part_out)
        in_own = in_own.transpose(2, 0, 1, 3).reshape(n_seq, part_in, n_fsdp * part_out)
        in_pair = lax.all_to_all(in_own, "seq", split_axis=0, concat_axis=0, tiled=True)
        in_pair = in_pair.reshape(n_seq * part_in, n_fsdp * part_out)
        w_in = lax.all_gather(in_pair, "fsdp", axis=0, tiled=True)
        w_out = lax.all_gather(pick(expert_out), "fsdp", axis=0, tiled=True)
        dy_all = lax.all_gather(cotangent, plane, axis=0, tiled=True)
        pack = pack_small(router, gain_attn, gain_ffn, buckets, rel_table, routes, span)

    q, k, v, o, lse, x_mid, message, probs, h_all, *gathered = attention_forward(
        place,
        x_all,
        weights,
        pack,
        n_rows,
        n_experts,
        head_dim,
        Background(n_fsdp) if near else None,
        (cotangent, w_in) if near else (),
    )
    behind = ()
    if near:
        dy_all, w_in = gathered
        w_in = w_in.reshape(width, n_fsdp * part_out)
        message_all, act, slope, dw_out, w_out = experts_up(
            message, dy_all, w_in, expert_out, n_experts, n_fsdp
        )
        back, out_half, dw_in, sum_out = experts_down(
            message_all,
            dy_all,
            act,
            slope,
            w_in,
            w_out.reshape(n_fsdp * part_out, width),
            dw_out.reshape(n_fsdp, part_out, width),
            n_experts,
            n_fsdp,
        )
        behind = (out_half, dw_in.reshape(n_fsdp, n_seq * part_in, n_fsdp * part_out))
    else:
        message_all = lax.all_gather(message, plane, axis=0, tiled=True)
        out_part, back_part, dw_in, dw_out = experts(
            rep[None].astype(jnp.int32), message_all, dy_all, w_in, w_out, n_experts, n_rows
        )
        back = lax.psum_scatter(back_part, plane, scatter_dimension=0, tiled=True)
        out_sum = lax.psum_scatter(out_part, plane, scatter_dimension=0, tiled=True)
        out_rows = (x_mid + out_sum.astype(f32)).astype(bf16)

    grads = attention_backward(
        place,
        back,
        cotangent,
        x_mid,
        message,
        probs,
        pack,
        h_all,
        weights,
        q,
        k,
        v,
        o,
        lse,
        n_experts,
        head_dim,
        BackgroundBack(n_fsdp) if near else None,
        behind,
    )
    if near:
        dh_own, dh_other, dx_mid, dgain_two, drouter, ddist, out_rows, sum_in, plane_sum = grads
        attn_sum, grad_in, grad_out, grad_tokens, small = finish(
            plane_sum,
            sum_in.reshape(n_seq, part_in, n_fsdp * part_out),
            sum_out,
            dh_other,
            dh_own,
            dx_mid,
            tokens,
            pack,
            dgain_two,
            drouter,
            ddist,
            n_fsdp,
            n_experts,
            n_heads,
            hidden,
        )
        *wide, grad_one, grad_two, grad_table, grad_router = widen(
            attn_sum, grad_in, grad_out, small, n_heads, n_buckets
        )
        return (
            out_rows,
            grad_tokens,
            *wide,
            grad_one,
            grad_two,
            grad_table.T,
            grad_router.T,
        )
    dwq, dwk, dwv, dwo, dh_own, dh_other, dx_mid, dgain_two, drouter, ddist = grads
    sum_out = lax.psum_scatter(dw_out, "fsdp", scatter_dimension=0, tiled=True)
    sum_in = lax.psum_scatter(dw_in, "fsdp", scatter_dimension=0, tiled=True)
    sum_in = sum_in.reshape(n_seq, part_in, n_fsdp * part_out)
    sum_in = lax.all_to_all(sum_in, "seq", split_axis=0, concat_axis=0, tiled=True)
    sum_in = sum_in.reshape(n_seq, part_in, n_fsdp, part_out).transpose(1, 2, 0, 3)
    sum_in = sum_in.reshape(part_in, hidden)
    grad_out = lax.all_gather(sum_out, "rep", axis=0, tiled=False)
    grad_in = lax.all_gather(sum_in, "rep", axis=0, tiled=False)
    swap = [(0, 1), (1, 0)]
    dh_one = dh_own + lax.ppermute(dh_other, "seq", swap).astype(f32)
    dx, dgain_one = norm_back(tokens.astype(f32), gain_attn[None, :], dh_one)
    grad_tokens = (dx_mid + dx).astype(bf16)
    attn_grads = jnp.stack([dwq, dwk, dwv, dwo])
    attn_grads = attn_grads.reshape(n_rep, n_fsdp, n_seq, part_attn, width)
    attn_grads = attn_grads.transpose(0, 2, 1, 3, 4)
    attn_grads = attn_grads.reshape(n_rep * n_seq * n_fsdp * part_attn, width)
    attn_sum = lax.psum_scatter(attn_grads, plane, scatter_dimension=0, tiled=True)
    attn_sum = lax.psum_scatter(attn_sum, "fsdp", scatter_dimension=0, tiled=True)
    attn_sum = lax.all_gather(attn_sum, "rep", axis=0, tiled=False)
    ddist = ddist[:n_heads, : buckets.shape[0]]
    match = (buckets[:, None] == jnp.arange(n_buckets)[None, :]).astype(f32)
    table = lax.dot_general(
        match,
        ddist,
        (((0,), (1,)), ((), ())),
        precision=highest,
        preferred_element_type=f32,
    )
    grad_one, grad_two, grad_table, grad_router = lax.psum(
        (dgain_one[0], dgain_two[0], table, drouter[:n_experts].T), ("rep", "fsdp", "seq")
    )
    attn_sum = attn_sum.astype(f32)
    return (
        out_rows,
        grad_tokens,
        attn_sum[0],
        attn_sum[1],
        attn_sum[2],
        attn_sum[3],
        grad_in.astype(f32),
        grad_out.astype(f32),
        grad_one,
        grad_two,
        grad_table,
        grad_router,
    )


def solution(mesh):
    rows = P(("rep", "fsdp", "seq"), None)
    owned = P(("fsdp", "seq"), None)
    expert = P(None, ("fsdp", "seq"), None)
    in_specs = (
        rows,
        P(("rep", "fsdp"), None),
        rows,
        P(),
        owned,
        owned,
        owned,
        owned,
        expert,
        expert,
        P(),
        P(),
        P(),
        P(),
        rows,
    )
    out_specs = (
        rows,
        rows,
        owned,
        owned,
        owned,
        owned,
        expert,
        expert,
        P(),
        P(),
        P(),
        P(),
    )
    return jax.shard_map(
        per_device, mesh=mesh, in_specs=in_specs, out_specs=out_specs, check_vma=False
    )
```

```python
import functools

import jax
import jax.numpy as jnp
from jax import lax
from jax.experimental import pallas as pl
from jax.experimental.pallas import tpu as pltpu
from jax.sharding import PartitionSpec as P

PIECE = 256
LANES = 128
epsilon = 1e-06
masked_out = -1e30
highest = lax.Precision.HIGHEST
f32 = jnp.float32
bf16 = jnp.bfloat16
VMEM_LIMIT = 58 * 1024 * 1024


def dot(a, b):
    return jnp.dot(a, b, preferred_element_type=f32)


def dot_t(a, b):
    return lax.dot_general(a, b, (((1,), (1,)), ((), ())), preferred_element_type=f32)


def t_dot(a, b):
    return lax.dot_general(a, b, (((0,), (0,)), ((), ())), preferred_element_type=f32)


def exact_dot(a, b):
    return jnp.dot(a, b, precision=highest, preferred_element_type=f32)


def exact_dot_t(a, b):
    return lax.dot_general(
        a, b, (((1,), (1,)), ((), ())), precision=highest, preferred_element_type=f32
    )


def inverse_rms(values):
    return lax.rsqrt(jnp.mean(values * values, -1, keepdims=True) + epsilon)


def norm_back(values, gain, grad):
    scale = inverse_rms(values)
    scaled = values * scale
    grad_gain = jnp.sum(grad * scaled, 0, keepdims=True)
    weighted = gain * grad
    grad_values = scale * weighted - (
        values * (scale * scale * scale) * jnp.mean(weighted * values, -1, keepdims=True)
    )
    return grad_values, grad_gain


def first_row(rows):
    return lax.axis_index("seq") * rows


def make_mask(place_ref, mask_ref):
    shape = mask_ref.shape
    pos_q = first_row(shape[0]) + lax.broadcasted_iota(jnp.int32, shape, 0)
    pos_k = lax.broadcasted_iota(jnp.int32, shape, 1)
    allowed = pos_k <= pos_q
    for piece in range(2):
        start = place_ref[piece]
        in_q = (pos_q >= start) & (pos_q < start + PIECE)
        in_k = (pos_k >= start) & (pos_k < start + PIECE)
        allowed = allowed | (in_q & in_k)
    mask_ref[...] = jnp.where(allowed, 0.0, masked_out)


def spread(row, block, width):
    return pltpu.roll(
        jnp.broadcast_to(row, (block, width)), width - (block - 1), 1, stride=1, stride_axis=0
    )


def by_head(values, first_half):
    zero = jnp.zeros((), values.dtype)
    return jnp.concatenate(
        [jnp.where(first_half, values, zero), jnp.where(first_half, zero, values)]
    )


def of_head(stacked, first_half):
    block = stacked.shape[0] // 2
    return jnp.where(first_half, stacked[:block], stacked[block:])


def gather_diagonals(sums):
    rows = sums.shape[0]
    while rows > 1:
        half = rows // 2
        sums = pltpu.roll(sums[:half], half, 1) + sums[half:]
        rows = half
    return sums


def chosen_experts(pack_ref, shape):
    lane = lax.broadcasted_iota(jnp.int32, shape, 1).astype(f32)
    routes = pack_ref[24:32, : shape[0]].T
    return (lane == routes[:, 0:1]) | (lane == routes[:, 1:2])


def pack_small(router, gain_attn, gain_ffn, buckets, rel_table, routes, span):
    def rows(array, count):
        array = array.astype(f32)
        return jnp.pad(array, ((0, count - array.shape[0]), (0, span - array.shape[1])))

    return jnp.concatenate(
        [
            rows(router.T, 4),
            rows(gain_attn[None, :], 1),
            rows(gain_ffn[None, :], 1),
            rows(buckets[None, :], 2),
            rows(rel_table.T, 16),
            rows(routes.T, 8),
        ]
    )


def router_rows(pack_ref, n_experts, width):
    first = pack_ref[0:8, :width]
    row = lax.broadcasted_iota(jnp.int32, first.shape, 0)
    first = jnp.where(row < n_experts, first, 0.0)
    return jnp.concatenate([first, jnp.zeros((LANES - 8, width), f32)])


def bucket_match(pack_ref):
    shape = (LANES, pack_ref.shape[1])
    bucket = lax.broadcasted_iota(jnp.int32, shape, 0).astype(f32)
    return (bucket == pack_ref[6:7, :]).astype(f32)


def distances(pack_ref):
    return exact_dot(pack_ref[8:24, :LANES], bucket_match(pack_ref))


MESH = pl.DeviceIdType.MESH


class Place:
    def __init__(self, n_fsdp):
        self.rep = lax.axis_index("rep")
        self.line = lax.axis_index("fsdp")
        self.seq = lax.axis_index("seq")
        self.n_fsdp = n_fsdp
        self.row = self.rep // 2
        self.core = self.rep % 2

    def mate(self):
        return (self.row * 2 + 1 - self.core, self.line, self.seq)

    def chip(self, rows, columns, core=None):
        core = self.core if core is None else core
        row = (self.row + rows) % 2
        return (row * 2 + core, self.line, (self.seq + columns) % 2)

    def along(self, steps):
        return (self.rep, (self.line + steps) % self.n_fsdp, self.seq)


def meet(partners):
    barrier = pltpu.get_barrier_semaphore()
    for partner in partners:
        pl.semaphore_signal(barrier, inc=1, device_id=partner, device_id_type=MESH)
    pl.semaphore_wait(barrier, len(partners))


class Wires:
    def __init__(self, send, recv):
        self.send, self.recv = send, recv
        self.names = {}

    def copy(self, name, source, target, device):
        index = self.names.setdefault(name, len(self.names))
        return pltpu.make_async_remote_copy(
            src_ref=source,
            dst_ref=target,
            send_sem=self.send.at[index],
            recv_sem=self.recv.at[index],
            device_id=device,
            device_id_type=MESH,
        )


class Planned:
    def __init__(self, plan, send, recv):
        self.plan, self.send, self.recv = plan, send, recv
        self.order = list(plan)

    def __getitem__(self, name):
        source, target, device = self.plan[name]
        index = self.order.index(name)
        return pltpu.make_async_remote_copy(
            src_ref=source,
            dst_ref=target,
            send_sem=self.send.at[index],
            recv_sem=self.recv.at[index],
            device_id=device,
            device_id_type=MESH,
        )


def gather_kernel(
    n_fsdp,
    part_out,
    attn_q,
    attn_k,
    attn_v,
    attn_o,
    tokens,
    expert_in,
    router,
    gain_attn,
    gain_ffn,
    buckets,
    rel_table,
    routes,
    weights,
    x_all,
    w_in,
    pack,
    attn_held,
    tokens_held,
    in_held,
    send,
    recv,
    local,
):
    me = Place(n_fsdp)
    rep, line, seq = me.rep, me.line, me.seq
    far_row = (me.row + 1) % 2 * 2 + me.core
    mate, across, beside = me.mate(), me.chip(1, 0), me.chip(0, 1)
    part_in = expert_in.shape[1]
    wires = Wires(send, recv)
    meet([mate, across, beside, me.along(1), me.along(-1), me.along(2)])
    started = []

    def start(copy):
        copy.start()
        started.append(copy)
        return copy

    for i, matrix in enumerate((attn_q, attn_k, attn_v, attn_o)):

        @pl.when(rep == i)
        def _():
            own = pltpu.make_async_copy(matrix, attn_held, local.at[0])
            own.start()
            own.wait()

    mine = lambda z, r=rep, x=seq: weights.at[r, z, x]
    shifts = (0, 1, -1, 2)
    at = {0: line}
    z_copies = {}
    for shift in shifts[1:]:
        at[shift] = (line - shift) % n_fsdp
        z_copies[shift] = start(
            wires.copy(("z", shift), attn_held, mine(line), me.along(shift))
        )
    x_copies, y_copies, c_copies, far_copies = {}, {}, [], {}

    def spread_out(shift):
        z = at[shift]
        source = mine(z) if shift else attn_held
        x_copies[shift] = start(wires.copy(("x", shift), source, mine(z), beside))
        y_copies[shift] = start(wires.copy(("y", shift), source, mine(z), across))
        c_copies.append(start(wires.copy(("c", shift), source, mine(z), mate)))

    spread_out(0)
    columns = lambda z, x: pl.ds(pl.multiple_of((z * 2 + x) * part_out, LANES), part_out)
    rows = lambda x: pl.ds(pl.multiple_of(x * part_in, part_in), part_in)
    in_x, in_own = [], []
    for z in range(n_fsdp):
        here = pl.ds(z * part_out, part_out)
        target = w_in.at[line, rows(seq), here]
        in_x.append(
            start(wires.copy(("in", z), expert_in.at[rep, :, columns(z, 1 - seq)], target, beside))
        )
        copy = pltpu.make_async_copy(
            expert_in.at[rep, :, columns(z, seq)], in_held.at[:, here], local.at[1 + z]
        )
        copy.start()
        in_own.append(copy)
    own_attn = pltpu.make_async_copy(attn_held, mine(line), local.at[0])
    own_attn.start()
    x_own = Bounce(tokens, tokens_held, x_all.at[seq], local.at[pl.ds(n_fsdp + 1, 2)])
    x_own.start()
    for copy in in_own:
        copy.wait()
    own_in = pltpu.make_async_copy(in_held, w_in.at[line, rows(seq)], local.at[n_fsdp + 3])
    own_in.start()
    x_own.turn()
    pack[...] = jnp.zeros_like(pack)
    pack[0 : router.shape[0], : router.shape[1]] = router[...]
    pack[4, : gain_attn.shape[0]] = gain_attn[...]
    pack[5, : gain_ffn.shape[0]] = gain_ffn[...]
    pack[6, : buckets.shape[0]] = buckets[...].astype(f32)
    pack[8 : 8 + rel_table.shape[0], : rel_table.shape[1]] = rel_table[...]
    pack[24:26, : routes.shape[1]] = routes[...].astype(f32)
    for shift in shifts[1:]:
        z_copies[shift].wait_recv()
        spread_out(shift)
    for copy in in_x:
        copy.wait_recv()
    own_in.wait()
    in_copies = []
    for i, shift in enumerate((1, -1)):
        half = w_in.at[line, pl.ds(i * part_in, part_in)]
        in_copies.append(start(wires.copy(("line", shift), half, half, me.along(shift))))
    token_copy = start(wires.copy("tokens", tokens, x_all.at[seq], beside))
    for shift in shifts:
        z = at[shift]
        x_copies[shift].wait_recv()
        near = mine(z, rep, 1 - seq)
        far_copies[shift] = start(wires.copy(("far", shift), near, near, across))
        c_copies.append(start(wires.copy(("cx", shift), near, near, mate)))
    for shift in shifts:
        z = at[shift]
        y_copies[shift].wait_recv()
        there = mine(z, far_row, seq)
        c_copies.append(start(wires.copy(("cy", shift), there, there, mate)))
    for shift in shifts:
        z = at[shift]
        far_copies[shift].wait_recv()
        there = mine(z, far_row, 1 - seq)
        c_copies.append(start(wires.copy(("cf", shift), there, there, mate)))
    for copy in c_copies + in_copies + [token_copy]:
        copy.wait_recv()
    x_own.wait()
    own_attn.wait()
    for copy in started:
        copy.wait_send()


def gather(attn, tokens, expert_in, part_out, n_fsdp, small, span):
    part_attn, width = attn[0].shape
    n_rows = tokens.shape[0]
    n_experts, part_in, hidden = expert_in.shape
    anywhere = pl.BlockSpec(memory_space=pl.ANY)
    inside = pl.BlockSpec(memory_space=pltpu.VMEM)
    weights, x_all, w_in, pack = pl.pallas_call(
        functools.partial(gather_kernel, n_fsdp, part_out),
        out_shape=[
            jax.ShapeDtypeStruct((4, n_fsdp, 2, part_attn, width), bf16),
            jax.ShapeDtypeStruct((2, n_rows, width), bf16),
            jax.ShapeDtypeStruct((n_fsdp, 2 * part_in, n_fsdp * part_out), bf16),
            jax.ShapeDtypeStruct((32, span), f32),
        ],
        in_specs=[anywhere] * 6 + [inside] * 6,
        out_specs=[anywhere] * 3 + [inside],
        scratch_shapes=[
            pltpu.VMEM((part_attn, width), bf16),
            pltpu.VMEM((n_rows, width), bf16),
            pltpu.VMEM((part_in, n_fsdp * part_out), bf16),
            pltpu.SemaphoreType.DMA((48,)),
            pltpu.SemaphoreType.DMA((48,)),
            pltpu.SemaphoreType.DMA((8,)),
        ],
        compiler_params=pltpu.CompilerParams(collective_id=0, has_side_effects=True),
        name="gather_weights",
    )(*attn, tokens, expert_in, *small)
    return (
        weights.reshape(4, n_fsdp * 2 * part_attn, width),
        x_all.reshape(2 * n_rows, width),
        w_in,
        pack,
    )


class Bounce:
    def __init__(self, source, held, target, sems):
        self.load = lambda: pltpu.make_async_copy(source, held, sems.at[0])
        self.store = lambda: pltpu.make_async_copy(held, target, sems.at[1])

    def start(self):
        self.load().start()

    def turn(self):
        self.load().wait()
        self.store().start()

    def wait(self):
        self.store().wait()


def line_plan(me, own, pieces):
    rows = pieces.shape[1] // 2
    plan = {}
    for i, shift in enumerate((1, -1)):
        first, rest = pl.ds(i * rows, rows), pl.ds((1 - i) * rows, rows)
        target = pieces.at[me.line]
        piece = pieces.at[(me.line - shift) % me.n_fsdp, first]
        plan["first", shift] = (own.at[first], target.at[first], me.along(shift))
        plan["rest", shift] = (own.at[rest], target.at[rest], me.along(shift))
        plan["relay", shift] = (piece, piece, me.along(shift))
    return plan


class Background:
    n_in, n_out = 2, 2

    def __init__(self, n_fsdp):
        self.n_fsdp = n_fsdp

    def out_shape(self, dy, w_in):
        return [
            jax.ShapeDtypeStruct((8,) + dy.shape, bf16),
            jax.ShapeDtypeStruct(w_in.shape, bf16),
        ]

    def scratch(self, dy, w_in):
        return [
            pltpu.SemaphoreType.DMA((16,)),
            pltpu.SemaphoreType.DMA((16,)),
            pltpu.SemaphoreType.DMA((2,)),
            pltpu.VMEM(dy.shape, bf16),
        ]

    def run(self, step, before, ins, outs, scratch):
        dy, _ = ins
        dy_all, w_in = outs
        send, recv, local, dy_held = scratch
        me = Place(self.n_fsdp)
        half = dy.shape[0] // 2
        first, second = pl.ds(0, half), pl.ds(half, half)
        core = me.core
        own = 7 * (1 - core)
        mate, across, beside = me.mate(), me.chip(1, 0), me.chip(0, 1)
        slot = dy_all.at
        plan = {
            "x": (dy, slot[1 + core], beside),
            "y": (dy, slot[3 + core], across),
            "c0": (dy, slot[own], mate),
            "c1": (slot[1 + core], slot[1 + core], mate),
            "c2": (slot[3 + core], slot[3 + core], mate),
            "c3": (slot[5 + core], slot[5 + core], mate),
            "xy": (slot[1 + core, first], slot[5 + core, first], across),
            "yx": (slot[3 + core, second], slot[5 + core, second], beside),
        }
        line = line_plan(me, w_in.at[me.line], w_in)
        plan |= {name: line[name] for name in line if name[0] != "first"}
        copies = Planned(plan, send, recv)
        own_dy = Bounce(dy, dy_held, slot[own], local.at[pl.ds(0, 2)])
        if before:

            @pl.when(step == 0)
            def _():
                meet([mate, across, beside, me.along(1), me.along(-1)])
                for name in line:
                    if name[0] != "first":
                        copies[name].start()
                for name in ("x", "y", "c0"):
                    copies[name].start()
                own_dy.start()

            @pl.when(step == 3)
            def _():
                own_dy.turn()
                copies["x"].wait_recv()
                copies["xy"].start()
                copies["c1"].start()
                copies["y"].wait_recv()
                copies["yx"].start()
                copies["c2"].start()

            return

        @pl.when(step == pl.num_programs(0) - 1)
        def _():
            copies["xy"].wait_recv()
            copies["yx"].wait_recv()
            copies["c3"].start()
            for name in plan:
                if name not in ("x", "y", "xy", "yx"):
                    copies[name].wait_recv()
            own_dy.wait()
            for name in plan:
                copies[name].wait_send()


def forward_kernel(
    background,
    n_experts,
    head_dim,
    place_ref,
    x_ref,
    wq_ref,
    wk_ref,
    wv_ref,
    wo_ref,
    pack_ref,
    *refs,
):
    step = pl.program_id(0)
    n_in, n_out = (background.n_in, background.n_out) if background else (0, 0)
    behind_in, refs = refs[:n_in], refs[n_in:]
    q_out, k_out, v_out, o_out, p_out, x_mid_out, message_out, probs_out, h_out = refs[:9]
    behind_out, refs = refs[9 : 9 + n_out], refs[9 + n_out :]
    total_ref, mask_ref, bias_ref, dist_ref = refs[:4]
    if background:
        background.run(step, True, behind_in, behind_out, refs[4:])
    rows = x_mid_out.shape[0]
    length, width = x_ref.shape
    own = pl.ds(pl.multiple_of(first_row(rows), rows), rows)

    @pl.when(step == 0)
    def _():
        values = x_ref[...].astype(f32)
        gain_one = pack_ref[4:5, :width]
        h_out[...] = (values * inverse_rms(values) * gain_one).astype(bf16)
        dist_ref[...] = distances(pack_ref)
        total_ref[...] = jnp.zeros_like(total_ref)
        make_mask(place_ref, mask_ref)

    h_all = h_out[...]
    q_low = dot(h_out[own, :], wq_ref[...]).astype(bf16) * (head_dim**-0.5)
    kv_low = dot(h_all, jnp.concatenate([wk_ref[...], wv_ref[...]], 1)).astype(bf16)
    k_low, v_low = kv_low[:, :LANES], kv_low[:, LANES:]
    q_out[...] = q_low
    k_out[...] = k_low
    v_out[...] = v_low
    block = LANES
    span = pack_ref.shape[1]
    first_half = lax.broadcasted_iota(jnp.int32, (block, LANES), 1) < head_dim
    for head in range(2):
        bias_ref[head] = spread(dist_ref[pl.ds(2 * step + head, 1), :], block, span)
    for b in range(rows // block):
        here = slice(b * block, (b + 1) * block)
        offset = pl.multiple_of(length - LANES - block * b - first_row(rows), LANES)
        scores = dot_t(by_head(q_low[here], first_half), k_low).reshape(2, block, length)
        scores = scores + bias_ref[:, :, pl.ds(offset, length)] + mask_ref[here, :]
        top = jnp.max(scores, -1, keepdims=True)
        exp_scores = jnp.exp(scores - top)
        total = jnp.sum(exp_scores, -1, keepdims=True)
        probs = (exp_scores * (1.0 / total)).astype(bf16)
        p_out[:, here, :] = probs
        heads = dot(probs.reshape(2 * block, length), v_low)
        o_out[here, :] = of_head(heads, first_half).astype(bf16)
    total_ref[...] += dot(o_out[...], wo_ref[...])

    @pl.when(step == pl.num_programs(0) - 1)
    def _():
        x_mid = x_ref[own, :].astype(f32) + total_ref[...]
        x_mid_out[...] = x_mid
        h_two = (x_mid * inverse_rms(x_mid) * pack_ref[5:6, :width]).astype(bf16)
        message_out[:, :width] = h_two
        logits = exact_dot_t(h_two.astype(f32), router_rows(pack_ref, n_experts, width))
        lane = lax.broadcasted_iota(jnp.int32, logits.shape, 1)
        logits = jnp.where(lane < n_experts, logits, masked_out)
        exp_logits = jnp.exp(logits - jnp.max(logits, -1, keepdims=True))
        probs = exp_logits / jnp.sum(exp_logits, -1, keepdims=True)
        probs_out[...] = probs
        chosen = jnp.where(chosen_experts(pack_ref, probs.shape), probs, 0.0)
        gate = chosen / jnp.sum(chosen, -1, keepdims=True)
        high = gate.astype(bf16)
        low = gate - high.astype(f32)
        message_out[:, width:] = (high.astype(f32) + pltpu.roll(low, n_experts, 1)).astype(bf16)

    if background:
        background.run(step, False, behind_in, behind_out, refs[4:])


def attention_forward(
    place,
    x_all,
    weights,
    pack,
    n_rows,
    n_experts,
    head_dim,
    background=None,
    behind=(),
):
    length, width = x_all.shape
    pairs = width // LANES
    span = pack.shape[1]
    whole = lambda shape: pl.BlockSpec(shape, lambda p, *_: (0,) * len(shape))
    columns = lambda rows: pl.BlockSpec((rows, LANES), lambda p, *_: (0, p))
    matrix = lambda i: pl.BlockSpec((None, width, LANES), lambda p, *_: (i, 0, p))
    out_shape = [
        jax.ShapeDtypeStruct((n_rows, width), bf16),
        jax.ShapeDtypeStruct((length, width), bf16),
        jax.ShapeDtypeStruct((length, width), bf16),
        jax.ShapeDtypeStruct((n_rows, width), bf16),
        jax.ShapeDtypeStruct((pairs, 2, n_rows, length), bf16),
        jax.ShapeDtypeStruct((n_rows, width), f32),
        jax.ShapeDtypeStruct((n_rows, width + LANES), bf16),
        jax.ShapeDtypeStruct((n_rows, LANES), f32),
        jax.ShapeDtypeStruct((length, width), bf16),
    ]
    anywhere = pl.BlockSpec(memory_space=pl.ANY)
    params, aliases = {}, {}
    if background:
        out_shape += background.out_shape(*behind)
        params = {"collective_id": 1, "has_side_effects": True}
        aliases = {8: 10}
    return pl.pallas_call(
        functools.partial(forward_kernel, background, n_experts, head_dim),
        out_shape=out_shape,
        grid_spec=pltpu.PrefetchScalarGridSpec(
            num_scalar_prefetch=1,
            grid=(pairs,),
            in_specs=[
                whole((length, width)),
                matrix(0),
                matrix(1),
                matrix(2),
                pl.BlockSpec((None, LANES, width), lambda p, *_: (3, p, 0)),
                whole(pack.shape),
            ]
            + [anywhere] * len(behind),
            out_specs=[
                columns(n_rows),
                columns(length),
                columns(length),
                columns(n_rows),
                pl.BlockSpec((None, 2, n_rows, length), lambda p, *_: (p, 0, 0, 0)),
                whole((n_rows, width)),
                whole((n_rows, width + LANES)),
                whole((n_rows, LANES)),
                whole((length, width)),
            ]
            + [anywhere] * (background.n_out if background else 0),
            scratch_shapes=[
                pltpu.VMEM((n_rows, width), f32),
                pltpu.VMEM((n_rows, length), f32),
                pltpu.VMEM((2, LANES, span), f32),
                pltpu.VMEM((16, span), f32),
            ]
            + (background.scratch(*behind) if background else []),
        ),
        input_output_aliases=aliases,
        compiler_params=pltpu.CompilerParams(vmem_limit_bytes=VMEM_LIMIT, **params),
        cost_estimate=pl.CostEstimate(
            flops=20_000_000_000, transcendentals=0, bytes_accessed=20_000_000
        ),
        name="attention_forward",
    )(
        place,
        x_all,
        weights,
        weights,
        weights,
        weights,
        pack,
        *behind,
    )


GELU_A = 0.7978845608028654
GELU_B = 0.044715 * GELU_A


def experts_kernel(
    n_experts,
    chunk,
    expert_ref,
    message_ref,
    dy_ref,
    w_in_ref,
    w_out_ref,
    out_ref,
    dh_ref,
    dw_in_ref,
    dw_out_ref,
    dw_in_acc,
    dw_out_acc,
):
    step = pl.program_id(0)
    width = dy_ref.shape[1]
    hidden = w_in_ref.shape[1]
    expert = expert_ref[0]

    @pl.when(step == 0)
    def _():
        dw_in_acc[...] = jnp.zeros_like(dw_in_acc)
        dw_out_acc[...] = jnp.zeros_like(dw_out_acc)

    h = message_ref[:, :width]
    extra = message_ref[:, width:].astype(f32)
    lane = lax.broadcasted_iota(jnp.int32, extra.shape, 1)
    mine = (lane == expert) | (lane == expert + n_experts)
    gate = jnp.sum(jnp.where(mine, extra, 0.0), -1, keepdims=True)
    dy = dy_ref[...]
    out_total = None
    dh_total = None
    dgate = None
    for start in range(0, hidden, chunk):
        part = slice(start, start + chunk)
        up = dot(h, w_in_ref[:, part])
        dact = dot_t(dy, w_out_ref[part, :])
        square = up * up
        tanh = jnp.tanh(up * (GELU_A + GELU_B * square))
        half = 0.5 * up
        more = 1.0 + tanh
        act = half * more
        slope = 0.5 * more + half * (1.0 - tanh * tanh) * (GELU_A + 3.0 * GELU_B * square)
        gated = (gate * act).astype(bf16)
        dgate_part = jnp.sum(act * dact, -1, keepdims=True)
        dup = (gate * dact * slope).astype(bf16)
        out_part = dot(gated, w_out_ref[part, :])
        dh_part = dot_t(dup, w_in_ref[:, part])
        out_total = out_part if out_total is None else out_total + out_part
        dh_total = dh_part if dh_total is None else dh_total + dh_part
        dgate = dgate_part if dgate is None else dgate + dgate_part
        dw_out_acc[part, :] += t_dot(gated, dy)
        dw_in_acc[:, part] += t_dot(h, dup)
    out_ref[...] = out_total.astype(bf16)
    dh_ref[:, :width] = dh_total.astype(bf16)
    high = dgate.astype(bf16).astype(f32)
    low = dgate - high
    dh_ref[:, width:] = jnp.where(
        lane == expert, high, jnp.where(lane == expert + n_experts, low, 0.0)
    ).astype(bf16)

    @pl.when(step == pl.num_programs(0) - 1)
    def _():
        dw_in_ref[...] = dw_in_acc[...].astype(bf16)
        dw_out_ref[...] = dw_out_acc[...].astype(bf16)


def experts(expert, message, dy, w_in, w_out, n_experts, block):
    tokens, width = dy.shape
    hidden = w_in.shape[1]
    whole = lambda shape: pl.BlockSpec(shape, lambda i, *_: (0,) * len(shape))
    rows = lambda columns: pl.BlockSpec((block, columns), lambda i, *_: (i, 0))
    return pl.pallas_call(
        functools.partial(experts_kernel, n_experts, 512),
        out_shape=[
            jax.ShapeDtypeStruct((tokens, width), bf16),
            jax.ShapeDtypeStruct((tokens, width + LANES), bf16),
            jax.ShapeDtypeStruct((width, hidden), bf16),
            jax.ShapeDtypeStruct((hidden, width), bf16),
        ],
        grid_spec=pltpu.PrefetchScalarGridSpec(
            num_scalar_prefetch=1,
            grid=(tokens // block,),
            in_specs=[
                rows(width + LANES),
                rows(width),
                whole((width, hidden)),
                whole((hidden, width)),
            ],
            out_specs=[
                rows(width),
                rows(width + LANES),
                whole((width, hidden)),
                whole((hidden, width)),
            ],
            scratch_shapes=[
                pltpu.VMEM((width, hidden), f32),
                pltpu.VMEM((hidden, width), f32),
            ],
        ),
        compiler_params=pltpu.CompilerParams(vmem_limit_bytes=VMEM_LIMIT),
        cost_estimate=pl.CostEstimate(
            flops=60_000_000_000, transcendentals=0, bytes_accessed=30_000_000
        ),
        name="experts",
    )(expert, message, dy, w_in, w_out)


def plane_slot(j):
    return (j + 1) // 2 % 4, (j + 1) % 2


def down_order(step):
    inner = (13 - step) // 8
    return inner * ((step + 4) % 6 + 1) + (1 - inner) * (step - 6) * 7


def experts_up_kernel(
    n_experts,
    chunk,
    n_fsdp,
    message_ref,
    dy_ref,
    w_in,
    expert_out,
    h_out,
    act_out,
    slope_out,
    dw_out_ref,
    w_out,
    h_ref,
    dw_out_acc,
    w_in_ref,
    gated_ref,
    dy_pair_ref,
    out_held,
    send,
    recv,
    local,
):
    step = pl.program_id(0)
    last = pl.num_programs(0) - 1
    me = Place(n_fsdp)
    core = me.core
    rows, width = dy_ref.shape
    hidden = w_in_ref.shape[1]
    half = rows // 2
    first, second = pl.ds(0, half), pl.ds(half, half)
    mate, across, beside = me.mate(), me.chip(1, 0), me.chip(0, 1)
    own = 7 * (1 - core)
    slot = h_ref.at
    plan = {
        "x": (message_ref, slot[1 + core], beside),
        "y": (message_ref, slot[3 + core], across),
        "c0": (message_ref, slot[own], mate),
        "c1": (slot[1 + core], slot[1 + core], mate),
        "c2": (slot[3 + core], slot[3 + core], mate),
        "c3": (slot[5 + core], slot[5 + core], mate),
        "xy": (slot[1 + core, first], slot[5 + core, first], across),
        "yx": (slot[3 + core, second], slot[5 + core, second], beside),
    } | line_plan(me, expert_out.at[me.rep], w_out)
    copies = Planned(plan, send, recv)
    own_out = Bounce(expert_out.at[me.rep], out_held, w_out.at[me.line], local.at[pl.ds(0, 2)])

    @pl.when(step == 0)
    def _():
        load = pltpu.make_async_copy(w_in, w_in_ref, local.at[2])
        load.start()
        meet([mate, across, beside, me.along(1), me.along(-1)])
        for name in ("c0", "x", "y", ("first", 1), ("first", -1)):
            copies[name].start()
        own_out.start()
        h_ref[own] = message_ref[...]
        dw_out_acc[...] = jnp.zeros_like(dw_out_acc)
        load.wait()

    @pl.when(step == 1)
    def _():
        own_out.turn()
        for shift in (1, -1):
            copies["rest", shift].start()

    @pl.when(step == 2)
    def _():
        for shift in (1, -1):
            copies["first", shift].wait_recv()
            copies["relay", shift].start()
        copies["x"].wait_recv()
        copies["c1"].start()
        copies["xy"].start()
        copies["y"].wait_recv()
        copies["c2"].start()
        copies["yx"].start()

    @pl.when(step == 6)
    def _():
        copies["xy"].wait_recv()
        copies["yx"].wait_recv()
        copies["c3"].start()

    for q in range(4):

        @pl.when(step == 2 * q + 1 - core)
        def _():
            copies[f"c{q}"].wait_recv()

    now = (step + 7) % 8
    expert = me.rep
    h_out[...] = h_ref[now]
    h = h_ref[now, :, :width]
    extra = h_ref[now, :, width:].astype(f32)
    lane = lax.broadcasted_iota(jnp.int32, extra.shape, 1)
    mine = (lane == expert) | (lane == expert + n_experts)
    gate = jnp.sum(jnp.where(mine, extra, 0.0), -1, keepdims=True)
    place = pl.ds(pl.multiple_of(step % 2 * rows, rows), rows)
    dy_pair_ref[place, :] = dy_ref[...]
    for start in range(0, hidden, chunk):
        piece = slice(start, start + chunk)
        up = dot(h, w_in_ref[:, piece])
        square = up * up
        tanh = jnp.tanh(up * (GELU_A + GELU_B * square))
        halved = 0.5 * up
        more = 1.0 + tanh
        act = (halved * more).astype(bf16)
        slope = 0.5 * more + halved * (1.0 - tanh * tanh) * (GELU_A + 3.0 * GELU_B * square)
        act_out[:, piece] = act
        slope_out[:, piece] = slope.astype(bf16)
        gated_ref[place, piece] = (gate * act.astype(f32)).astype(bf16)

    @pl.when(step % 2 == 1)
    def _():
        dw_out_acc[...] += t_dot(gated_ref[...], dy_pair_ref[...])

    @pl.when(step == last)
    def _():
        dw_out_ref[...] = dw_out_acc[...].astype(bf16)
        own_out.wait()
        for shift in (1, -1):
            copies["rest", shift].wait_recv()
            copies["relay", shift].wait_recv()
        for name in plan:
            copies[name].wait_send()


def experts_up(message, dy_all, w_in, expert_out, n_experts, n_fsdp):
    blocks, rows, width = dy_all.shape
    long = message.shape[1]
    hidden = w_in.shape[1]
    once = pl.Buffered(1)
    whole = lambda shape: pl.BlockSpec(shape, lambda i: (0,) * len(shape), pipeline_mode=once)
    turn = lambda columns: pl.BlockSpec((None, rows, columns), lambda i: ((i + 7) % 8, 0, 0))
    anywhere = pl.BlockSpec(memory_space=pl.ANY)
    dma = lambda *shape: pltpu.SemaphoreType.DMA(shape)
    return pl.pallas_call(
        functools.partial(experts_up_kernel, n_experts, hidden // 2, n_fsdp),
        out_shape=[
            jax.ShapeDtypeStruct((blocks, rows, long), bf16),
            jax.ShapeDtypeStruct((blocks, rows, hidden), bf16),
            jax.ShapeDtypeStruct((blocks, rows, hidden), bf16),
            jax.ShapeDtypeStruct((hidden, width), bf16),
            jax.ShapeDtypeStruct((n_fsdp,) + expert_out.shape[1:], bf16),
        ],
        grid=(blocks,),
        in_specs=[whole((rows, long)), turn(width), anywhere, anywhere],
        out_specs=[turn(long), turn(hidden), turn(hidden), whole((hidden, width)), anywhere],
        scratch_shapes=[
            pltpu.VMEM((blocks, rows, long), bf16),
            pltpu.VMEM((hidden, width), f32),
            pltpu.VMEM((width, hidden), bf16),
            pltpu.VMEM((2 * rows, hidden), bf16),
            pltpu.VMEM((2 * rows, width), bf16),
            pltpu.VMEM(expert_out.shape[1:], bf16),
            dma(16),
            dma(16),
            dma(3),
        ],
        compiler_params=pltpu.CompilerParams(
            vmem_limit_bytes=VMEM_LIMIT, collective_id=2, has_side_effects=True
        ),
        cost_estimate=pl.CostEstimate(
            flops=20_000_000_000, transcendentals=0, bytes_accessed=30_000_000
        ),
        name="experts_up",
    )(message, dy_all, w_in, expert_out)


def experts_down_kernel(
    n_experts,
    chunk,
    n_fsdp,
    message_ref,
    dy_ref,
    act_ref,
    slope_ref,
    w_in,
    w_out,
    dw_out,
    back_ref,
    out_half,
    dw_in_ref,
    sum_out,
    part_ref,
    tx_ref,
    rx_ref,
    fin_ref,
    fin_out_ref,
    land_ref,
    dw_in_acc,
    w_in_ref,
    w_out_ref,
    h_pair_ref,
    dup_ref,
    tx_send,
    tx_recv,
    fin_sem,
    land_sem,
    local,
    near,
    mid,
    far,
    own_ref,
    line_send,
    line_recv,
    line_local,
):
    step = pl.program_id(0)
    last = 7
    me = Place(n_fsdp)
    core = me.core
    rows, width = dy_ref.shape
    hidden = w_in_ref.shape[1]
    long = message_ref.shape[1]
    half = rows // 2
    mate = me.mate()
    adds = LineSum(me, dw_out, near, mid, far, own_ref, line_send, line_recv, line_local)

    def to_mate(j):
        return pltpu.make_async_remote_copy(
            src_ref=tx_ref.at[j % 2],
            dst_ref=rx_ref.at[j],
            send_sem=tx_send.at[j],
            recv_sem=tx_recv.at[j],
            device_id=mate,
            device_id_type=MESH,
        )

    def to_owner(j):
        q, k = plane_slot(down_order(j))
        return pltpu.make_async_remote_copy(
            src_ref=fin_ref.at[j % 2],
            dst_ref=land_ref.at[q, core],
            send_sem=fin_sem.at[j],
            recv_sem=land_sem.at[q, core],
            device_id=me.chip(q // 2, q % 2, k),
            device_id_type=MESH,
        )

    def keep_out(j):
        return pltpu.make_async_copy(fin_out_ref.at[j % 2], out_half.at[down_order(j)], local.at[j])

    def stays(j):
        q, k = plane_slot(down_order(j))
        return (q == 0) & (k == core)

    def finish_block(j):
        to_mate(j).wait_recv()
        mine = part_ref.at[j % 2, pl.ds(core * half, half)]

        @pl.when(j >= 2)
        def _():
            keep_out(j - 2).wait()

        @pl.when((j >= 2) & ~stays(j - 2))
        def _():
            to_owner(j - 2).wait_send()

        fin_ref[j % 2] = (mine[:, :long] + rx_ref[j, :, :long].astype(f32)).astype(bf16)

        @pl.when(stays(j))
        def _():
            land_ref[0, core] = fin_ref[j % 2]

        @pl.when(~stays(j))
        def _():
            to_owner(j).start()

        fin_out_ref[j % 2] = (mine[:, long:] + rx_ref[j, :, long:].astype(f32)).astype(bf16)
        keep_out(j).start()

    @pl.when(step == 0)
    def _():
        loads = [
            pltpu.make_async_copy(w_in, w_in_ref, local.at[0]),
            pltpu.make_async_copy(w_out, w_out_ref, local.at[1]),
        ]
        for load in loads:
            load.start()
        partners = [mate, me.along(1), me.along(-1)]
        for q in (1, 2, 3):
            for k in (0, 1):
                partners.append(me.chip(q // 2, q % 2, (core + k) % 2))
        meet(partners)
        adds.start()
        dw_in_acc[...] = jnp.zeros_like(dw_in_acc)
        for load in loads:
            load.wait()

    @pl.when(step == 3)
    def _():
        adds.turn()

    expert = me.rep
    place = pl.ds(pl.multiple_of(step % 2 * rows, rows), rows)
    h_pair_ref[:, place] = message_ref[:, :width].T
    extra = message_ref[:, width:].astype(f32)
    lane = lax.broadcasted_iota(jnp.int32, extra.shape, 1)
    mine = (lane == expert) | (lane == expert + n_experts)
    gate = jnp.sum(jnp.where(mine, extra, 0.0), -1, keepdims=True)
    dy = dy_ref[...]
    dgate = None
    part = part_ref.at[step % 2]
    for start in range(0, hidden, chunk):
        piece = slice(start, start + chunk)
        act = act_ref[:, piece].astype(f32)
        dact = dot_t(dy, w_out_ref[piece, :])
        gated = (gate * act).astype(bf16)
        dgate_part = jnp.sum(act * dact, -1, keepdims=True)
        dup = (gate * dact * slope_ref[:, piece].astype(f32)).astype(bf16)
        out_part = dot(gated, w_out_ref[piece, :])
        dh_part = dot_t(dup, w_in_ref[:, piece])
        if start == 0:
            part[:, long:] = out_part
            part[:, :width] = dh_part
        else:
            part[:, long:] += out_part
            part[:, :width] += dh_part
        dgate = dgate_part if dgate is None else dgate + dgate_part
        dup_ref[place, piece] = dup
        if start == chunk:

            @pl.when(step >= 1)
            def _():
                finish_block(step - 1)

    @pl.when(step % 2 == 1)
    def _():
        dw_in_acc[...] += dot(h_pair_ref[...], dup_ref[...])

    high = dgate.astype(bf16).astype(f32)
    low = dgate - high
    part[:, width:long] = jnp.where(
        lane == expert, high, jnp.where(lane == expert + n_experts, low, 0.0)
    )

    @pl.when(step >= 2)
    def _():
        to_mate(step - 2).wait_send()

    tx_ref[step % 2] = part_ref[step % 2, pl.ds((1 - core) * half, half)].astype(bf16)
    to_mate(step).start()

    @pl.when(step == last)
    def _():
        dw_in_ref[...] = dw_in_acc[...].astype(bf16)
        finish_block(last)
        sum_out[...] = adds.total()
        to_mate(last - 1).wait_send()
        to_mate(last).wait_send()
        keep_out(last - 1).wait()
        keep_out(last).wait()
        for j in (last - 1, last):

            @pl.when(~stays(j))
            def _():
                to_owner(j).wait_send()

        for side in range(2):
            total = None
            for q in range(4):
                arrived = pltpu.make_async_remote_copy(
                    src_ref=fin_ref.at[0],
                    dst_ref=land_ref.at[q, side],
                    send_sem=fin_sem.at[0],
                    recv_sem=land_sem.at[q, side],
                    device_id=mate,
                    device_id_type=MESH,
                )
                if q == 0:

                    @pl.when(core != side)
                    def _():
                        arrived.wait_recv()

                else:
                    arrived.wait_recv()
                landed = land_ref[q, side].astype(f32)
                total = landed if total is None else total + landed
            back_ref[side * half : (side + 1) * half, :] = total


def experts_down(message_all, dy_all, act, slope, w_in, w_out, dw_out, n_experts, n_fsdp):
    blocks, rows, width = dy_all.shape
    long = message_all.shape[2]
    hidden = w_in.shape[1]
    half = rows // 2
    once = pl.Buffered(1)
    whole = lambda shape: pl.BlockSpec(shape, lambda i: (0,) * len(shape), pipeline_mode=once)
    block = lambda columns: pl.BlockSpec(
        (None, rows, columns), lambda i: (down_order(i), 0, 0)
    )
    anywhere = pl.BlockSpec(memory_space=pl.ANY)
    both = long + width
    dma = lambda *shape: pltpu.SemaphoreType.DMA(shape)
    return pl.pallas_call(
        functools.partial(experts_down_kernel, n_experts, hidden // 2, n_fsdp),
        out_shape=[
            jax.ShapeDtypeStruct((rows, long), f32),
            jax.ShapeDtypeStruct((blocks, half, width), bf16),
            jax.ShapeDtypeStruct((width, hidden), bf16),
            jax.ShapeDtypeStruct(dw_out.shape[1:], bf16),
        ],
        grid=(blocks,),
        in_specs=[
            block(long),
            block(width),
            block(hidden),
            block(hidden),
            anywhere,
            anywhere,
            anywhere,
        ],
        out_specs=[
            whole((rows, long)),
            anywhere,
            whole((width, hidden)),
            whole(dw_out.shape[1:]),
        ],
        scratch_shapes=[
            pltpu.VMEM((2, rows, both), f32),
            pltpu.VMEM((2, half, both), bf16),
            pltpu.VMEM((blocks, half, both), bf16),
            pltpu.VMEM((2, half, long), bf16),
            pltpu.VMEM((2, half, width), bf16),
            pltpu.VMEM((4, 2, half, long), bf16),
            pltpu.VMEM((width, hidden), f32),
            pltpu.VMEM((width, hidden), bf16),
            pltpu.VMEM((hidden, width), bf16),
            pltpu.VMEM((width, 2 * rows), bf16),
            pltpu.VMEM((2 * rows, hidden), bf16),
            dma(8),
            dma(8),
            dma(8),
            dma(4, 2),
            dma(8),
        ]
        + LineSum.scratch(*dw_out.shape[1:]),
        compiler_params=pltpu.CompilerParams(
            vmem_limit_bytes=VMEM_LIMIT, collective_id=3, has_side_effects=True
        ),
        cost_estimate=pl.CostEstimate(
            flops=40_000_000_000, transcendentals=0, bytes_accessed=40_000_000
        ),
        name="experts_down",
    )(message_all, dy_all, act, slope, w_in, w_out, dw_out)


class LineSum:
    def __init__(self, me, whole, near, mid, far, mine, send, recv, local):
        self.me, self.whole, self.near, self.mid, self.far = me, whole, near, mid, far
        self.mine, self.local = mine, local
        rows = whole.shape[1]
        half = rows // 2
        self.parts = {1: slice(0, half), -1: slice(half, rows)}
        plan = {}
        for i, shift in enumerate((1, -1)):
            part = pl.ds(i * half, half)
            target = (me.line + 2) % me.n_fsdp
            plan["near", shift] = (whole.at[target, part], near.at[i], me.along(shift))
            plan["far", shift] = (mid.at[i], far.at[i], me.along(shift))
        self.copies = Planned(plan, send, recv)

    def loads(self):
        me = self.me
        for i, shift in enumerate((1, -1)):
            source = self.whole.at[(me.line + shift) % me.n_fsdp]
            yield pltpu.make_async_copy(source, self.mid.at[i], self.local.at[i])
        yield pltpu.make_async_copy(self.whole.at[me.line], self.mine, self.local.at[2])

    def start(self):
        for shift in (1, -1):
            self.copies["near", shift].start()
        for load in self.loads():
            load.start()

    def turn(self):
        for load in self.loads():
            load.wait()
        for i, shift in enumerate((1, -1)):
            self.copies["near", shift].wait_recv()
            part = self.parts[shift]
            total = self.mid[i, part, :].astype(f32) + self.near[i].astype(f32)
            self.mid[i, part, :] = total.astype(bf16)
            self.copies["far", shift].start()

    def total(self):
        for shift in (1, -1):
            self.copies["far", shift].wait_recv()
        total = self.mine[...].astype(f32) + self.far[0].astype(f32) + self.far[1].astype(f32)
        for shift in (1, -1):
            self.copies["near", shift].wait_send()
            self.copies["far", shift].wait_send()
        return total.astype(bf16)

    @staticmethod
    def scratch(rows, columns):
        return [
            pltpu.VMEM((2, rows // 2, columns), bf16),
            pltpu.VMEM((2, rows, columns), bf16),
            pltpu.VMEM((2, rows, columns), bf16),
            pltpu.VMEM((rows, columns), bf16),
            pltpu.SemaphoreType.DMA((4,)),
            pltpu.SemaphoreType.DMA((4,)),
            pltpu.SemaphoreType.DMA((3,)),
        ]


class BackgroundBack:
    n_in, n_out = 2, 4

    def __init__(self, n_fsdp):
        self.n_fsdp = n_fsdp

    def out_shape(self, out_half, dw_in):
        half, width = out_half.shape[1:]
        return [
            jax.ShapeDtypeStruct((2 * half, width), bf16),
            jax.ShapeDtypeStruct(dw_in.shape[1:], bf16),
            jax.ShapeDtypeStruct(
                (self.n_fsdp, width // (2 * self.n_fsdp), width - LANES), bf16
            ),
            jax.ShapeDtypeStruct((4,) + self.split(width), bf16),
        ]

    def out_specs(self, shapes):
        whole = lambda shape: pl.BlockSpec(shape, lambda p, *_: (0,) * len(shape))
        return [whole(s.shape) for s in shapes]

    def scratch(self, out_half, dw_in):
        half, width = out_half.shape[1:]
        pairs = width // LANES - 1
        return [
            pltpu.VMEM((4, 2, half, width), bf16),
            pltpu.SemaphoreType.DMA((8,)),
            pltpu.SemaphoreType.DMA((4, 2)),
            pltpu.VMEM((2, 4) + self.split(width), bf16),
            pltpu.VMEM((pairs, 2) + self.split(width), bf16),
            pltpu.VMEM((pairs, 2) + self.split(width), bf16),
            pltpu.VMEM((pairs, 3, self.n_fsdp) + self.split(width)[2:], bf16),
            pltpu.SemaphoreType.DMA((pairs, 2)),
            pltpu.SemaphoreType.DMA((pairs, 2)),
            pltpu.SemaphoreType.DMA((pairs, 3)),
            pltpu.SemaphoreType.DMA((pairs, 3)),
        ] + LineSum.scratch(*dw_in.shape[1:])

    def split(self, width):
        return (self.n_fsdp, 2, width // (2 * self.n_fsdp), LANES)

    def to_mate(self, pair, i, scratch):
        me = Place(self.n_fsdp)
        own, given = scratch[3:5]
        send, recv = scratch[7:9]
        return pltpu.make_async_remote_copy(
            src_ref=own.at[pair % 2, 2 * i + 1 - me.core],
            dst_ref=given.at[pair, i],
            send_sem=send.at[pair, i],
            recv_sem=recv.at[pair, i],
            device_id=me.mate(),
            device_id_type=MESH,
        )

    def to_chip(self, pair, i, scratch):
        me = Place(self.n_fsdp)
        added, landed = scratch[5:7]
        send, recv = scratch[9:11]
        rows, columns = ((0, 1), (1, 0), (1, 1))[i]
        row, column = (me.row + rows) % 2, (me.seq + columns) % 2
        return pltpu.make_async_remote_copy(
            src_ref=added.at[pair, row, :, column],
            dst_ref=landed.at[pair, i],
            send_sem=send.at[pair, i],
            recv_sem=recv.at[pair, i],
            device_id=me.chip(rows, columns),
            device_id_type=MESH,
        )

    def give(self, pair, grads, scratch, last_out):
        own = scratch[3]
        last = pl.num_programs(0) - 1

        @pl.when(pair >= 2)
        def _():
            for i in (0, 1):
                self.to_mate(pair - 2, i, scratch).wait_send()

        @pl.when(pair < last)
        def _():
            for i, grad in enumerate(grads):
                own[pair % 2, i] = grad.reshape(own.shape[2:])
            for i in (0, 1):
                self.to_mate(pair, i, scratch).start()

        @pl.when(pair == last)
        def _():
            for i, grad in enumerate(grads):
                last_out[i] = grad.reshape(own.shape[2:])

    def collect(self, pair, scratch):
        core = Place(self.n_fsdp).core
        own, given, added = scratch[3:6]
        for i in (0, 1):
            self.to_mate(pair, i, scratch).wait_recv()
            total = own[pair % 2, 2 * i + core].astype(f32) + given[pair, i].astype(f32)
            added[pair, i] = total.astype(bf16)
        for i in range(3):
            self.to_chip(pair, i, scratch).start()

    def collect_before(self, pair, scratch):
        @pl.when(pair >= 1)
        def _():
            self.collect(pair - 1, scratch)

    def run(self, step, before, ins, outs, scratch, x_mid):
        out_half, dw_in = ins
        out_rows, sum_in, plane_sum, _ = outs
        land, send, recv = scratch[:3]
        near, mid, far, mine, line_send, line_recv, line_local = scratch[11:]
        me = Place(self.n_fsdp)
        core = me.core
        half = out_half.shape[1]
        line = LineSum(me, dw_in, near, mid, far, mine, line_send, line_recv, line_local)

        def to_owner(j):
            q, k = plane_slot(j)
            return pltpu.make_async_remote_copy(
                src_ref=out_half.at[j],
                dst_ref=land.at[q, core],
                send_sem=send.at[j],
                recv_sem=recv.at[q, core],
                device_id=me.chip(q // 2, q % 2, k),
                device_id_type=MESH,
            )

        def stay(j):
            return pltpu.make_async_copy(out_half.at[j], land.at[0, core], send.at[j])

        if before:

            @pl.when(step == 0)
            def _():
                partners = [me.mate(), me.along(1), me.along(-1)]
                for q in (1, 2, 3):
                    for k in (0, 1):
                        partners.append(me.chip(q // 2, q % 2, (core + k) % 2))
                meet(partners)
                line.start()
                for j in range(8):
                    if j in (0, 7):

                        @pl.when(core == (j + 1) % 2)
                        def _():
                            stay(j).start()

                        @pl.when(core != (j + 1) % 2)
                        def _():
                            to_owner(j).start()

                    else:
                        to_owner(j).start()

            @pl.when(step == 2)
            def _():
                line.turn()

            return

        @pl.when(step == pl.num_programs(0) - 1)
        def _():
            added, landed = scratch[5:7]
            pairs = landed.shape[0]
            sum_in[...] = line.total()
            for j in range(8):
                if j in (0, 7):

                    @pl.when(core == (j + 1) % 2)
                    def _():
                        stay(j).wait()

                    @pl.when(core != (j + 1) % 2)
                    def _():
                        to_owner(j).wait_send()

                else:
                    to_owner(j).wait_send()
            for side in range(2):
                here = slice(side * half, (side + 1) * half)
                total = x_mid[here, :]
                for q in range(4):
                    arrived = pltpu.make_async_remote_copy(
                        src_ref=out_half.at[0],
                        dst_ref=land.at[q, side],
                        send_sem=send.at[0],
                        recv_sem=recv.at[q, side],
                        device_id=me.mate(),
                        device_id_type=MESH,
                    )
                    if q == 0:

                        @pl.when(core != side)
                        def _():
                            arrived.wait_recv()

                    else:
                        arrived.wait_recv()
                    total = total + land[q, side].astype(f32)
                out_rows[here, :] = total.astype(bf16)
            for i in (0, 1):
                self.to_mate(pairs - 1, i, scratch).wait_send()
            for pair in range(pairs):
                total = added[pair, me.row, :, me.seq].astype(f32)
                for i in range(3):
                    self.to_chip(pair, i, scratch).wait_recv()
                    total = total + landed[pair, i].astype(f32)
                plane_sum[:, :, pair * LANES : (pair + 1) * LANES] = total.astype(bf16)
            for pair in range(pairs):
                for i in range(3):
                    self.to_chip(pair, i, scratch).wait_send()


def backward_kernel(
    background,
    n_experts,
    head_dim,
    back_ref,
    dy_ref,
    x_mid_ref,
    message_ref,
    probs_ref,
    pack_ref,
    h_ref,
    wq_ref,
    wk_ref,
    wv_ref,
    wo_ref,
    q_ref,
    k_ref,
    v_ref,
    o_ref,
    p_ref,
    *refs,
):
    step = pl.program_id(0)
    n_in, n_out = (background.n_in, background.n_out) if background else (0, 0)
    behind_in, refs = refs[:n_in], refs[n_in:]
    n_grads = 0 if background else 4
    grad_outs, refs = refs[:n_grads], refs[n_grads:]
    dh_own_out, dh_other_out, dx_mid_out, gain_out, router_out, ddist_out = refs[:6]
    behind_out, refs = refs[6 : 6 + n_out], refs[6 + n_out :]
    da_ref, dh_all_ref, dh_mine_ref, dbias_ref, dq_ref, h_turned_ref, o_turned_ref = refs[:7]
    if background:
        background.run(step, True, behind_in, behind_out, refs[7:], x_mid_ref)
    rows, width = x_mid_ref.shape
    length = h_ref.shape[0]
    own = pl.ds(pl.multiple_of(first_row(rows), rows), rows)

    @pl.when(step == 0)
    def _():
        probs = probs_ref[...]
        chosen = chosen_experts(pack_ref, probs.shape)
        picked = jnp.where(chosen, probs, 0.0)
        total = jnp.sum(picked, -1, keepdims=True)
        gate = picked / total
        extra = back_ref[:, width:].astype(f32)
        dgate = extra + pltpu.roll(extra, LANES - n_experts, 1)
        dgate = jnp.where(chosen, dgate, 0.0)
        shared = jnp.sum(dgate * gate, -1, keepdims=True)
        dprobs = jnp.where(chosen, (dgate - shared) / total, 0.0)
        dlogits = probs * (dprobs - jnp.sum(probs * dprobs, -1, keepdims=True))
        h_two = message_ref[:, :width].astype(f32)
        router_out[...] = lax.dot_general(
            dlogits,
            h_two,
            (((0,), (0,)), ((), ())),
            precision=highest,
            preferred_element_type=f32,
        )
        dh_two = back_ref[:, :width].astype(f32) + exact_dot(
            dlogits, router_rows(pack_ref, n_experts, width)
        )
        dx, dgain = norm_back(x_mid_ref[...], pack_ref[5:6, :width], dh_two)
        gain_out[...] = dgain
        dx_mid = dx + dy_ref[...].astype(f32)
        dx_mid_out[...] = dx_mid
        da_ref[...] = dx_mid.astype(bf16)
        dh_all_ref[...] = jnp.zeros_like(dh_all_ref)
        dh_mine_ref[...] = jnp.zeros_like(dh_mine_ref)
        ddist_out[...] = jnp.zeros_like(ddist_out)
        h_turned_ref[...] = h_ref[...].T
        o_turned_ref[...] = o_ref[...].T

    da = da_ref[...]
    do = dot_t(da, wo_ref[...]).astype(bf16)
    block = LANES
    first_half = lax.broadcasted_iota(jnp.int32, (block, LANES), 1) < head_dim
    zero = jnp.zeros((), bf16)
    k_low = k_ref[...]
    v_low = v_ref[...]
    dk = None
    dv = None
    for head in range(2):
        dbias_ref[head] = jnp.zeros_like(dbias_ref[head])
    for b in range(rows // block):
        here = slice(b * block, (b + 1) * block)
        offset = pl.multiple_of(length - LANES - block * b - first_row(rows), LANES)
        q_heads = by_head(q_ref[here, :], first_half)
        do_heads = by_head(do[here], first_half)
        probs_low = p_ref[:, here, :]
        probs = probs_low.astype(f32)
        dprobs = dot_t(do_heads, v_low).reshape(2, block, length)
        weighted = probs * dprobs
        ds = weighted - probs * jnp.sum(weighted, -1, keepdims=True)
        dbias_ref[:, :, pl.ds(offset, length)] += ds
        ds_low = ds.astype(bf16).reshape(2 * block, length)
        probs_low = probs_low.reshape(2 * block, length)
        dq_heads = dot(ds_low, k_low)
        dk_part = t_dot(ds_low, q_heads)
        dv_part = t_dot(probs_low, do_heads)
        dk = dk_part if dk is None else dk + dk_part
        dv = dv_part if dv is None else dv + dv_part
        dq_ref[here, :] = (of_head(dq_heads, first_half) * (head_dim**-0.5)).astype(bf16)
    for head in range(2):
        ddist_out[pl.ds(2 * step + head, 1), :] = gather_diagonals(dbias_ref[head])
    dq = dq_ref[...]
    dkv = jnp.concatenate([dk, dv], 1).astype(bf16)
    da_columns = da_ref[:, pl.ds(pl.multiple_of(step * LANES, LANES), LANES)]
    if background:
        background.collect_before(step, refs[7:])
    mine = pl.ds(pl.multiple_of(first_row(rows), rows), rows)
    grads_kv = dot(h_turned_ref[...], dkv).astype(bf16)
    grads = [
        dot(h_turned_ref[:, mine], dq).astype(bf16),
        grads_kv[:, :LANES],
        grads_kv[:, LANES:],
        dot(o_turned_ref[...], da_columns).astype(bf16),
    ]
    if background:
        background.give(step, grads, refs[7:], behind_out[3])
    else:
        for target, grad in zip(grad_outs, grads):
            target[...] = grad
    dh_all_ref[...] += dot_t(dkv, jnp.concatenate([wk_ref[...], wv_ref[...]], 1))
    dh_mine_ref[...] += dot_t(dq, wq_ref[...])

    @pl.when(step == pl.num_programs(0) - 1)
    def _():
        other = pl.ds(pl.multiple_of(length - rows - first_row(rows), rows), rows)
        dh_own_out[...] = dh_mine_ref[...] + dh_all_ref[own, :]
        dh_other_out[...] = dh_all_ref[other, :].astype(bf16)

    if background:
        background.run(step, False, behind_in, behind_out, refs[7:], x_mid_ref)


def attention_backward(
    back,
    dy,
    x_mid,
    message,
    probs,
    pack,
    h_all,
    weights,
    q,
    k,
    v,
    o,
    p,
    n_experts,
    head_dim,
    background=None,
    behind=(),
):
    n_rows, width = x_mid.shape
    length = h_all.shape[0]
    pairs = width // LANES
    span = pack.shape[1]
    more_shapes, more_scratch, params = [], [], {}
    n_grads = 0 if background else 4
    if background:
        more_shapes = background.out_shape(*behind)
        more_scratch = background.scratch(*behind)
        params = {"collective_id": 4, "has_side_effects": True}
    anywhere = pl.BlockSpec(memory_space=pl.ANY)
    whole = lambda shape: pl.BlockSpec(shape, lambda p, *_: (0,) * len(shape))
    columns = lambda rows: pl.BlockSpec((rows, LANES), lambda p, *_: (0, p))
    matrix = lambda i: pl.BlockSpec((None, width, LANES), lambda p, *_: (i, 0, p))
    return pl.pallas_call(
        functools.partial(backward_kernel, background, n_experts, head_dim),
        out_shape=[jax.ShapeDtypeStruct((width, width), bf16)] * n_grads
        + [
            jax.ShapeDtypeStruct((n_rows, width), f32),
            jax.ShapeDtypeStruct((n_rows, width), bf16),
            jax.ShapeDtypeStruct((n_rows, width), f32),
            jax.ShapeDtypeStruct((1, width), f32),
            jax.ShapeDtypeStruct((LANES, width), f32),
            jax.ShapeDtypeStruct((16, span), f32),
        ]
        + more_shapes,
        grid_spec=pltpu.PrefetchScalarGridSpec(
            num_scalar_prefetch=0,
            grid=(pairs,),
            in_specs=[
                whole((n_rows, width + LANES)),
                whole((n_rows, width)),
                whole((n_rows, width)),
                whole((n_rows, width + LANES)),
                whole((n_rows, LANES)),
                whole(pack.shape),
                whole((length, width)),
                matrix(0),
                matrix(1),
                matrix(2),
                pl.BlockSpec((None, LANES, width), lambda p, *_: (3, p, 0)),
                columns(n_rows),
                columns(length),
                columns(length),
                whole((n_rows, width)),
                pl.BlockSpec((None, 2, n_rows, length), lambda p, *_: (p, 0, 0, 0)),
            ]
            + [anywhere] * len(behind),
            out_specs=[columns(width)] * n_grads
            + [
                whole((n_rows, width)),
                whole((n_rows, width)),
                whole((n_rows, width)),
                whole((1, width)),
                whole((LANES, width)),
                whole((16, span)),
            ]
            + (background.out_specs(more_shapes) if background else []),
            scratch_shapes=[
                pltpu.VMEM((n_rows, width), bf16),
                pltpu.VMEM((length, width), f32),
                pltpu.VMEM((n_rows, width), f32),
                pltpu.VMEM((2, LANES, span), f32),
                pltpu.VMEM((n_rows, LANES), bf16),
                pltpu.VMEM((width, length), bf16),
                pltpu.VMEM((width, n_rows), bf16),
            ]
            + more_scratch,
        ),
        compiler_params=pltpu.CompilerParams(vmem_limit_bytes=VMEM_LIMIT, **params),
        cost_estimate=pl.CostEstimate(
            flops=40_000_000_000, transcendentals=0, bytes_accessed=30_000_000
        ),
        name="attention_backward",
    )(
        back,
        dy,
        x_mid,
        message,
        probs,
        pack,
        h_all,
        weights,
        weights,
        weights,
        weights,
        q,
        k,
        v,
        o,
        p,
        *behind,
    )


def finish_kernel(
    n_fsdp,
    n_experts,
    n_heads,
    sum_in,
    sum_out,
    dh_other,
    line_ref,
    last_ref,
    dh_own_ref,
    dx_mid_ref,
    tokens_ref,
    pack_ref,
    dgain_two_ref,
    drouter_ref,
    ddist_ref,
    attn_out,
    grad_in,
    grad_out,
    tokens_out,
    small_out,
    line_land,
    last_given,
    last_added,
    last_land,
    last_line,
    last_line_land,
    attn_held,
    dh_land,
    small_plane,
    small_line,
    in_held,
    out_held,
    send,
    recv,
    local,
):
    me = Place(n_fsdp)
    rep, line, seq, core, row = me.rep, me.line, me.seq, me.core, me.row
    width = tokens_ref.shape[1]
    mate, across, beside, corner = me.mate(), me.chip(1, 0), me.chip(0, 1), me.chip(1, 1)
    far_row = (row + 1) % 2
    far_rep = far_row * 2 + core
    part_out = sum_out.shape[0]
    columns = lambda z, x: pl.ds(pl.multiple_of((z * 2 + x) * part_out, LANES), part_out)
    here = rep * 2 + seq
    peers = [mate, across, beside, corner]
    peers += [me.chip(1, 0, 1 - core), me.chip(0, 1, 1 - core), me.chip(1, 1, 1 - core)]
    shifts = (1, -1, 2)
    plan = {
        "dh": (dh_other, dh_land, beside),
        "out_c": (sum_out, grad_out.at[rep], mate),
        "out_y": (sum_out, grad_out.at[rep], across),
        "out_f": (grad_out.at[far_rep], grad_out.at[far_rep], mate),
        "attn_c": (attn_held, attn_out.at[rep], mate),
        "attn_y": (attn_held, attn_out.at[rep], across),
        "attn_f": (attn_out.at[far_rep], attn_out.at[far_rep], mate),
        "in_c": (grad_in.at[rep], grad_in.at[rep], mate),
        "in_y": (grad_in.at[rep], grad_in.at[rep], across),
        "in_f": (grad_in.at[far_rep], grad_in.at[far_rep], mate),
    }
    for i, shift in enumerate(shifts):
        target = (line + shift) % n_fsdp
        plan["line", i] = (line_ref.at[target], line_land.at[i], me.along(shift))
        plan["last_z", i] = (last_line.at[target], last_line_land.at[i], me.along(shift))
        plan["small_z", i] = (small_line.at[line], small_line.at[line], me.along(shift))
    for z in range(n_fsdp):
        plan["in_x", z] = (
            sum_in.at[1 - seq, :, pl.ds(z * part_out, part_out)],
            grad_in.at[rep, :, columns(z, seq)],
            beside,
        )
    for i, peer in enumerate(peers):
        plan["small", i] = (small_plane.at[here], small_plane.at[here], peer)
    for i in (0, 1):
        plan["last_c", i] = (last_ref.at[2 * i + 1 - core], last_given.at[i], mate)
    chips = ((row, 1 - seq, beside), (far_row, seq, across), (far_row, 1 - seq, corner))
    for i, (to_row, to_column, chip) in enumerate(chips):
        plan["last", i] = (last_added.at[to_row, :, to_column], last_land.at[i], chip)
    copies = Planned(plan, send, recv)
    meet(peers + [me.along(shift) for shift in shifts])
    for i in (0, 1):
        copies["last_c", i].start()
    for i in range(3):
        copies["line", i].start()
    for z in range(n_fsdp):
        copies["in_x", z].start()
    copies["out_y"].start()
    copies["dh"].start()
    copies["out_c"].start()
    own_in = pltpu.make_async_copy(sum_in.at[seq], in_held, local.at[2])
    own_in.start()
    own_out = Bounce(sum_out, out_held, grad_out.at[rep], local.at[pl.ds(8, 2)])
    own_out.start()
    own_in.wait()
    kept = []
    for z in range(n_fsdp):
        source = in_held.at[:, pl.ds(z * part_out, part_out)]
        target = grad_in.at[rep, :, columns(z, seq)]
        kept.append(pltpu.make_async_copy(source, target, local.at[4 + z]))
        kept[-1].start()
    own_out.turn()
    for i in (0, 1):
        copies["last_c", i].wait_recv()
        total = last_ref[2 * i + core].astype(f32) + last_given[i].astype(f32)
        last_added[i] = total.astype(bf16)
    for i in range(3):
        copies["last", i].start()
    table = exact_dot_t(ddist_ref[...], bucket_match(pack_ref))
    small = small_plane.at[here]
    small[...] = jnp.zeros_like(small_out)
    small[1:2, :] = dgain_two_ref[...]
    small[2 : 2 + n_experts, :] = drouter_ref[:n_experts, :]
    for head in range(n_heads):
        at = head % 6 * LANES
        small[6 + head // 6, at : at + LANES] = table[head]
    for copy in kept:
        copy.wait()
    for z in range(n_fsdp):
        copies["in_x", z].wait_recv()
    copies["in_y"].start()
    copies["in_c"].start()
    total = last_added[row, :, seq].astype(f32)
    for i in range(3):
        copies["last", i].wait_recv()
        total = total + last_land[i].astype(f32)
    last_line[...] = total.astype(bf16)
    for i in range(3):
        copies["last_z", i].start()
    total = line_ref[line].astype(f32)
    for i in range(3):
        copies["line", i].wait_recv()
        total = total + line_land[i].astype(f32)
    early = total.shape[1]
    attn_held[:, :early] = total.astype(bf16)
    copies["out_y"].wait_recv()
    copies["out_f"].start()
    copies["dh"].wait_recv()
    dh_one = dh_own_ref[...] + dh_land[...].astype(f32)
    gain_one = pack_ref[4:5, :width]
    dx, dgain_one = norm_back(tokens_ref[...].astype(f32), gain_one, dh_one)
    small[0:1, :] = dgain_one
    for i in range(len(peers)):
        copies["small", i].start()
    total = last_line[line].astype(f32)
    for i in range(3):
        copies["last_z", i].wait_recv()
        total = total + last_line_land[i].astype(f32)
    attn_held[:, early:] = total.astype(bf16)
    copies["attn_y"].start()
    copies["attn_c"].start()
    own_attn = pltpu.make_async_copy(attn_held, attn_out.at[rep], local.at[3])
    own_attn.start()
    tokens_out[...] = (dx_mid_ref[...] + dx).astype(bf16)
    copies["attn_y"].wait_recv()
    copies["attn_f"].start()
    for i in range(len(peers)):
        copies["small", i].wait_recv()
    total = small_plane[0]
    for i in range(1, 8):
        total = total + small_plane[i]
    small_line[line] = total
    for i in range(3):
        copies["small_z", i].start()
    copies["in_y"].wait_recv()
    copies["in_f"].start()
    for i in range(3):
        copies["small_z", i].wait_recv()
    total = small_line[0]
    for i in range(1, n_fsdp):
        total = total + small_line[i]
    small_out[...] = total
    own_attn.wait()
    own_out.wait()
    for name in ("attn_c", "attn_f", "in_c", "in_f", "out_c", "out_f"):
        copies[name].wait_recv()
    for name in plan:
        copies[name].wait_send()


def finish(
    plane_sum,
    last_grads,
    sum_in,
    sum_out,
    dh_other,
    dh_own,
    dx_mid,
    tokens,
    pack,
    dgain_two,
    drouter,
    ddist,
    n_fsdp,
    n_experts,
    n_heads,
    hidden,
):
    n_rows, width = tokens.shape
    part_attn = plane_sum.shape[1]
    split = last_grads.shape[1:]
    part_in = sum_in.shape[1]
    anywhere = pl.BlockSpec(memory_space=pl.ANY)
    inside = pl.BlockSpec(memory_space=pltpu.VMEM)
    dma = lambda n: pltpu.SemaphoreType.DMA((n,))
    return pl.pallas_call(
        functools.partial(finish_kernel, n_fsdp, n_experts, n_heads),
        out_shape=[
            jax.ShapeDtypeStruct((4, part_attn, width), bf16),
            jax.ShapeDtypeStruct((n_experts, part_in, hidden), bf16),
            jax.ShapeDtypeStruct((n_experts,) + sum_out.shape, bf16),
            jax.ShapeDtypeStruct((n_rows, width), bf16),
            jax.ShapeDtypeStruct((8, width), f32),
        ],
        in_specs=[anywhere] * 3 + [inside] * 9,
        out_specs=[anywhere] * 3 + [inside] * 2,
        scratch_shapes=[
            pltpu.VMEM((3,) + plane_sum.shape[1:], bf16),
            pltpu.VMEM((2,) + split, bf16),
            pltpu.VMEM((2,) + split, bf16),
            pltpu.VMEM((3, n_fsdp) + split[2:], bf16),
            pltpu.VMEM((n_fsdp,) + split[2:], bf16),
            pltpu.VMEM((3,) + split[2:], bf16),
            pltpu.VMEM((part_attn, width), bf16),
            pltpu.VMEM((n_rows, width), bf16),
            pltpu.VMEM((8, 8, width), f32),
            pltpu.VMEM((n_fsdp, 8, width), f32),
            pltpu.VMEM(sum_in.shape[1:], bf16),
            pltpu.VMEM(sum_out.shape, bf16),
            dma(40),
            dma(40),
            dma(12),
        ],
        compiler_params=pltpu.CompilerParams(
            vmem_limit_bytes=VMEM_LIMIT, collective_id=5, has_side_effects=True
        ),
        name="finish_gradients",
    )(
        sum_in,
        sum_out,
        dh_other,
        plane_sum,
        last_grads,
        dh_own,
        dx_mid,
        tokens,
        pack,
        dgain_two,
        drouter,
        ddist,
    )


def widen_kernel(
    n_experts, n_heads, n_buckets, attn, grad_in, grad_out, small, q, k, v, o, win, wout, *rest
):
    step = pl.program_id(0)
    for i, target in enumerate((q, k, v, o)):

        @pl.when(step == i)
        def _():
            target[...] = attn[...].astype(f32)

    win[...] = grad_in[...].astype(f32)
    wout[...] = grad_out[...].astype(f32)
    gain_one, gain_two, table, router = rest

    @pl.when(step == 0)
    def _():
        gain_one[...] = small[0, :]
        gain_two[...] = small[1, :]
        router[...] = small[2 : 2 + n_experts, :]
        for head in range(n_heads):
            at = head % 6 * LANES
            table[head : head + 1, :] = small[
                6 + head // 6 : 7 + head // 6, at : at + n_buckets
            ]


def widen(attn, grad_in, grad_out, small, n_heads, n_buckets):
    n_experts = grad_in.shape[0]
    width = small.shape[1]
    own = lambda a: pl.BlockSpec((None,) + a.shape[1:], lambda i: (i, 0, 0))
    whole = lambda shape: pl.BlockSpec(shape, lambda i: (0,) * len(shape))
    small_shapes = [(width,), (width,), (n_heads, n_buckets), (n_experts, width)]
    wide = [attn.shape[1:]] * 4
    return pl.pallas_call(
        functools.partial(widen_kernel, n_experts, n_heads, n_buckets),
        out_shape=[jax.ShapeDtypeStruct(shape, f32) for shape in wide]
        + [jax.ShapeDtypeStruct(a.shape, f32) for a in (grad_in, grad_out)]
        + [jax.ShapeDtypeStruct(shape, f32) for shape in small_shapes],
        grid=(n_experts,),
        in_specs=[own(attn), own(grad_in), own(grad_out), whole(small.shape)],
        out_specs=[whole(shape) for shape in wide]
        + [own(grad_in), own(grad_out)]
        + [whole(shape) for shape in small_shapes],
        compiler_params=pltpu.CompilerParams(vmem_limit_bytes=VMEM_LIMIT),
        name="widen",
    )(attn, grad_in, grad_out, small)


def per_device(
    tokens,
    piece_starts,
    routes,
    buckets,
    attn_q,
    attn_k,
    attn_v,
    attn_o,
    expert_in,
    expert_out,
    gain_attn,
    gain_ffn,
    rel_table,
    router,
    cotangent,
):
    n_rep, n_fsdp, n_seq = (lax.axis_size(a) for a in ("rep", "fsdp", "seq"))
    rep = lax.axis_index("rep")
    seq = lax.axis_index("seq")
    plane = ("rep", "seq")
    n_rows, width = tokens.shape
    n_buckets, n_heads = rel_table.shape
    head_dim = width // n_heads
    n_experts, part_in, hidden = expert_in.shape
    part_out = expert_out.shape[1]
    part_attn = attn_q.shape[0]
    length = n_rows * n_seq
    assert n_experts == n_rep == 4 and n_seq == 2 and 2 * head_dim == LANES
    pairs = n_heads // 2

    place = piece_starts[0]
    near = n_fsdp == 4 and part_attn % 16 == 0
    pick = lambda array: lax.dynamic_index_in_dim(array, rep, 0, keepdims=False)
    span = -(-buckets.shape[0] // LANES) * LANES
    if near:
        weights, x_all, w_in, pack = gather(
            (attn_q, attn_k, attn_v, attn_o),
            tokens,
            expert_in,
            part_out,
            n_fsdp,
            (router.T, gain_attn, gain_ffn, buckets, rel_table.T, routes.T),
            span,
        )
    else:
        attn_own = pick(jnp.stack([attn_q, attn_k, attn_v, attn_o]))
        attn_line = lax.all_gather(attn_own, "fsdp", axis=0, tiled=False)
        attn_all = lax.all_gather(attn_line, plane, axis=0, tiled=False)
        attn_all = attn_all.reshape(n_rep, n_seq, n_fsdp, part_attn, width)
        weights = attn_all.transpose(0, 2, 1, 3, 4).reshape(n_rep, width, width)
        x_all = lax.all_gather(tokens, "seq", axis=0, tiled=True)
        in_own = pick(expert_in).reshape(part_in, n_fsdp, n_seq, part_out)
        in_own = in_own.transpose(2, 0, 1, 3).reshape(n_seq, part_in, n_fsdp * part_out)
        in_pair = lax.all_to_all(in_own, "seq", split_axis=0, concat_axis=0, tiled=True)
        in_pair = in_pair.reshape(n_seq * part_in, n_fsdp * part_out)
        w_in = lax.all_gather(in_pair, "fsdp", axis=0, tiled=True)
        w_out = lax.all_gather(pick(expert_out), "fsdp", axis=0, tiled=True)
        dy_all = lax.all_gather(cotangent, plane, axis=0, tiled=True)
        pack = pack_small(router, gain_attn, gain_ffn, buckets, rel_table, routes, span)

    q, k, v, o, p, x_mid, message, probs, h_all, *gathered = attention_forward(
        place,
        x_all,
        weights,
        pack,
        n_rows,
        n_experts,
        head_dim,
        Background(n_fsdp) if near else None,
        (cotangent, w_in) if near else (),
    )
    behind = ()
    if near:
        dy_all, w_in = gathered
        w_in = w_in.reshape(width, n_fsdp * part_out)
        message_all, act, slope, dw_out, w_out = experts_up(
            message, dy_all, w_in, expert_out, n_experts, n_fsdp
        )
        back, out_half, dw_in, sum_out = experts_down(
            message_all,
            dy_all,
            act,
            slope,
            w_in,
            w_out.reshape(n_fsdp * part_out, width),
            dw_out.reshape(n_fsdp, part_out, width),
            n_experts,
            n_fsdp,
        )
        behind = (out_half, dw_in.reshape(n_fsdp, n_seq * part_in, n_fsdp * part_out))
    else:
        message_all = lax.all_gather(message, plane, axis=0, tiled=True)
        out_part, back_part, dw_in, dw_out = experts(
            rep[None].astype(jnp.int32), message_all, dy_all, w_in, w_out, n_experts, n_rows
        )
        back = lax.psum_scatter(back_part, plane, scatter_dimension=0, tiled=True)
        out_sum = lax.psum_scatter(out_part, plane, scatter_dimension=0, tiled=True)
        out_rows = (x_mid + out_sum.astype(f32)).astype(bf16)

    grads = attention_backward(
        back,
        cotangent,
        x_mid,
        message,
        probs,
        pack,
        h_all,
        weights,
        q,
        k,
        v,
        o,
        p,
        n_experts,
        head_dim,
        BackgroundBack(n_fsdp) if near else None,
        behind,
    )
    if near:
        dh_own, dh_other, dx_mid, dgain_two, drouter, ddist = grads[:6]
        out_rows, sum_in, plane_sum, last_grads = grads[6:]
        attn_sum, grad_in, grad_out, grad_tokens, small = finish(
            plane_sum,
            last_grads,
            sum_in.reshape(n_seq, part_in, n_fsdp * part_out),
            sum_out,
            dh_other,
            dh_own,
            dx_mid,
            tokens,
            pack,
            dgain_two,
            drouter,
            ddist,
            n_fsdp,
            n_experts,
            n_heads,
            hidden,
        )
        *wide, grad_one, grad_two, grad_table, grad_router = widen(
            attn_sum, grad_in, grad_out, small, n_heads, n_buckets
        )
        return (
            out_rows,
            grad_tokens,
            *wide,
            grad_one,
            grad_two,
            grad_table.T,
            grad_router.T,
        )
    dwq, dwk, dwv, dwo, dh_own, dh_other, dx_mid, dgain_two, drouter, ddist = grads
    sum_out = lax.psum_scatter(dw_out, "fsdp", scatter_dimension=0, tiled=True)
    sum_in = lax.psum_scatter(dw_in, "fsdp", scatter_dimension=0, tiled=True)
    sum_in = sum_in.reshape(n_seq, part_in, n_fsdp * part_out)
    sum_in = lax.all_to_all(sum_in, "seq", split_axis=0, concat_axis=0, tiled=True)
    sum_in = sum_in.reshape(n_seq, part_in, n_fsdp, part_out).transpose(1, 2, 0, 3)
    sum_in = sum_in.reshape(part_in, hidden)
    grad_out = lax.all_gather(sum_out, "rep", axis=0, tiled=False)
    grad_in = lax.all_gather(sum_in, "rep", axis=0, tiled=False)
    swap = [(0, 1), (1, 0)]
    dh_one = dh_own + lax.ppermute(dh_other, "seq", swap).astype(f32)
    dx, dgain_one = norm_back(tokens.astype(f32), gain_attn[None, :], dh_one)
    grad_tokens = (dx_mid + dx).astype(bf16)
    attn_grads = jnp.stack([dwq, dwk, dwv, dwo])
    attn_grads = attn_grads.reshape(n_rep, n_fsdp, n_seq, part_attn, width)
    attn_grads = attn_grads.transpose(0, 2, 1, 3, 4)
    attn_grads = attn_grads.reshape(n_rep * n_seq * n_fsdp * part_attn, width)
    attn_sum = lax.psum_scatter(attn_grads, plane, scatter_dimension=0, tiled=True)
    attn_sum = lax.psum_scatter(attn_sum, "fsdp", scatter_dimension=0, tiled=True)
    attn_sum = lax.all_gather(attn_sum, "rep", axis=0, tiled=False)
    ddist = ddist[:n_heads, : buckets.shape[0]]
    match = (buckets[:, None] == jnp.arange(n_buckets)[None, :]).astype(f32)
    table = lax.dot_general(
        match,
        ddist,
        (((0,), (1,)), ((), ())),
        precision=highest,
        preferred_element_type=f32,
    )
    grad_one, grad_two, grad_table, grad_router = lax.psum(
        (dgain_one[0], dgain_two[0], table, drouter[:n_experts].T), ("rep", "fsdp", "seq")
    )
    attn_sum = attn_sum.astype(f32)
    return (
        out_rows,
        grad_tokens,
        attn_sum[0],
        attn_sum[1],
        attn_sum[2],
        attn_sum[3],
        grad_in.astype(f32),
        grad_out.astype(f32),
        grad_one,
        grad_two,
        grad_table,
        grad_router,
    )


def solution(mesh):
    rows = P(("rep", "fsdp", "seq"), None)
    owned = P(("fsdp", "seq"), None)
    expert = P(None, ("fsdp", "seq"), None)
    in_specs = (
        rows,
        P(("rep", "fsdp"), None),
        rows,
        P(),
        owned,
        owned,
        owned,
        owned,
        expert,
        expert,
        P(),
        P(),
        P(),
        P(),
        rows,
    )
    out_specs = (
        rows,
        rows,
        owned,
        owned,
        owned,
        owned,
        expert,
        expert,
        P(),
        P(),
        P(),
        P(),
    )
    return jax.shard_map(
        per_device, mesh=mesh, in_specs=in_specs, out_specs=out_specs, check_vma=False
    )
```

```python
import functools

import jax
import jax.numpy as jnp
from jax import lax
from jax.experimental import pallas as pl
from jax.experimental.pallas import tpu as pltpu
from jax.sharding import PartitionSpec as P

PIECE = 256
LANES = 128
epsilon = 1e-06
masked_out = -1e30
highest = lax.Precision.HIGHEST
f32 = jnp.float32
bf16 = jnp.bfloat16
VMEM_LIMIT = 58 * 1024 * 1024


def dot(a, b):
    return jnp.dot(a, b, preferred_element_type=f32)


def dot_t(a, b):
    return lax.dot_general(a, b, (((1,), (1,)), ((), ())), preferred_element_type=f32)


def t_dot(a, b):
    return lax.dot_general(a, b, (((0,), (0,)), ((), ())), preferred_element_type=f32)


def exact_dot(a, b):
    return jnp.dot(a, b, precision=highest, preferred_element_type=f32)


def exact_dot_t(a, b):
    return lax.dot_general(
        a, b, (((1,), (1,)), ((), ())), precision=highest, preferred_element_type=f32
    )


def inverse_rms(values):
    return lax.rsqrt(jnp.mean(values * values, -1, keepdims=True) + epsilon)


def norm_back(values, gain, grad):
    scale = inverse_rms(values)
    scaled = values * scale
    grad_gain = jnp.sum(grad * scaled, 0, keepdims=True)
    weighted = gain * grad
    grad_values = scale * weighted - (
        values * (scale * scale * scale) * jnp.mean(weighted * values, -1, keepdims=True)
    )
    return grad_values, grad_gain


def first_row(rows):
    return lax.axis_index("seq") * rows


def make_mask(place_ref, mask_ref):
    shape = mask_ref.shape
    pos_q = first_row(shape[0]) + lax.broadcasted_iota(jnp.int32, shape, 0)
    pos_k = lax.broadcasted_iota(jnp.int32, shape, 1)
    allowed = pos_k <= pos_q
    for piece in range(2):
        start = place_ref[piece]
        in_q = (pos_q >= start) & (pos_q < start + PIECE)
        in_k = (pos_k >= start) & (pos_k < start + PIECE)
        allowed = allowed | (in_q & in_k)
    mask_ref[...] = jnp.where(allowed, 0.0, masked_out)


def spread(row, block, width):
    return pltpu.roll(
        jnp.broadcast_to(row, (block, width)), width - (block - 1), 1, stride=1, stride_axis=0
    )


def by_head(values, first_half):
    zero = jnp.zeros((), values.dtype)
    return jnp.concatenate(
        [jnp.where(first_half, values, zero), jnp.where(first_half, zero, values)]
    )


def of_head(stacked, first_half):
    block = stacked.shape[0] // 2
    return jnp.where(first_half, stacked[:block], stacked[block:])


def gather_diagonals(sums):
    rows = sums.shape[0]
    while rows > 1:
        half = rows // 2
        sums = pltpu.roll(sums[:half], half, 1) + sums[half:]
        rows = half
    return sums


def chosen_experts(pack_ref, shape):
    lane = lax.broadcasted_iota(jnp.int32, shape, 1).astype(f32)
    routes = pack_ref[24:32, : shape[0]].T
    return (lane == routes[:, 0:1]) | (lane == routes[:, 1:2])


def pack_small(router, gain_attn, gain_ffn, buckets, rel_table, routes, span):
    def rows(array, count):
        array = array.astype(f32)
        return jnp.pad(array, ((0, count - array.shape[0]), (0, span - array.shape[1])))

    return jnp.concatenate(
        [
            rows(router.T, 4),
            rows(gain_attn[None, :], 1),
            rows(gain_ffn[None, :], 1),
            rows(buckets[None, :], 2),
            rows(rel_table.T, 16),
            rows(routes.T, 8),
        ]
    )


def router_rows(pack_ref, n_experts, width):
    first = pack_ref[0:8, :width]
    row = lax.broadcasted_iota(jnp.int32, first.shape, 0)
    first = jnp.where(row < n_experts, first, 0.0)
    return jnp.concatenate([first, jnp.zeros((LANES - 8, width), f32)])


def bucket_match(pack_ref):
    shape = (LANES, pack_ref.shape[1])
    bucket = lax.broadcasted_iota(jnp.int32, shape, 0).astype(f32)
    return (bucket == pack_ref[6:7, :]).astype(f32)


def distances(pack_ref):
    return exact_dot(pack_ref[8:24, :LANES], bucket_match(pack_ref))


MESH = pl.DeviceIdType.MESH


class Place:
    def __init__(self, n_fsdp):
        self.rep = lax.axis_index("rep")
        self.line = lax.axis_index("fsdp")
        self.seq = lax.axis_index("seq")
        self.n_fsdp = n_fsdp
        self.row = self.rep // 2
        self.core = self.rep % 2

    def mate(self):
        return (self.row * 2 + 1 - self.core, self.line, self.seq)

    def chip(self, rows, columns, core=None):
        core = self.core if core is None else core
        row = (self.row + rows) % 2
        return (row * 2 + core, self.line, (self.seq + columns) % 2)

    def along(self, steps):
        return (self.rep, (self.line + steps) % self.n_fsdp, self.seq)


def meet(partners):
    barrier = pltpu.get_barrier_semaphore()
    for partner in partners:
        pl.semaphore_signal(barrier, inc=1, device_id=partner, device_id_type=MESH)
    pl.semaphore_wait(barrier, len(partners))


class Wires:
    def __init__(self, send, recv):
        self.send, self.recv = send, recv
        self.names = {}

    def copy(self, name, source, target, device):
        index = self.names.setdefault(name, len(self.names))
        return pltpu.make_async_remote_copy(
            src_ref=source,
            dst_ref=target,
            send_sem=self.send.at[index],
            recv_sem=self.recv.at[index],
            device_id=device,
            device_id_type=MESH,
        )


class Planned:
    def __init__(self, plan, send, recv):
        self.plan, self.send, self.recv = plan, send, recv
        self.order = list(plan)

    def __getitem__(self, name):
        source, target, device = self.plan[name]
        index = self.order.index(name)
        return pltpu.make_async_remote_copy(
            src_ref=source,
            dst_ref=target,
            send_sem=self.send.at[index],
            recv_sem=self.recv.at[index],
            device_id=device,
            device_id_type=MESH,
        )


def gather_kernel(
    n_fsdp,
    part_out,
    attn_q,
    attn_k,
    attn_v,
    attn_o,
    tokens,
    expert_in,
    router,
    gain_attn,
    gain_ffn,
    buckets,
    rel_table,
    routes,
    weights,
    x_all,
    w_in,
    pack,
    attn_held,
    tokens_held,
    in_held,
    send,
    recv,
    local,
):
    me = Place(n_fsdp)
    rep, line, seq = me.rep, me.line, me.seq
    far_row = (me.row + 1) % 2 * 2 + me.core
    mate, across, beside = me.mate(), me.chip(1, 0), me.chip(0, 1)
    part_in = expert_in.shape[1]
    wires = Wires(send, recv)
    meet([mate, across, beside, me.along(1), me.along(-1), me.along(2)])
    started = []

    def start(copy):
        copy.start()
        started.append(copy)
        return copy

    for i, matrix in enumerate((attn_q, attn_k, attn_v, attn_o)):

        @pl.when(rep == i)
        def _():
            own = pltpu.make_async_copy(matrix, attn_held, local.at[0])
            own.start()
            own.wait()

    mine = lambda z, r=rep, x=seq: weights.at[r, z, x]
    shifts = (0, 1, -1, 2)
    at = {0: line}
    z_copies = {}
    for shift in shifts[1:]:
        at[shift] = (line - shift) % n_fsdp
        z_copies[shift] = start(
            wires.copy(("z", shift), attn_held, mine(line), me.along(shift))
        )
    x_copies, y_copies, c_copies, far_copies = {}, {}, [], {}

    def spread_out(shift):
        z = at[shift]
        source = mine(z) if shift else attn_held
        x_copies[shift] = start(wires.copy(("x", shift), source, mine(z), beside))
        y_copies[shift] = start(wires.copy(("y", shift), source, mine(z), across))
        c_copies.append(start(wires.copy(("c", shift), source, mine(z), mate)))

    spread_out(0)
    columns = lambda z, x: pl.ds(pl.multiple_of((z * 2 + x) * part_out, LANES), part_out)
    rows = lambda x: pl.ds(pl.multiple_of(x * part_in, part_in), part_in)
    in_x, in_own = [], []
    for z in range(n_fsdp):
        here = pl.ds(z * part_out, part_out)
        target = w_in.at[line, rows(seq), here]
        in_x.append(
            start(wires.copy(("in", z), expert_in.at[rep, :, columns(z, 1 - seq)], target, beside))
        )
        copy = pltpu.make_async_copy(
            expert_in.at[rep, :, columns(z, seq)], in_held.at[:, here], local.at[1 + z]
        )
        copy.start()
        in_own.append(copy)
    own_attn = pltpu.make_async_copy(attn_held, mine(line), local.at[0])
    own_attn.start()
    x_own = Bounce(tokens, tokens_held, x_all.at[seq], local.at[pl.ds(n_fsdp + 1, 2)])
    x_own.start()
    for copy in in_own:
        copy.wait()
    own_in = pltpu.make_async_copy(in_held, w_in.at[line, rows(seq)], local.at[n_fsdp + 3])
    own_in.start()
    x_own.turn()
    pack[...] = jnp.zeros_like(pack)
    pack[0 : router.shape[0], : router.shape[1]] = router[...]
    pack[4, : gain_attn.shape[0]] = gain_attn[...]
    pack[5, : gain_ffn.shape[0]] = gain_ffn[...]
    pack[6, : buckets.shape[0]] = buckets[...].astype(f32)
    pack[8 : 8 + rel_table.shape[0], : rel_table.shape[1]] = rel_table[...]
    pack[24:26, : routes.shape[1]] = routes[...].astype(f32)
    for shift in shifts[1:]:
        z_copies[shift].wait_recv()
        spread_out(shift)
    for copy in in_x:
        copy.wait_recv()
    own_in.wait()
    in_copies = []
    for i, shift in enumerate((1, -1)):
        half = w_in.at[line, pl.ds(i * part_in, part_in)]
        in_copies.append(start(wires.copy(("line", shift), half, half, me.along(shift))))
    token_copy = start(wires.copy("tokens", tokens, x_all.at[seq], beside))
    for shift in shifts:
        z = at[shift]
        x_copies[shift].wait_recv()
        near = mine(z, rep, 1 - seq)
        far_copies[shift] = start(wires.copy(("far", shift), near, near, across))
        c_copies.append(start(wires.copy(("cx", shift), near, near, mate)))
    for shift in shifts:
        z = at[shift]
        y_copies[shift].wait_recv()
        there = mine(z, far_row, seq)
        c_copies.append(start(wires.copy(("cy", shift), there, there, mate)))
    for shift in shifts:
        z = at[shift]
        far_copies[shift].wait_recv()
        there = mine(z, far_row, 1 - seq)
        c_copies.append(start(wires.copy(("cf", shift), there, there, mate)))
    for copy in c_copies + in_copies + [token_copy]:
        copy.wait_recv()
    x_own.wait()
    own_attn.wait()
    for copy in started:
        copy.wait_send()


def gather(attn, tokens, expert_in, part_out, n_fsdp, small, span):
    part_attn, width = attn[0].shape
    n_rows = tokens.shape[0]
    n_experts, part_in, hidden = expert_in.shape
    anywhere = pl.BlockSpec(memory_space=pl.ANY)
    inside = pl.BlockSpec(memory_space=pltpu.VMEM)
    weights, x_all, w_in, pack = pl.pallas_call(
        functools.partial(gather_kernel, n_fsdp, part_out),
        out_shape=[
            jax.ShapeDtypeStruct((4, n_fsdp, 2, part_attn, width), bf16),
            jax.ShapeDtypeStruct((2, n_rows, width), bf16),
            jax.ShapeDtypeStruct((n_fsdp, 2 * part_in, n_fsdp * part_out), bf16),
            jax.ShapeDtypeStruct((32, span), f32),
        ],
        in_specs=[anywhere] * 6 + [inside] * 6,
        out_specs=[anywhere] * 3 + [inside],
        scratch_shapes=[
            pltpu.VMEM((part_attn, width), bf16),
            pltpu.VMEM((n_rows, width), bf16),
            pltpu.VMEM((part_in, n_fsdp * part_out), bf16),
            pltpu.SemaphoreType.DMA((48,)),
            pltpu.SemaphoreType.DMA((48,)),
            pltpu.SemaphoreType.DMA((8,)),
        ],
        compiler_params=pltpu.CompilerParams(collective_id=0, has_side_effects=True),
        name="gather_weights",
    )(*attn, tokens, expert_in, *small)
    return (
        weights.reshape(4, n_fsdp * 2 * part_attn, width),
        x_all.reshape(2 * n_rows, width),
        w_in,
        pack,
    )


class Bounce:
    def __init__(self, source, held, target, sems):
        self.load = lambda: pltpu.make_async_copy(source, held, sems.at[0])
        self.store = lambda: pltpu.make_async_copy(held, target, sems.at[1])

    def start(self):
        self.load().start()

    def turn(self):
        self.load().wait()
        self.store().start()

    def wait(self):
        self.store().wait()


def line_plan(me, own, pieces):
    rows = pieces.shape[1] // 2
    plan = {}
    for i, shift in enumerate((1, -1)):
        first, rest = pl.ds(i * rows, rows), pl.ds((1 - i) * rows, rows)
        target = pieces.at[me.line]
        piece = pieces.at[(me.line - shift) % me.n_fsdp, first]
        plan["first", shift] = (own.at[first], target.at[first], me.along(shift))
        plan["rest", shift] = (own.at[rest], target.at[rest], me.along(shift))
        plan["relay", shift] = (piece, piece, me.along(shift))
    return plan


class Background:
    n_in, n_out = 2, 2

    def __init__(self, n_fsdp):
        self.n_fsdp = n_fsdp

    def out_shape(self, dy, w_in):
        return [
            jax.ShapeDtypeStruct((8,) + dy.shape, bf16),
            jax.ShapeDtypeStruct(w_in.shape, bf16),
        ]

    def scratch(self, dy, w_in):
        return [
            pltpu.SemaphoreType.DMA((16,)),
            pltpu.SemaphoreType.DMA((16,)),
            pltpu.SemaphoreType.DMA((2,)),
            pltpu.VMEM(dy.shape, bf16),
        ]

    def run(self, step, before, ins, outs, scratch):
        dy, _ = ins
        dy_all, w_in = outs
        send, recv, local, dy_held = scratch
        me = Place(self.n_fsdp)
        half = dy.shape[0] // 2
        first, second = pl.ds(0, half), pl.ds(half, half)
        core = me.core
        own = 7 * (1 - core)
        mate, across, beside = me.mate(), me.chip(1, 0), me.chip(0, 1)
        slot = dy_all.at
        plan = {
            "x": (dy, slot[1 + core], beside),
            "y": (dy, slot[3 + core], across),
            "c0": (dy, slot[own], mate),
            "c1": (slot[1 + core], slot[1 + core], mate),
            "c2": (slot[3 + core], slot[3 + core], mate),
            "c3": (slot[5 + core], slot[5 + core], mate),
            "xy": (slot[1 + core, first], slot[5 + core, first], across),
            "yx": (slot[3 + core, second], slot[5 + core, second], beside),
        }
        line = line_plan(me, w_in.at[me.line], w_in)
        plan |= {name: line[name] for name in line if name[0] != "first"}
        copies = Planned(plan, send, recv)
        own_dy = Bounce(dy, dy_held, slot[own], local.at[pl.ds(0, 2)])
        if before:

            @pl.when(step == 0)
            def _():
                meet([mate, across, beside, me.along(1), me.along(-1)])
                for name in line:
                    if name[0] != "first":
                        copies[name].start()
                for name in ("x", "y", "c0"):
                    copies[name].start()
                own_dy.start()

            @pl.when(step == 3)
            def _():
                own_dy.turn()
                copies["x"].wait_recv()
                copies["xy"].start()
                copies["c1"].start()
                copies["y"].wait_recv()
                copies["yx"].start()
                copies["c2"].start()

            return

        @pl.when(step == pl.num_programs(0) - 1)
        def _():
            copies["xy"].wait_recv()
            copies["yx"].wait_recv()
            copies["c3"].start()
            for name in plan:
                if name not in ("x", "y", "xy", "yx"):
                    copies[name].wait_recv()
            own_dy.wait()
            for name in plan:
                copies[name].wait_send()


def forward_kernel(
    background,
    n_experts,
    head_dim,
    place_ref,
    x_ref,
    wq_ref,
    wk_ref,
    wv_ref,
    wo_ref,
    pack_ref,
    *refs,
):
    step = pl.program_id(0)
    n_in, n_out = (background.n_in, background.n_out) if background else (0, 0)
    behind_in, refs = refs[:n_in], refs[n_in:]
    q_out, k_out, v_out, o_out, p_out, x_mid_out, message_out, probs_out, h_out = refs[:9]
    behind_out, refs = refs[9 : 9 + n_out], refs[9 + n_out :]
    total_ref, mask_ref, bias_ref, dist_ref = refs[:4]
    if background:
        background.run(step, True, behind_in, behind_out, refs[4:])
    rows = x_mid_out.shape[0]
    length, width = x_ref.shape
    own = pl.ds(pl.multiple_of(first_row(rows), rows), rows)

    @pl.when(step == 0)
    def _():
        values = x_ref[...].astype(f32)
        gain_one = pack_ref[4:5, :width]
        h_out[...] = (values * inverse_rms(values) * gain_one).astype(bf16)
        dist_ref[...] = distances(pack_ref)
        total_ref[...] = jnp.zeros_like(total_ref)
        make_mask(place_ref, mask_ref)

    h_all = h_out[...]
    q_low = dot(h_out[own, :], wq_ref[...]).astype(bf16) * (head_dim**-0.5)
    kv_low = dot(h_all, jnp.concatenate([wk_ref[...], wv_ref[...]], 1)).astype(bf16)
    k_low, v_low = kv_low[:, :LANES], kv_low[:, LANES:]
    q_out[...] = q_low
    k_out[...] = k_low
    v_out[...] = v_low
    block = LANES
    span = pack_ref.shape[1]
    first_half = lax.broadcasted_iota(jnp.int32, (block, LANES), 1) < head_dim
    for head in range(2):
        bias_ref[head] = spread(dist_ref[pl.ds(2 * step + head, 1), :], block, span)
    for b in range(rows // block):
        here = slice(b * block, (b + 1) * block)
        offset = pl.multiple_of(length - LANES - block * b - first_row(rows), LANES)
        scores = dot_t(by_head(q_low[here], first_half), k_low).reshape(2, block, length)
        scores = scores + bias_ref[:, :, pl.ds(offset, length)] + mask_ref[here, :]
        top = jnp.max(scores, -1, keepdims=True)
        exp_scores = jnp.exp(scores - top)
        total = jnp.sum(exp_scores, -1, keepdims=True)
        probs = (exp_scores * (1.0 / total)).astype(bf16)
        p_out[:, here, :] = probs
        heads = dot(probs.reshape(2 * block, length), v_low)
        o_out[here, :] = of_head(heads, first_half).astype(bf16)
    total_ref[...] += dot(o_out[...], wo_ref[...])

    @pl.when(step == pl.num_programs(0) - 1)
    def _():
        x_mid = x_ref[own, :].astype(f32) + total_ref[...]
        x_mid_out[...] = x_mid
        h_two = (x_mid * inverse_rms(x_mid) * pack_ref[5:6, :width]).astype(bf16)
        message_out[:, :width] = h_two
        logits = exact_dot_t(h_two.astype(f32), router_rows(pack_ref, n_experts, width))
        lane = lax.broadcasted_iota(jnp.int32, logits.shape, 1)
        logits = jnp.where(lane < n_experts, logits, masked_out)
        exp_logits = jnp.exp(logits - jnp.max(logits, -1, keepdims=True))
        probs = exp_logits / jnp.sum(exp_logits, -1, keepdims=True)
        probs_out[...] = probs
        chosen = jnp.where(chosen_experts(pack_ref, probs.shape), probs, 0.0)
        gate = chosen / jnp.sum(chosen, -1, keepdims=True)
        high = gate.astype(bf16)
        low = gate - high.astype(f32)
        message_out[:, width:] = (high.astype(f32) + pltpu.roll(low, n_experts, 1)).astype(bf16)

    if background:
        background.run(step, False, behind_in, behind_out, refs[4:])


def attention_forward(
    place,
    x_all,
    weights,
    pack,
    n_rows,
    n_experts,
    head_dim,
    background=None,
    behind=(),
):
    length, width = x_all.shape
    pairs = width // LANES
    span = pack.shape[1]
    whole = lambda shape: pl.BlockSpec(shape, lambda p, *_: (0,) * len(shape))
    columns = lambda rows: pl.BlockSpec((rows, LANES), lambda p, *_: (0, p))
    matrix = lambda i: pl.BlockSpec((None, width, LANES), lambda p, *_: (i, 0, p))
    out_shape = [
        jax.ShapeDtypeStruct((n_rows, width), bf16),
        jax.ShapeDtypeStruct((length, width), bf16),
        jax.ShapeDtypeStruct((length, width), bf16),
        jax.ShapeDtypeStruct((n_rows, width), bf16),
        jax.ShapeDtypeStruct((pairs, 2, n_rows, length), bf16),
        jax.ShapeDtypeStruct((n_rows, width), f32),
        jax.ShapeDtypeStruct((n_rows, width + LANES), bf16),
        jax.ShapeDtypeStruct((n_rows, LANES), f32),
        jax.ShapeDtypeStruct((length, width), bf16),
    ]
    anywhere = pl.BlockSpec(memory_space=pl.ANY)
    params, aliases = {}, {}
    if background:
        out_shape += background.out_shape(*behind)
        params = {"collective_id": 1, "has_side_effects": True}
        aliases = {8: 10}
    return pl.pallas_call(
        functools.partial(forward_kernel, background, n_experts, head_dim),
        out_shape=out_shape,
        grid_spec=pltpu.PrefetchScalarGridSpec(
            num_scalar_prefetch=1,
            grid=(pairs,),
            in_specs=[
                whole((length, width)),
                matrix(0),
                matrix(1),
                matrix(2),
                pl.BlockSpec((None, LANES, width), lambda p, *_: (3, p, 0)),
                whole(pack.shape),
            ]
            + [anywhere] * len(behind),
            out_specs=[
                columns(n_rows),
                columns(length),
                columns(length),
                columns(n_rows),
                pl.BlockSpec((None, 2, n_rows, length), lambda p, *_: (p, 0, 0, 0)),
                whole((n_rows, width)),
                whole((n_rows, width + LANES)),
                whole((n_rows, LANES)),
                whole((length, width)),
            ]
            + [anywhere] * (background.n_out if background else 0),
            scratch_shapes=[
                pltpu.VMEM((n_rows, width), f32),
                pltpu.VMEM((n_rows, length), f32),
                pltpu.VMEM((2, LANES, span), f32),
                pltpu.VMEM((16, span), f32),
            ]
            + (background.scratch(*behind) if background else []),
        ),
        input_output_aliases=aliases,
        compiler_params=pltpu.CompilerParams(vmem_limit_bytes=VMEM_LIMIT, **params),
        cost_estimate=pl.CostEstimate(
            flops=20_000_000_000, transcendentals=0, bytes_accessed=20_000_000
        ),
        name="attention_forward",
    )(
        place,
        x_all,
        weights,
        weights,
        weights,
        weights,
        pack,
        *behind,
    )


GELU_A = 0.7978845608028654
GELU_B = 0.044715 * GELU_A


def experts_kernel(
    n_experts,
    chunk,
    expert_ref,
    message_ref,
    dy_ref,
    w_in_ref,
    w_out_ref,
    out_ref,
    dh_ref,
    dw_in_ref,
    dw_out_ref,
    dw_in_acc,
    dw_out_acc,
):
    step = pl.program_id(0)
    width = dy_ref.shape[1]
    hidden = w_in_ref.shape[1]
    expert = expert_ref[0]

    @pl.when(step == 0)
    def _():
        dw_in_acc[...] = jnp.zeros_like(dw_in_acc)
        dw_out_acc[...] = jnp.zeros_like(dw_out_acc)

    h = message_ref[:, :width]
    extra = message_ref[:, width:].astype(f32)
    lane = lax.broadcasted_iota(jnp.int32, extra.shape, 1)
    mine = (lane == expert) | (lane == expert + n_experts)
    gate = jnp.sum(jnp.where(mine, extra, 0.0), -1, keepdims=True)
    dy = dy_ref[...]
    out_total = None
    dh_total = None
    dgate = None
    for start in range(0, hidden, chunk):
        part = slice(start, start + chunk)
        up = dot(h, w_in_ref[:, part])
        dact = dot_t(dy, w_out_ref[part, :])
        square = up * up
        tanh = jnp.tanh(up * (GELU_A + GELU_B * square))
        half = 0.5 * up
        more = 1.0 + tanh
        act = half * more
        slope = 0.5 * more + half * (1.0 - tanh * tanh) * (GELU_A + 3.0 * GELU_B * square)
        gated = (gate * act).astype(bf16)
        dgate_part = jnp.sum(act * dact, -1, keepdims=True)
        dup = (gate * dact * slope).astype(bf16)
        out_part = dot(gated, w_out_ref[part, :])
        dh_part = dot_t(dup, w_in_ref[:, part])
        out_total = out_part if out_total is None else out_total + out_part
        dh_total = dh_part if dh_total is None else dh_total + dh_part
        dgate = dgate_part if dgate is None else dgate + dgate_part
        dw_out_acc[part, :] += t_dot(gated, dy)
        dw_in_acc[:, part] += t_dot(h, dup)
    out_ref[...] = out_total.astype(bf16)
    dh_ref[:, :width] = dh_total.astype(bf16)
    high = dgate.astype(bf16).astype(f32)
    low = dgate - high
    dh_ref[:, width:] = jnp.where(
        lane == expert, high, jnp.where(lane == expert + n_experts, low, 0.0)
    ).astype(bf16)

    @pl.when(step == pl.num_programs(0) - 1)
    def _():
        dw_in_ref[...] = dw_in_acc[...].astype(bf16)
        dw_out_ref[...] = dw_out_acc[...].astype(bf16)


def experts(expert, message, dy, w_in, w_out, n_experts, block):
    tokens, width = dy.shape
    hidden = w_in.shape[1]
    whole = lambda shape: pl.BlockSpec(shape, lambda i, *_: (0,) * len(shape))
    rows = lambda columns: pl.BlockSpec((block, columns), lambda i, *_: (i, 0))
    return pl.pallas_call(
        functools.partial(experts_kernel, n_experts, 512),
        out_shape=[
            jax.ShapeDtypeStruct((tokens, width), bf16),
            jax.ShapeDtypeStruct((tokens, width + LANES), bf16),
            jax.ShapeDtypeStruct((width, hidden), bf16),
            jax.ShapeDtypeStruct((hidden, width), bf16),
        ],
        grid_spec=pltpu.PrefetchScalarGridSpec(
            num_scalar_prefetch=1,
            grid=(tokens // block,),
            in_specs=[
                rows(width + LANES),
                rows(width),
                whole((width, hidden)),
                whole((hidden, width)),
            ],
            out_specs=[
                rows(width),
                rows(width + LANES),
                whole((width, hidden)),
                whole((hidden, width)),
            ],
            scratch_shapes=[
                pltpu.VMEM((width, hidden), f32),
                pltpu.VMEM((hidden, width), f32),
            ],
        ),
        compiler_params=pltpu.CompilerParams(vmem_limit_bytes=VMEM_LIMIT),
        cost_estimate=pl.CostEstimate(
            flops=60_000_000_000, transcendentals=0, bytes_accessed=30_000_000
        ),
        name="experts",
    )(expert, message, dy, w_in, w_out)


def plane_slot(j):
    return (j + 1) // 2 % 4, (j + 1) % 2


def down_order(step):
    inner = (13 - step) // 8
    return inner * ((step + 4) % 6 + 1) + (1 - inner) * (step - 6) * 7


def experts_up_kernel(
    n_experts,
    chunk,
    n_fsdp,
    message_ref,
    dy_ref,
    w_in,
    expert_out,
    h_out,
    act_out,
    slope_out,
    dw_out_ref,
    w_out,
    h_ref,
    dw_out_acc,
    w_in_ref,
    gated_ref,
    dy_pair_ref,
    out_held,
    send,
    recv,
    local,
):
    step = pl.program_id(0)
    last = pl.num_programs(0) - 1
    me = Place(n_fsdp)
    core = me.core
    rows, width = dy_ref.shape
    hidden = w_in_ref.shape[1]
    half = rows // 2
    first, second = pl.ds(0, half), pl.ds(half, half)
    mate, across, beside = me.mate(), me.chip(1, 0), me.chip(0, 1)
    own = 7 * (1 - core)
    slot = h_ref.at
    plan = {
        "x": (message_ref, slot[1 + core], beside),
        "y": (message_ref, slot[3 + core], across),
        "c0": (message_ref, slot[own], mate),
        "c1": (slot[1 + core], slot[1 + core], mate),
        "c2": (slot[3 + core], slot[3 + core], mate),
        "c3": (slot[5 + core], slot[5 + core], mate),
        "xy": (slot[1 + core, first], slot[5 + core, first], across),
        "yx": (slot[3 + core, second], slot[5 + core, second], beside),
    } | line_plan(me, expert_out.at[me.rep], w_out)
    copies = Planned(plan, send, recv)
    own_out = Bounce(expert_out.at[me.rep], out_held, w_out.at[me.line], local.at[pl.ds(0, 2)])

    @pl.when(step == 0)
    def _():
        load = pltpu.make_async_copy(w_in, w_in_ref, local.at[2])
        load.start()
        meet([mate, across, beside, me.along(1), me.along(-1)])
        for name in ("c0", "x", "y", ("first", 1), ("first", -1)):
            copies[name].start()
        own_out.start()
        h_ref[own] = message_ref[...]
        dw_out_acc[...] = jnp.zeros_like(dw_out_acc)
        load.wait()

    @pl.when(step == 1)
    def _():
        own_out.turn()
        for shift in (1, -1):
            copies["rest", shift].start()

    @pl.when(step == 2)
    def _():
        for shift in (1, -1):
            copies["first", shift].wait_recv()
            copies["relay", shift].start()
        copies["x"].wait_recv()
        copies["c1"].start()
        copies["xy"].start()
        copies["y"].wait_recv()
        copies["c2"].start()
        copies["yx"].start()

    @pl.when(step == 6)
    def _():
        copies["xy"].wait_recv()
        copies["yx"].wait_recv()
        copies["c3"].start()

    for q in range(4):

        @pl.when(step == 2 * q + 1 - core)
        def _():
            copies[f"c{q}"].wait_recv()

    now = (step + 7) % 8
    expert = me.rep
    h_out[...] = h_ref[now]
    h = h_ref[now, :, :width]
    extra = h_ref[now, :, width:].astype(f32)
    lane = lax.broadcasted_iota(jnp.int32, extra.shape, 1)
    mine = (lane == expert) | (lane == expert + n_experts)
    gate = jnp.sum(jnp.where(mine, extra, 0.0), -1, keepdims=True)
    place = pl.ds(pl.multiple_of(step % 2 * rows, rows), rows)
    dy_pair_ref[place, :] = dy_ref[...]
    for start in range(0, hidden, chunk):
        piece = slice(start, start + chunk)
        up = dot(h, w_in_ref[:, piece])
        square = up * up
        tanh = jnp.tanh(up * (GELU_A + GELU_B * square))
        halved = 0.5 * up
        more = 1.0 + tanh
        act = (halved * more).astype(bf16)
        slope = 0.5 * more + halved * (1.0 - tanh * tanh) * (GELU_A + 3.0 * GELU_B * square)
        act_out[:, piece] = act
        slope_out[:, piece] = slope.astype(bf16)
        gated_ref[place, piece] = (gate * act.astype(f32)).astype(bf16)

    @pl.when(step % 2 == 1)
    def _():
        dw_out_acc[...] += t_dot(gated_ref[...], dy_pair_ref[...])

    @pl.when(step == last)
    def _():
        dw_out_ref[...] = dw_out_acc[...].astype(bf16)
        own_out.wait()
        for shift in (1, -1):
            copies["rest", shift].wait_recv()
            copies["relay", shift].wait_recv()
        for name in plan:
            copies[name].wait_send()


def experts_up(message, dy_all, w_in, expert_out, n_experts, n_fsdp):
    blocks, rows, width = dy_all.shape
    long = message.shape[1]
    hidden = w_in.shape[1]
    once = pl.Buffered(1)
    whole = lambda shape: pl.BlockSpec(shape, lambda i: (0,) * len(shape), pipeline_mode=once)
    turn = lambda columns: pl.BlockSpec((None, rows, columns), lambda i: ((i + 7) % 8, 0, 0))
    anywhere = pl.BlockSpec(memory_space=pl.ANY)
    dma = lambda *shape: pltpu.SemaphoreType.DMA(shape)
    return pl.pallas_call(
        functools.partial(experts_up_kernel, n_experts, hidden // 2, n_fsdp),
        out_shape=[
            jax.ShapeDtypeStruct((blocks, rows, long), bf16),
            jax.ShapeDtypeStruct((blocks, rows, hidden), bf16),
            jax.ShapeDtypeStruct((blocks, rows, hidden), bf16),
            jax.ShapeDtypeStruct((hidden, width), bf16),
            jax.ShapeDtypeStruct((n_fsdp,) + expert_out.shape[1:], bf16),
        ],
        grid=(blocks,),
        in_specs=[whole((rows, long)), turn(width), anywhere, anywhere],
        out_specs=[turn(long), turn(hidden), turn(hidden), whole((hidden, width)), anywhere],
        scratch_shapes=[
            pltpu.VMEM((blocks, rows, long), bf16),
            pltpu.VMEM((hidden, width), f32),
            pltpu.VMEM((width, hidden), bf16),
            pltpu.VMEM((2 * rows, hidden), bf16),
            pltpu.VMEM((2 * rows, width), bf16),
            pltpu.VMEM(expert_out.shape[1:], bf16),
            dma(16),
            dma(16),
            dma(3),
        ],
        compiler_params=pltpu.CompilerParams(
            vmem_limit_bytes=VMEM_LIMIT, collective_id=2, has_side_effects=True
        ),
        cost_estimate=pl.CostEstimate(
            flops=20_000_000_000, transcendentals=0, bytes_accessed=30_000_000
        ),
        name="experts_up",
    )(message, dy_all, w_in, expert_out)


def experts_down_kernel(
    n_experts,
    chunk,
    n_fsdp,
    message_ref,
    dy_ref,
    act_ref,
    slope_ref,
    w_in,
    w_out,
    dw_out,
    back_ref,
    out_half,
    dw_in_ref,
    sum_out,
    part_ref,
    tx_ref,
    rx_ref,
    fin_ref,
    fin_out_ref,
    land_ref,
    dw_in_acc,
    w_in_ref,
    w_out_ref,
    h_pair_ref,
    dup_ref,
    tx_send,
    tx_recv,
    fin_sem,
    land_sem,
    local,
    near,
    mid,
    far,
    own_ref,
    line_send,
    line_recv,
    line_local,
):
    step = pl.program_id(0)
    last = 7
    me = Place(n_fsdp)
    core = me.core
    rows, width = dy_ref.shape
    hidden = w_in_ref.shape[1]
    long = message_ref.shape[1]
    half = rows // 2
    mate = me.mate()
    adds = LineSum(me, dw_out, near, mid, far, own_ref, line_send, line_recv, line_local)

    def to_mate(j):
        return pltpu.make_async_remote_copy(
            src_ref=tx_ref.at[j % 2],
            dst_ref=rx_ref.at[j],
            send_sem=tx_send.at[j],
            recv_sem=tx_recv.at[j],
            device_id=mate,
            device_id_type=MESH,
        )

    def to_owner(j):
        q, k = plane_slot(down_order(j))
        return pltpu.make_async_remote_copy(
            src_ref=fin_ref.at[j % 2],
            dst_ref=land_ref.at[q, core],
            send_sem=fin_sem.at[j],
            recv_sem=land_sem.at[q, core],
            device_id=me.chip(q // 2, q % 2, k),
            device_id_type=MESH,
        )

    def keep_out(j):
        return pltpu.make_async_copy(fin_out_ref.at[j % 2], out_half.at[down_order(j)], local.at[j])

    def stays(j):
        q, k = plane_slot(down_order(j))
        return (q == 0) & (k == core)

    def finish_block(j):
        to_mate(j).wait_recv()
        mine = part_ref.at[j % 2, pl.ds(core * half, half)]

        @pl.when(j >= 2)
        def _():
            keep_out(j - 2).wait()

        @pl.when((j >= 2) & ~stays(j - 2))
        def _():
            to_owner(j - 2).wait_send()

        fin_ref[j % 2] = (mine[:, :long] + rx_ref[j, :, :long].astype(f32)).astype(bf16)

        @pl.when(stays(j))
        def _():
            land_ref[0, core] = fin_ref[j % 2]

        @pl.when(~stays(j))
        def _():
            to_owner(j).start()

        fin_out_ref[j % 2] = (mine[:, long:] + rx_ref[j, :, long:].astype(f32)).astype(bf16)
        keep_out(j).start()

    @pl.when(step == 0)
    def _():
        loads = [
            pltpu.make_async_copy(w_in, w_in_ref, local.at[0]),
            pltpu.make_async_copy(w_out, w_out_ref, local.at[1]),
        ]
        for load in loads:
            load.start()
        partners = [mate, me.along(1), me.along(-1)]
        for q in (1, 2, 3):
            for k in (0, 1):
                partners.append(me.chip(q // 2, q % 2, (core + k) % 2))
        meet(partners)
        adds.start()
        dw_in_acc[...] = jnp.zeros_like(dw_in_acc)
        for load in loads:
            load.wait()

    @pl.when(step == 3)
    def _():
        adds.turn()

    expert = me.rep
    place = pl.ds(pl.multiple_of(step % 2 * rows, rows), rows)
    h_pair_ref[:, place] = message_ref[:, :width].T
    extra = message_ref[:, width:].astype(f32)
    lane = lax.broadcasted_iota(jnp.int32, extra.shape, 1)
    mine = (lane == expert) | (lane == expert + n_experts)
    gate = jnp.sum(jnp.where(mine, extra, 0.0), -1, keepdims=True)
    dy = dy_ref[...]
    dgate = None
    part = part_ref.at[step % 2]
    for start in range(0, hidden, chunk):
        piece = slice(start, start + chunk)
        act = act_ref[:, piece].astype(f32)
        dact = dot_t(dy, w_out_ref[piece, :])
        gated = (gate * act).astype(bf16)
        dgate_part = jnp.sum(act * dact, -1, keepdims=True)
        dup = (gate * dact * slope_ref[:, piece].astype(f32)).astype(bf16)
        out_part = dot(gated, w_out_ref[piece, :])
        dh_part = dot_t(dup, w_in_ref[:, piece])
        if start == 0:
            part[:, long:] = out_part
            part[:, :width] = dh_part
        else:
            part[:, long:] += out_part
            part[:, :width] += dh_part
        dgate = dgate_part if dgate is None else dgate + dgate_part
        dup_ref[place, piece] = dup
        if start == chunk:

            @pl.when(step >= 1)
            def _():
                finish_block(step - 1)

    @pl.when(step % 2 == 1)
    def _():
        dw_in_acc[...] += dot(h_pair_ref[...], dup_ref[...])

    high = dgate.astype(bf16).astype(f32)
    low = dgate - high
    part[:, width:long] = jnp.where(
        lane == expert, high, jnp.where(lane == expert + n_experts, low, 0.0)
    )

    @pl.when(step >= 2)
    def _():
        to_mate(step - 2).wait_send()

    tx_ref[step % 2] = part_ref[step % 2, pl.ds((1 - core) * half, half)].astype(bf16)
    to_mate(step).start()

    @pl.when(step == last)
    def _():
        dw_in_ref[...] = dw_in_acc[...].astype(bf16)
        finish_block(last)
        sum_out[...] = adds.total()
        to_mate(last - 1).wait_send()
        to_mate(last).wait_send()
        keep_out(last - 1).wait()
        keep_out(last).wait()
        for j in (last - 1, last):

            @pl.when(~stays(j))
            def _():
                to_owner(j).wait_send()

        for side in range(2):
            total = None
            for q in range(4):
                arrived = pltpu.make_async_remote_copy(
                    src_ref=fin_ref.at[0],
                    dst_ref=land_ref.at[q, side],
                    send_sem=fin_sem.at[0],
                    recv_sem=land_sem.at[q, side],
                    device_id=mate,
                    device_id_type=MESH,
                )
                if q == 0:

                    @pl.when(core != side)
                    def _():
                        arrived.wait_recv()

                else:
                    arrived.wait_recv()
                landed = land_ref[q, side].astype(f32)
                total = landed if total is None else total + landed
            back_ref[side * half : (side + 1) * half, :] = total


def experts_down(message_all, dy_all, act, slope, w_in, w_out, dw_out, n_experts, n_fsdp):
    blocks, rows, width = dy_all.shape
    long = message_all.shape[2]
    hidden = w_in.shape[1]
    half = rows // 2
    once = pl.Buffered(1)
    whole = lambda shape: pl.BlockSpec(shape, lambda i: (0,) * len(shape), pipeline_mode=once)
    block = lambda columns: pl.BlockSpec(
        (None, rows, columns), lambda i: (down_order(i), 0, 0)
    )
    anywhere = pl.BlockSpec(memory_space=pl.ANY)
    both = long + width
    dma = lambda *shape: pltpu.SemaphoreType.DMA(shape)
    return pl.pallas_call(
        functools.partial(experts_down_kernel, n_experts, hidden // 2, n_fsdp),
        out_shape=[
            jax.ShapeDtypeStruct((rows, long), f32),
            jax.ShapeDtypeStruct((blocks, half, width), bf16),
            jax.ShapeDtypeStruct((width, hidden), bf16),
            jax.ShapeDtypeStruct(dw_out.shape[1:], bf16),
        ],
        grid=(blocks,),
        in_specs=[
            block(long),
            block(width),
            block(hidden),
            block(hidden),
            anywhere,
            anywhere,
            anywhere,
        ],
        out_specs=[
            whole((rows, long)),
            anywhere,
            whole((width, hidden)),
            whole(dw_out.shape[1:]),
        ],
        scratch_shapes=[
            pltpu.VMEM((2, rows, both), f32),
            pltpu.VMEM((2, half, both), bf16),
            pltpu.VMEM((blocks, half, both), bf16),
            pltpu.VMEM((2, half, long), bf16),
            pltpu.VMEM((2, half, width), bf16),
            pltpu.VMEM((4, 2, half, long), bf16),
            pltpu.VMEM((width, hidden), f32),
            pltpu.VMEM((width, hidden), bf16),
            pltpu.VMEM((hidden, width), bf16),
            pltpu.VMEM((width, 2 * rows), bf16),
            pltpu.VMEM((2 * rows, hidden), bf16),
            dma(8),
            dma(8),
            dma(8),
            dma(4, 2),
            dma(8),
        ]
        + LineSum.scratch(*dw_out.shape[1:]),
        compiler_params=pltpu.CompilerParams(
            vmem_limit_bytes=VMEM_LIMIT, collective_id=3, has_side_effects=True
        ),
        cost_estimate=pl.CostEstimate(
            flops=40_000_000_000, transcendentals=0, bytes_accessed=40_000_000
        ),
        name="experts_down",
    )(message_all, dy_all, act, slope, w_in, w_out, dw_out)


class LineSum:
    def __init__(self, me, whole, near, mid, far, mine, send, recv, local):
        self.me, self.whole, self.near, self.mid, self.far = me, whole, near, mid, far
        self.mine, self.local = mine, local
        rows = whole.shape[1]
        half = rows // 2
        self.parts = {1: slice(0, half), -1: slice(half, rows)}
        plan = {}
        for i, shift in enumerate((1, -1)):
            part = pl.ds(i * half, half)
            target = (me.line + 2) % me.n_fsdp
            plan["near", shift] = (whole.at[target, part], near.at[i], me.along(shift))
            plan["far", shift] = (mid.at[i], far.at[i], me.along(shift))
        self.copies = Planned(plan, send, recv)

    def loads(self):
        me = self.me
        for i, shift in enumerate((1, -1)):
            source = self.whole.at[(me.line + shift) % me.n_fsdp]
            yield pltpu.make_async_copy(source, self.mid.at[i], self.local.at[i])
        yield pltpu.make_async_copy(self.whole.at[me.line], self.mine, self.local.at[2])

    def start(self):
        for shift in (1, -1):
            self.copies["near", shift].start()
        for load in self.loads():
            load.start()

    def turn(self):
        for load in self.loads():
            load.wait()
        for i, shift in enumerate((1, -1)):
            self.copies["near", shift].wait_recv()
            part = self.parts[shift]
            total = self.mid[i, part, :].astype(f32) + self.near[i].astype(f32)
            self.mid[i, part, :] = total.astype(bf16)
            self.copies["far", shift].start()

    def total(self):
        for shift in (1, -1):
            self.copies["far", shift].wait_recv()
        total = self.mine[...].astype(f32) + self.far[0].astype(f32) + self.far[1].astype(f32)
        for shift in (1, -1):
            self.copies["near", shift].wait_send()
            self.copies["far", shift].wait_send()
        return total.astype(bf16)

    @staticmethod
    def scratch(rows, columns):
        return [
            pltpu.VMEM((2, rows // 2, columns), bf16),
            pltpu.VMEM((2, rows, columns), bf16),
            pltpu.VMEM((2, rows, columns), bf16),
            pltpu.VMEM((rows, columns), bf16),
            pltpu.SemaphoreType.DMA((4,)),
            pltpu.SemaphoreType.DMA((4,)),
            pltpu.SemaphoreType.DMA((3,)),
        ]


class BackgroundBack:
    n_in, n_out = 2, 4

    def __init__(self, n_fsdp):
        self.n_fsdp = n_fsdp

    def out_shape(self, out_half, dw_in):
        half, width = out_half.shape[1:]
        return [
            jax.ShapeDtypeStruct((2 * half, width), bf16),
            jax.ShapeDtypeStruct(dw_in.shape[1:], bf16),
            jax.ShapeDtypeStruct(
                (self.n_fsdp, width // (2 * self.n_fsdp), width - LANES), bf16
            ),
            jax.ShapeDtypeStruct((4,) + self.split(width), bf16),
        ]

    def out_specs(self, shapes):
        whole = lambda shape: pl.BlockSpec(shape, lambda p, *_: (0,) * len(shape))
        return [whole(s.shape) for s in shapes]

    def scratch(self, out_half, dw_in):
        half, width = out_half.shape[1:]
        pairs = width // LANES - 1
        return [
            pltpu.VMEM((3, 2, half, width), bf16),
            pltpu.SemaphoreType.DMA((8,)),
            pltpu.SemaphoreType.DMA((3, 2)),
            pltpu.VMEM((2, 4) + self.split(width), bf16),
            pltpu.VMEM((pairs, 2) + self.split(width), bf16),
            pltpu.VMEM((pairs, 2) + self.split(width), bf16),
            pltpu.VMEM((pairs, 3, self.n_fsdp) + self.split(width)[2:], bf16),
            pltpu.SemaphoreType.DMA((pairs, 2)),
            pltpu.SemaphoreType.DMA((pairs, 2)),
            pltpu.SemaphoreType.DMA((pairs, 3)),
            pltpu.SemaphoreType.DMA((pairs, 3)),
            pltpu.VMEM((2, half, width), bf16),
            pltpu.VMEM((2, half, width), bf16),
            pltpu.SemaphoreType.DMA((2,)),
            pltpu.SemaphoreType.DMA((2,)),
        ] + LineSum.scratch(*dw_in.shape[1:])

    def split(self, width):
        return (self.n_fsdp, 2, width // (2 * self.n_fsdp), LANES)

    def to_mate(self, pair, i, scratch):
        me = Place(self.n_fsdp)
        own, given = scratch[3:5]
        send, recv = scratch[7:9]
        return pltpu.make_async_remote_copy(
            src_ref=own.at[pair % 2, 2 * i + 1 - me.core],
            dst_ref=given.at[pair, i],
            send_sem=send.at[pair, i],
            recv_sem=recv.at[pair, i],
            device_id=me.mate(),
            device_id_type=MESH,
        )

    def to_chip(self, pair, i, scratch):
        me = Place(self.n_fsdp)
        added, landed = scratch[5:7]
        send, recv = scratch[9:11]
        rows, columns = ((0, 1), (1, 0), (1, 1))[i]
        row, column = (me.row + rows) % 2, (me.seq + columns) % 2
        return pltpu.make_async_remote_copy(
            src_ref=added.at[pair, row, :, column],
            dst_ref=landed.at[pair, i],
            send_sem=send.at[pair, i],
            recv_sem=recv.at[pair, i],
            device_id=me.chip(rows, columns),
            device_id_type=MESH,
        )

    def give(self, pair, grads, scratch, last_out):
        own = scratch[3]
        last = pl.num_programs(0) - 1

        @pl.when(pair >= 2)
        def _():
            for i in (0, 1):
                self.to_mate(pair - 2, i, scratch).wait_send()

        @pl.when(pair < last)
        def _():
            for i, grad in enumerate(grads):
                own[pair % 2, i] = grad.reshape(own.shape[2:])
            for i in (0, 1):
                self.to_mate(pair, i, scratch).start()

        @pl.when(pair == last)
        def _():
            for i, grad in enumerate(grads):
                last_out[i] = grad.reshape(own.shape[2:])

    def collect(self, pair, scratch):
        core = Place(self.n_fsdp).core
        own, given, added = scratch[3:6]
        for i in (0, 1):
            self.to_mate(pair, i, scratch).wait_recv()
            total = own[pair % 2, 2 * i + core].astype(f32) + given[pair, i].astype(f32)
            added[pair, i] = total.astype(bf16)
        for i in range(3):
            self.to_chip(pair, i, scratch).start()

    def collect_before(self, pair, scratch):
        @pl.when(pair >= 1)
        def _():
            self.collect(pair - 1, scratch)

    def run(self, step, before, ins, outs, scratch, x_mid):
        out_half, dw_in = ins
        out_rows, sum_in, plane_sum, _ = outs
        land, send, recv = scratch[:3]
        relay, hop, relay_recv, hop_sem = scratch[11:15]
        near, mid, far, mine, line_send, line_recv, line_local = scratch[15:]
        me = Place(self.n_fsdp)
        core = me.core
        half = out_half.shape[1]
        line = LineSum(me, dw_in, near, mid, far, mine, line_send, line_recv, line_local)

        across, beside = (lambda k: me.chip(1, 0, k)), (lambda k: me.chip(0, 1, k))
        plan = {
            "mate": (out_half.at[7 * core], land.at[0, core], me.mate(), recv.at[0, core]),
            "direct0": (out_half.at[3], land.at[2, core], across(0), recv.at[2, core]),
            "direct1": (out_half.at[2], land.at[1, core], beside(1), recv.at[1, core]),
            "hop0": (out_half.at[5], relay.at[0], across(core), relay_recv.at[0]),
            "hop1": (out_half.at[6], relay.at[1], beside(core), relay_recv.at[1]),
            "sum0": (hop.at[0], land.at[1, core], beside(0), recv.at[1, core]),
            "sum1": (hop.at[1], land.at[2, core], across(1), recv.at[2, core]),
        }

        def result(name):
            source, target, device, arrival = plan[name]
            return pltpu.make_async_remote_copy(
                src_ref=source,
                dst_ref=target,
                send_sem=send.at[list(plan).index(name)],
                recv_sem=arrival,
                device_id=device,
                device_id_type=MESH,
            )

        def own_parts():
            yield pltpu.make_async_copy(out_half.at[1], hop.at[0], hop_sem.at[0])
            yield pltpu.make_async_copy(out_half.at[4], hop.at[1], hop_sem.at[1])

        stay = lambda: pltpu.make_async_copy(
            out_half.at[7 * (1 - core)], land.at[0, core], send.at[7]
        )

        if before:

            @pl.when(step == 0)
            def _():
                partners = [me.mate(), me.along(1), me.along(-1)]
                for q in (1, 2, 3):
                    for k in (0, 1):
                        partners.append(me.chip(q // 2, q % 2, (core + k) % 2))
                meet(partners)
                line.start()
                for name in ("hop0", "hop1", "direct0", "direct1", "mate"):
                    result(name).start()
                stay().start()
                for part in own_parts():
                    part.start()

            @pl.when(step == 2)
            def _():
                line.turn()

            @pl.when(step == 3)
            def _():
                for part in own_parts():
                    part.wait()
                for k in (0, 1):
                    result(f"hop{k}").wait_recv()
                    hop[k] = (hop[k].astype(f32) + relay[k].astype(f32)).astype(bf16)
                    result(f"sum{k}").start()

            return

        @pl.when(step == pl.num_programs(0) - 1)
        def _():
            added, landed = scratch[5:7]
            pairs = landed.shape[0]
            sum_in[...] = line.total()
            for name in plan:
                result(name).wait_send()
            stay().wait()
            for side in range(2):
                here = slice(side * half, (side + 1) * half)
                total = x_mid[here, :]
                for q in range(3):
                    arrived = pltpu.make_async_remote_copy(
                        src_ref=out_half.at[0],
                        dst_ref=land.at[q, side],
                        send_sem=send.at[0],
                        recv_sem=recv.at[q, side],
                        device_id=me.mate(),
                        device_id_type=MESH,
                    )
                    if q == 0:

                        @pl.when(core != side)
                        def _():
                            arrived.wait_recv()

                    else:
                        arrived.wait_recv()
                    total = total + land[q, side].astype(f32)
                out_rows[here, :] = total.astype(bf16)
            for i in (0, 1):
                self.to_mate(pairs - 1, i, scratch).wait_send()
            for pair in range(pairs):
                total = added[pair, me.row, :, me.seq].astype(f32)
                for i in range(3):
                    self.to_chip(pair, i, scratch).wait_recv()
                    total = total + landed[pair, i].astype(f32)
                plane_sum[:, :, pair * LANES : (pair + 1) * LANES] = total.astype(bf16)
            for pair in range(pairs):
                for i in range(3):
                    self.to_chip(pair, i, scratch).wait_send()


def backward_kernel(
    background,
    n_experts,
    head_dim,
    back_ref,
    dy_ref,
    x_mid_ref,
    message_ref,
    probs_ref,
    pack_ref,
    h_ref,
    wq_ref,
    wk_ref,
    wv_ref,
    wo_ref,
    q_ref,
    k_ref,
    v_ref,
    o_ref,
    p_ref,
    x_ref,
    *refs,
):
    step = pl.program_id(0)
    n_in, n_out = (background.n_in, background.n_out) if background else (0, 0)
    behind_in, refs = refs[:n_in], refs[n_in:]
    n_grads = 0 if background else 4
    grad_outs, refs = refs[:n_grads], refs[n_grads:]
    dh_own_out, dh_other_out, dx_mid_out, gain_out, router_out, ddist_out = refs[:6]
    gain_one_out, refs = refs[6], refs[7:]
    behind_out, refs = refs[:n_out], refs[n_out:]
    da_ref, dh_all_ref, dh_mine_ref, dbias_ref, dq_ref, h_turned_ref, o_turned_ref = refs[:7]
    if background:
        background.run(step, True, behind_in, behind_out, refs[7:], x_mid_ref)
    rows, width = x_mid_ref.shape
    length = h_ref.shape[0]
    own = pl.ds(pl.multiple_of(first_row(rows), rows), rows)

    @pl.when(step == 0)
    def _():
        probs = probs_ref[...]
        chosen = chosen_experts(pack_ref, probs.shape)
        picked = jnp.where(chosen, probs, 0.0)
        total = jnp.sum(picked, -1, keepdims=True)
        gate = picked / total
        extra = back_ref[:, width:].astype(f32)
        dgate = extra + pltpu.roll(extra, LANES - n_experts, 1)
        dgate = jnp.where(chosen, dgate, 0.0)
        shared = jnp.sum(dgate * gate, -1, keepdims=True)
        dprobs = jnp.where(chosen, (dgate - shared) / total, 0.0)
        dlogits = probs * (dprobs - jnp.sum(probs * dprobs, -1, keepdims=True))
        h_two = message_ref[:, :width].astype(f32)
        router_out[...] = lax.dot_general(
            dlogits,
            h_two,
            (((0,), (0,)), ((), ())),
            precision=highest,
            preferred_element_type=f32,
        )
        dh_two = back_ref[:, :width].astype(f32) + exact_dot(
            dlogits, router_rows(pack_ref, n_experts, width)
        )
        dx, dgain = norm_back(x_mid_ref[...], pack_ref[5:6, :width], dh_two)
        gain_out[...] = dgain
        dx_mid = dx + dy_ref[...].astype(f32)
        dx_mid_out[...] = dx_mid
        da_ref[...] = dx_mid.astype(bf16)
        dh_all_ref[...] = jnp.zeros_like(dh_all_ref)
        dh_mine_ref[...] = jnp.zeros_like(dh_mine_ref)
        ddist_out[...] = jnp.zeros_like(ddist_out)
        h_turned_ref[...] = h_ref[...].T
        o_turned_ref[...] = o_ref[...].T

    da = da_ref[...]
    do = dot_t(da, wo_ref[...]).astype(bf16)
    block = LANES
    first_half = lax.broadcasted_iota(jnp.int32, (block, LANES), 1) < head_dim
    zero = jnp.zeros((), bf16)
    k_low = k_ref[...]
    v_low = v_ref[...]
    dk = None
    dv = None
    for head in range(2):
        dbias_ref[head] = jnp.zeros_like(dbias_ref[head])
    for b in range(rows // block):
        here = slice(b * block, (b + 1) * block)
        offset = pl.multiple_of(length - LANES - block * b - first_row(rows), LANES)
        q_heads = by_head(q_ref[here, :], first_half)
        do_heads = by_head(do[here], first_half)
        probs_low = p_ref[:, here, :]
        probs = probs_low.astype(f32)
        dprobs = dot_t(do_heads, v_low).reshape(2, block, length)
        weighted = probs * dprobs
        ds = weighted - probs * jnp.sum(weighted, -1, keepdims=True)
        dbias_ref[:, :, pl.ds(offset, length)] += ds
        ds_low = ds.astype(bf16).reshape(2 * block, length)
        probs_low = probs_low.reshape(2 * block, length)
        dq_heads = dot(ds_low, k_low)
        dk_part = t_dot(ds_low, q_heads)
        dv_part = t_dot(probs_low, do_heads)
        dk = dk_part if dk is None else dk + dk_part
        dv = dv_part if dv is None else dv + dv_part
        dq_ref[here, :] = (of_head(dq_heads, first_half) * (head_dim**-0.5)).astype(bf16)
    for head in range(2):
        ddist_out[pl.ds(2 * step + head, 1), :] = gather_diagonals(dbias_ref[head])
    dq = dq_ref[...]
    dkv = jnp.concatenate([dk, dv], 1).astype(bf16)
    da_columns = da_ref[:, pl.ds(pl.multiple_of(step * LANES, LANES), LANES)]
    if background:
        background.collect_before(step, refs[7:])
    mine = pl.ds(pl.multiple_of(first_row(rows), rows), rows)
    grads_kv = dot(h_turned_ref[...], dkv).astype(bf16)
    grads = [
        dot(h_turned_ref[:, mine], dq).astype(bf16),
        grads_kv[:, :LANES],
        grads_kv[:, LANES:],
        dot(o_turned_ref[...], da_columns).astype(bf16),
    ]
    if background:
        background.give(step, grads, refs[7:], behind_out[3])
    else:
        for target, grad in zip(grad_outs, grads):
            target[...] = grad
    dh_all_ref[...] += dot_t(dkv, jnp.concatenate([wk_ref[...], wv_ref[...]], 1))
    dh_mine_ref[...] += dot_t(dq, wq_ref[...])

    @pl.when(step == pl.num_programs(0) - 1)
    def _():
        other = pl.ds(pl.multiple_of(length - rows - first_row(rows), rows), rows)
        dh_own_out[...] = dh_mine_ref[...] + dh_all_ref[own, :]
        dh_other_out[...] = dh_all_ref[other, :].astype(bf16)
        for start in range(0, length, rows):
            here = slice(start, start + rows)
            values = x_ref[here, :].astype(f32)
            part = jnp.sum(dh_all_ref[here, :] * (values * inverse_rms(values)), 0, keepdims=True)
            gain_one_out[...] = part if start == 0 else gain_one_out[...] + part
        values = x_ref[own, :].astype(f32)
        scaled = values * inverse_rms(values)
        gain_one_out[...] += jnp.sum(dh_mine_ref[...] * scaled, 0, keepdims=True)

    if background:
        background.run(step, False, behind_in, behind_out, refs[7:], x_mid_ref)


def attention_backward(
    back,
    dy,
    x_mid,
    message,
    probs,
    pack,
    h_all,
    weights,
    q,
    k,
    v,
    o,
    p,
    x_all,
    n_experts,
    head_dim,
    background=None,
    behind=(),
):
    n_rows, width = x_mid.shape
    length = h_all.shape[0]
    pairs = width // LANES
    span = pack.shape[1]
    more_shapes, more_scratch, params = [], [], {}
    n_grads = 0 if background else 4
    if background:
        more_shapes = background.out_shape(*behind)
        more_scratch = background.scratch(*behind)
        params = {"collective_id": 4, "has_side_effects": True}
    anywhere = pl.BlockSpec(memory_space=pl.ANY)
    whole = lambda shape: pl.BlockSpec(shape, lambda p, *_: (0,) * len(shape))
    columns = lambda rows: pl.BlockSpec((rows, LANES), lambda p, *_: (0, p))
    matrix = lambda i: pl.BlockSpec((None, width, LANES), lambda p, *_: (i, 0, p))
    return pl.pallas_call(
        functools.partial(backward_kernel, background, n_experts, head_dim),
        out_shape=[jax.ShapeDtypeStruct((width, width), bf16)] * n_grads
        + [
            jax.ShapeDtypeStruct((n_rows, width), f32),
            jax.ShapeDtypeStruct((n_rows, width), bf16),
            jax.ShapeDtypeStruct((n_rows, width), f32),
            jax.ShapeDtypeStruct((1, width), f32),
            jax.ShapeDtypeStruct((LANES, width), f32),
            jax.ShapeDtypeStruct((16, span), f32),
            jax.ShapeDtypeStruct((1, width), f32),
        ]
        + more_shapes,
        grid_spec=pltpu.PrefetchScalarGridSpec(
            num_scalar_prefetch=0,
            grid=(pairs,),
            in_specs=[
                whole((n_rows, width + LANES)),
                whole((n_rows, width)),
                whole((n_rows, width)),
                whole((n_rows, width + LANES)),
                whole((n_rows, LANES)),
                whole(pack.shape),
                whole((length, width)),
                matrix(0),
                matrix(1),
                matrix(2),
                pl.BlockSpec((None, LANES, width), lambda p, *_: (3, p, 0)),
                columns(n_rows),
                columns(length),
                columns(length),
                whole((n_rows, width)),
                pl.BlockSpec((None, 2, n_rows, length), lambda p, *_: (p, 0, 0, 0)),
                whole((length, width)),
            ]
            + [anywhere] * len(behind),
            out_specs=[columns(width)] * n_grads
            + [
                whole((n_rows, width)),
                whole((n_rows, width)),
                whole((n_rows, width)),
                whole((1, width)),
                whole((LANES, width)),
                whole((16, span)),
                whole((1, width)),
            ]
            + (background.out_specs(more_shapes) if background else []),
            scratch_shapes=[
                pltpu.VMEM((n_rows, width), bf16),
                pltpu.VMEM((length, width), f32),
                pltpu.VMEM((n_rows, width), f32),
                pltpu.VMEM((2, LANES, span), f32),
                pltpu.VMEM((n_rows, LANES), bf16),
                pltpu.VMEM((width, length), bf16),
                pltpu.VMEM((width, n_rows), bf16),
            ]
            + more_scratch,
        ),
        compiler_params=pltpu.CompilerParams(vmem_limit_bytes=VMEM_LIMIT, **params),
        cost_estimate=pl.CostEstimate(
            flops=40_000_000_000, transcendentals=0, bytes_accessed=30_000_000
        ),
        name="attention_backward",
    )(
        back,
        dy,
        x_mid,
        message,
        probs,
        pack,
        h_all,
        weights,
        weights,
        weights,
        weights,
        q,
        k,
        v,
        o,
        p,
        x_all,
        *behind,
    )


def finish_kernel(
    n_fsdp,
    n_experts,
    n_heads,
    sum_in,
    sum_out,
    dh_other,
    line_ref,
    last_ref,
    dh_own_ref,
    dx_mid_ref,
    tokens_ref,
    pack_ref,
    dgain_one_ref,
    dgain_two_ref,
    drouter_ref,
    ddist_ref,
    attn_out,
    grad_in,
    grad_out,
    tokens_out,
    small_out,
    line_land,
    last_given,
    last_added,
    last_land,
    last_line,
    last_line_land,
    attn_held,
    dh_land,
    small_plane,
    small_line,
    in_held,
    out_held,
    send,
    recv,
    local,
):
    me = Place(n_fsdp)
    rep, line, seq, core, row = me.rep, me.line, me.seq, me.core, me.row
    width = tokens_ref.shape[1]
    mate, across, beside, corner = me.mate(), me.chip(1, 0), me.chip(0, 1), me.chip(1, 1)
    far_row = (row + 1) % 2
    far_rep = far_row * 2 + core
    part_out = sum_out.shape[0]
    columns = lambda z, x: pl.ds(pl.multiple_of((z * 2 + x) * part_out, LANES), part_out)
    here = rep * 2 + seq
    peers = [mate, across, beside, corner]
    peers += [me.chip(1, 0, 1 - core), me.chip(0, 1, 1 - core), me.chip(1, 1, 1 - core)]
    shifts = (1, -1, 2)
    plan = {
        "dh": (dh_other, dh_land, beside),
        "out_c": (sum_out, grad_out.at[rep], mate),
        "out_y": (sum_out, grad_out.at[rep], across),
        "out_f": (grad_out.at[far_rep], grad_out.at[far_rep], mate),
        "attn_c": (attn_held, attn_out.at[rep], mate),
        "attn_y": (attn_held, attn_out.at[rep], across),
        "attn_f": (attn_out.at[far_rep], attn_out.at[far_rep], mate),
        "in_c": (grad_in.at[rep], grad_in.at[rep], mate),
        "in_y": (grad_in.at[rep], grad_in.at[rep], across),
        "in_f": (grad_in.at[far_rep], grad_in.at[far_rep], mate),
    }
    for i, shift in enumerate(shifts):
        target = (line + shift) % n_fsdp
        plan["line", i] = (line_ref.at[target], line_land.at[i], me.along(shift))
        plan["last_z", i] = (last_line.at[target], last_line_land.at[i], me.along(shift))
        plan["small_z", i] = (small_line.at[line], small_line.at[line], me.along(shift))
    for z in range(n_fsdp):
        plan["in_x", z] = (
            sum_in.at[1 - seq, :, pl.ds(z * part_out, part_out)],
            grad_in.at[rep, :, columns(z, seq)],
            beside,
        )
    for i, peer in enumerate(peers):
        plan["small", i] = (small_plane.at[here], small_plane.at[here], peer)
    for i in (0, 1):
        plan["last_c", i] = (last_ref.at[2 * i + 1 - core], last_given.at[i], mate)
    chips = ((row, 1 - seq, beside), (far_row, seq, across), (far_row, 1 - seq, corner))
    for i, (to_row, to_column, chip) in enumerate(chips):
        plan["last", i] = (last_added.at[to_row, :, to_column], last_land.at[i], chip)
    copies = Planned(plan, send, recv)
    meet(peers + [me.along(shift) for shift in shifts])
    for i in (0, 1):
        copies["last_c", i].start()
    for i in range(3):
        copies["line", i].start()
    for z in range(n_fsdp):
        copies["in_x", z].start()
    copies["out_y"].start()
    copies["dh"].start()
    copies["out_c"].start()
    own_in = pltpu.make_async_copy(sum_in.at[seq], in_held, local.at[2])
    own_in.start()
    own_out = Bounce(sum_out, out_held, grad_out.at[rep], local.at[pl.ds(8, 2)])
    own_out.start()
    own_in.wait()
    kept = []
    for z in range(n_fsdp):
        source = in_held.at[:, pl.ds(z * part_out, part_out)]
        target = grad_in.at[rep, :, columns(z, seq)]
        kept.append(pltpu.make_async_copy(source, target, local.at[4 + z]))
        kept[-1].start()
    own_out.turn()
    for i in (0, 1):
        copies["last_c", i].wait_recv()
        total = last_ref[2 * i + core].astype(f32) + last_given[i].astype(f32)
        last_added[i] = total.astype(bf16)
    for i in range(3):
        copies["last", i].start()
    table = exact_dot_t(ddist_ref[...], bucket_match(pack_ref))
    small = small_plane.at[here]
    small[...] = jnp.zeros_like(small_out)
    small[0:1, :] = dgain_one_ref[...]
    small[1:2, :] = dgain_two_ref[...]
    small[2 : 2 + n_experts, :] = drouter_ref[:n_experts, :]
    for head in range(n_heads):
        at = head % 6 * LANES
        small[6 + head // 6, at : at + LANES] = table[head]
    for i in range(len(peers)):
        copies["small", i].start()
    for copy in kept:
        copy.wait()
    for z in range(n_fsdp):
        copies["in_x", z].wait_recv()
    copies["in_y"].start()
    copies["in_c"].start()
    total = last_added[row, :, seq].astype(f32)
    for i in range(3):
        copies["last", i].wait_recv()
        total = total + last_land[i].astype(f32)
    last_line[...] = total.astype(bf16)
    for i in range(3):
        copies["last_z", i].start()
    for i in range(len(peers)):
        copies["small", i].wait_recv()
    total = small_plane[0]
    for i in range(1, 8):
        total = total + small_plane[i]
    small_line[line] = total
    for i in range(3):
        copies["small_z", i].start()
    total = line_ref[line].astype(f32)
    for i in range(3):
        copies["line", i].wait_recv()
        total = total + line_land[i].astype(f32)
    early = total.shape[1]
    attn_held[:, :early] = total.astype(bf16)
    copies["out_y"].wait_recv()
    copies["out_f"].start()
    total = last_line[line].astype(f32)
    for i in range(3):
        copies["last_z", i].wait_recv()
        total = total + last_line_land[i].astype(f32)
    attn_held[:, early:] = total.astype(bf16)
    copies["attn_y"].start()
    copies["attn_c"].start()
    own_attn = pltpu.make_async_copy(attn_held, attn_out.at[rep], local.at[3])
    own_attn.start()
    copies["dh"].wait_recv()
    dh_one = dh_own_ref[...] + dh_land[...].astype(f32)
    dx, _ = norm_back(tokens_ref[...].astype(f32), pack_ref[4:5, :width], dh_one)
    tokens_out[...] = (dx_mid_ref[...] + dx).astype(bf16)
    for i in range(3):
        copies["small_z", i].wait_recv()
    total = small_line[0]
    for i in range(1, n_fsdp):
        total = total + small_line[i]
    small_out[...] = total
    copies["in_y"].wait_recv()
    copies["in_f"].start()
    copies["attn_y"].wait_recv()
    copies["attn_f"].start()
    own_attn.wait()
    own_out.wait()
    for name in ("attn_c", "attn_f", "in_c", "in_f", "out_c", "out_f"):
        copies[name].wait_recv()
    for name in plan:
        copies[name].wait_send()


def finish(
    plane_sum,
    last_grads,
    sum_in,
    sum_out,
    dh_other,
    dh_own,
    dx_mid,
    tokens,
    pack,
    dgain_one,
    dgain_two,
    drouter,
    ddist,
    n_fsdp,
    n_experts,
    n_heads,
    hidden,
):
    n_rows, width = tokens.shape
    part_attn = plane_sum.shape[1]
    split = last_grads.shape[1:]
    part_in = sum_in.shape[1]
    anywhere = pl.BlockSpec(memory_space=pl.ANY)
    inside = pl.BlockSpec(memory_space=pltpu.VMEM)
    dma = lambda n: pltpu.SemaphoreType.DMA((n,))
    return pl.pallas_call(
        functools.partial(finish_kernel, n_fsdp, n_experts, n_heads),
        out_shape=[
            jax.ShapeDtypeStruct((4, part_attn, width), bf16),
            jax.ShapeDtypeStruct((n_experts, part_in, hidden), bf16),
            jax.ShapeDtypeStruct((n_experts,) + sum_out.shape, bf16),
            jax.ShapeDtypeStruct((n_rows, width), bf16),
            jax.ShapeDtypeStruct((8, width), f32),
        ],
        in_specs=[anywhere] * 3 + [inside] * 10,
        out_specs=[anywhere] * 3 + [inside] * 2,
        scratch_shapes=[
            pltpu.VMEM((3,) + plane_sum.shape[1:], bf16),
            pltpu.VMEM((2,) + split, bf16),
            pltpu.VMEM((2,) + split, bf16),
            pltpu.VMEM((3, n_fsdp) + split[2:], bf16),
            pltpu.VMEM((n_fsdp,) + split[2:], bf16),
            pltpu.VMEM((3,) + split[2:], bf16),
            pltpu.VMEM((part_attn, width), bf16),
            pltpu.VMEM((n_rows, width), bf16),
            pltpu.VMEM((8, 8, width), f32),
            pltpu.VMEM((n_fsdp, 8, width), f32),
            pltpu.VMEM(sum_in.shape[1:], bf16),
            pltpu.VMEM(sum_out.shape, bf16),
            dma(40),
            dma(40),
            dma(12),
        ],
        compiler_params=pltpu.CompilerParams(
            vmem_limit_bytes=VMEM_LIMIT, collective_id=5, has_side_effects=True
        ),
        name="finish_gradients",
    )(
        sum_in,
        sum_out,
        dh_other,
        plane_sum,
        last_grads,
        dh_own,
        dx_mid,
        tokens,
        pack,
        dgain_one,
        dgain_two,
        drouter,
        ddist,
    )


def widen_kernel(
    n_experts, n_heads, n_buckets, attn, grad_in, grad_out, small, q, k, v, o, win, wout, *rest
):
    step = pl.program_id(0)
    for i, target in enumerate((q, k, v, o)):

        @pl.when(step == i)
        def _():
            target[...] = attn[...].astype(f32)

    win[...] = grad_in[...].astype(f32)
    wout[...] = grad_out[...].astype(f32)
    gain_one, gain_two, table, router = rest

    @pl.when(step == 0)
    def _():
        gain_one[...] = small[0, :]
        gain_two[...] = small[1, :]
        router[...] = small[2 : 2 + n_experts, :]
        for head in range(n_heads):
            at = head % 6 * LANES
            table[head : head + 1, :] = small[
                6 + head // 6 : 7 + head // 6, at : at + n_buckets
            ]


def widen(attn, grad_in, grad_out, small, n_heads, n_buckets):
    n_experts = grad_in.shape[0]
    width = small.shape[1]
    own = lambda a: pl.BlockSpec((None,) + a.shape[1:], lambda i: (i, 0, 0))
    whole = lambda shape: pl.BlockSpec(shape, lambda i: (0,) * len(shape))
    small_shapes = [(width,), (width,), (n_heads, n_buckets), (n_experts, width)]
    wide = [attn.shape[1:]] * 4
    return pl.pallas_call(
        functools.partial(widen_kernel, n_experts, n_heads, n_buckets),
        out_shape=[jax.ShapeDtypeStruct(shape, f32) for shape in wide]
        + [jax.ShapeDtypeStruct(a.shape, f32) for a in (grad_in, grad_out)]
        + [jax.ShapeDtypeStruct(shape, f32) for shape in small_shapes],
        grid=(n_experts,),
        in_specs=[own(attn), own(grad_in), own(grad_out), whole(small.shape)],
        out_specs=[whole(shape) for shape in wide]
        + [own(grad_in), own(grad_out)]
        + [whole(shape) for shape in small_shapes],
        compiler_params=pltpu.CompilerParams(vmem_limit_bytes=VMEM_LIMIT),
        name="widen",
    )(attn, grad_in, grad_out, small)


def per_device(
    tokens,
    piece_starts,
    routes,
    buckets,
    attn_q,
    attn_k,
    attn_v,
    attn_o,
    expert_in,
    expert_out,
    gain_attn,
    gain_ffn,
    rel_table,
    router,
    cotangent,
):
    n_rep, n_fsdp, n_seq = (lax.axis_size(a) for a in ("rep", "fsdp", "seq"))
    rep = lax.axis_index("rep")
    seq = lax.axis_index("seq")
    plane = ("rep", "seq")
    n_rows, width = tokens.shape
    n_buckets, n_heads = rel_table.shape
    head_dim = width // n_heads
    n_experts, part_in, hidden = expert_in.shape
    part_out = expert_out.shape[1]
    part_attn = attn_q.shape[0]
    length = n_rows * n_seq
    assert n_experts == n_rep == 4 and n_seq == 2 and 2 * head_dim == LANES
    pairs = n_heads // 2

    place = piece_starts[0]
    near = n_fsdp == 4 and part_attn % 16 == 0
    pick = lambda array: lax.dynamic_index_in_dim(array, rep, 0, keepdims=False)
    span = -(-buckets.shape[0] // LANES) * LANES
    if near:
        weights, x_all, w_in, pack = gather(
            (attn_q, attn_k, attn_v, attn_o),
            tokens,
            expert_in,
            part_out,
            n_fsdp,
            (router.T, gain_attn, gain_ffn, buckets, rel_table.T, routes.T),
            span,
        )
    else:
        attn_own = pick(jnp.stack([attn_q, attn_k, attn_v, attn_o]))
        attn_line = lax.all_gather(attn_own, "fsdp", axis=0, tiled=False)
        attn_all = lax.all_gather(attn_line, plane, axis=0, tiled=False)
        attn_all = attn_all.reshape(n_rep, n_seq, n_fsdp, part_attn, width)
        weights = attn_all.transpose(0, 2, 1, 3, 4).reshape(n_rep, width, width)
        x_all = lax.all_gather(tokens, "seq", axis=0, tiled=True)
        in_own = pick(expert_in).reshape(part_in, n_fsdp, n_seq, part_out)
        in_own = in_own.transpose(2, 0, 1, 3).reshape(n_seq, part_in, n_fsdp * part_out)
        in_pair = lax.all_to_all(in_own, "seq", split_axis=0, concat_axis=0, tiled=True)
        in_pair = in_pair.reshape(n_seq * part_in, n_fsdp * part_out)
        w_in = lax.all_gather(in_pair, "fsdp", axis=0, tiled=True)
        w_out = lax.all_gather(pick(expert_out), "fsdp", axis=0, tiled=True)
        dy_all = lax.all_gather(cotangent, plane, axis=0, tiled=True)
        pack = pack_small(router, gain_attn, gain_ffn, buckets, rel_table, routes, span)

    q, k, v, o, p, x_mid, message, probs, h_all, *gathered = attention_forward(
        place,
        x_all,
        weights,
        pack,
        n_rows,
        n_experts,
        head_dim,
        Background(n_fsdp) if near else None,
        (cotangent, w_in) if near else (),
    )
    behind = ()
    if near:
        dy_all, w_in = gathered
        w_in = w_in.reshape(width, n_fsdp * part_out)
        message_all, act, slope, dw_out, w_out = experts_up(
            message, dy_all, w_in, expert_out, n_experts, n_fsdp
        )
        back, out_half, dw_in, sum_out = experts_down(
            message_all,
            dy_all,
            act,
            slope,
            w_in,
            w_out.reshape(n_fsdp * part_out, width),
            dw_out.reshape(n_fsdp, part_out, width),
            n_experts,
            n_fsdp,
        )
        behind = (out_half, dw_in.reshape(n_fsdp, n_seq * part_in, n_fsdp * part_out))
    else:
        message_all = lax.all_gather(message, plane, axis=0, tiled=True)
        out_part, back_part, dw_in, dw_out = experts(
            rep[None].astype(jnp.int32), message_all, dy_all, w_in, w_out, n_experts, n_rows
        )
        back = lax.psum_scatter(back_part, plane, scatter_dimension=0, tiled=True)
        out_sum = lax.psum_scatter(out_part, plane, scatter_dimension=0, tiled=True)
        out_rows = (x_mid + out_sum.astype(f32)).astype(bf16)

    grads = attention_backward(
        back,
        cotangent,
        x_mid,
        message,
        probs,
        pack,
        h_all,
        weights,
        q,
        k,
        v,
        o,
        p,
        x_all,
        n_experts,
        head_dim,
        BackgroundBack(n_fsdp) if near else None,
        behind,
    )
    if near:
        dh_own, dh_other, dx_mid, dgain_two, drouter, ddist, dgain_one = grads[:7]
        out_rows, sum_in, plane_sum, last_grads = grads[7:]
        attn_sum, grad_in, grad_out, grad_tokens, small = finish(
            plane_sum,
            last_grads,
            sum_in.reshape(n_seq, part_in, n_fsdp * part_out),
            sum_out,
            dh_other,
            dh_own,
            dx_mid,
            tokens,
            pack,
            dgain_one,
            dgain_two,
            drouter,
            ddist,
            n_fsdp,
            n_experts,
            n_heads,
            hidden,
        )
        *wide, grad_one, grad_two, grad_table, grad_router = widen(
            attn_sum, grad_in, grad_out, small, n_heads, n_buckets
        )
        return (
            out_rows,
            grad_tokens,
            *wide,
            grad_one,
            grad_two,
            grad_table.T,
            grad_router.T,
        )
    dwq, dwk, dwv, dwo, dh_own, dh_other, dx_mid, dgain_two, drouter, ddist, dgain_one = grads
    sum_out = lax.psum_scatter(dw_out, "fsdp", scatter_dimension=0, tiled=True)
    sum_in = lax.psum_scatter(dw_in, "fsdp", scatter_dimension=0, tiled=True)
    sum_in = sum_in.reshape(n_seq, part_in, n_fsdp * part_out)
    sum_in = lax.all_to_all(sum_in, "seq", split_axis=0, concat_axis=0, tiled=True)
    sum_in = sum_in.reshape(n_seq, part_in, n_fsdp, part_out).transpose(1, 2, 0, 3)
    sum_in = sum_in.reshape(part_in, hidden)
    grad_out = lax.all_gather(sum_out, "rep", axis=0, tiled=False)
    grad_in = lax.all_gather(sum_in, "rep", axis=0, tiled=False)
    swap = [(0, 1), (1, 0)]
    dh_one = dh_own + lax.ppermute(dh_other, "seq", swap).astype(f32)
    dx, _ = norm_back(tokens.astype(f32), gain_attn[None, :], dh_one)
    grad_tokens = (dx_mid + dx).astype(bf16)
    attn_grads = jnp.stack([dwq, dwk, dwv, dwo])
    attn_grads = attn_grads.reshape(n_rep, n_fsdp, n_seq, part_attn, width)
    attn_grads = attn_grads.transpose(0, 2, 1, 3, 4)
    attn_grads = attn_grads.reshape(n_rep * n_seq * n_fsdp * part_attn, width)
    attn_sum = lax.psum_scatter(attn_grads, plane, scatter_dimension=0, tiled=True)
    attn_sum = lax.psum_scatter(attn_sum, "fsdp", scatter_dimension=0, tiled=True)
    attn_sum = lax.all_gather(attn_sum, "rep", axis=0, tiled=False)
    ddist = ddist[:n_heads, : buckets.shape[0]]
    match = (buckets[:, None] == jnp.arange(n_buckets)[None, :]).astype(f32)
    table = lax.dot_general(
        match,
        ddist,
        (((0,), (1,)), ((), ())),
        precision=highest,
        preferred_element_type=f32,
    )
    grad_one, grad_two, grad_table, grad_router = lax.psum(
        (dgain_one[0], dgain_two[0], table, drouter[:n_experts].T), ("rep", "fsdp", "seq")
    )
    attn_sum = attn_sum.astype(f32)
    return (
        out_rows,
        grad_tokens,
        attn_sum[0],
        attn_sum[1],
        attn_sum[2],
        attn_sum[3],
        grad_in.astype(f32),
        grad_out.astype(f32),
        grad_one,
        grad_two,
        grad_table,
        grad_router,
    )


def solution(mesh):
    rows = P(("rep", "fsdp", "seq"), None)
    owned = P(("fsdp", "seq"), None)
    expert = P(None, ("fsdp", "seq"), None)
    in_specs = (
        rows,
        P(("rep", "fsdp"), None),
        rows,
        P(),
        owned,
        owned,
        owned,
        owned,
        expert,
        expert,
        P(),
        P(),
        P(),
        P(),
        rows,
    )
    out_specs = (
        rows,
        rows,
        owned,
        owned,
        owned,
        owned,
        expert,
        expert,
        P(),
        P(),
        P(),
        P(),
    )
    return jax.shard_map(
        per_device, mesh=mesh, in_specs=in_specs, out_specs=out_specs, check_vma=False
    )
```

```python
import functools

import jax
import jax.numpy as jnp
from jax import lax
from jax.experimental import pallas as pl
from jax.experimental.pallas import tpu as pltpu
from jax.sharding import PartitionSpec as P

PIECE = 256
LANES = 128
epsilon = 1e-06
masked_out = -1e30
highest = lax.Precision.HIGHEST
f32 = jnp.float32
bf16 = jnp.bfloat16
VMEM_LIMIT = 58 * 1024 * 1024


def dot(a, b):
    return jnp.dot(a, b, preferred_element_type=f32)


def dot_t(a, b):
    return lax.dot_general(a, b, (((1,), (1,)), ((), ())), preferred_element_type=f32)


def t_dot(a, b):
    return lax.dot_general(a, b, (((0,), (0,)), ((), ())), preferred_element_type=f32)


def exact_dot(a, b):
    return jnp.dot(a, b, precision=highest, preferred_element_type=f32)


def exact_dot_t(a, b):
    return lax.dot_general(
        a, b, (((1,), (1,)), ((), ())), precision=highest, preferred_element_type=f32
    )


def inverse_rms(values):
    return lax.rsqrt(jnp.mean(values * values, -1, keepdims=True) + epsilon)


def norm_back(values, gain, grad):
    scale = inverse_rms(values)
    scaled = values * scale
    grad_gain = jnp.sum(grad * scaled, 0, keepdims=True)
    weighted = gain * grad
    grad_values = scale * weighted - (
        values * (scale * scale * scale) * jnp.mean(weighted * values, -1, keepdims=True)
    )
    return grad_values, grad_gain


def first_row(rows):
    return lax.axis_index("seq") * rows


def make_mask(place_ref, mask_ref):
    shape = mask_ref.shape
    pos_q = first_row(shape[0]) + lax.broadcasted_iota(jnp.int32, shape, 0)
    pos_k = lax.broadcasted_iota(jnp.int32, shape, 1)
    allowed = pos_k <= pos_q
    for piece in range(2):
        start = place_ref[piece]
        in_q = (pos_q >= start) & (pos_q < start + PIECE)
        in_k = (pos_k >= start) & (pos_k < start + PIECE)
        allowed = allowed | (in_q & in_k)
    mask_ref[...] = jnp.where(allowed, 0.0, masked_out)


def spread(row, block, width):
    return pltpu.roll(
        jnp.broadcast_to(row, (block, width)), width - (block - 1), 1, stride=1, stride_axis=0
    )


def by_head(values, first_half):
    zero = jnp.zeros((), values.dtype)
    return jnp.concatenate(
        [jnp.where(first_half, values, zero), jnp.where(first_half, zero, values)]
    )


def of_head(stacked, first_half):
    block = stacked.shape[0] // 2
    return jnp.where(first_half, stacked[:block], stacked[block:])


def gather_diagonals(sums):
    rows = sums.shape[0]
    while rows > 1:
        half = rows // 2
        sums = pltpu.roll(sums[:half], half, 1) + sums[half:]
        rows = half
    return sums


def chosen_experts(pack_ref, shape):
    lane = lax.broadcasted_iota(jnp.int32, shape, 1).astype(f32)
    routes = pack_ref[24:32, : shape[0]].T
    return (lane == routes[:, 0:1]) | (lane == routes[:, 1:2])


def pack_small(router, gain_attn, gain_ffn, buckets, rel_table, routes, span):
    def rows(array, count):
        array = array.astype(f32)
        return jnp.pad(array, ((0, count - array.shape[0]), (0, span - array.shape[1])))

    return jnp.concatenate(
        [
            rows(router.T, 4),
            rows(gain_attn[None, :], 1),
            rows(gain_ffn[None, :], 1),
            rows(buckets[None, :], 2),
            rows(rel_table.T, 16),
            rows(routes.T, 8),
        ]
    )


def router_rows(pack_ref, n_experts, width):
    first = pack_ref[0:8, :width]
    row = lax.broadcasted_iota(jnp.int32, first.shape, 0)
    first = jnp.where(row < n_experts, first, 0.0)
    return jnp.concatenate([first, jnp.zeros((LANES - 8, width), f32)])


def bucket_match(pack_ref):
    shape = (LANES, pack_ref.shape[1])
    bucket = lax.broadcasted_iota(jnp.int32, shape, 0).astype(f32)
    return (bucket == pack_ref[6:7, :]).astype(f32)


def distances(pack_ref):
    return exact_dot(pack_ref[8:24, :LANES], bucket_match(pack_ref))


MESH = pl.DeviceIdType.MESH


class Place:
    def __init__(self, n_fsdp):
        self.rep = lax.axis_index("rep")
        self.line = lax.axis_index("fsdp")
        self.seq = lax.axis_index("seq")
        self.n_fsdp = n_fsdp
        self.row = self.rep // 2
        self.core = self.rep % 2

    def mate(self):
        return (self.row * 2 + 1 - self.core, self.line, self.seq)

    def chip(self, rows, columns, core=None):
        core = self.core if core is None else core
        row = (self.row + rows) % 2
        return (row * 2 + core, self.line, (self.seq + columns) % 2)

    def along(self, steps):
        return (self.rep, (self.line + steps) % self.n_fsdp, self.seq)


def meet(partners):
    barrier = pltpu.get_barrier_semaphore()
    for partner in partners:
        pl.semaphore_signal(barrier, inc=1, device_id=partner, device_id_type=MESH)
    pl.semaphore_wait(barrier, len(partners))


class Wires:
    def __init__(self, send, recv):
        self.send, self.recv = send, recv
        self.names = {}

    def copy(self, name, source, target, device):
        index = self.names.setdefault(name, len(self.names))
        return pltpu.make_async_remote_copy(
            src_ref=source,
            dst_ref=target,
            send_sem=self.send.at[index],
            recv_sem=self.recv.at[index],
            device_id=device,
            device_id_type=MESH,
        )


class Planned:
    def __init__(self, plan, send, recv):
        self.plan, self.send, self.recv = plan, send, recv
        self.order = list(plan)

    def __getitem__(self, name):
        source, target, device = self.plan[name]
        index = self.order.index(name)
        return pltpu.make_async_remote_copy(
            src_ref=source,
            dst_ref=target,
            send_sem=self.send.at[index],
            recv_sem=self.recv.at[index],
            device_id=device,
            device_id_type=MESH,
        )


def gather_kernel(
    n_fsdp,
    part_out,
    attn_q,
    attn_k,
    attn_v,
    attn_o,
    tokens,
    expert_in,
    expert_out,
    router,
    gain_attn,
    gain_ffn,
    buckets,
    rel_table,
    routes,
    weights,
    x_all,
    w_in,
    w_out,
    pack,
    attn_held,
    tokens_held,
    in_held,
    send,
    recv,
    local,
):
    me = Place(n_fsdp)
    rep, line, seq = me.rep, me.line, me.seq
    far_row = (me.row + 1) % 2 * 2 + me.core
    mate, across, beside = me.mate(), me.chip(1, 0), me.chip(0, 1)
    part_in = expert_in.shape[1]
    wires = Wires(send, recv)
    meet([mate, across, beside, me.along(1), me.along(-1), me.along(2)])
    started = []

    def start(copy):
        copy.start()
        started.append(copy)
        return copy

    for i, matrix in enumerate((attn_q, attn_k, attn_v, attn_o)):

        @pl.when(rep == i)
        def _():
            own = pltpu.make_async_copy(matrix, attn_held, local.at[0])
            own.start()
            own.wait()

    mine = lambda z, r=rep, x=seq: weights.at[r, z, x]
    shifts = (0, 1, -1, 2)
    at = {0: line}
    z_copies = {}
    for shift in shifts[1:]:
        at[shift] = (line - shift) % n_fsdp
        z_copies[shift] = start(
            wires.copy(("z", shift), attn_held, mine(line), me.along(shift))
        )
    x_copies, y_copies, c_copies, far_copies = {}, {}, [], {}

    def spread_out(shift):
        z = at[shift]
        source = mine(z) if shift else attn_held
        x_copies[shift] = start(wires.copy(("x", shift), source, mine(z), beside))
        y_copies[shift] = start(wires.copy(("y", shift), source, mine(z), across))
        c_copies.append(start(wires.copy(("c", shift), source, mine(z), mate)))

    spread_out(0)
    columns = lambda z, x: pl.ds(pl.multiple_of((z * 2 + x) * part_out, LANES), part_out)
    rows = lambda x: pl.ds(pl.multiple_of(x * part_in, part_in), part_in)
    in_x, in_own = [], []
    for z in range(n_fsdp):
        here = pl.ds(z * part_out, part_out)
        target = w_in.at[line, rows(seq), here]
        in_x.append(
            start(wires.copy(("in", z), expert_in.at[rep, :, columns(z, 1 - seq)], target, beside))
        )
        copy = pltpu.make_async_copy(
            expert_in.at[rep, :, columns(z, seq)], in_held.at[:, here], local.at[1 + z]
        )
        copy.start()
        in_own.append(copy)
    own_attn = pltpu.make_async_copy(attn_held, mine(line), local.at[0])
    own_attn.start()
    x_own = Bounce(tokens, tokens_held, x_all.at[seq], local.at[pl.ds(n_fsdp + 1, 2)])
    x_own.start()
    for copy in in_own:
        copy.wait()
    own_in = pltpu.make_async_copy(in_held, w_in.at[line, rows(seq)], local.at[n_fsdp + 3])
    own_in.start()
    x_own.turn()
    pack[...] = jnp.zeros_like(pack)
    pack[0 : router.shape[0], : router.shape[1]] = router[...]
    pack[4, : gain_attn.shape[0]] = gain_attn[...]
    pack[5, : gain_ffn.shape[0]] = gain_ffn[...]
    pack[6, : buckets.shape[0]] = buckets[...].astype(f32)
    pack[8 : 8 + rel_table.shape[0], : rel_table.shape[1]] = rel_table[...]
    pack[24:26, : routes.shape[1]] = routes[...].astype(f32)
    for shift in shifts[1:]:
        z_copies[shift].wait_recv()
        spread_out(shift)
    for copy in in_x:
        copy.wait_recv()
    own_in.wait()
    in_copies = []
    for i, shift in enumerate((1, -1)):
        half = w_in.at[line, pl.ds(i * part_in, part_in)]
        in_copies.append(start(wires.copy(("line", shift), half, half, me.along(shift))))
    plan = line_plan(me, expert_out.at[rep], w_out)
    in_copies.append(start(wires.copy("out", *plan["first", 1])))
    token_copy = start(wires.copy("tokens", tokens, x_all.at[seq], beside))
    for shift in shifts:
        z = at[shift]
        x_copies[shift].wait_recv()
        near = mine(z, rep, 1 - seq)
        far_copies[shift] = start(wires.copy(("far", shift), near, near, across))
        c_copies.append(start(wires.copy(("cx", shift), near, near, mate)))
    for shift in shifts:
        z = at[shift]
        y_copies[shift].wait_recv()
        there = mine(z, far_row, seq)
        c_copies.append(start(wires.copy(("cy", shift), there, there, mate)))
    for shift in shifts:
        z = at[shift]
        far_copies[shift].wait_recv()
        there = mine(z, far_row, 1 - seq)
        c_copies.append(start(wires.copy(("cf", shift), there, there, mate)))
    for copy in c_copies + in_copies + [token_copy]:
        copy.wait_recv()
    x_own.wait()
    own_attn.wait()
    for copy in started:
        copy.wait_send()


def gather(attn, tokens, expert_in, expert_out, n_fsdp, small, span):
    part_attn, width = attn[0].shape
    n_rows = tokens.shape[0]
    n_experts, part_in, hidden = expert_in.shape
    part_out = expert_out.shape[1]
    anywhere = pl.BlockSpec(memory_space=pl.ANY)
    inside = pl.BlockSpec(memory_space=pltpu.VMEM)
    weights, x_all, w_in, w_out, pack = pl.pallas_call(
        functools.partial(gather_kernel, n_fsdp, part_out),
        out_shape=[
            jax.ShapeDtypeStruct((4, n_fsdp, 2, part_attn, width), bf16),
            jax.ShapeDtypeStruct((2, n_rows, width), bf16),
            jax.ShapeDtypeStruct((n_fsdp, 2 * part_in, n_fsdp * part_out), bf16),
            jax.ShapeDtypeStruct((n_fsdp,) + expert_out.shape[1:], bf16),
            jax.ShapeDtypeStruct((32, span), f32),
        ],
        in_specs=[anywhere] * 7 + [inside] * 6,
        out_specs=[anywhere] * 4 + [inside],
        scratch_shapes=[
            pltpu.VMEM((part_attn, width), bf16),
            pltpu.VMEM((n_rows, width), bf16),
            pltpu.VMEM((part_in, n_fsdp * part_out), bf16),
            pltpu.SemaphoreType.DMA((48,)),
            pltpu.SemaphoreType.DMA((48,)),
            pltpu.SemaphoreType.DMA((8,)),
        ],
        compiler_params=pltpu.CompilerParams(collective_id=0, has_side_effects=True),
        name="gather_weights",
    )(*attn, tokens, expert_in, expert_out, *small)
    return (
        weights.reshape(4, n_fsdp * 2 * part_attn, width),
        x_all.reshape(2 * n_rows, width),
        w_in,
        w_out,
        pack,
    )


class Bounce:
    def __init__(self, source, held, target, sems):
        self.load = lambda: pltpu.make_async_copy(source, held, sems.at[0])
        self.store = lambda: pltpu.make_async_copy(held, target, sems.at[1])

    def start(self):
        self.load().start()

    def turn(self):
        self.load().wait()
        self.store().start()

    def wait(self):
        self.store().wait()


def line_plan(me, own, pieces):
    rows = pieces.shape[1] // 2
    plan = {}
    for i, shift in enumerate((1, -1)):
        first, rest = pl.ds(i * rows, rows), pl.ds((1 - i) * rows, rows)
        target = pieces.at[me.line]
        piece = pieces.at[(me.line - shift) % me.n_fsdp, first]
        plan["first", shift] = (own.at[first], target.at[first], me.along(shift))
        plan["rest", shift] = (own.at[rest], target.at[rest], me.along(shift))
        plan["relay", shift] = (piece, piece, me.along(shift))
    return plan


class Background:
    n_in, n_out = 2, 2

    def __init__(self, n_fsdp):
        self.n_fsdp = n_fsdp

    def out_shape(self, dy, w_in):
        return [
            jax.ShapeDtypeStruct((8,) + dy.shape, bf16),
            jax.ShapeDtypeStruct(w_in.shape, bf16),
        ]

    def scratch(self, dy, w_in):
        return [
            pltpu.SemaphoreType.DMA((16,)),
            pltpu.SemaphoreType.DMA((16,)),
            pltpu.SemaphoreType.DMA((2,)),
            pltpu.VMEM(dy.shape, bf16),
        ]

    def run(self, step, before, ins, outs, scratch):
        dy, _ = ins
        dy_all, w_in = outs
        send, recv, local, dy_held = scratch
        me = Place(self.n_fsdp)
        half = dy.shape[0] // 2
        first, second = pl.ds(0, half), pl.ds(half, half)
        core = me.core
        own = 6 + core
        mate, across, beside = me.mate(), me.chip(1, 0), me.chip(0, 1)
        slot = dy_all.at
        plan = {
            "x": (dy, slot[core], beside),
            "y": (dy, slot[2 + core], across),
            "c0": (dy, slot[own], mate),
            "c1": (slot[core], slot[core], mate),
            "c2": (slot[2 + core], slot[2 + core], mate),
            "c3": (slot[4 + core], slot[4 + core], mate),
            "xy": (slot[core, first], slot[4 + core, first], across),
            "yx": (slot[2 + core, second], slot[4 + core, second], beside),
        }
        line = line_plan(me, w_in.at[me.line], w_in)
        plan |= {name: line[name] for name in line if name[0] != "first"}
        copies = Planned(plan, send, recv)
        own_dy = Bounce(dy, dy_held, slot[own], local.at[pl.ds(0, 2)])
        if before:

            @pl.when(step == 0)
            def _():
                meet([mate, across, beside, me.along(1), me.along(-1)])
                for name in line:
                    if name[0] != "first":
                        copies[name].start()
                for name in ("x", "y", "c0"):
                    copies[name].start()
                own_dy.start()

            @pl.when(step == 3)
            def _():
                own_dy.turn()
                copies["x"].wait_recv()
                copies["xy"].start()
                copies["c1"].start()
                copies["y"].wait_recv()
                copies["yx"].start()
                copies["c2"].start()

            return

        @pl.when(step == pl.num_programs(0) - 1)
        def _():
            copies["xy"].wait_recv()
            copies["yx"].wait_recv()
            copies["c3"].start()
            for name in plan:
                if name not in ("x", "y", "xy", "yx"):
                    copies[name].wait_recv()
            own_dy.wait()
            for name in plan:
                copies[name].wait_send()


def forward_kernel(
    background,
    n_experts,
    head_dim,
    place_ref,
    x_ref,
    wq_ref,
    wk_ref,
    wv_ref,
    wo_ref,
    pack_ref,
    *refs,
):
    step = pl.program_id(0)
    n_in, n_out = (background.n_in, background.n_out) if background else (0, 0)
    behind_in, refs = refs[:n_in], refs[n_in:]
    q_out, k_out, v_out, o_out, p_out, x_mid_out, message_out, probs_out, h_out = refs[:9]
    behind_out, refs = refs[9 : 9 + n_out], refs[9 + n_out :]
    total_ref, mask_ref, bias_ref, dist_ref = refs[:4]
    if background:
        background.run(step, True, behind_in, behind_out, refs[4:])
    rows = x_mid_out.shape[0]
    length, width = x_ref.shape
    own = pl.ds(pl.multiple_of(first_row(rows), rows), rows)

    @pl.when(step == 0)
    def _():
        values = x_ref[...].astype(f32)
        gain_one = pack_ref[4:5, :width]
        h_out[...] = (values * inverse_rms(values) * gain_one).astype(bf16)
        dist_ref[...] = distances(pack_ref)
        total_ref[...] = jnp.zeros_like(total_ref)
        make_mask(place_ref, mask_ref)

    h_all = h_out[...]
    q_low = dot(h_out[own, :], wq_ref[...]).astype(bf16) * (head_dim**-0.5)
    kv_low = dot(h_all, jnp.concatenate([wk_ref[...], wv_ref[...]], 1)).astype(bf16)
    k_low, v_low = kv_low[:, :LANES], kv_low[:, LANES:]
    q_out[...] = q_low
    k_out[...] = k_low
    v_out[...] = v_low
    block = LANES
    span = pack_ref.shape[1]
    first_half = lax.broadcasted_iota(jnp.int32, (block, LANES), 1) < head_dim
    for head in range(2):
        bias_ref[head] = spread(dist_ref[pl.ds(2 * step + head, 1), :], block, span)
    for b in range(rows // block):
        here = slice(b * block, (b + 1) * block)
        offset = pl.multiple_of(length - LANES - block * b - first_row(rows), LANES)
        scores = dot_t(by_head(q_low[here], first_half), k_low).reshape(2, block, length)
        scores = scores + bias_ref[:, :, pl.ds(offset, length)] + mask_ref[here, :]
        top = jnp.max(scores, -1, keepdims=True)
        exp_scores = jnp.exp(scores - top)
        total = jnp.sum(exp_scores, -1, keepdims=True)
        probs = (exp_scores * (1.0 / total)).astype(bf16)
        p_out[:, here, :] = probs
        heads = dot(probs.reshape(2 * block, length), v_low)
        o_out[here, :] = of_head(heads, first_half).astype(bf16)
    total_ref[...] += dot(o_out[...], wo_ref[...])

    @pl.when(step == pl.num_programs(0) - 1)
    def _():
        x_mid = x_ref[own, :].astype(f32) + total_ref[...]
        x_mid_out[...] = x_mid
        h_two = (x_mid * inverse_rms(x_mid) * pack_ref[5:6, :width]).astype(bf16)
        message_out[:, :width] = h_two
        logits = exact_dot_t(h_two.astype(f32), router_rows(pack_ref, n_experts, width))
        lane = lax.broadcasted_iota(jnp.int32, logits.shape, 1)
        logits = jnp.where(lane < n_experts, logits, masked_out)
        exp_logits = jnp.exp(logits - jnp.max(logits, -1, keepdims=True))
        probs = exp_logits / jnp.sum(exp_logits, -1, keepdims=True)
        probs_out[...] = probs
        chosen = jnp.where(chosen_experts(pack_ref, probs.shape), probs, 0.0)
        gate = chosen / jnp.sum(chosen, -1, keepdims=True)
        high = gate.astype(bf16)
        low = gate - high.astype(f32)
        message_out[:, width:] = (high.astype(f32) + pltpu.roll(low, n_experts, 1)).astype(bf16)

    if background:
        background.run(step, False, behind_in, behind_out, refs[4:])


def attention_forward(
    place,
    x_all,
    weights,
    pack,
    n_rows,
    n_experts,
    head_dim,
    background=None,
    behind=(),
):
    length, width = x_all.shape
    pairs = width // LANES
    span = pack.shape[1]
    whole = lambda shape: pl.BlockSpec(shape, lambda p, *_: (0,) * len(shape))
    columns = lambda rows: pl.BlockSpec((rows, LANES), lambda p, *_: (0, p))
    matrix = lambda i: pl.BlockSpec((None, width, LANES), lambda p, *_: (i, 0, p))
    out_shape = [
        jax.ShapeDtypeStruct((n_rows, width), bf16),
        jax.ShapeDtypeStruct((length, width), bf16),
        jax.ShapeDtypeStruct((length, width), bf16),
        jax.ShapeDtypeStruct((n_rows, width), bf16),
        jax.ShapeDtypeStruct((pairs, 2, n_rows, length), bf16),
        jax.ShapeDtypeStruct((n_rows, width), f32),
        jax.ShapeDtypeStruct((n_rows, width + LANES), bf16),
        jax.ShapeDtypeStruct((n_rows, LANES), f32),
        jax.ShapeDtypeStruct((length, width), bf16),
    ]
    anywhere = pl.BlockSpec(memory_space=pl.ANY)
    params, aliases = {}, {}
    if background:
        out_shape += background.out_shape(*behind)
        params = {"collective_id": 1, "has_side_effects": True}
        aliases = {8: 10}
    return pl.pallas_call(
        functools.partial(forward_kernel, background, n_experts, head_dim),
        out_shape=out_shape,
        grid_spec=pltpu.PrefetchScalarGridSpec(
            num_scalar_prefetch=1,
            grid=(pairs,),
            in_specs=[
                whole((length, width)),
                matrix(0),
                matrix(1),
                matrix(2),
                pl.BlockSpec((None, LANES, width), lambda p, *_: (3, p, 0)),
                whole(pack.shape),
            ]
            + [anywhere] * len(behind),
            out_specs=[
                columns(n_rows),
                columns(length),
                columns(length),
                columns(n_rows),
                pl.BlockSpec((None, 2, n_rows, length), lambda p, *_: (p, 0, 0, 0)),
                whole((n_rows, width)),
                whole((n_rows, width + LANES)),
                whole((n_rows, LANES)),
                whole((length, width)),
            ]
            + [anywhere] * (background.n_out if background else 0),
            scratch_shapes=[
                pltpu.VMEM((n_rows, width), f32),
                pltpu.VMEM((n_rows, length), f32),
                pltpu.VMEM((2, LANES, span), f32),
                pltpu.VMEM((16, span), f32),
            ]
            + (background.scratch(*behind) if background else []),
        ),
        input_output_aliases=aliases,
        compiler_params=pltpu.CompilerParams(vmem_limit_bytes=VMEM_LIMIT, **params),
        cost_estimate=pl.CostEstimate(
            flops=20_000_000_000, transcendentals=0, bytes_accessed=20_000_000
        ),
        name="attention_forward",
    )(
        place,
        x_all,
        weights,
        weights,
        weights,
        weights,
        pack,
        *behind,
    )


GELU_A = 0.7978845608028654
GELU_B = 0.044715 * GELU_A


def experts_kernel(
    n_experts,
    chunk,
    expert_ref,
    message_ref,
    dy_ref,
    w_in_ref,
    w_out_ref,
    out_ref,
    dh_ref,
    dw_in_ref,
    dw_out_ref,
    dw_in_acc,
    dw_out_acc,
):
    step = pl.program_id(0)
    width = dy_ref.shape[1]
    hidden = w_in_ref.shape[1]
    expert = expert_ref[0]

    @pl.when(step == 0)
    def _():
        dw_in_acc[...] = jnp.zeros_like(dw_in_acc)
        dw_out_acc[...] = jnp.zeros_like(dw_out_acc)

    h = message_ref[:, :width]
    extra = message_ref[:, width:].astype(f32)
    lane = lax.broadcasted_iota(jnp.int32, extra.shape, 1)
    mine = (lane == expert) | (lane == expert + n_experts)
    gate = jnp.sum(jnp.where(mine, extra, 0.0), -1, keepdims=True)
    dy = dy_ref[...]
    out_total = None
    dh_total = None
    dgate = None
    for start in range(0, hidden, chunk):
        part = slice(start, start + chunk)
        up = dot(h, w_in_ref[:, part])
        dact = dot_t(dy, w_out_ref[part, :])
        square = up * up
        tanh = jnp.tanh(up * (GELU_A + GELU_B * square))
        half = 0.5 * up
        more = 1.0 + tanh
        act = half * more
        slope = 0.5 * more + half * (1.0 - tanh * tanh) * (GELU_A + 3.0 * GELU_B * square)
        gated = (gate * act).astype(bf16)
        dgate_part = jnp.sum(act * dact, -1, keepdims=True)
        dup = (gate * dact * slope).astype(bf16)
        out_part = dot(gated, w_out_ref[part, :])
        dh_part = dot_t(dup, w_in_ref[:, part])
        out_total = out_part if out_total is None else out_total + out_part
        dh_total = dh_part if dh_total is None else dh_total + dh_part
        dgate = dgate_part if dgate is None else dgate + dgate_part
        dw_out_acc[part, :] += t_dot(gated, dy)
        dw_in_acc[:, part] += t_dot(h, dup)
    out_ref[...] = out_total.astype(bf16)
    dh_ref[:, :width] = dh_total.astype(bf16)
    high = dgate.astype(bf16).astype(f32)
    low = dgate - high
    dh_ref[:, width:] = jnp.where(
        lane == expert, high, jnp.where(lane == expert + n_experts, low, 0.0)
    ).astype(bf16)

    @pl.when(step == pl.num_programs(0) - 1)
    def _():
        dw_in_ref[...] = dw_in_acc[...].astype(bf16)
        dw_out_ref[...] = dw_out_acc[...].astype(bf16)


def experts(expert, message, dy, w_in, w_out, n_experts, block):
    tokens, width = dy.shape
    hidden = w_in.shape[1]
    whole = lambda shape: pl.BlockSpec(shape, lambda i, *_: (0,) * len(shape))
    rows = lambda columns: pl.BlockSpec((block, columns), lambda i, *_: (i, 0))
    return pl.pallas_call(
        functools.partial(experts_kernel, n_experts, 512),
        out_shape=[
            jax.ShapeDtypeStruct((tokens, width), bf16),
            jax.ShapeDtypeStruct((tokens, width + LANES), bf16),
            jax.ShapeDtypeStruct((width, hidden), bf16),
            jax.ShapeDtypeStruct((hidden, width), bf16),
        ],
        grid_spec=pltpu.PrefetchScalarGridSpec(
            num_scalar_prefetch=1,
            grid=(tokens // block,),
            in_specs=[
                rows(width + LANES),
                rows(width),
                whole((width, hidden)),
                whole((hidden, width)),
            ],
            out_specs=[
                rows(width),
                rows(width + LANES),
                whole((width, hidden)),
                whole((hidden, width)),
            ],
            scratch_shapes=[
                pltpu.VMEM((width, hidden), f32),
                pltpu.VMEM((hidden, width), f32),
            ],
        ),
        compiler_params=pltpu.CompilerParams(vmem_limit_bytes=VMEM_LIMIT),
        cost_estimate=pl.CostEstimate(
            flops=60_000_000_000, transcendentals=0, bytes_accessed=30_000_000
        ),
        name="experts",
    )(expert, message, dy, w_in, w_out)


def plane_slot(j):
    return (j // 2 + 1) % 4, j % 2


def down_order(step):
    inner = (13 - step) // 8
    return inner * ((step + 4) % 6) + (1 - inner) * step


def up_order(step):
    other, corner = (step + 6) // 8, (step + 2) // 8
    pair = 3 * (1 - other) + (other - corner) * (step % 2) + 2 * corner
    return pair, (step % 2 + step // 4 - corner) % 2


def experts_up_kernel(
    n_experts,
    chunk,
    n_fsdp,
    message_ref,
    dy_ref,
    w_in,
    expert_out,
    _,
    h_out,
    act_out,
    slope_out,
    dw_out_ref,
    w_out,
    h_ref,
    dw_out_acc,
    w_in_ref,
    gated_ref,
    dy_pair_ref,
    out_held,
    send,
    recv,
    local,
):
    step = pl.program_id(0)
    last = pl.num_programs(0) - 1
    me = Place(n_fsdp)
    core = me.core
    half, width = dy_ref.shape[1:]
    rows = 2 * half
    hidden = w_in_ref.shape[1]
    mate, across, beside = me.mate(), me.chip(1, 0), me.chip(0, 1)
    block = h_ref.at
    plan = {
        "x0": (message_ref.at[0], block[0, core, 0], beside),
        "x1": (message_ref.at[1], block[0, core, 1], beside),
        "y0": (message_ref.at[0], block[1, core, 0], across),
        "y1": (message_ref.at[1], block[1, core, 1], across),
        "xy": (block[0, core, 0], block[2, core, 0], across),
        "yx": (block[1, core, 1], block[2, core, 1], beside),
        ("c", 3, 0): (message_ref.at[0], block[3, core, 0], mate),
        ("c", 3, 1): (message_ref.at[1], block[3, core, 1], mate),
    }
    for pair in range(3):
        for side in range(2):
            piece = block[pair, core, side]
            plan["c", pair, side] = (piece, piece, mate)
    plan |= line_plan(me, expert_out.at[me.rep], w_out)
    del plan["first", 1]
    copies = Planned(plan, send, recv)
    own_out = Bounce(expert_out.at[me.rep], out_held, w_out.at[me.line], local.at[pl.ds(0, 2)])

    @pl.when(step == 0)
    def _():
        load = pltpu.make_async_copy(w_in, w_in_ref, local.at[2])
        load.start()
        meet([mate, across, beside, me.along(1), me.along(-1)])
        for name in (("c", 3, 0), ("c", 3, 1), "x0", "y1", ("relay", 1), ("first", -1)):
            copies[name].start()
        own_out.start()
        h_ref[3, core] = message_ref[...]
        dw_out_acc[...] = jnp.zeros_like(dw_out_acc)
        load.wait()

    @pl.when(step == 1)
    def _():
        own_out.turn()
        for name in ("x1", "y0", ("rest", 1), ("rest", -1)):
            copies[name].start()

    @pl.when(step == 2)
    def _():
        copies["x0"].wait_recv()
        copies["c", 0, 0].start()
        copies["xy"].start()
        copies["y1"].wait_recv()
        copies["c", 1, 1].start()
        copies["yx"].start()
        copies["first", -1].wait_recv()
        copies["relay", -1].start()

    @pl.when(step == 3)
    def _():
        copies["x1"].wait_recv()
        copies["c", 0, 1].start()
        copies["y0"].wait_recv()
        copies["c", 1, 0].start()

    @pl.when(step == 5)
    def _():
        copies["xy"].wait_recv()
        copies["c", 2, 0].start()
        copies["yx"].wait_recv()
        copies["c", 2, 1].start()

    for turn in range(8):

        @pl.when(step == turn)
        def _():
            copies[("c",) + up_order(turn)].wait_recv()

    pair, side = up_order(step)
    message = h_ref[pair, :, side]
    expert = me.rep
    h_out[...] = message
    message = message.reshape(rows, message.shape[2])
    h = message[:, :width]
    extra = message[:, width:].astype(f32)
    lane = lax.broadcasted_iota(jnp.int32, extra.shape, 1)
    mine = (lane == expert) | (lane == expert + n_experts)
    gate = jnp.sum(jnp.where(mine, extra, 0.0), -1, keepdims=True)
    place = pl.ds(pl.multiple_of(step % 2 * rows, rows), rows)
    dy_pair_ref[place, :] = dy_ref[...].reshape(rows, width)
    for start in range(0, hidden, chunk):
        piece = slice(start, start + chunk)
        up = dot(h, w_in_ref[:, piece])
        square = up * up
        tanh = jnp.tanh(up * (GELU_A + GELU_B * square))
        halved = 0.5 * up
        more = 1.0 + tanh
        act = (halved * more).astype(bf16)
        slope = 0.5 * more + halved * (1.0 - tanh * tanh) * (GELU_A + 3.0 * GELU_B * square)
        act_out[:, :, piece] = act.reshape(2, half, chunk)
        slope_out[:, :, piece] = slope.astype(bf16).reshape(2, half, chunk)
        gated_ref[place, piece] = (gate * act.astype(f32)).astype(bf16)

    @pl.when(step % 2 == 1)
    def _():
        dw_out_acc[...] += t_dot(gated_ref[...], dy_pair_ref[...])

    @pl.when(step == last)
    def _():
        dw_out_ref[...] = dw_out_acc[...].astype(bf16)
        own_out.wait()
        for shift in (1, -1):
            copies["rest", shift].wait_recv()
            copies["relay", shift].wait_recv()
        for name in plan:
            copies[name].wait_send()


def experts_up(message, dy_all, w_in, expert_out, w_out, n_experts, n_fsdp):
    blocks, rows, width = dy_all.shape
    long = message.shape[1]
    hidden = w_in.shape[1]
    once = pl.Buffered(1)
    whole = lambda shape: pl.BlockSpec(shape, lambda i: (0,) * len(shape), pipeline_mode=once)
    half = rows // 2

    def turn(columns):
        def index(i):
            pair, side = up_order(i)
            return pair, 0, side, 0, 0

        return pl.BlockSpec((None, 2, None, half, columns), index)

    halves = lambda columns: (blocks // 2, 2, 2, half, columns)
    anywhere = pl.BlockSpec(memory_space=pl.ANY)
    dma = lambda *shape: pltpu.SemaphoreType.DMA(shape)
    message_all, act, slope, dw_out, w_out = pl.pallas_call(
        functools.partial(experts_up_kernel, n_experts, hidden // 2, n_fsdp),
        out_shape=[
            jax.ShapeDtypeStruct(halves(long), bf16),
            jax.ShapeDtypeStruct(halves(hidden), bf16),
            jax.ShapeDtypeStruct(halves(hidden), bf16),
            jax.ShapeDtypeStruct((hidden, width), bf16),
            jax.ShapeDtypeStruct((n_fsdp,) + expert_out.shape[1:], bf16),
        ],
        grid=(blocks,),
        in_specs=[whole((2, half, long)), turn(width), anywhere, anywhere, anywhere],
        out_specs=[turn(long), turn(hidden), turn(hidden), whole((hidden, width)), anywhere],
        scratch_shapes=[
            pltpu.VMEM(halves(long), bf16),
            pltpu.VMEM((hidden, width), f32),
            pltpu.VMEM((width, hidden), bf16),
            pltpu.VMEM((2 * rows, hidden), bf16),
            pltpu.VMEM((2 * rows, width), bf16),
            pltpu.VMEM(expert_out.shape[1:], bf16),
            dma(24),
            dma(24),
            dma(3),
        ],
        input_output_aliases={4: 4},
        compiler_params=pltpu.CompilerParams(
            vmem_limit_bytes=VMEM_LIMIT, collective_id=2, has_side_effects=True
        ),
        cost_estimate=pl.CostEstimate(
            flops=20_000_000_000, transcendentals=0, bytes_accessed=30_000_000
        ),
        name="experts_up",
    )(message.reshape(2, half, long), dy_all.reshape(halves(width)), w_in, expert_out, w_out)
    whole_blocks = lambda array: array.reshape(blocks, rows, array.shape[4])
    return whole_blocks(message_all), whole_blocks(act), whole_blocks(slope), dw_out, w_out


def experts_down_kernel(
    n_experts,
    chunk,
    n_fsdp,
    message_ref,
    dy_ref,
    act_ref,
    slope_ref,
    w_in,
    w_out,
    dw_out,
    back_ref,
    out_half,
    dw_in_ref,
    sum_out,
    part_ref,
    tx_ref,
    rx_ref,
    fin_ref,
    fin_out_ref,
    land_ref,
    dw_in_acc,
    w_in_ref,
    w_out_ref,
    h_pair_ref,
    dup_ref,
    tx_send,
    tx_recv,
    fin_sem,
    land_sem,
    local,
    near,
    mid,
    far,
    own_ref,
    line_send,
    line_recv,
    line_local,
):
    step = pl.program_id(0)
    last = 7
    me = Place(n_fsdp)
    core = me.core
    rows, width = dy_ref.shape
    hidden = w_in_ref.shape[1]
    long = message_ref.shape[1]
    half = rows // 2
    mate = me.mate()
    adds = LineSum(me, dw_out, near, mid, far, own_ref, line_send, line_recv, line_local)

    def to_mate(j):
        return pltpu.make_async_remote_copy(
            src_ref=tx_ref.at[j % 2],
            dst_ref=rx_ref.at[j],
            send_sem=tx_send.at[j],
            recv_sem=tx_recv.at[j],
            device_id=mate,
            device_id_type=MESH,
        )

    def to_owner(j):
        q, k = plane_slot(down_order(j))
        return pltpu.make_async_remote_copy(
            src_ref=fin_ref.at[j % 2],
            dst_ref=land_ref.at[q, core],
            send_sem=fin_sem.at[j],
            recv_sem=land_sem.at[q, core],
            device_id=me.chip(q // 2, q % 2, k),
            device_id_type=MESH,
        )

    def keep_out(j):
        return pltpu.make_async_copy(fin_out_ref.at[j % 2], out_half.at[down_order(j)], local.at[j])

    def stays(j):
        q, k = plane_slot(down_order(j))
        return (q == 0) & (k == core)

    def finish_block(j):
        to_mate(j).wait_recv()
        mine = part_ref.at[j % 2, pl.ds(core * half, half)]

        @pl.when(j >= 2)
        def _():
            keep_out(j - 2).wait()

        @pl.when((j >= 2) & ~stays(j - 2))
        def _():
            to_owner(j - 2).wait_send()

        fin_ref[j % 2] = (mine[:, :long] + rx_ref[j, :, :long].astype(f32)).astype(bf16)

        @pl.when(stays(j))
        def _():
            land_ref[0, core] = fin_ref[j % 2]

        @pl.when(~stays(j))
        def _():
            to_owner(j).start()

        fin_out_ref[j % 2] = (mine[:, long:] + rx_ref[j, :, long:].astype(f32)).astype(bf16)
        keep_out(j).start()

    @pl.when(step == 0)
    def _():
        loads = [
            pltpu.make_async_copy(w_in, w_in_ref, local.at[0]),
            pltpu.make_async_copy(w_out, w_out_ref, local.at[1]),
        ]
        for load in loads:
            load.start()
        partners = [mate, me.along(1), me.along(-1)]
        for q in (1, 2, 3):
            for k in (0, 1):
                partners.append(me.chip(q // 2, q % 2, (core + k) % 2))
        meet(partners)
        adds.start()
        dw_in_acc[...] = jnp.zeros_like(dw_in_acc)
        for load in loads:
            load.wait()

    @pl.when(step == 3)
    def _():
        adds.turn()

    expert = me.rep
    place = pl.ds(pl.multiple_of(step % 2 * rows, rows), rows)
    h_pair_ref[:, place] = message_ref[:, :width].T
    extra = message_ref[:, width:].astype(f32)
    lane = lax.broadcasted_iota(jnp.int32, extra.shape, 1)
    mine = (lane == expert) | (lane == expert + n_experts)
    gate = jnp.sum(jnp.where(mine, extra, 0.0), -1, keepdims=True)
    dy = dy_ref[...]
    dgate = None
    part = part_ref.at[step % 2]
    for start in range(0, hidden, chunk):
        piece = slice(start, start + chunk)
        act = act_ref[:, piece].astype(f32)
        dact = dot_t(dy, w_out_ref[piece, :])
        gated = (gate * act).astype(bf16)
        dgate_part = jnp.sum(act * dact, -1, keepdims=True)
        dup = (gate * dact * slope_ref[:, piece].astype(f32)).astype(bf16)
        out_part = dot(gated, w_out_ref[piece, :])
        dh_part = dot_t(dup, w_in_ref[:, piece])
        if start == 0:
            part[:, long:] = out_part
            part[:, :width] = dh_part
        else:
            part[:, long:] += out_part
            part[:, :width] += dh_part
        dgate = dgate_part if dgate is None else dgate + dgate_part
        dup_ref[place, piece] = dup
        if start == chunk:

            @pl.when(step >= 1)
            def _():
                finish_block(step - 1)

    @pl.when(step % 2 == 1)
    def _():
        dw_in_acc[...] += dot(h_pair_ref[...], dup_ref[...])

    high = dgate.astype(bf16).astype(f32)
    low = dgate - high
    part[:, width:long] = jnp.where(
        lane == expert, high, jnp.where(lane == expert + n_experts, low, 0.0)
    )

    @pl.when(step >= 2)
    def _():
        to_mate(step - 2).wait_send()

    tx_ref[step % 2] = part_ref[step % 2, pl.ds((1 - core) * half, half)].astype(bf16)
    to_mate(step).start()

    @pl.when(step == last)
    def _():
        dw_in_ref[...] = dw_in_acc[...].astype(bf16)
        finish_block(last)
        sum_out[...] = adds.total()
        to_mate(last - 1).wait_send()
        to_mate(last).wait_send()
        keep_out(last - 1).wait()
        keep_out(last).wait()
        for j in (last - 1, last):

            @pl.when(~stays(j))
            def _():
                to_owner(j).wait_send()

        for side in range(2):
            total = None
            for q in range(4):
                arrived = pltpu.make_async_remote_copy(
                    src_ref=fin_ref.at[0],
                    dst_ref=land_ref.at[q, side],
                    send_sem=fin_sem.at[0],
                    recv_sem=land_sem.at[q, side],
                    device_id=mate,
                    device_id_type=MESH,
                )
                if q == 0:

                    @pl.when(core != side)
                    def _():
                        arrived.wait_recv()

                else:
                    arrived.wait_recv()
                landed = land_ref[q, side].astype(f32)
                total = landed if total is None else total + landed
            back_ref[side * half : (side + 1) * half, :] = total


def experts_down(message_all, dy_all, act, slope, w_in, w_out, dw_out, n_experts, n_fsdp):
    blocks, rows, width = dy_all.shape
    long = message_all.shape[2]
    hidden = w_in.shape[1]
    half = rows // 2
    once = pl.Buffered(1)
    whole = lambda shape: pl.BlockSpec(shape, lambda i: (0,) * len(shape), pipeline_mode=once)
    block = lambda columns: pl.BlockSpec(
        (None, rows, columns), lambda i: (down_order(i), 0, 0)
    )
    anywhere = pl.BlockSpec(memory_space=pl.ANY)
    both = long + width
    dma = lambda *shape: pltpu.SemaphoreType.DMA(shape)
    return pl.pallas_call(
        functools.partial(experts_down_kernel, n_experts, hidden // 2, n_fsdp),
        out_shape=[
            jax.ShapeDtypeStruct((rows, long), f32),
            jax.ShapeDtypeStruct((blocks, half, width), bf16),
            jax.ShapeDtypeStruct((width, hidden), bf16),
            jax.ShapeDtypeStruct(dw_out.shape[1:], bf16),
        ],
        grid=(blocks,),
        in_specs=[
            block(long),
            block(width),
            block(hidden),
            block(hidden),
            anywhere,
            anywhere,
            anywhere,
        ],
        out_specs=[
            whole((rows, long)),
            anywhere,
            whole((width, hidden)),
            whole(dw_out.shape[1:]),
        ],
        scratch_shapes=[
            pltpu.VMEM((2, rows, both), f32),
            pltpu.VMEM((2, half, both), bf16),
            pltpu.VMEM((blocks, half, both), bf16),
            pltpu.VMEM((2, half, long), bf16),
            pltpu.VMEM((2, half, width), bf16),
            pltpu.VMEM((4, 2, half, long), bf16),
            pltpu.VMEM((width, hidden), f32),
            pltpu.VMEM((width, hidden), bf16),
            pltpu.VMEM((hidden, width), bf16),
            pltpu.VMEM((width, 2 * rows), bf16),
            pltpu.VMEM((2 * rows, hidden), bf16),
            dma(8),
            dma(8),
            dma(8),
            dma(4, 2),
            dma(8),
        ]
        + LineSum.scratch(*dw_out.shape[1:]),
        compiler_params=pltpu.CompilerParams(
            vmem_limit_bytes=VMEM_LIMIT, collective_id=3, has_side_effects=True
        ),
        cost_estimate=pl.CostEstimate(
            flops=40_000_000_000, transcendentals=0, bytes_accessed=40_000_000
        ),
        name="experts_down",
    )(message_all, dy_all, act, slope, w_in, w_out, dw_out)


class LineSum:
    def __init__(self, me, whole, near, mid, far, mine, send, recv, local):
        self.me, self.whole, self.near, self.mid, self.far = me, whole, near, mid, far
        self.mine, self.local = mine, local
        rows = whole.shape[1]
        half = rows // 2
        self.parts = {1: slice(0, half), -1: slice(half, rows)}
        plan = {}
        for i, shift in enumerate((1, -1)):
            part = pl.ds(i * half, half)
            target = (me.line + 2) % me.n_fsdp
            plan["near", shift] = (whole.at[target, part], near.at[i], me.along(shift))
            plan["far", shift] = (mid.at[i], far.at[i], me.along(shift))
        self.copies = Planned(plan, send, recv)

    def loads(self):
        me = self.me
        for i, shift in enumerate((1, -1)):
            source = self.whole.at[(me.line + shift) % me.n_fsdp]
            yield pltpu.make_async_copy(source, self.mid.at[i], self.local.at[i])
        yield pltpu.make_async_copy(self.whole.at[me.line], self.mine, self.local.at[2])

    def start(self):
        for shift in (1, -1):
            self.copies["near", shift].start()
        for load in self.loads():
            load.start()

    def turn(self):
        for load in self.loads():
            load.wait()
        for i, shift in enumerate((1, -1)):
            self.copies["near", shift].wait_recv()
            part = self.parts[shift]
            total = self.mid[i, part, :].astype(f32) + self.near[i].astype(f32)
            self.mid[i, part, :] = total.astype(bf16)
            self.copies["far", shift].start()

    def total(self):
        for shift in (1, -1):
            self.copies["far", shift].wait_recv()
        total = self.mine[...].astype(f32) + self.far[0].astype(f32) + self.far[1].astype(f32)
        for shift in (1, -1):
            self.copies["near", shift].wait_send()
            self.copies["far", shift].wait_send()
        return total.astype(bf16)

    @staticmethod
    def scratch(rows, columns):
        return [
            pltpu.VMEM((2, rows // 2, columns), bf16),
            pltpu.VMEM((2, rows, columns), bf16),
            pltpu.VMEM((2, rows, columns), bf16),
            pltpu.VMEM((rows, columns), bf16),
            pltpu.SemaphoreType.DMA((4,)),
            pltpu.SemaphoreType.DMA((4,)),
            pltpu.SemaphoreType.DMA((3,)),
        ]


class BackgroundBack:
    n_in, n_out = 2, 4

    def __init__(self, n_fsdp):
        self.n_fsdp = n_fsdp

    def out_shape(self, out_half, dw_in):
        half, width = out_half.shape[1:]
        return [
            jax.ShapeDtypeStruct((2 * half, width), bf16),
            jax.ShapeDtypeStruct(dw_in.shape[1:], bf16),
            jax.ShapeDtypeStruct(
                (self.n_fsdp, width // (2 * self.n_fsdp), width - LANES), bf16
            ),
            jax.ShapeDtypeStruct((4,) + self.split(width), bf16),
        ]

    def out_specs(self, shapes):
        whole = lambda shape: pl.BlockSpec(shape, lambda p, *_: (0,) * len(shape))
        return [whole(s.shape) for s in shapes]

    def scratch(self, out_half, dw_in):
        half, width = out_half.shape[1:]
        pairs = width // LANES - 1
        return [
            pltpu.VMEM((3, 2, half, width), bf16),
            pltpu.SemaphoreType.DMA((8,)),
            pltpu.SemaphoreType.DMA((3, 2)),
            pltpu.VMEM((2, 4) + self.split(width), bf16),
            pltpu.VMEM((pairs, 2) + self.split(width), bf16),
            pltpu.VMEM((pairs, 2) + self.split(width), bf16),
            pltpu.VMEM((pairs, 3, self.n_fsdp) + self.split(width)[2:], bf16),
            pltpu.SemaphoreType.DMA((pairs, 2)),
            pltpu.SemaphoreType.DMA((pairs, 2)),
            pltpu.SemaphoreType.DMA((pairs, 3)),
            pltpu.SemaphoreType.DMA((pairs, 3)),
            pltpu.VMEM((2, half, width), bf16),
            pltpu.VMEM((2, half, width), bf16),
            pltpu.SemaphoreType.DMA((2,)),
            pltpu.SemaphoreType.DMA((2,)),
        ] + LineSum.scratch(*dw_in.shape[1:])

    def split(self, width):
        return (self.n_fsdp, 2, width // (2 * self.n_fsdp), LANES)

    def to_mate(self, pair, i, scratch):
        me = Place(self.n_fsdp)
        own, given = scratch[3:5]
        send, recv = scratch[7:9]
        return pltpu.make_async_remote_copy(
            src_ref=own.at[pair % 2, 2 * i + 1 - me.core],
            dst_ref=given.at[pair, i],
            send_sem=send.at[pair, i],
            recv_sem=recv.at[pair, i],
            device_id=me.mate(),
            device_id_type=MESH,
        )

    def to_chip(self, pair, i, scratch):
        me = Place(self.n_fsdp)
        added, landed = scratch[5:7]
        send, recv = scratch[9:11]
        rows, columns = ((0, 1), (1, 0), (1, 1))[i]
        row, column = (me.row + rows) % 2, (me.seq + columns) % 2
        return pltpu.make_async_remote_copy(
            src_ref=added.at[pair, row, :, column],
            dst_ref=landed.at[pair, i],
            send_sem=send.at[pair, i],
            recv_sem=recv.at[pair, i],
            device_id=me.chip(rows, columns),
            device_id_type=MESH,
        )

    def give(self, pair, grads, scratch, last_out):
        own = scratch[3]
        last = pl.num_programs(0) - 1

        @pl.when(pair >= 2)
        def _():
            for i in (0, 1):
                self.to_mate(pair - 2, i, scratch).wait_send()

        @pl.when(pair < last)
        def _():
            for i, grad in enumerate(grads):
                own[pair % 2, i] = grad.reshape(own.shape[2:])
            for i in (0, 1):
                self.to_mate(pair, i, scratch).start()

        @pl.when(pair == last)
        def _():
            for i, grad in enumerate(grads):
                last_out[i] = grad.reshape(own.shape[2:])

    def collect(self, pair, scratch):
        core = Place(self.n_fsdp).core
        own, given, added = scratch[3:6]
        for i in (0, 1):
            self.to_mate(pair, i, scratch).wait_recv()
            total = own[pair % 2, 2 * i + core].astype(f32) + given[pair, i].astype(f32)
            added[pair, i] = total.astype(bf16)
        for i in range(3):
            self.to_chip(pair, i, scratch).start()

    def collect_before(self, pair, scratch):
        @pl.when(pair >= 1)
        def _():
            self.collect(pair - 1, scratch)

    def run(self, step, before, ins, outs, scratch, x_mid):
        out_half, dw_in = ins
        out_rows, sum_in, plane_sum, _ = outs
        land, send, recv = scratch[:3]
        relay, hop, relay_recv, hop_sem = scratch[11:15]
        near, mid, far, mine, line_send, line_recv, line_local = scratch[15:]
        me = Place(self.n_fsdp)
        core = me.core
        half = out_half.shape[1]
        line = LineSum(me, dw_in, near, mid, far, mine, line_send, line_recv, line_local)

        across, beside = (lambda k: me.chip(1, 0, k)), (lambda k: me.chip(0, 1, k))
        plan = {
            "mate": (out_half.at[7 - core], land.at[0, core], me.mate(), recv.at[0, core]),
            "direct0": (out_half.at[2], land.at[2, core], across(0), recv.at[2, core]),
            "direct1": (out_half.at[1], land.at[1, core], beside(1), recv.at[1, core]),
            "hop0": (out_half.at[4], relay.at[0], across(core), relay_recv.at[0]),
            "hop1": (out_half.at[5], relay.at[1], beside(core), relay_recv.at[1]),
            "sum0": (hop.at[0], land.at[1, core], beside(0), recv.at[1, core]),
            "sum1": (hop.at[1], land.at[2, core], across(1), recv.at[2, core]),
        }

        def result(name):
            source, target, device, arrival = plan[name]
            return pltpu.make_async_remote_copy(
                src_ref=source,
                dst_ref=target,
                send_sem=send.at[list(plan).index(name)],
                recv_sem=arrival,
                device_id=device,
                device_id_type=MESH,
            )

        def own_parts():
            yield pltpu.make_async_copy(out_half.at[0], hop.at[0], hop_sem.at[0])
            yield pltpu.make_async_copy(out_half.at[3], hop.at[1], hop_sem.at[1])

        stay = lambda: pltpu.make_async_copy(
            out_half.at[6 + core], land.at[0, core], send.at[7]
        )

        if before:

            @pl.when(step == 0)
            def _():
                partners = [me.mate(), me.along(1), me.along(-1)]
                for q in (1, 2, 3):
                    for k in (0, 1):
                        partners.append(me.chip(q // 2, q % 2, (core + k) % 2))
                meet(partners)
                line.start()
                for name in ("hop0", "hop1", "direct0", "direct1", "mate"):
                    result(name).start()
                stay().start()
                for part in own_parts():
                    part.start()

            @pl.when(step == 2)
            def _():
                line.turn()

            @pl.when(step == 3)
            def _():
                for part in own_parts():
                    part.wait()
                for k in (0, 1):
                    result(f"hop{k}").wait_recv()
                    hop[k] = (hop[k].astype(f32) + relay[k].astype(f32)).astype(bf16)
                    result(f"sum{k}").start()

            return

        @pl.when(step == pl.num_programs(0) - 1)
        def _():
            added, landed = scratch[5:7]
            pairs = landed.shape[0]
            sum_in[...] = line.total()
            for name in plan:
                result(name).wait_send()
            stay().wait()
            for side in range(2):
                here = slice(side * half, (side + 1) * half)
                total = x_mid[here, :]
                for q in range(3):
                    arrived = pltpu.make_async_remote_copy(
                        src_ref=out_half.at[0],
                        dst_ref=land.at[q, side],
                        send_sem=send.at[0],
                        recv_sem=recv.at[q, side],
                        device_id=me.mate(),
                        device_id_type=MESH,
                    )
                    if q == 0:

                        @pl.when(core != side)
                        def _():
                            arrived.wait_recv()

                    else:
                        arrived.wait_recv()
                    total = total + land[q, side].astype(f32)
                out_rows[here, :] = total.astype(bf16)
            for i in (0, 1):
                self.to_mate(pairs - 1, i, scratch).wait_send()
            for pair in range(pairs):
                total = added[pair, me.row, :, me.seq].astype(f32)
                for i in range(3):
                    self.to_chip(pair, i, scratch).wait_recv()
                    total = total + landed[pair, i].astype(f32)
                plane_sum[:, :, pair * LANES : (pair + 1) * LANES] = total.astype(bf16)
            for pair in range(pairs):
                for i in range(3):
                    self.to_chip(pair, i, scratch).wait_send()


def backward_kernel(
    background,
    n_experts,
    head_dim,
    back_ref,
    dy_ref,
    x_mid_ref,
    message_ref,
    probs_ref,
    pack_ref,
    h_ref,
    wq_ref,
    wk_ref,
    wv_ref,
    wo_ref,
    q_ref,
    k_ref,
    v_ref,
    o_ref,
    p_ref,
    x_ref,
    *refs,
):
    step = pl.program_id(0)
    n_in, n_out = (background.n_in, background.n_out) if background else (0, 0)
    behind_in, refs = refs[:n_in], refs[n_in:]
    n_grads = 0 if background else 4
    grad_outs, refs = refs[:n_grads], refs[n_grads:]
    dh_own_out, dh_other_out, dx_mid_out, gain_out, router_out, ddist_out = refs[:6]
    gain_one_out, refs = refs[6], refs[7:]
    behind_out, refs = refs[:n_out], refs[n_out:]
    da_ref, dh_all_ref, dh_mine_ref, dbias_ref, dq_ref, h_turned_ref, o_turned_ref = refs[:7]
    if background:
        background.run(step, True, behind_in, behind_out, refs[7:], x_mid_ref)
    rows, width = x_mid_ref.shape
    length = h_ref.shape[0]
    own = pl.ds(pl.multiple_of(first_row(rows), rows), rows)

    @pl.when(step == 0)
    def _():
        probs = probs_ref[...]
        chosen = chosen_experts(pack_ref, probs.shape)
        picked = jnp.where(chosen, probs, 0.0)
        total = jnp.sum(picked, -1, keepdims=True)
        gate = picked / total
        extra = back_ref[:, width:].astype(f32)
        dgate = extra + pltpu.roll(extra, LANES - n_experts, 1)
        dgate = jnp.where(chosen, dgate, 0.0)
        shared = jnp.sum(dgate * gate, -1, keepdims=True)
        dprobs = jnp.where(chosen, (dgate - shared) / total, 0.0)
        dlogits = probs * (dprobs - jnp.sum(probs * dprobs, -1, keepdims=True))
        h_two = message_ref[:, :width].astype(f32)
        router_out[...] = lax.dot_general(
            dlogits,
            h_two,
            (((0,), (0,)), ((), ())),
            precision=highest,
            preferred_element_type=f32,
        )
        dh_two = back_ref[:, :width].astype(f32) + exact_dot(
            dlogits, router_rows(pack_ref, n_experts, width)
        )
        dx, dgain = norm_back(x_mid_ref[...], pack_ref[5:6, :width], dh_two)
        gain_out[...] = dgain
        dx_mid = dx + dy_ref[...].astype(f32)
        dx_mid_out[...] = dx_mid
        da_ref[...] = dx_mid.astype(bf16)
        dh_all_ref[...] = jnp.zeros_like(dh_all_ref)
        dh_mine_ref[...] = jnp.zeros_like(dh_mine_ref)
        ddist_out[...] = jnp.zeros_like(ddist_out)
        h_turned_ref[...] = h_ref[...].T
        o_turned_ref[...] = o_ref[...].T

    da = da_ref[...]
    do = dot_t(da, wo_ref[...]).astype(bf16)
    block = LANES
    first_half = lax.broadcasted_iota(jnp.int32, (block, LANES), 1) < head_dim
    zero = jnp.zeros((), bf16)
    k_low = k_ref[...]
    v_low = v_ref[...]
    dk = None
    dv = None
    for head in range(2):
        dbias_ref[head] = jnp.zeros_like(dbias_ref[head])
    for b in range(rows // block):
        here = slice(b * block, (b + 1) * block)
        offset = pl.multiple_of(length - LANES - block * b - first_row(rows), LANES)
        q_heads = by_head(q_ref[here, :], first_half)
        do_heads = by_head(do[here], first_half)
        probs_low = p_ref[:, here, :]
        probs = probs_low.astype(f32)
        dprobs = dot_t(do_heads, v_low).reshape(2, block, length)
        weighted = probs * dprobs
        ds = weighted - probs * jnp.sum(weighted, -1, keepdims=True)
        dbias_ref[:, :, pl.ds(offset, length)] += ds
        ds_low = ds.astype(bf16).reshape(2 * block, length)
        probs_low = probs_low.reshape(2 * block, length)
        dq_heads = dot(ds_low, k_low)
        dk_part = t_dot(ds_low, q_heads)
        dv_part = t_dot(probs_low, do_heads)
        dk = dk_part if dk is None else dk + dk_part
        dv = dv_part if dv is None else dv + dv_part
        dq_ref[here, :] = (of_head(dq_heads, first_half) * (head_dim**-0.5)).astype(bf16)
    for head in range(2):
        ddist_out[pl.ds(2 * step + head, 1), :] = gather_diagonals(dbias_ref[head])
    dq = dq_ref[...]
    dkv = jnp.concatenate([dk, dv], 1).astype(bf16)
    da_columns = da_ref[:, pl.ds(pl.multiple_of(step * LANES, LANES), LANES)]
    if background:
        background.collect_before(step, refs[7:])
    mine = pl.ds(pl.multiple_of(first_row(rows), rows), rows)
    grads_kv = dot(h_turned_ref[...], dkv).astype(bf16)
    grads = [
        dot(h_turned_ref[:, mine], dq).astype(bf16),
        grads_kv[:, :LANES],
        grads_kv[:, LANES:],
        dot(o_turned_ref[...], da_columns).astype(bf16),
    ]
    if background:
        background.give(step, grads, refs[7:], behind_out[3])
    else:
        for target, grad in zip(grad_outs, grads):
            target[...] = grad
    dh_all_ref[...] += dot_t(dkv, jnp.concatenate([wk_ref[...], wv_ref[...]], 1))
    dh_mine_ref[...] += dot_t(dq, wq_ref[...])

    @pl.when(step == pl.num_programs(0) - 1)
    def _():
        other = pl.ds(pl.multiple_of(length - rows - first_row(rows), rows), rows)
        dh_own_out[...] = dh_mine_ref[...] + dh_all_ref[own, :]
        dh_other_out[...] = dh_all_ref[other, :].astype(bf16)
        for start in range(0, length, rows):
            here = slice(start, start + rows)
            values = x_ref[here, :].astype(f32)
            part = jnp.sum(dh_all_ref[here, :] * (values * inverse_rms(values)), 0, keepdims=True)
            gain_one_out[...] = part if start == 0 else gain_one_out[...] + part
        values = x_ref[own, :].astype(f32)
        scaled = values * inverse_rms(values)
        gain_one_out[...] += jnp.sum(dh_mine_ref[...] * scaled, 0, keepdims=True)

    if background:
        background.run(step, False, behind_in, behind_out, refs[7:], x_mid_ref)


def attention_backward(
    back,
    dy,
    x_mid,
    message,
    probs,
    pack,
    h_all,
    weights,
    q,
    k,
    v,
    o,
    p,
    x_all,
    n_experts,
    head_dim,
    background=None,
    behind=(),
):
    n_rows, width = x_mid.shape
    length = h_all.shape[0]
    pairs = width // LANES
    span = pack.shape[1]
    more_shapes, more_scratch, params = [], [], {}
    n_grads = 0 if background else 4
    if background:
        more_shapes = background.out_shape(*behind)
        more_scratch = background.scratch(*behind)
        params = {"collective_id": 4, "has_side_effects": True}
    anywhere = pl.BlockSpec(memory_space=pl.ANY)
    whole = lambda shape: pl.BlockSpec(shape, lambda p, *_: (0,) * len(shape))
    columns = lambda rows: pl.BlockSpec((rows, LANES), lambda p, *_: (0, p))
    matrix = lambda i: pl.BlockSpec((None, width, LANES), lambda p, *_: (i, 0, p))
    return pl.pallas_call(
        functools.partial(backward_kernel, background, n_experts, head_dim),
        out_shape=[jax.ShapeDtypeStruct((width, width), bf16)] * n_grads
        + [
            jax.ShapeDtypeStruct((n_rows, width), f32),
            jax.ShapeDtypeStruct((n_rows, width), bf16),
            jax.ShapeDtypeStruct((n_rows, width), f32),
            jax.ShapeDtypeStruct((1, width), f32),
            jax.ShapeDtypeStruct((LANES, width), f32),
            jax.ShapeDtypeStruct((16, span), f32),
            jax.ShapeDtypeStruct((1, width), f32),
        ]
        + more_shapes,
        grid_spec=pltpu.PrefetchScalarGridSpec(
            num_scalar_prefetch=0,
            grid=(pairs,),
            in_specs=[
                whole((n_rows, width + LANES)),
                whole((n_rows, width)),
                whole((n_rows, width)),
                whole((n_rows, width + LANES)),
                whole((n_rows, LANES)),
                whole(pack.shape),
                whole((length, width)),
                matrix(0),
                matrix(1),
                matrix(2),
                pl.BlockSpec((None, LANES, width), lambda p, *_: (3, p, 0)),
                columns(n_rows),
                columns(length),
                columns(length),
                whole((n_rows, width)),
                pl.BlockSpec((None, 2, n_rows, length), lambda p, *_: (p, 0, 0, 0)),
                whole((length, width)),
            ]
            + [anywhere] * len(behind),
            out_specs=[columns(width)] * n_grads
            + [
                whole((n_rows, width)),
                whole((n_rows, width)),
                whole((n_rows, width)),
                whole((1, width)),
                whole((LANES, width)),
                whole((16, span)),
                whole((1, width)),
            ]
            + (background.out_specs(more_shapes) if background else []),
            scratch_shapes=[
                pltpu.VMEM((n_rows, width), bf16),
                pltpu.VMEM((length, width), f32),
                pltpu.VMEM((n_rows, width), f32),
                pltpu.VMEM((2, LANES, span), f32),
                pltpu.VMEM((n_rows, LANES), bf16),
                pltpu.VMEM((width, length), bf16),
                pltpu.VMEM((width, n_rows), bf16),
            ]
            + more_scratch,
        ),
        compiler_params=pltpu.CompilerParams(vmem_limit_bytes=VMEM_LIMIT, **params),
        cost_estimate=pl.CostEstimate(
            flops=40_000_000_000, transcendentals=0, bytes_accessed=30_000_000
        ),
        name="attention_backward",
    )(
        back,
        dy,
        x_mid,
        message,
        probs,
        pack,
        h_all,
        weights,
        weights,
        weights,
        weights,
        q,
        k,
        v,
        o,
        p,
        x_all,
        *behind,
    )


def finish_kernel(
    n_fsdp,
    n_experts,
    n_heads,
    sum_in,
    sum_out,
    dh_other,
    line_ref,
    last_ref,
    dh_own_ref,
    dx_mid_ref,
    tokens_ref,
    pack_ref,
    dgain_one_ref,
    dgain_two_ref,
    drouter_ref,
    ddist_ref,
    attn_out,
    grad_in,
    grad_out,
    tokens_out,
    small_out,
    line_land,
    last_given,
    last_added,
    last_land,
    last_line,
    last_line_land,
    attn_held,
    dh_land,
    small_plane,
    small_line,
    in_held,
    out_held,
    send,
    recv,
    local,
):
    me = Place(n_fsdp)
    rep, line, seq, core, row = me.rep, me.line, me.seq, me.core, me.row
    width = tokens_ref.shape[1]
    mate, across, beside, corner = me.mate(), me.chip(1, 0), me.chip(0, 1), me.chip(1, 1)
    far_row = (row + 1) % 2
    far_rep = far_row * 2 + core
    part_out = sum_out.shape[0]
    columns = lambda z, x: pl.ds(pl.multiple_of((z * 2 + x) * part_out, LANES), part_out)
    here = rep * 2 + seq
    peers = [mate, across, beside, corner]
    peers += [me.chip(1, 0, 1 - core), me.chip(0, 1, 1 - core), me.chip(1, 1, 1 - core)]
    shifts = (1, -1, 2)
    plan = {
        "dh": (dh_other, dh_land, beside),
        "out_c": (sum_out, grad_out.at[rep], mate),
        "out_y": (sum_out, grad_out.at[rep], across),
        "out_f": (grad_out.at[far_rep], grad_out.at[far_rep], mate),
        "attn_c": (attn_held, attn_out.at[rep], mate),
        "attn_y": (attn_held, attn_out.at[rep], across),
        "attn_f": (attn_out.at[far_rep], attn_out.at[far_rep], mate),
        "in_c": (grad_in.at[rep], grad_in.at[rep], mate),
        "in_y": (grad_in.at[rep], grad_in.at[rep], across),
        "in_f": (grad_in.at[far_rep], grad_in.at[far_rep], mate),
    }
    for i, shift in enumerate(shifts):
        target = (line + shift) % n_fsdp
        plan["line", i] = (line_ref.at[target], line_land.at[i], me.along(shift))
        plan["last_z", i] = (last_line.at[target], last_line_land.at[i], me.along(shift))
        plan["small_z", i] = (small_line.at[line], small_line.at[line], me.along(shift))
    for z in range(n_fsdp):
        plan["in_x", z] = (
            sum_in.at[1 - seq, :, pl.ds(z * part_out, part_out)],
            grad_in.at[rep, :, columns(z, seq)],
            beside,
        )
    for i, peer in enumerate(peers):
        plan["small", i] = (small_plane.at[here], small_plane.at[here], peer)
    for i in (0, 1):
        plan["last_c", i] = (last_ref.at[2 * i + 1 - core], last_given.at[i], mate)
    chips = ((row, 1 - seq, beside), (far_row, seq, across), (far_row, 1 - seq, corner))
    for i, (to_row, to_column, chip) in enumerate(chips):
        plan["last", i] = (last_added.at[to_row, :, to_column], last_land.at[i], chip)
    copies = Planned(plan, send, recv)
    meet(peers + [me.along(shift) for shift in shifts])
    for i in (0, 1):
        copies["last_c", i].start()
    for i in range(3):
        copies["line", i].start()
    for z in range(n_fsdp):
        copies["in_x", z].start()
    copies["out_y"].start()
    copies["out_c"].start()
    own_in = pltpu.make_async_copy(sum_in.at[seq], in_held, local.at[2])
    own_in.start()
    own_out = Bounce(sum_out, out_held, grad_out.at[rep], local.at[pl.ds(8, 2)])
    own_out.start()
    own_in.wait()
    kept = []
    for z in range(n_fsdp):
        source = in_held.at[:, pl.ds(z * part_out, part_out)]
        target = grad_in.at[rep, :, columns(z, seq)]
        kept.append(pltpu.make_async_copy(source, target, local.at[4 + z]))
        kept[-1].start()
    own_out.turn()
    for i in (0, 1):
        copies["last_c", i].wait_recv()
        total = last_ref[2 * i + core].astype(f32) + last_given[i].astype(f32)
        last_added[i] = total.astype(bf16)
    for i in range(3):
        copies["last", i].start()
    table = exact_dot_t(ddist_ref[...], bucket_match(pack_ref))
    small = small_plane.at[here]
    small[...] = jnp.zeros_like(small_out)
    small[0:1, :] = dgain_one_ref[...]
    small[1:2, :] = dgain_two_ref[...]
    small[2 : 2 + n_experts, :] = drouter_ref[:n_experts, :]
    for head in range(n_heads):
        at = head % 6 * LANES
        small[6 + head // 6, at : at + LANES] = table[head]
    for i in range(len(peers)):
        copies["small", i].start()
    for copy in kept:
        copy.wait()
    for z in range(n_fsdp):
        copies["in_x", z].wait_recv()
    copies["in_y"].start()
    copies["dh"].start()
    copies["in_c"].start()
    total = last_added[row, :, seq].astype(f32)
    for i in range(3):
        copies["last", i].wait_recv()
        total = total + last_land[i].astype(f32)
    last_line[...] = total.astype(bf16)
    for i in range(3):
        copies["last_z", i].start()
    for i in range(len(peers)):
        copies["small", i].wait_recv()
    total = small_plane[0]
    for i in range(1, 8):
        total = total + small_plane[i]
    small_line[line] = total
    for i in range(3):
        copies["small_z", i].start()
    total = line_ref[line].astype(f32)
    for i in range(3):
        copies["line", i].wait_recv()
        total = total + line_land[i].astype(f32)
    early = total.shape[1]
    attn_held[:, :early] = total.astype(bf16)
    copies["out_y"].wait_recv()
    copies["out_f"].start()
    total = last_line[line].astype(f32)
    for i in range(3):
        copies["last_z", i].wait_recv()
        total = total + last_line_land[i].astype(f32)
    attn_held[:, early:] = total.astype(bf16)
    copies["attn_y"].start()
    copies["attn_c"].start()
    own_attn = pltpu.make_async_copy(attn_held, attn_out.at[rep], local.at[3])
    own_attn.start()
    copies["dh"].wait_recv()
    dh_one = dh_own_ref[...] + dh_land[...].astype(f32)
    dx, _ = norm_back(tokens_ref[...].astype(f32), pack_ref[4:5, :width], dh_one)
    tokens_out[...] = (dx_mid_ref[...] + dx).astype(bf16)
    for i in range(3):
        copies["small_z", i].wait_recv()
    total = small_line[0]
    for i in range(1, n_fsdp):
        total = total + small_line[i]
    small_out[...] = total
    copies["in_y"].wait_recv()
    copies["in_f"].start()
    copies["attn_y"].wait_recv()
    copies["attn_f"].start()
    own_attn.wait()
    own_out.wait()
    for name in ("attn_c", "attn_f", "in_c", "in_f", "out_c", "out_f"):
        copies[name].wait_recv()
    for name in plan:
        copies[name].wait_send()


def finish(
    plane_sum,
    last_grads,
    sum_in,
    sum_out,
    dh_other,
    dh_own,
    dx_mid,
    tokens,
    pack,
    dgain_one,
    dgain_two,
    drouter,
    ddist,
    n_fsdp,
    n_experts,
    n_heads,
    hidden,
):
    n_rows, width = tokens.shape
    part_attn = plane_sum.shape[1]
    split = last_grads.shape[1:]
    part_in = sum_in.shape[1]
    anywhere = pl.BlockSpec(memory_space=pl.ANY)
    inside = pl.BlockSpec(memory_space=pltpu.VMEM)
    dma = lambda n: pltpu.SemaphoreType.DMA((n,))
    return pl.pallas_call(
        functools.partial(finish_kernel, n_fsdp, n_experts, n_heads),
        out_shape=[
            jax.ShapeDtypeStruct((4, part_attn, width), bf16),
            jax.ShapeDtypeStruct((n_experts, part_in, hidden), bf16),
            jax.ShapeDtypeStruct((n_experts,) + sum_out.shape, bf16),
            jax.ShapeDtypeStruct((n_rows, width), bf16),
            jax.ShapeDtypeStruct((8, width), f32),
        ],
        in_specs=[anywhere] * 3 + [inside] * 10,
        out_specs=[anywhere] * 3 + [inside] * 2,
        scratch_shapes=[
            pltpu.VMEM((3,) + plane_sum.shape[1:], bf16),
            pltpu.VMEM((2,) + split, bf16),
            pltpu.VMEM((2,) + split, bf16),
            pltpu.VMEM((3, n_fsdp) + split[2:], bf16),
            pltpu.VMEM((n_fsdp,) + split[2:], bf16),
            pltpu.VMEM((3,) + split[2:], bf16),
            pltpu.VMEM((part_attn, width), bf16),
            pltpu.VMEM((n_rows, width), bf16),
            pltpu.VMEM((8, 8, width), f32),
            pltpu.VMEM((n_fsdp, 8, width), f32),
            pltpu.VMEM(sum_in.shape[1:], bf16),
            pltpu.VMEM(sum_out.shape, bf16),
            dma(40),
            dma(40),
            dma(12),
        ],
        compiler_params=pltpu.CompilerParams(
            vmem_limit_bytes=VMEM_LIMIT, collective_id=5, has_side_effects=True
        ),
        name="finish_gradients",
    )(
        sum_in,
        sum_out,
        dh_other,
        plane_sum,
        last_grads,
        dh_own,
        dx_mid,
        tokens,
        pack,
        dgain_one,
        dgain_two,
        drouter,
        ddist,
    )


def widen_kernel(
    n_experts,
    n_heads,
    n_buckets,
    out_rows,
    tokens,
    attn,
    grad_in,
    grad_out,
    small,
    out_rows_copy,
    tokens_copy,
    q,
    k,
    v,
    o,
    win,
    wout,
    *rest,
):
    step = pl.program_id(0)
    out_rows_copy[...] = out_rows[...]
    tokens_copy[...] = tokens[...]
    for i, target in enumerate((q, k, v, o)):

        @pl.when(step == i)
        def _():
            target[...] = attn[...].astype(f32)

    win[...] = grad_in[...].astype(f32)
    wout[...] = grad_out[...].astype(f32)
    gain_one, gain_two, table, router = rest

    @pl.when(step == 0)
    def _():
        gain_one[...] = small[0, :]
        gain_two[...] = small[1, :]
        router[...] = small[2 : 2 + n_experts, :]
        for head in range(n_heads):
            at = head % 6 * LANES
            table[head : head + 1, :] = small[
                6 + head // 6 : 7 + head // 6, at : at + n_buckets
            ]


def widen(out_rows, tokens, attn, grad_in, grad_out, small, n_heads, n_buckets):
    n_experts = grad_in.shape[0]
    rows = pl.BlockSpec((tokens.shape[0] // n_experts, tokens.shape[1]), lambda i: (i, 0))
    width = small.shape[1]
    own = lambda a: pl.BlockSpec((None,) + a.shape[1:], lambda i: (i, 0, 0))
    whole = lambda shape: pl.BlockSpec(shape, lambda i: (0,) * len(shape))
    small_shapes = [(width,), (width,), (n_heads, n_buckets), (n_experts, width)]
    wide = [attn.shape[1:]] * 4
    return pl.pallas_call(
        functools.partial(widen_kernel, n_experts, n_heads, n_buckets),
        out_shape=[jax.ShapeDtypeStruct(tokens.shape, bf16)] * 2
        + [jax.ShapeDtypeStruct(shape, f32) for shape in wide]
        + [jax.ShapeDtypeStruct(a.shape, f32) for a in (grad_in, grad_out)]
        + [jax.ShapeDtypeStruct(shape, f32) for shape in small_shapes],
        grid=(n_experts,),
        in_specs=[rows, rows, own(attn), own(grad_in), own(grad_out), whole(small.shape)],
        out_specs=[rows, rows]
        + [whole(shape) for shape in wide]
        + [own(grad_in), own(grad_out)]
        + [whole(shape) for shape in small_shapes],
        compiler_params=pltpu.CompilerParams(vmem_limit_bytes=VMEM_LIMIT),
        name="widen",
    )(out_rows, tokens, attn, grad_in, grad_out, small)


def per_device(
    tokens,
    piece_starts,
    routes,
    buckets,
    attn_q,
    attn_k,
    attn_v,
    attn_o,
    expert_in,
    expert_out,
    gain_attn,
    gain_ffn,
    rel_table,
    router,
    cotangent,
):
    n_rep, n_fsdp, n_seq = (lax.axis_size(a) for a in ("rep", "fsdp", "seq"))
    rep = lax.axis_index("rep")
    seq = lax.axis_index("seq")
    plane = ("rep", "seq")
    n_rows, width = tokens.shape
    n_buckets, n_heads = rel_table.shape
    head_dim = width // n_heads
    n_experts, part_in, hidden = expert_in.shape
    part_out = expert_out.shape[1]
    part_attn = attn_q.shape[0]
    length = n_rows * n_seq
    assert n_experts == n_rep == 4 and n_seq == 2 and 2 * head_dim == LANES
    pairs = n_heads // 2

    place = piece_starts[0]
    near = n_fsdp == 4 and part_attn % 16 == 0
    pick = lambda array: lax.dynamic_index_in_dim(array, rep, 0, keepdims=False)
    span = -(-buckets.shape[0] // LANES) * LANES
    if near:
        weights, x_all, w_in, w_out, pack = gather(
            (attn_q, attn_k, attn_v, attn_o),
            tokens,
            expert_in,
            expert_out,
            n_fsdp,
            (router.T, gain_attn, gain_ffn, buckets, rel_table.T, routes.T),
            span,
        )
    else:
        attn_own = pick(jnp.stack([attn_q, attn_k, attn_v, attn_o]))
        attn_line = lax.all_gather(attn_own, "fsdp", axis=0, tiled=False)
        attn_all = lax.all_gather(attn_line, plane, axis=0, tiled=False)
        attn_all = attn_all.reshape(n_rep, n_seq, n_fsdp, part_attn, width)
        weights = attn_all.transpose(0, 2, 1, 3, 4).reshape(n_rep, width, width)
        x_all = lax.all_gather(tokens, "seq", axis=0, tiled=True)
        in_own = pick(expert_in).reshape(part_in, n_fsdp, n_seq, part_out)
        in_own = in_own.transpose(2, 0, 1, 3).reshape(n_seq, part_in, n_fsdp * part_out)
        in_pair = lax.all_to_all(in_own, "seq", split_axis=0, concat_axis=0, tiled=True)
        in_pair = in_pair.reshape(n_seq * part_in, n_fsdp * part_out)
        w_in = lax.all_gather(in_pair, "fsdp", axis=0, tiled=True)
        w_out = lax.all_gather(pick(expert_out), "fsdp", axis=0, tiled=True)
        dy_all = lax.all_gather(cotangent, plane, axis=0, tiled=True)
        pack = pack_small(router, gain_attn, gain_ffn, buckets, rel_table, routes, span)

    q, k, v, o, p, x_mid, message, probs, h_all, *gathered = attention_forward(
        place,
        x_all,
        weights,
        pack,
        n_rows,
        n_experts,
        head_dim,
        Background(n_fsdp) if near else None,
        (cotangent, w_in) if near else (),
    )
    behind = ()
    if near:
        dy_all, w_in = gathered
        w_in = w_in.reshape(width, n_fsdp * part_out)
        message_all, act, slope, dw_out, w_out = experts_up(
            message, dy_all, w_in, expert_out, w_out, n_experts, n_fsdp
        )
        back, out_half, dw_in, sum_out = experts_down(
            message_all,
            dy_all,
            act,
            slope,
            w_in,
            w_out.reshape(n_fsdp * part_out, width),
            dw_out.reshape(n_fsdp, part_out, width),
            n_experts,
            n_fsdp,
        )
        behind = (out_half, dw_in.reshape(n_fsdp, n_seq * part_in, n_fsdp * part_out))
    else:
        message_all = lax.all_gather(message, plane, axis=0, tiled=True)
        out_part, back_part, dw_in, dw_out = experts(
            rep[None].astype(jnp.int32), message_all, dy_all, w_in, w_out, n_experts, n_rows
        )
        back = lax.psum_scatter(back_part, plane, scatter_dimension=0, tiled=True)
        out_sum = lax.psum_scatter(out_part, plane, scatter_dimension=0, tiled=True)
        out_rows = (x_mid + out_sum.astype(f32)).astype(bf16)

    grads = attention_backward(
        back,
        cotangent,
        x_mid,
        message,
        probs,
        pack,
        h_all,
        weights,
        q,
        k,
        v,
        o,
        p,
        x_all,
        n_experts,
        head_dim,
        BackgroundBack(n_fsdp) if near else None,
        behind,
    )
    if near:
        dh_own, dh_other, dx_mid, dgain_two, drouter, ddist, dgain_one = grads[:7]
        out_rows, sum_in, plane_sum, last_grads = grads[7:]
        attn_sum, grad_in, grad_out, grad_tokens, small = finish(
            plane_sum,
            last_grads,
            sum_in.reshape(n_seq, part_in, n_fsdp * part_out),
            sum_out,
            dh_other,
            dh_own,
            dx_mid,
            tokens,
            pack,
            dgain_one,
            dgain_two,
            drouter,
            ddist,
            n_fsdp,
            n_experts,
            n_heads,
            hidden,
        )
        out_rows, grad_tokens, *wide, grad_one, grad_two, grad_table, grad_router = widen(
            out_rows, grad_tokens, attn_sum, grad_in, grad_out, small, n_heads, n_buckets
        )
        return (
            out_rows,
            grad_tokens,
            *wide,
            grad_one,
            grad_two,
            grad_table.T,
            grad_router.T,
        )
    dwq, dwk, dwv, dwo, dh_own, dh_other, dx_mid, dgain_two, drouter, ddist, dgain_one = grads
    sum_out = lax.psum_scatter(dw_out, "fsdp", scatter_dimension=0, tiled=True)
    sum_in = lax.psum_scatter(dw_in, "fsdp", scatter_dimension=0, tiled=True)
    sum_in = sum_in.reshape(n_seq, part_in, n_fsdp * part_out)
    sum_in = lax.all_to_all(sum_in, "seq", split_axis=0, concat_axis=0, tiled=True)
    sum_in = sum_in.reshape(n_seq, part_in, n_fsdp, part_out).transpose(1, 2, 0, 3)
    sum_in = sum_in.reshape(part_in, hidden)
    grad_out = lax.all_gather(sum_out, "rep", axis=0, tiled=False)
    grad_in = lax.all_gather(sum_in, "rep", axis=0, tiled=False)
    swap = [(0, 1), (1, 0)]
    dh_one = dh_own + lax.ppermute(dh_other, "seq", swap).astype(f32)
    dx, _ = norm_back(tokens.astype(f32), gain_attn[None, :], dh_one)
    grad_tokens = (dx_mid + dx).astype(bf16)
    attn_grads = jnp.stack([dwq, dwk, dwv, dwo])
    attn_grads = attn_grads.reshape(n_rep, n_fsdp, n_seq, part_attn, width)
    attn_grads = attn_grads.transpose(0, 2, 1, 3, 4)
    attn_grads = attn_grads.reshape(n_rep * n_seq * n_fsdp * part_attn, width)
    attn_sum = lax.psum_scatter(attn_grads, plane, scatter_dimension=0, tiled=True)
    attn_sum = lax.psum_scatter(attn_sum, "fsdp", scatter_dimension=0, tiled=True)
    attn_sum = lax.all_gather(attn_sum, "rep", axis=0, tiled=False)
    ddist = ddist[:n_heads, : buckets.shape[0]]
    match = (buckets[:, None] == jnp.arange(n_buckets)[None, :]).astype(f32)
    table = lax.dot_general(
        match,
        ddist,
        (((0,), (1,)), ((), ())),
        precision=highest,
        preferred_element_type=f32,
    )
    grad_one, grad_two, grad_table, grad_router = lax.psum(
        (dgain_one[0], dgain_two[0], table, drouter[:n_experts].T), ("rep", "fsdp", "seq")
    )
    attn_sum = attn_sum.astype(f32)
    return (
        out_rows,
        grad_tokens,
        attn_sum[0],
        attn_sum[1],
        attn_sum[2],
        attn_sum[3],
        grad_in.astype(f32),
        grad_out.astype(f32),
        grad_one,
        grad_two,
        grad_table,
        grad_router,
    )


def solution(mesh):
    rows = P(("rep", "fsdp", "seq"), None)
    owned = P(("fsdp", "seq"), None)
    expert = P(None, ("fsdp", "seq"), None)
    in_specs = (
        rows,
        P(("rep", "fsdp"), None),
        rows,
        P(),
        owned,
        owned,
        owned,
        owned,
        expert,
        expert,
        P(),
        P(),
        P(),
        P(),
        rows,
    )
    out_specs = (
        rows,
        rows,
        owned,
        owned,
        owned,
        owned,
        expert,
        expert,
        P(),
        P(),
        P(),
        P(),
    )
    return jax.shard_map(
        per_device, mesh=mesh, in_specs=in_specs, out_specs=out_specs, check_vma=False
    )
```

```python
import functools

import jax
import jax.numpy as jnp
from jax import lax
from jax.experimental import pallas as pl
from jax.experimental.pallas import tpu as pltpu
from jax.sharding import PartitionSpec as P

PIECE = 256
LANES = 128
epsilon = 1e-06
masked_out = -1e30
highest = lax.Precision.HIGHEST
f32 = jnp.float32
bf16 = jnp.bfloat16
VMEM_LIMIT = 58 * 1024 * 1024


def dot(a, b):
    return jnp.dot(a, b, preferred_element_type=f32)


def dot_t(a, b):
    return lax.dot_general(a, b, (((1,), (1,)), ((), ())), preferred_element_type=f32)


def t_dot(a, b):
    return lax.dot_general(a, b, (((0,), (0,)), ((), ())), preferred_element_type=f32)


def exact_dot(a, b):
    return jnp.dot(a, b, precision=highest, preferred_element_type=f32)


def exact_dot_t(a, b):
    return lax.dot_general(
        a, b, (((1,), (1,)), ((), ())), precision=highest, preferred_element_type=f32
    )


def inverse_rms(values):
    return lax.rsqrt(jnp.mean(values * values, -1, keepdims=True) + epsilon)


def norm_back(values, gain, grad):
    scale = inverse_rms(values)
    scaled = values * scale
    grad_gain = jnp.sum(grad * scaled, 0, keepdims=True)
    weighted = gain * grad
    grad_values = scale * weighted - (
        values * (scale * scale * scale) * jnp.mean(weighted * values, -1, keepdims=True)
    )
    return grad_values, grad_gain


def first_row(rows):
    return lax.axis_index("seq") * rows


def make_mask(place_ref, mask_ref):
    shape = mask_ref.shape
    pos_q = first_row(shape[0]) + lax.broadcasted_iota(jnp.int32, shape, 0)
    pos_k = lax.broadcasted_iota(jnp.int32, shape, 1)
    allowed = pos_k <= pos_q
    for piece in range(2):
        start = place_ref[piece]
        in_q = (pos_q >= start) & (pos_q < start + PIECE)
        in_k = (pos_k >= start) & (pos_k < start + PIECE)
        allowed = allowed | (in_q & in_k)
    mask_ref[...] = jnp.where(allowed, 0.0, masked_out)


def spread(row, block, width):
    return pltpu.roll(
        jnp.broadcast_to(row, (block, width)), width - (block - 1), 1, stride=1, stride_axis=0
    )


def by_head(values, first_half):
    zero = jnp.zeros((), values.dtype)
    return jnp.concatenate(
        [jnp.where(first_half, values, zero), jnp.where(first_half, zero, values)]
    )


def of_head(stacked, first_half):
    block = stacked.shape[0] // 2
    return jnp.where(first_half, stacked[:block], stacked[block:])


def gather_diagonals(sums):
    rows = sums.shape[0]
    while rows > 1:
        half = rows // 2
        sums = pltpu.roll(sums[:half], half, 1) + sums[half:]
        rows = half
    return sums


def chosen_experts(pack_ref, shape):
    lane = lax.broadcasted_iota(jnp.int32, shape, 1).astype(f32)
    routes = pack_ref[24:32, : shape[0]].T
    return (lane == routes[:, 0:1]) | (lane == routes[:, 1:2])


def pack_small(router, gain_attn, gain_ffn, buckets, rel_table, routes, span):
    def rows(array, count):
        array = array.astype(f32)
        return jnp.pad(array, ((0, count - array.shape[0]), (0, span - array.shape[1])))

    return jnp.concatenate(
        [
            rows(router.T, 4),
            rows(gain_attn[None, :], 1),
            rows(gain_ffn[None, :], 1),
            rows(buckets[None, :], 2),
            rows(rel_table.T, 16),
            rows(routes.T, 8),
        ]
    )


def router_rows(pack_ref, n_experts, width):
    first = pack_ref[0:8, :width]
    row = lax.broadcasted_iota(jnp.int32, first.shape, 0)
    first = jnp.where(row < n_experts, first, 0.0)
    return jnp.concatenate([first, jnp.zeros((LANES - 8, width), f32)])


def bucket_match(pack_ref):
    shape = (LANES, pack_ref.shape[1])
    bucket = lax.broadcasted_iota(jnp.int32, shape, 0).astype(f32)
    return (bucket == pack_ref[6:7, :]).astype(f32)


def distances(pack_ref):
    return exact_dot(pack_ref[8:24, :LANES], bucket_match(pack_ref))


MESH = pl.DeviceIdType.MESH


class Place:
    def __init__(self, n_fsdp):
        self.rep = lax.axis_index("rep")
        self.line = lax.axis_index("fsdp")
        self.seq = lax.axis_index("seq")
        self.n_fsdp = n_fsdp
        self.row = self.rep // 2
        self.core = self.rep % 2

    def mate(self):
        return (self.row * 2 + 1 - self.core, self.line, self.seq)

    def chip(self, rows, columns, core=None):
        core = self.core if core is None else core
        row = (self.row + rows) % 2
        return (row * 2 + core, self.line, (self.seq + columns) % 2)

    def along(self, steps):
        return (self.rep, (self.line + steps) % self.n_fsdp, self.seq)


def meet(partners):
    barrier = pltpu.get_barrier_semaphore()
    for partner in partners:
        pl.semaphore_signal(barrier, inc=1, device_id=partner, device_id_type=MESH)
    pl.semaphore_wait(barrier, len(partners))


class Wires:
    def __init__(self, send, recv):
        self.send, self.recv = send, recv
        self.names = {}

    def copy(self, name, source, target, device):
        index = self.names.setdefault(name, len(self.names))
        return pltpu.make_async_remote_copy(
            src_ref=source,
            dst_ref=target,
            send_sem=self.send.at[index],
            recv_sem=self.recv.at[index],
            device_id=device,
            device_id_type=MESH,
        )


class Planned:
    def __init__(self, plan, send, recv):
        self.plan, self.send, self.recv = plan, send, recv
        self.order = list(plan)

    def __getitem__(self, name):
        source, target, device = self.plan[name]
        index = self.order.index(name)
        return pltpu.make_async_remote_copy(
            src_ref=source,
            dst_ref=target,
            send_sem=self.send.at[index],
            recv_sem=self.recv.at[index],
            device_id=device,
            device_id_type=MESH,
        )


def gather_kernel(
    n_fsdp,
    part_out,
    attn_q,
    attn_k,
    attn_v,
    attn_o,
    tokens,
    expert_in,
    expert_out,
    router,
    gain_attn,
    gain_ffn,
    buckets,
    rel_table,
    routes,
    weights,
    x_all,
    w_in,
    w_out,
    pack,
    attn_held,
    tokens_held,
    in_held,
    send,
    recv,
    local,
):
    me = Place(n_fsdp)
    rep, line, seq = me.rep, me.line, me.seq
    far_row = (me.row + 1) % 2 * 2 + me.core
    mate, across, beside = me.mate(), me.chip(1, 0), me.chip(0, 1)
    part_in = expert_in.shape[1]
    wires = Wires(send, recv)
    meet([mate, across, beside, me.along(1), me.along(-1), me.along(2)])
    started = []

    def start(copy):
        copy.start()
        started.append(copy)
        return copy

    for i, matrix in enumerate((attn_q, attn_k, attn_v, attn_o)):

        @pl.when(rep == i)
        def _():
            own = pltpu.make_async_copy(matrix, attn_held, local.at[0])
            own.start()
            own.wait()

    mine = lambda z, r=rep, x=seq: weights.at[r, z, x]
    shifts = (0, 1, -1, 2)
    at = {0: line}
    z_copies = {}
    for shift in shifts[1:]:
        at[shift] = (line - shift) % n_fsdp
        z_copies[shift] = start(
            wires.copy(("z", shift), attn_held, mine(line), me.along(shift))
        )
    x_copies, y_copies, c_copies, far_copies = {}, {}, [], {}

    def spread_out(shift):
        z = at[shift]
        source = mine(z) if shift else attn_held
        x_copies[shift] = start(wires.copy(("x", shift), source, mine(z), beside))
        y_copies[shift] = start(wires.copy(("y", shift), source, mine(z), across))
        c_copies.append(start(wires.copy(("c", shift), source, mine(z), mate)))

    spread_out(0)
    columns = lambda z, x: pl.ds(pl.multiple_of((z * 2 + x) * part_out, LANES), part_out)
    rows = lambda x: pl.ds(pl.multiple_of(x * part_in, part_in), part_in)
    in_x, in_own = [], []
    for z in range(n_fsdp):
        here = pl.ds(z * part_out, part_out)
        target = w_in.at[line, rows(seq), here]
        in_x.append(
            start(wires.copy(("in", z), expert_in.at[rep, :, columns(z, 1 - seq)], target, beside))
        )
        copy = pltpu.make_async_copy(
            expert_in.at[rep, :, columns(z, seq)], in_held.at[:, here], local.at[1 + z]
        )
        copy.start()
        in_own.append(copy)
    own_attn = pltpu.make_async_copy(attn_held, mine(line), local.at[0])
    own_attn.start()
    x_own = Bounce(tokens, tokens_held, x_all.at[seq], local.at[pl.ds(n_fsdp + 1, 2)])
    x_own.start()
    for copy in in_own:
        copy.wait()
    own_in = pltpu.make_async_copy(in_held, w_in.at[line, rows(seq)], local.at[n_fsdp + 3])
    own_in.start()
    x_own.turn()
    pack[...] = jnp.zeros_like(pack)
    pack[0 : router.shape[0], : router.shape[1]] = router[...]
    pack[4, : gain_attn.shape[0]] = gain_attn[...]
    pack[5, : gain_ffn.shape[0]] = gain_ffn[...]
    pack[6, : buckets.shape[0]] = buckets[...].astype(f32)
    pack[8 : 8 + rel_table.shape[0], : rel_table.shape[1]] = rel_table[...]
    pack[24:26, : routes.shape[1]] = routes[...].astype(f32)
    for shift in shifts[1:]:
        z_copies[shift].wait_recv()
        spread_out(shift)
    for copy in in_x:
        copy.wait_recv()
    own_in.wait()
    in_copies = []
    for i, shift in enumerate((1, -1)):
        half = w_in.at[line, pl.ds(i * part_in, part_in)]
        in_copies.append(start(wires.copy(("line", shift), half, half, me.along(shift))))
    plan = line_plan(me, expert_out.at[rep], w_out)
    in_copies.append(start(wires.copy("out", *plan["first", 1])))
    token_copy = start(wires.copy("tokens", tokens, x_all.at[seq], beside))
    for shift in shifts:
        z = at[shift]
        x_copies[shift].wait_recv()
        near = mine(z, rep, 1 - seq)
        far_copies[shift] = start(wires.copy(("far", shift), near, near, across))
        c_copies.append(start(wires.copy(("cx", shift), near, near, mate)))
    for shift in shifts:
        z = at[shift]
        y_copies[shift].wait_recv()
        there = mine(z, far_row, seq)
        c_copies.append(start(wires.copy(("cy", shift), there, there, mate)))
    for shift in shifts:
        z = at[shift]
        far_copies[shift].wait_recv()
        there = mine(z, far_row, 1 - seq)
        c_copies.append(start(wires.copy(("cf", shift), there, there, mate)))
    for copy in c_copies + in_copies + [token_copy]:
        copy.wait_recv()
    x_own.wait()
    own_attn.wait()
    for copy in started:
        copy.wait_send()


def gather(attn, tokens, expert_in, expert_out, n_fsdp, small, span):
    part_attn, width = attn[0].shape
    n_rows = tokens.shape[0]
    n_experts, part_in, hidden = expert_in.shape
    part_out = expert_out.shape[1]
    anywhere = pl.BlockSpec(memory_space=pl.ANY)
    inside = pl.BlockSpec(memory_space=pltpu.VMEM)
    weights, x_all, w_in, w_out, pack = pl.pallas_call(
        functools.partial(gather_kernel, n_fsdp, part_out),
        out_shape=[
            jax.ShapeDtypeStruct((4, n_fsdp, 2, part_attn, width), bf16),
            jax.ShapeDtypeStruct((2, n_rows, width), bf16),
            jax.ShapeDtypeStruct((n_fsdp, 2 * part_in, n_fsdp * part_out), bf16),
            jax.ShapeDtypeStruct((n_fsdp,) + expert_out.shape[1:], bf16),
            jax.ShapeDtypeStruct((32, span), f32),
        ],
        in_specs=[anywhere] * 7 + [inside] * 6,
        out_specs=[anywhere] * 4 + [inside],
        scratch_shapes=[
            pltpu.VMEM((part_attn, width), bf16),
            pltpu.VMEM((n_rows, width), bf16),
            pltpu.VMEM((part_in, n_fsdp * part_out), bf16),
            pltpu.SemaphoreType.DMA((48,)),
            pltpu.SemaphoreType.DMA((48,)),
            pltpu.SemaphoreType.DMA((8,)),
        ],
        compiler_params=pltpu.CompilerParams(collective_id=0, has_side_effects=True),
        name="gather_weights",
    )(*attn, tokens, expert_in, expert_out, *small)
    return (
        weights.reshape(4, n_fsdp * 2 * part_attn, width),
        x_all.reshape(2 * n_rows, width),
        w_in,
        w_out,
        pack,
    )


class Bounce:
    def __init__(self, source, held, target, sems):
        self.load = lambda: pltpu.make_async_copy(source, held, sems.at[0])
        self.store = lambda: pltpu.make_async_copy(held, target, sems.at[1])

    def start(self):
        self.load().start()

    def turn(self):
        self.load().wait()
        self.store().start()

    def wait(self):
        self.store().wait()


def line_plan(me, own, pieces):
    rows = pieces.shape[1] // 2
    plan = {}
    for i, shift in enumerate((1, -1)):
        first, rest = pl.ds(i * rows, rows), pl.ds((1 - i) * rows, rows)
        target = pieces.at[me.line]
        piece = pieces.at[(me.line - shift) % me.n_fsdp, first]
        plan["first", shift] = (own.at[first], target.at[first], me.along(shift))
        plan["rest", shift] = (own.at[rest], target.at[rest], me.along(shift))
        plan["relay", shift] = (piece, piece, me.along(shift))
    return plan


class Background:
    n_in, n_out = 2, 2

    def __init__(self, n_fsdp):
        self.n_fsdp = n_fsdp

    def out_shape(self, dy, w_in):
        return [
            jax.ShapeDtypeStruct((8,) + dy.shape, bf16),
            jax.ShapeDtypeStruct(w_in.shape, bf16),
        ]

    def scratch(self, dy, w_in):
        return [
            pltpu.SemaphoreType.DMA((16,)),
            pltpu.SemaphoreType.DMA((16,)),
            pltpu.SemaphoreType.DMA((2,)),
            pltpu.VMEM(dy.shape, bf16),
        ]

    def run(self, step, before, ins, outs, scratch):
        dy, _ = ins
        dy_all, w_in = outs
        send, recv, local, dy_held = scratch
        me = Place(self.n_fsdp)
        half = dy.shape[0] // 2
        first, second = pl.ds(0, half), pl.ds(half, half)
        core = me.core
        own = 6 + core
        mate, across, beside = me.mate(), me.chip(1, 0), me.chip(0, 1)
        slot = dy_all.at
        plan = {
            "x": (dy, slot[core], beside),
            "y": (dy, slot[2 + core], across),
            "c0": (dy, slot[own], mate),
            "c1": (slot[core], slot[core], mate),
            "c2": (slot[2 + core], slot[2 + core], mate),
            "c3": (slot[4 + core], slot[4 + core], mate),
            "xy": (slot[core, first], slot[4 + core, first], across),
            "yx": (slot[2 + core, second], slot[4 + core, second], beside),
        }
        line = line_plan(me, w_in.at[me.line], w_in)
        plan |= {name: line[name] for name in line if name[0] != "first"}
        copies = Planned(plan, send, recv)
        own_dy = Bounce(dy, dy_held, slot[own], local.at[pl.ds(0, 2)])
        if before:

            @pl.when(step == 0)
            def _():
                meet([mate, across, beside, me.along(1), me.along(-1)])
                for name in line:
                    if name[0] != "first":
                        copies[name].start()
                for name in ("x", "y", "c0"):
                    copies[name].start()
                own_dy.start()

            @pl.when(step == 3)
            def _():
                own_dy.turn()
                copies["x"].wait_recv()
                copies["xy"].start()
                copies["c1"].start()
                copies["y"].wait_recv()
                copies["yx"].start()
                copies["c2"].start()

            return

        @pl.when(step == pl.num_programs(0) - 1)
        def _():
            copies["xy"].wait_recv()
            copies["yx"].wait_recv()
            copies["c3"].start()
            for name in plan:
                if name not in ("x", "y", "xy", "yx"):
                    copies[name].wait_recv()
            own_dy.wait()
            for name in plan:
                copies[name].wait_send()


def forward_kernel(
    background,
    n_experts,
    head_dim,
    place_ref,
    x_ref,
    wq_ref,
    wk_ref,
    wv_ref,
    wo_ref,
    pack_ref,
    *refs,
):
    step = pl.program_id(0)
    n_in, n_out = (background.n_in, background.n_out) if background else (0, 0)
    behind_in, refs = refs[:n_in], refs[n_in:]
    q_out, k_out, v_out, o_out, p_out, x_mid_out, message_out, probs_out, h_out = refs[:9]
    behind_out, refs = refs[9 : 9 + n_out], refs[9 + n_out :]
    total_ref, mask_ref, bias_ref, dist_ref = refs[:4]
    if background:
        background.run(step, True, behind_in, behind_out, refs[4:])
    rows = x_mid_out.shape[0]
    length, width = x_ref.shape
    own = pl.ds(pl.multiple_of(first_row(rows), rows), rows)

    @pl.when(step == 0)
    def _():
        values = x_ref[...].astype(f32)
        gain_one = pack_ref[4:5, :width]
        h_out[...] = (values * inverse_rms(values) * gain_one).astype(bf16)
        dist_ref[...] = distances(pack_ref)
        total_ref[...] = jnp.zeros_like(total_ref)
        make_mask(place_ref, mask_ref)

    h_all = h_out[...]
    q_low = dot(h_out[own, :], wq_ref[...]).astype(bf16) * (head_dim**-0.5)
    kv_low = dot(h_all, jnp.concatenate([wk_ref[...], wv_ref[...]], 1)).astype(bf16)
    k_low, v_low = kv_low[:, :LANES], kv_low[:, LANES:]
    q_out[...] = q_low
    k_out[...] = k_low
    v_out[...] = v_low
    block = LANES
    span = pack_ref.shape[1]
    first_half = lax.broadcasted_iota(jnp.int32, (block, LANES), 1) < head_dim
    for head in range(2):
        bias_ref[head] = spread(dist_ref[pl.ds(2 * step + head, 1), :], block, span)
    for b in range(rows // block):
        here = slice(b * block, (b + 1) * block)
        offset = pl.multiple_of(length - LANES - block * b - first_row(rows), LANES)
        scores = dot_t(by_head(q_low[here], first_half), k_low).reshape(2, block, length)
        scores = scores + bias_ref[:, :, pl.ds(offset, length)] + mask_ref[here, :]
        top = jnp.max(scores, -1, keepdims=True)
        exp_scores = jnp.exp(scores - top)
        total = jnp.sum(exp_scores, -1, keepdims=True)
        probs = (exp_scores * (1.0 / total)).astype(bf16)
        p_out[:, here, :] = probs
        heads = dot(probs.reshape(2 * block, length), v_low)
        o_out[here, :] = of_head(heads, first_half).astype(bf16)
    total_ref[...] += dot(o_out[...], wo_ref[...])

    @pl.when(step == pl.num_programs(0) - 1)
    def _():
        x_mid = x_ref[own, :].astype(f32) + total_ref[...]
        x_mid_out[...] = x_mid
        h_two = (x_mid * inverse_rms(x_mid) * pack_ref[5:6, :width]).astype(bf16)
        message_out[:, :width] = h_two
        logits = exact_dot_t(h_two.astype(f32), router_rows(pack_ref, n_experts, width))
        lane = lax.broadcasted_iota(jnp.int32, logits.shape, 1)
        logits = jnp.where(lane < n_experts, logits, masked_out)
        exp_logits = jnp.exp(logits - jnp.max(logits, -1, keepdims=True))
        probs = exp_logits / jnp.sum(exp_logits, -1, keepdims=True)
        probs_out[...] = probs
        chosen = jnp.where(chosen_experts(pack_ref, probs.shape), probs, 0.0)
        gate = chosen / jnp.sum(chosen, -1, keepdims=True)
        high = gate.astype(bf16)
        low = gate - high.astype(f32)
        message_out[:, width:] = (high.astype(f32) + pltpu.roll(low, n_experts, 1)).astype(bf16)

    if background:
        background.run(step, False, behind_in, behind_out, refs[4:])


def attention_forward(
    place,
    x_all,
    weights,
    pack,
    n_rows,
    n_experts,
    head_dim,
    background=None,
    behind=(),
):
    length, width = x_all.shape
    pairs = width // LANES
    span = pack.shape[1]
    whole = lambda shape: pl.BlockSpec(shape, lambda p, *_: (0,) * len(shape))
    columns = lambda rows: pl.BlockSpec((rows, LANES), lambda p, *_: (0, p))
    matrix = lambda i: pl.BlockSpec((None, width, LANES), lambda p, *_: (i, 0, p))
    out_shape = [
        jax.ShapeDtypeStruct((n_rows, width), bf16),
        jax.ShapeDtypeStruct((length, width), bf16),
        jax.ShapeDtypeStruct((length, width), bf16),
        jax.ShapeDtypeStruct((n_rows, width), bf16),
        jax.ShapeDtypeStruct((pairs, 2, n_rows, length), bf16),
        jax.ShapeDtypeStruct((n_rows, width), f32),
        jax.ShapeDtypeStruct((n_rows, width + LANES), bf16),
        jax.ShapeDtypeStruct((n_rows, LANES), f32),
        jax.ShapeDtypeStruct((length, width), bf16),
    ]
    anywhere = pl.BlockSpec(memory_space=pl.ANY)
    params, aliases = {}, {}
    if background:
        out_shape += background.out_shape(*behind)
        params = {"collective_id": 1, "has_side_effects": True}
        aliases = {8: 10}
    return pl.pallas_call(
        functools.partial(forward_kernel, background, n_experts, head_dim),
        out_shape=out_shape,
        grid_spec=pltpu.PrefetchScalarGridSpec(
            num_scalar_prefetch=1,
            grid=(pairs,),
            in_specs=[
                whole((length, width)),
                matrix(0),
                matrix(1),
                matrix(2),
                pl.BlockSpec((None, LANES, width), lambda p, *_: (3, p, 0)),
                whole(pack.shape),
            ]
            + [anywhere] * len(behind),
            out_specs=[
                columns(n_rows),
                columns(length),
                columns(length),
                columns(n_rows),
                pl.BlockSpec((None, 2, n_rows, length), lambda p, *_: (p, 0, 0, 0)),
                whole((n_rows, width)),
                whole((n_rows, width + LANES)),
                whole((n_rows, LANES)),
                whole((length, width)),
            ]
            + [anywhere] * (background.n_out if background else 0),
            scratch_shapes=[
                pltpu.VMEM((n_rows, width), f32),
                pltpu.VMEM((n_rows, length), f32),
                pltpu.VMEM((2, LANES, span), f32),
                pltpu.VMEM((16, span), f32),
            ]
            + (background.scratch(*behind) if background else []),
        ),
        input_output_aliases=aliases,
        compiler_params=pltpu.CompilerParams(vmem_limit_bytes=VMEM_LIMIT, **params),
        cost_estimate=pl.CostEstimate(
            flops=20_000_000_000, transcendentals=0, bytes_accessed=20_000_000
        ),
        name="attention_forward",
    )(
        place,
        x_all,
        weights,
        weights,
        weights,
        weights,
        pack,
        *behind,
    )


GELU_A = 0.7978845608028654
GELU_B = 0.044715 * GELU_A


def experts_kernel(
    n_experts,
    chunk,
    expert_ref,
    message_ref,
    dy_ref,
    w_in_ref,
    w_out_ref,
    out_ref,
    dh_ref,
    dw_in_ref,
    dw_out_ref,
    dw_in_acc,
    dw_out_acc,
):
    step = pl.program_id(0)
    width = dy_ref.shape[1]
    hidden = w_in_ref.shape[1]
    expert = expert_ref[0]

    @pl.when(step == 0)
    def _():
        dw_in_acc[...] = jnp.zeros_like(dw_in_acc)
        dw_out_acc[...] = jnp.zeros_like(dw_out_acc)

    h = message_ref[:, :width]
    extra = message_ref[:, width:].astype(f32)
    lane = lax.broadcasted_iota(jnp.int32, extra.shape, 1)
    mine = (lane == expert) | (lane == expert + n_experts)
    gate = jnp.sum(jnp.where(mine, extra, 0.0), -1, keepdims=True)
    dy = dy_ref[...]
    out_total = None
    dh_total = None
    dgate = None
    for start in range(0, hidden, chunk):
        part = slice(start, start + chunk)
        up = dot(h, w_in_ref[:, part])
        dact = dot_t(dy, w_out_ref[part, :])
        square = up * up
        tanh = jnp.tanh(up * (GELU_A + GELU_B * square))
        half = 0.5 * up
        more = 1.0 + tanh
        act = half * more
        slope = 0.5 * more + half * (1.0 - tanh * tanh) * (GELU_A + 3.0 * GELU_B * square)
        gated = (gate * act).astype(bf16)
        dgate_part = jnp.sum(act * dact, -1, keepdims=True)
        dup = (gate * dact * slope).astype(bf16)
        out_part = dot(gated, w_out_ref[part, :])
        dh_part = dot_t(dup, w_in_ref[:, part])
        out_total = out_part if out_total is None else out_total + out_part
        dh_total = dh_part if dh_total is None else dh_total + dh_part
        dgate = dgate_part if dgate is None else dgate + dgate_part
        dw_out_acc[part, :] += t_dot(gated, dy)
        dw_in_acc[:, part] += t_dot(h, dup)
    out_ref[...] = out_total.astype(bf16)
    dh_ref[:, :width] = dh_total.astype(bf16)
    high = dgate.astype(bf16).astype(f32)
    low = dgate - high
    dh_ref[:, width:] = jnp.where(
        lane == expert, high, jnp.where(lane == expert + n_experts, low, 0.0)
    ).astype(bf16)

    @pl.when(step == pl.num_programs(0) - 1)
    def _():
        dw_in_ref[...] = dw_in_acc[...].astype(bf16)
        dw_out_ref[...] = dw_out_acc[...].astype(bf16)


def experts(expert, message, dy, w_in, w_out, n_experts, block):
    tokens, width = dy.shape
    hidden = w_in.shape[1]
    whole = lambda shape: pl.BlockSpec(shape, lambda i, *_: (0,) * len(shape))
    rows = lambda columns: pl.BlockSpec((block, columns), lambda i, *_: (i, 0))
    return pl.pallas_call(
        functools.partial(experts_kernel, n_experts, 512),
        out_shape=[
            jax.ShapeDtypeStruct((tokens, width), bf16),
            jax.ShapeDtypeStruct((tokens, width + LANES), bf16),
            jax.ShapeDtypeStruct((width, hidden), bf16),
            jax.ShapeDtypeStruct((hidden, width), bf16),
        ],
        grid_spec=pltpu.PrefetchScalarGridSpec(
            num_scalar_prefetch=1,
            grid=(tokens // block,),
            in_specs=[
                rows(width + LANES),
                rows(width),
                whole((width, hidden)),
                whole((hidden, width)),
            ],
            out_specs=[
                rows(width),
                rows(width + LANES),
                whole((width, hidden)),
                whole((hidden, width)),
            ],
            scratch_shapes=[
                pltpu.VMEM((width, hidden), f32),
                pltpu.VMEM((hidden, width), f32),
            ],
        ),
        compiler_params=pltpu.CompilerParams(vmem_limit_bytes=VMEM_LIMIT),
        cost_estimate=pl.CostEstimate(
            flops=60_000_000_000, transcendentals=0, bytes_accessed=30_000_000
        ),
        name="experts",
    )(expert, message, dy, w_in, w_out)


def plane_slot(j):
    return (j // 2 + 1) % 4, j % 2


def down_order(step):
    inner = (13 - step) // 8
    return inner * ((step + 4) % 6) + (1 - inner) * step


def up_order(step):
    other, corner = (step + 6) // 8, (step + 2) // 8
    pair = 3 * (1 - other) + (other - corner) * (step % 2) + 2 * corner
    return pair, (step % 2 + step // 4 - corner) % 2


def experts_up_kernel(
    n_experts,
    chunk,
    n_fsdp,
    message_ref,
    dy_ref,
    w_in,
    expert_out,
    _,
    h_out,
    act_out,
    slope_out,
    dw_out_ref,
    w_out,
    h_ref,
    dw_out_acc,
    w_in_ref,
    gated_ref,
    dy_pair_ref,
    out_held,
    send,
    recv,
    local,
):
    step = pl.program_id(0)
    last = pl.num_programs(0) - 1
    me = Place(n_fsdp)
    core = me.core
    half, width = dy_ref.shape[1:]
    rows = 2 * half
    hidden = w_in_ref.shape[1]
    mate, across, beside = me.mate(), me.chip(1, 0), me.chip(0, 1)
    block = h_ref.at
    plan = {
        "x0": (message_ref.at[0], block[0, core, 0], beside),
        "x1": (message_ref.at[1], block[0, core, 1], beside),
        "y0": (message_ref.at[0], block[1, core, 0], across),
        "y1": (message_ref.at[1], block[1, core, 1], across),
        "xy": (block[0, core, 0], block[2, core, 0], across),
        "yx": (block[1, core, 1], block[2, core, 1], beside),
        ("c", 3, 0): (message_ref.at[0], block[3, core, 0], mate),
        ("c", 3, 1): (message_ref.at[1], block[3, core, 1], mate),
    }
    for pair in range(3):
        for side in range(2):
            piece = block[pair, core, side]
            plan["c", pair, side] = (piece, piece, mate)
    plan |= line_plan(me, expert_out.at[me.rep], w_out)
    del plan["first", 1]
    copies = Planned(plan, send, recv)
    own_out = Bounce(expert_out.at[me.rep], out_held, w_out.at[me.line], local.at[pl.ds(0, 2)])

    @pl.when(step == 0)
    def _():
        load = pltpu.make_async_copy(w_in, w_in_ref, local.at[2])
        load.start()
        meet([mate, across, beside, me.along(1), me.along(-1)])
        for name in (("c", 3, 0), ("c", 3, 1), "x0", "y1", ("relay", 1), ("first", -1)):
            copies[name].start()
        own_out.start()
        h_ref[3, core] = message_ref[...]
        dw_out_acc[...] = jnp.zeros_like(dw_out_acc)
        load.wait()

    @pl.when(step == 1)
    def _():
        own_out.turn()
        for name in ("x1", "y0", ("rest", 1), ("rest", -1)):
            copies[name].start()

    @pl.when(step == 2)
    def _():
        copies["x0"].wait_recv()
        copies["c", 0, 0].start()
        copies["xy"].start()
        copies["y1"].wait_recv()
        copies["c", 1, 1].start()
        copies["yx"].start()
        copies["first", -1].wait_recv()
        copies["relay", -1].start()

    @pl.when(step == 3)
    def _():
        copies["x1"].wait_recv()
        copies["c", 0, 1].start()
        copies["y0"].wait_recv()
        copies["c", 1, 0].start()

    @pl.when(step == 5)
    def _():
        copies["xy"].wait_recv()
        copies["c", 2, 0].start()
        copies["yx"].wait_recv()
        copies["c", 2, 1].start()

    for turn in range(8):

        @pl.when(step == turn)
        def _():
            copies[("c",) + up_order(turn)].wait_recv()

    pair, side = up_order(step)
    message = h_ref[pair, :, side]
    expert = me.rep
    h_out[...] = message
    message = message.reshape(rows, message.shape[2])
    h = message[:, :width]
    extra = message[:, width:].astype(f32)
    lane = lax.broadcasted_iota(jnp.int32, extra.shape, 1)
    mine = (lane == expert) | (lane == expert + n_experts)
    gate = jnp.sum(jnp.where(mine, extra, 0.0), -1, keepdims=True)
    place = pl.ds(pl.multiple_of(step % 2 * rows, rows), rows)
    dy_pair_ref[place, :] = dy_ref[...].reshape(rows, width)
    for start in range(0, hidden, chunk):
        piece = slice(start, start + chunk)
        up = dot(h, w_in_ref[:, piece])
        square = up * up
        tanh = jnp.tanh(up * (GELU_A + GELU_B * square))
        halved = 0.5 * up
        more = 1.0 + tanh
        act = (halved * more).astype(bf16)
        slope = 0.5 * more + halved * (1.0 - tanh * tanh) * (GELU_A + 3.0 * GELU_B * square)
        act_out[:, :, piece] = act.reshape(2, half, chunk)
        slope_out[:, :, piece] = slope.astype(bf16).reshape(2, half, chunk)
        gated_ref[place, piece] = (gate * act.astype(f32)).astype(bf16)

    @pl.when(step % 2 == 1)
    def _():
        dw_out_acc[...] += t_dot(gated_ref[...], dy_pair_ref[...])

    @pl.when(step == last)
    def _():
        dw_out_ref[...] = dw_out_acc[...].astype(bf16)
        own_out.wait()
        for shift in (1, -1):
            copies["rest", shift].wait_recv()
            copies["relay", shift].wait_recv()
        for name in plan:
            copies[name].wait_send()


def experts_up(message, dy_all, w_in, expert_out, w_out, n_experts, n_fsdp):
    blocks, rows, width = dy_all.shape
    long = message.shape[1]
    hidden = w_in.shape[1]
    once = pl.Buffered(1)
    whole = lambda shape: pl.BlockSpec(shape, lambda i: (0,) * len(shape), pipeline_mode=once)
    half = rows // 2

    def turn(columns):
        def index(i):
            pair, side = up_order(i)
            return pair, 0, side, 0, 0

        return pl.BlockSpec((None, 2, None, half, columns), index)

    halves = lambda columns: (blocks // 2, 2, 2, half, columns)
    anywhere = pl.BlockSpec(memory_space=pl.ANY)
    dma = lambda *shape: pltpu.SemaphoreType.DMA(shape)
    message_all, act, slope, dw_out, w_out = pl.pallas_call(
        functools.partial(experts_up_kernel, n_experts, hidden // 2, n_fsdp),
        out_shape=[
            jax.ShapeDtypeStruct(halves(long), bf16),
            jax.ShapeDtypeStruct(halves(hidden), bf16),
            jax.ShapeDtypeStruct(halves(hidden), bf16),
            jax.ShapeDtypeStruct((hidden, width), bf16),
            jax.ShapeDtypeStruct((n_fsdp,) + expert_out.shape[1:], bf16),
        ],
        grid=(blocks,),
        in_specs=[whole((2, half, long)), turn(width), anywhere, anywhere, anywhere],
        out_specs=[turn(long), turn(hidden), turn(hidden), whole((hidden, width)), anywhere],
        scratch_shapes=[
            pltpu.VMEM(halves(long), bf16),
            pltpu.VMEM((hidden, width), f32),
            pltpu.VMEM((width, hidden), bf16),
            pltpu.VMEM((2 * rows, hidden), bf16),
            pltpu.VMEM((2 * rows, width), bf16),
            pltpu.VMEM(expert_out.shape[1:], bf16),
            dma(24),
            dma(24),
            dma(3),
        ],
        input_output_aliases={4: 4},
        compiler_params=pltpu.CompilerParams(
            vmem_limit_bytes=VMEM_LIMIT, collective_id=2, has_side_effects=True
        ),
        cost_estimate=pl.CostEstimate(
            flops=20_000_000_000, transcendentals=0, bytes_accessed=30_000_000
        ),
        name="experts_up",
    )(message.reshape(2, half, long), dy_all.reshape(halves(width)), w_in, expert_out, w_out)
    whole_blocks = lambda array: array.reshape(blocks, rows, array.shape[4])
    return whole_blocks(message_all), whole_blocks(act), whole_blocks(slope), dw_out, w_out


def experts_down_kernel(
    n_experts,
    chunk,
    n_fsdp,
    message_ref,
    dy_ref,
    act_ref,
    slope_ref,
    w_in,
    w_out,
    dw_out,
    back_ref,
    out_half,
    dw_in_ref,
    sum_out,
    part_ref,
    tx_ref,
    rx_ref,
    fin_ref,
    fin_out_ref,
    land_ref,
    dw_in_acc,
    w_in_ref,
    w_out_ref,
    h_pair_ref,
    dup_ref,
    tx_send,
    tx_recv,
    fin_sem,
    land_sem,
    local,
    near,
    mid,
    far,
    own_ref,
    line_send,
    line_recv,
    line_local,
):
    step = pl.program_id(0)
    last = 7
    me = Place(n_fsdp)
    core = me.core
    rows, width = dy_ref.shape
    hidden = w_in_ref.shape[1]
    long = message_ref.shape[1]
    half = rows // 2
    mate = me.mate()
    adds = LineSum(me, dw_out, near, mid, far, own_ref, line_send, line_recv, line_local)

    def to_mate(j):
        return pltpu.make_async_remote_copy(
            src_ref=tx_ref.at[j % 2],
            dst_ref=rx_ref.at[j],
            send_sem=tx_send.at[j],
            recv_sem=tx_recv.at[j],
            device_id=mate,
            device_id_type=MESH,
        )

    def to_owner(j):
        q, k = plane_slot(down_order(j))
        return pltpu.make_async_remote_copy(
            src_ref=fin_ref.at[j % 2],
            dst_ref=land_ref.at[q, core],
            send_sem=fin_sem.at[j],
            recv_sem=land_sem.at[q, core],
            device_id=me.chip(q // 2, q % 2, k),
            device_id_type=MESH,
        )

    def keep_out(j):
        return pltpu.make_async_copy(fin_out_ref.at[j % 2], out_half.at[down_order(j)], local.at[j])

    def stays(j):
        q, k = plane_slot(down_order(j))
        return (q == 0) & (k == core)

    def finish_block(j):
        to_mate(j).wait_recv()
        mine = part_ref.at[j % 2, pl.ds(core * half, half)]

        @pl.when(j >= 2)
        def _():
            keep_out(j - 2).wait()

        @pl.when((j >= 2) & ~stays(j - 2))
        def _():
            to_owner(j - 2).wait_send()

        fin_ref[j % 2] = (mine[:, :long] + rx_ref[j, :, :long].astype(f32)).astype(bf16)

        @pl.when(stays(j))
        def _():
            land_ref[0, core] = fin_ref[j % 2]

        @pl.when(~stays(j))
        def _():
            to_owner(j).start()

        fin_out_ref[j % 2] = (mine[:, long:] + rx_ref[j, :, long:].astype(f32)).astype(bf16)
        keep_out(j).start()

    @pl.when(step == 0)
    def _():
        loads = [
            pltpu.make_async_copy(w_in, w_in_ref, local.at[0]),
            pltpu.make_async_copy(w_out, w_out_ref, local.at[1]),
        ]
        for load in loads:
            load.start()
        partners = [mate, me.along(1), me.along(-1)]
        for q in (1, 2, 3):
            for k in (0, 1):
                partners.append(me.chip(q // 2, q % 2, (core + k) % 2))
        meet(partners)
        adds.start()
        dw_in_acc[...] = jnp.zeros_like(dw_in_acc)
        for load in loads:
            load.wait()

    @pl.when(step == 3)
    def _():
        adds.turn()

    expert = me.rep
    place = pl.ds(pl.multiple_of(step % 2 * rows, rows), rows)
    h_pair_ref[:, place] = message_ref[:, :width].T
    extra = message_ref[:, width:].astype(f32)
    lane = lax.broadcasted_iota(jnp.int32, extra.shape, 1)
    mine = (lane == expert) | (lane == expert + n_experts)
    gate = jnp.sum(jnp.where(mine, extra, 0.0), -1, keepdims=True)
    dy = dy_ref[...]
    dgate = None
    part = part_ref.at[step % 2]
    for start in range(0, hidden, chunk):
        piece = slice(start, start + chunk)
        act = act_ref[:, piece].astype(f32)
        dact = dot_t(dy, w_out_ref[piece, :])
        gated = (gate * act).astype(bf16)
        dgate_part = jnp.sum(act * dact, -1, keepdims=True)
        dup = (gate * dact * slope_ref[:, piece].astype(f32)).astype(bf16)
        out_part = dot(gated, w_out_ref[piece, :])
        dh_part = dot_t(dup, w_in_ref[:, piece])
        if start == 0:
            part[:, long:] = out_part
            part[:, :width] = dh_part
        else:
            part[:, long:] += out_part
            part[:, :width] += dh_part
        dgate = dgate_part if dgate is None else dgate + dgate_part
        dup_ref[place, piece] = dup
        if start == chunk:

            @pl.when(step >= 1)
            def _():
                finish_block(step - 1)

    @pl.when(step % 2 == 1)
    def _():
        dw_in_acc[...] += dot(h_pair_ref[...], dup_ref[...])

    high = dgate.astype(bf16).astype(f32)
    low = dgate - high
    part[:, width:long] = jnp.where(
        lane == expert, high, jnp.where(lane == expert + n_experts, low, 0.0)
    )

    @pl.when(step >= 2)
    def _():
        to_mate(step - 2).wait_send()

    tx_ref[step % 2] = part_ref[step % 2, pl.ds((1 - core) * half, half)].astype(bf16)
    to_mate(step).start()

    @pl.when(step == last)
    def _():
        dw_in_ref[...] = dw_in_acc[...].astype(bf16)
        finish_block(last)
        sum_out[...] = adds.total()
        to_mate(last - 1).wait_send()
        to_mate(last).wait_send()
        keep_out(last - 1).wait()
        keep_out(last).wait()
        for j in (last - 1, last):

            @pl.when(~stays(j))
            def _():
                to_owner(j).wait_send()

        for side in range(2):
            total = None
            for q in range(4):
                arrived = pltpu.make_async_remote_copy(
                    src_ref=fin_ref.at[0],
                    dst_ref=land_ref.at[q, side],
                    send_sem=fin_sem.at[0],
                    recv_sem=land_sem.at[q, side],
                    device_id=mate,
                    device_id_type=MESH,
                )
                if q == 0:

                    @pl.when(core != side)
                    def _():
                        arrived.wait_recv()

                else:
                    arrived.wait_recv()
                landed = land_ref[q, side].astype(f32)
                total = landed if total is None else total + landed
            back_ref[side * half : (side + 1) * half, :] = total


def experts_down(message_all, dy_all, act, slope, w_in, w_out, dw_out, n_experts, n_fsdp):
    blocks, rows, width = dy_all.shape
    long = message_all.shape[2]
    hidden = w_in.shape[1]
    half = rows // 2
    once = pl.Buffered(1)
    whole = lambda shape: pl.BlockSpec(shape, lambda i: (0,) * len(shape), pipeline_mode=once)
    block = lambda columns: pl.BlockSpec(
        (None, rows, columns), lambda i: (down_order(i), 0, 0)
    )
    anywhere = pl.BlockSpec(memory_space=pl.ANY)
    both = long + width
    dma = lambda *shape: pltpu.SemaphoreType.DMA(shape)
    return pl.pallas_call(
        functools.partial(experts_down_kernel, n_experts, hidden // 2, n_fsdp),
        out_shape=[
            jax.ShapeDtypeStruct((rows, long), f32),
            jax.ShapeDtypeStruct((blocks, half, width), bf16),
            jax.ShapeDtypeStruct((width, hidden), bf16),
            jax.ShapeDtypeStruct(dw_out.shape[1:], bf16),
        ],
        grid=(blocks,),
        in_specs=[
            block(long),
            block(width),
            block(hidden),
            block(hidden),
            anywhere,
            anywhere,
            anywhere,
        ],
        out_specs=[
            whole((rows, long)),
            anywhere,
            whole((width, hidden)),
            whole(dw_out.shape[1:]),
        ],
        scratch_shapes=[
            pltpu.VMEM((2, rows, both), f32),
            pltpu.VMEM((2, half, both), bf16),
            pltpu.VMEM((blocks, half, both), bf16),
            pltpu.VMEM((2, half, long), bf16),
            pltpu.VMEM((2, half, width), bf16),
            pltpu.VMEM((4, 2, half, long), bf16),
            pltpu.VMEM((width, hidden), f32),
            pltpu.VMEM((width, hidden), bf16),
            pltpu.VMEM((hidden, width), bf16),
            pltpu.VMEM((width, 2 * rows), bf16),
            pltpu.VMEM((2 * rows, hidden), bf16),
            dma(8),
            dma(8),
            dma(8),
            dma(4, 2),
            dma(8),
        ]
        + LineSum.scratch(*dw_out.shape[1:]),
        compiler_params=pltpu.CompilerParams(
            vmem_limit_bytes=VMEM_LIMIT, collective_id=3, has_side_effects=True
        ),
        cost_estimate=pl.CostEstimate(
            flops=40_000_000_000, transcendentals=0, bytes_accessed=40_000_000
        ),
        name="experts_down",
    )(message_all, dy_all, act, slope, w_in, w_out, dw_out)


class LineSum:
    def __init__(self, me, whole, near, mid, far, mine, send, recv, local):
        self.me, self.whole, self.near, self.mid, self.far = me, whole, near, mid, far
        self.mine, self.local = mine, local
        rows = whole.shape[1]
        half = rows // 2
        self.parts = {1: slice(0, half), -1: slice(half, rows)}
        plan = {}
        for i, shift in enumerate((1, -1)):
            part = pl.ds(i * half, half)
            target = (me.line + 2) % me.n_fsdp
            plan["near", shift] = (whole.at[target, part], near.at[i], me.along(shift))
            plan["far", shift] = (mid.at[i], far.at[i], me.along(shift))
        self.copies = Planned(plan, send, recv)

    def loads(self):
        me = self.me
        for i, shift in enumerate((1, -1)):
            source = self.whole.at[(me.line + shift) % me.n_fsdp]
            yield pltpu.make_async_copy(source, self.mid.at[i], self.local.at[i])
        yield pltpu.make_async_copy(self.whole.at[me.line], self.mine, self.local.at[2])

    def start(self):
        for shift in (1, -1):
            self.copies["near", shift].start()
        for load in self.loads():
            load.start()

    def turn(self):
        for load in self.loads():
            load.wait()
        for i, shift in enumerate((1, -1)):
            self.copies["near", shift].wait_recv()
            part = self.parts[shift]
            total = self.mid[i, part, :].astype(f32) + self.near[i].astype(f32)
            self.mid[i, part, :] = total.astype(bf16)
            self.copies["far", shift].start()

    def total(self):
        for shift in (1, -1):
            self.copies["far", shift].wait_recv()
        total = self.mine[...].astype(f32) + self.far[0].astype(f32) + self.far[1].astype(f32)
        for shift in (1, -1):
            self.copies["near", shift].wait_send()
            self.copies["far", shift].wait_send()
        return total.astype(bf16)

    @staticmethod
    def scratch(rows, columns):
        return [
            pltpu.VMEM((2, rows // 2, columns), bf16),
            pltpu.VMEM((2, rows, columns), bf16),
            pltpu.VMEM((2, rows, columns), bf16),
            pltpu.VMEM((rows, columns), bf16),
            pltpu.SemaphoreType.DMA((4,)),
            pltpu.SemaphoreType.DMA((4,)),
            pltpu.SemaphoreType.DMA((3,)),
        ]


class BackgroundBack:
    n_in, n_out = 2, 4

    def __init__(self, n_fsdp):
        self.n_fsdp = n_fsdp

    def out_shape(self, out_half, dw_in):
        half, width = out_half.shape[1:]
        return [
            jax.ShapeDtypeStruct((2 * half, width), bf16),
            jax.ShapeDtypeStruct(dw_in.shape[1:], bf16),
            jax.ShapeDtypeStruct(
                (self.n_fsdp, width // (2 * self.n_fsdp), width - LANES), bf16
            ),
            jax.ShapeDtypeStruct((4,) + self.split(width), bf16),
        ]

    def out_specs(self, shapes):
        whole = lambda shape: pl.BlockSpec(shape, lambda p, *_: (0,) * len(shape))
        return [whole(s.shape) for s in shapes]

    def scratch(self, out_half, dw_in):
        half, width = out_half.shape[1:]
        pairs = width // LANES - 1
        return [
            pltpu.VMEM((3, 2, half, width), bf16),
            pltpu.SemaphoreType.DMA((8,)),
            pltpu.SemaphoreType.DMA((3, 2)),
            pltpu.VMEM((2, 4) + self.split(width), bf16),
            pltpu.VMEM((pairs, 2) + self.split(width), bf16),
            pltpu.VMEM((pairs, 2) + self.split(width), bf16),
            pltpu.VMEM((pairs, 3, self.n_fsdp) + self.split(width)[2:], bf16),
            pltpu.SemaphoreType.DMA((pairs, 2)),
            pltpu.SemaphoreType.DMA((pairs, 2)),
            pltpu.SemaphoreType.DMA((pairs, 3)),
            pltpu.SemaphoreType.DMA((pairs, 3)),
            pltpu.VMEM((2, half, width), bf16),
            pltpu.VMEM((2, half, width), bf16),
            pltpu.SemaphoreType.DMA((2,)),
            pltpu.SemaphoreType.DMA((2,)),
        ] + LineSum.scratch(*dw_in.shape[1:])

    def split(self, width):
        return (self.n_fsdp, 2, width // (2 * self.n_fsdp), LANES)

    def to_mate(self, pair, i, scratch):
        me = Place(self.n_fsdp)
        own, given = scratch[3:5]
        send, recv = scratch[7:9]
        return pltpu.make_async_remote_copy(
            src_ref=own.at[pair % 2, 2 * i + 1 - me.core],
            dst_ref=given.at[pair, i],
            send_sem=send.at[pair, i],
            recv_sem=recv.at[pair, i],
            device_id=me.mate(),
            device_id_type=MESH,
        )

    def to_chip(self, pair, i, scratch):
        me = Place(self.n_fsdp)
        added, landed = scratch[5:7]
        send, recv = scratch[9:11]
        rows, columns = ((0, 1), (1, 0), (1, 1))[i]
        row, column = (me.row + rows) % 2, (me.seq + columns) % 2
        return pltpu.make_async_remote_copy(
            src_ref=added.at[pair, row, :, column],
            dst_ref=landed.at[pair, i],
            send_sem=send.at[pair, i],
            recv_sem=recv.at[pair, i],
            device_id=me.chip(rows, columns),
            device_id_type=MESH,
        )

    def give(self, pair, grads, scratch, last_out):
        own = scratch[3]
        last = pl.num_programs(0) - 1

        @pl.when(pair >= 2)
        def _():
            for i in (0, 1):
                self.to_mate(pair - 2, i, scratch).wait_send()

        @pl.when(pair < last)
        def _():
            for i, grad in enumerate(grads):
                own[pair % 2, i] = grad.reshape(own.shape[2:])
            for i in (0, 1):
                self.to_mate(pair, i, scratch).start()

        @pl.when(pair == last)
        def _():
            for i, grad in enumerate(grads):
                last_out[i] = grad.reshape(own.shape[2:])

    def collect(self, pair, scratch):
        core = Place(self.n_fsdp).core
        own, given, added = scratch[3:6]
        for i in (0, 1):
            self.to_mate(pair, i, scratch).wait_recv()
            total = own[pair % 2, 2 * i + core].astype(f32) + given[pair, i].astype(f32)
            added[pair, i] = total.astype(bf16)
        for i in range(3):
            self.to_chip(pair, i, scratch).start()

    def collect_before(self, pair, scratch):
        @pl.when(pair >= 1)
        def _():
            self.collect(pair - 1, scratch)

    def run(self, step, before, ins, outs, scratch, x_mid):
        out_half, dw_in = ins
        out_rows, sum_in, plane_sum, _ = outs
        land, send, recv = scratch[:3]
        relay, hop, relay_recv, hop_sem = scratch[11:15]
        near, mid, far, mine, line_send, line_recv, line_local = scratch[15:]
        me = Place(self.n_fsdp)
        core = me.core
        half = out_half.shape[1]
        line = LineSum(me, dw_in, near, mid, far, mine, line_send, line_recv, line_local)

        across, beside = (lambda k: me.chip(1, 0, k)), (lambda k: me.chip(0, 1, k))
        plan = {
            "mate": (out_half.at[7 - core], land.at[0, core], me.mate(), recv.at[0, core]),
            "direct0": (out_half.at[2], land.at[2, core], across(0), recv.at[2, core]),
            "direct1": (out_half.at[1], land.at[1, core], beside(1), recv.at[1, core]),
            "hop0": (out_half.at[4], relay.at[0], across(core), relay_recv.at[0]),
            "hop1": (out_half.at[5], relay.at[1], beside(core), relay_recv.at[1]),
            "sum0": (hop.at[0], land.at[1, core], beside(0), recv.at[1, core]),
            "sum1": (hop.at[1], land.at[2, core], across(1), recv.at[2, core]),
        }

        def result(name):
            source, target, device, arrival = plan[name]
            return pltpu.make_async_remote_copy(
                src_ref=source,
                dst_ref=target,
                send_sem=send.at[list(plan).index(name)],
                recv_sem=arrival,
                device_id=device,
                device_id_type=MESH,
            )

        def own_parts():
            yield pltpu.make_async_copy(out_half.at[0], hop.at[0], hop_sem.at[0])
            yield pltpu.make_async_copy(out_half.at[3], hop.at[1], hop_sem.at[1])

        stay = lambda: pltpu.make_async_copy(
            out_half.at[6 + core], land.at[0, core], send.at[7]
        )

        if before:

            @pl.when(step == 0)
            def _():
                partners = [me.mate(), me.along(1), me.along(-1)]
                for q in (1, 2, 3):
                    for k in (0, 1):
                        partners.append(me.chip(q // 2, q % 2, (core + k) % 2))
                meet(partners)
                line.start()
                for name in ("hop0", "hop1", "direct0", "direct1", "mate"):
                    result(name).start()
                stay().start()
                for part in own_parts():
                    part.start()

            @pl.when(step == 2)
            def _():
                line.turn()

            @pl.when(step == 3)
            def _():
                for part in own_parts():
                    part.wait()
                for k in (0, 1):
                    result(f"hop{k}").wait_recv()
                    hop[k] = (hop[k].astype(f32) + relay[k].astype(f32)).astype(bf16)
                    result(f"sum{k}").start()

            return

        @pl.when(step == pl.num_programs(0) - 1)
        def _():
            added, landed = scratch[5:7]
            pairs = landed.shape[0]
            sum_in[...] = line.total()
            for name in plan:
                result(name).wait_send()
            stay().wait()
            for side in range(2):
                here = slice(side * half, (side + 1) * half)
                total = x_mid[here, :]
                for q in range(3):
                    arrived = pltpu.make_async_remote_copy(
                        src_ref=out_half.at[0],
                        dst_ref=land.at[q, side],
                        send_sem=send.at[0],
                        recv_sem=recv.at[q, side],
                        device_id=me.mate(),
                        device_id_type=MESH,
                    )
                    if q == 0:

                        @pl.when(core != side)
                        def _():
                            arrived.wait_recv()

                    else:
                        arrived.wait_recv()
                    total = total + land[q, side].astype(f32)
                out_rows[here, :] = total.astype(bf16)
            for i in (0, 1):
                self.to_mate(pairs - 1, i, scratch).wait_send()
            for pair in range(pairs):
                total = added[pair, me.row, :, me.seq].astype(f32)
                for i in range(3):
                    self.to_chip(pair, i, scratch).wait_recv()
                    total = total + landed[pair, i].astype(f32)
                plane_sum[:, :, pair * LANES : (pair + 1) * LANES] = total.astype(bf16)
            for pair in range(pairs):
                for i in range(3):
                    self.to_chip(pair, i, scratch).wait_send()


def backward_kernel(
    background,
    n_experts,
    head_dim,
    back,
    dy,
    x_mid,
    message_ref,
    probs_ref,
    pack_ref,
    h_all,
    wq_ref,
    wk_ref,
    wv_ref,
    wo_ref,
    q_ref,
    k_ref,
    v_ref,
    o_ref,
    p_ref,
    x_all,
    *refs,
):
    step = pl.program_id(0)
    n_in, n_out = (background.n_in, background.n_out) if background else (0, 0)
    behind_in, refs = refs[:n_in], refs[n_in:]
    n_grads = 0 if background else 4
    grad_outs, refs = refs[:n_grads], refs[n_grads:]
    dh_own_out, dh_other_out, dx_mid_out, gain_out, router_out, ddist_out = refs[:6]
    gain_one_out, refs = refs[6], refs[7:]
    behind_out, refs = refs[:n_out], refs[n_out:]
    da_ref, dh_all_ref, dh_mine_ref, dbias_ref, dq_ref, h_turned_ref, o_turned_ref = refs[:7]
    back_ref, dy_ref, x_mid_ref, h_ref, x_ref, load_sem = refs[7:13]
    held = ((back, back_ref), (dy, dy_ref), (x_mid, x_mid_ref), (h_all, h_ref), (x_all, x_ref))
    load = lambda i: pltpu.make_async_copy(*held[i], load_sem.at[i])

    @pl.when(step == 0)
    def _():
        for i in range(5):
            load(i).start()

    if background:
        background.run(step, True, behind_in, behind_out, refs[13:], x_mid_ref)
    rows, width = x_mid.shape
    length = h_all.shape[0]
    own = pl.ds(pl.multiple_of(first_row(rows), rows), rows)

    @pl.when(step == 0)
    def _():
        for i in range(4):
            load(i).wait()
        probs = probs_ref[...]
        chosen = chosen_experts(pack_ref, probs.shape)
        picked = jnp.where(chosen, probs, 0.0)
        total = jnp.sum(picked, -1, keepdims=True)
        gate = picked / total
        extra = back_ref[:, width:].astype(f32)
        dgate = extra + pltpu.roll(extra, LANES - n_experts, 1)
        dgate = jnp.where(chosen, dgate, 0.0)
        shared = jnp.sum(dgate * gate, -1, keepdims=True)
        dprobs = jnp.where(chosen, (dgate - shared) / total, 0.0)
        dlogits = probs * (dprobs - jnp.sum(probs * dprobs, -1, keepdims=True))
        h_two = message_ref[:, :width].astype(f32)
        router_out[...] = lax.dot_general(
            dlogits,
            h_two,
            (((0,), (0,)), ((), ())),
            precision=highest,
            preferred_element_type=f32,
        )
        dh_two = back_ref[:, :width].astype(f32) + exact_dot(
            dlogits, router_rows(pack_ref, n_experts, width)
        )
        dx, dgain = norm_back(x_mid_ref[...], pack_ref[5:6, :width], dh_two)
        gain_out[...] = dgain
        dx_mid = dx + dy_ref[...].astype(f32)
        dx_mid_out[...] = dx_mid
        da_ref[...] = dx_mid.astype(bf16)
        dh_all_ref[...] = jnp.zeros_like(dh_all_ref)
        dh_mine_ref[...] = jnp.zeros_like(dh_mine_ref)
        ddist_out[...] = jnp.zeros_like(ddist_out)
        h_turned_ref[...] = h_ref[...].T
        o_turned_ref[...] = o_ref[...].T

    da = da_ref[...]
    do = dot_t(da, wo_ref[...]).astype(bf16)
    block = LANES
    first_half = lax.broadcasted_iota(jnp.int32, (block, LANES), 1) < head_dim
    zero = jnp.zeros((), bf16)
    k_low = k_ref[...]
    v_low = v_ref[...]
    dk = None
    dv = None
    for head in range(2):
        dbias_ref[head] = jnp.zeros_like(dbias_ref[head])
    for b in range(rows // block):
        here = slice(b * block, (b + 1) * block)
        offset = pl.multiple_of(length - LANES - block * b - first_row(rows), LANES)
        q_heads = by_head(q_ref[here, :], first_half)
        do_heads = by_head(do[here], first_half)
        probs_low = p_ref[:, here, :]
        probs = probs_low.astype(f32)
        dprobs = dot_t(do_heads, v_low).reshape(2, block, length)
        weighted = probs * dprobs
        ds = weighted - probs * jnp.sum(weighted, -1, keepdims=True)
        dbias_ref[:, :, pl.ds(offset, length)] += ds
        ds_low = ds.astype(bf16).reshape(2 * block, length)
        probs_low = probs_low.reshape(2 * block, length)
        dq_heads = dot(ds_low, k_low)
        dk_part = t_dot(ds_low, q_heads)
        dv_part = t_dot(probs_low, do_heads)
        dk = dk_part if dk is None else dk + dk_part
        dv = dv_part if dv is None else dv + dv_part
        dq_ref[here, :] = (of_head(dq_heads, first_half) * (head_dim**-0.5)).astype(bf16)
    for head in range(2):
        ddist_out[pl.ds(2 * step + head, 1), :] = gather_diagonals(dbias_ref[head])
    dq = dq_ref[...]
    dkv = jnp.concatenate([dk, dv], 1).astype(bf16)
    da_columns = da_ref[:, pl.ds(pl.multiple_of(step * LANES, LANES), LANES)]
    if background:
        background.collect_before(step, refs[13:])
    mine = pl.ds(pl.multiple_of(first_row(rows), rows), rows)
    grads_kv = dot(h_turned_ref[...], dkv).astype(bf16)
    grads = [
        dot(h_turned_ref[:, mine], dq).astype(bf16),
        grads_kv[:, :LANES],
        grads_kv[:, LANES:],
        dot(o_turned_ref[...], da_columns).astype(bf16),
    ]
    if background:
        background.give(step, grads, refs[13:], behind_out[3])
    else:
        for target, grad in zip(grad_outs, grads):
            target[...] = grad
    dh_all_ref[...] += dot_t(dkv, jnp.concatenate([wk_ref[...], wv_ref[...]], 1))
    dh_mine_ref[...] += dot_t(dq, wq_ref[...])

    @pl.when(step == pl.num_programs(0) - 1)
    def _():
        other = pl.ds(pl.multiple_of(length - rows - first_row(rows), rows), rows)
        dh_own_out[...] = dh_mine_ref[...] + dh_all_ref[own, :]
        dh_other_out[...] = dh_all_ref[other, :].astype(bf16)
        load(4).wait()
        for start in range(0, length, rows):
            here = slice(start, start + rows)
            values = x_ref[here, :].astype(f32)
            part = jnp.sum(dh_all_ref[here, :] * (values * inverse_rms(values)), 0, keepdims=True)
            gain_one_out[...] = part if start == 0 else gain_one_out[...] + part
        values = x_ref[own, :].astype(f32)
        scaled = values * inverse_rms(values)
        gain_one_out[...] += jnp.sum(dh_mine_ref[...] * scaled, 0, keepdims=True)

    if background:
        background.run(step, False, behind_in, behind_out, refs[13:], x_mid_ref)


def attention_backward(
    back,
    dy,
    x_mid,
    message,
    probs,
    pack,
    h_all,
    weights,
    q,
    k,
    v,
    o,
    p,
    x_all,
    n_experts,
    head_dim,
    background=None,
    behind=(),
):
    n_rows, width = x_mid.shape
    length = h_all.shape[0]
    pairs = width // LANES
    span = pack.shape[1]
    more_shapes, more_scratch, params = [], [], {}
    n_grads = 0 if background else 4
    if background:
        more_shapes = background.out_shape(*behind)
        more_scratch = background.scratch(*behind)
        params = {"collective_id": 4, "has_side_effects": True}
    anywhere = pl.BlockSpec(memory_space=pl.ANY)
    whole = lambda shape: pl.BlockSpec(shape, lambda p, *_: (0,) * len(shape))
    columns = lambda rows: pl.BlockSpec((rows, LANES), lambda p, *_: (0, p))
    matrix = lambda i: pl.BlockSpec((None, width, LANES), lambda p, *_: (i, 0, p))
    return pl.pallas_call(
        functools.partial(backward_kernel, background, n_experts, head_dim),
        out_shape=[jax.ShapeDtypeStruct((width, width), bf16)] * n_grads
        + [
            jax.ShapeDtypeStruct((n_rows, width), f32),
            jax.ShapeDtypeStruct((n_rows, width), bf16),
            jax.ShapeDtypeStruct((n_rows, width), f32),
            jax.ShapeDtypeStruct((1, width), f32),
            jax.ShapeDtypeStruct((LANES, width), f32),
            jax.ShapeDtypeStruct((16, span), f32),
            jax.ShapeDtypeStruct((1, width), f32),
        ]
        + more_shapes,
        grid_spec=pltpu.PrefetchScalarGridSpec(
            num_scalar_prefetch=0,
            grid=(pairs,),
            in_specs=[
                anywhere,
                anywhere,
                anywhere,
                whole((n_rows, width + LANES)),
                whole((n_rows, LANES)),
                whole(pack.shape),
                anywhere,
                matrix(0),
                matrix(1),
                matrix(2),
                pl.BlockSpec((None, LANES, width), lambda p, *_: (3, p, 0)),
                columns(n_rows),
                columns(length),
                columns(length),
                whole((n_rows, width)),
                pl.BlockSpec((None, 2, n_rows, length), lambda p, *_: (p, 0, 0, 0)),
                anywhere,
            ]
            + [anywhere] * len(behind),
            out_specs=[columns(width)] * n_grads
            + [
                whole((n_rows, width)),
                whole((n_rows, width)),
                whole((n_rows, width)),
                whole((1, width)),
                whole((LANES, width)),
                whole((16, span)),
                whole((1, width)),
            ]
            + (background.out_specs(more_shapes) if background else []),
            scratch_shapes=[
                pltpu.VMEM((n_rows, width), bf16),
                pltpu.VMEM((length, width), f32),
                pltpu.VMEM((n_rows, width), f32),
                pltpu.VMEM((2, LANES, span), f32),
                pltpu.VMEM((n_rows, LANES), bf16),
                pltpu.VMEM((width, length), bf16),
                pltpu.VMEM((width, n_rows), bf16),
                pltpu.VMEM(back.shape, back.dtype),
                pltpu.VMEM((n_rows, width), bf16),
                pltpu.VMEM((n_rows, width), f32),
                pltpu.VMEM((length, width), bf16),
                pltpu.VMEM((length, width), bf16),
                pltpu.SemaphoreType.DMA((5,)),
            ]
            + more_scratch,
        ),
        compiler_params=pltpu.CompilerParams(vmem_limit_bytes=VMEM_LIMIT, **params),
        cost_estimate=pl.CostEstimate(
            flops=40_000_000_000, transcendentals=0, bytes_accessed=30_000_000
        ),
        name="attention_backward",
    )(
        back,
        dy,
        x_mid,
        message,
        probs,
        pack,
        h_all,
        weights,
        weights,
        weights,
        weights,
        q,
        k,
        v,
        o,
        p,
        x_all,
        *behind,
    )


def finish_kernel(
    n_fsdp,
    n_experts,
    n_heads,
    sum_in,
    sum_out,
    dh_other,
    line_ref,
    last_ref,
    dh_own,
    dx_mid,
    tokens,
    pack_ref,
    dgain_one_ref,
    dgain_two_ref,
    drouter_ref,
    ddist_ref,
    attn_out,
    grad_in,
    grad_out,
    tokens_out,
    small_out,
    line_land,
    last_given,
    last_added,
    last_land,
    last_line,
    last_line_land,
    attn_held,
    dh_land,
    small_plane,
    small_line,
    in_held,
    out_held,
    dh_own_ref,
    dx_mid_ref,
    tokens_ref,
    send,
    recv,
    local,
):
    me = Place(n_fsdp)
    rep, line, seq, core, row = me.rep, me.line, me.seq, me.core, me.row
    width = tokens_ref.shape[1]
    mate, across, beside, corner = me.mate(), me.chip(1, 0), me.chip(0, 1), me.chip(1, 1)
    far_row = (row + 1) % 2
    far_rep = far_row * 2 + core
    part_out = sum_out.shape[0]
    columns = lambda z, x: pl.ds(pl.multiple_of((z * 2 + x) * part_out, LANES), part_out)
    here = rep * 2 + seq
    peers = [mate, across, beside, corner]
    peers += [me.chip(1, 0, 1 - core), me.chip(0, 1, 1 - core), me.chip(1, 1, 1 - core)]
    shifts = (1, -1, 2)
    plan = {
        "dh": (dh_other, dh_land, beside),
        "out_c": (sum_out, grad_out.at[rep], mate),
        "out_y": (sum_out, grad_out.at[rep], across),
        "out_f": (grad_out.at[far_rep], grad_out.at[far_rep], mate),
        "attn_c": (attn_held, attn_out.at[rep], mate),
        "attn_y": (attn_held, attn_out.at[rep], across),
        "attn_f": (attn_out.at[far_rep], attn_out.at[far_rep], mate),
        "in_c": (grad_in.at[rep], grad_in.at[rep], mate),
        "in_y": (grad_in.at[rep], grad_in.at[rep], across),
        "in_f": (grad_in.at[far_rep], grad_in.at[far_rep], mate),
    }
    for i, shift in enumerate(shifts):
        target = (line + shift) % n_fsdp
        plan["line", i] = (line_ref.at[target], line_land.at[i], me.along(shift))
        plan["last_z", i] = (last_line.at[target], last_line_land.at[i], me.along(shift))
        plan["small_z", i] = (small_line.at[line], small_line.at[line], me.along(shift))
    for z in range(n_fsdp):
        plan["in_x", z] = (
            sum_in.at[1 - seq, :, pl.ds(z * part_out, part_out)],
            grad_in.at[rep, :, columns(z, seq)],
            beside,
        )
    for i, peer in enumerate(peers):
        plan["small", i] = (small_plane.at[here], small_plane.at[here], peer)
    for i in (0, 1):
        plan["last_c", i] = (last_ref.at[2 * i + 1 - core], last_given.at[i], mate)
    chips = ((row, 1 - seq, beside), (far_row, seq, across), (far_row, 1 - seq, corner))
    for i, (to_row, to_column, chip) in enumerate(chips):
        plan["last", i] = (last_added.at[to_row, :, to_column], last_land.at[i], chip)
    copies = Planned(plan, send, recv)
    held = ((dh_own, dh_own_ref), (dx_mid, dx_mid_ref), (tokens, tokens_ref))
    loads = [pltpu.make_async_copy(*held[i], local.at[10 + i]) for i in range(3)]
    for load in loads:
        load.start()
    meet(peers + [me.along(shift) for shift in shifts])
    for i in (0, 1):
        copies["last_c", i].start()
    for i in range(3):
        copies["line", i].start()
    for z in range(n_fsdp):
        copies["in_x", z].start()
    copies["out_y"].start()
    copies["out_c"].start()
    own_in = pltpu.make_async_copy(sum_in.at[seq], in_held, local.at[2])
    own_in.start()
    own_out = Bounce(sum_out, out_held, grad_out.at[rep], local.at[pl.ds(8, 2)])
    own_out.start()
    own_in.wait()
    kept = []
    for z in range(n_fsdp):
        source = in_held.at[:, pl.ds(z * part_out, part_out)]
        target = grad_in.at[rep, :, columns(z, seq)]
        kept.append(pltpu.make_async_copy(source, target, local.at[4 + z]))
        kept[-1].start()
    own_out.turn()
    for i in (0, 1):
        copies["last_c", i].wait_recv()
        total = last_ref[2 * i + core].astype(f32) + last_given[i].astype(f32)
        last_added[i] = total.astype(bf16)
    for i in range(3):
        copies["last", i].start()
    table = exact_dot_t(ddist_ref[...], bucket_match(pack_ref))
    small = small_plane.at[here]
    small[...] = jnp.zeros_like(small_out)
    small[0:1, :] = dgain_one_ref[...]
    small[1:2, :] = dgain_two_ref[...]
    small[2 : 2 + n_experts, :] = drouter_ref[:n_experts, :]
    for head in range(n_heads):
        at = head % 6 * LANES
        small[6 + head // 6, at : at + LANES] = table[head]
    for i in range(len(peers)):
        copies["small", i].start()
    for copy in kept:
        copy.wait()
    for z in range(n_fsdp):
        copies["in_x", z].wait_recv()
    copies["in_y"].start()
    copies["dh"].start()
    copies["in_c"].start()
    total = last_added[row, :, seq].astype(f32)
    for i in range(3):
        copies["last", i].wait_recv()
        total = total + last_land[i].astype(f32)
    last_line[...] = total.astype(bf16)
    for i in range(3):
        copies["last_z", i].start()
    for i in range(len(peers)):
        copies["small", i].wait_recv()
    total = small_plane[0]
    for i in range(1, 8):
        total = total + small_plane[i]
    small_line[line] = total
    for i in range(3):
        copies["small_z", i].start()
    total = line_ref[line].astype(f32)
    for i in range(3):
        copies["line", i].wait_recv()
        total = total + line_land[i].astype(f32)
    early = total.shape[1]
    attn_held[:, :early] = total.astype(bf16)
    copies["out_y"].wait_recv()
    copies["out_f"].start()
    total = last_line[line].astype(f32)
    for i in range(3):
        copies["last_z", i].wait_recv()
        total = total + last_line_land[i].astype(f32)
    attn_held[:, early:] = total.astype(bf16)
    copies["attn_y"].start()
    copies["attn_c"].start()
    own_attn = pltpu.make_async_copy(attn_held, attn_out.at[rep], local.at[3])
    own_attn.start()
    copies["dh"].wait_recv()
    for load in loads:
        load.wait()
    dh_one = dh_own_ref[...] + dh_land[...].astype(f32)
    dx, _ = norm_back(tokens_ref[...].astype(f32), pack_ref[4:5, :width], dh_one)
    tokens_out[...] = (dx_mid_ref[...] + dx).astype(bf16)
    for i in range(3):
        copies["small_z", i].wait_recv()
    total = small_line[0]
    for i in range(1, n_fsdp):
        total = total + small_line[i]
    small_out[...] = total
    copies["in_y"].wait_recv()
    copies["in_f"].start()
    copies["attn_y"].wait_recv()
    copies["attn_f"].start()
    own_attn.wait()
    own_out.wait()
    for name in ("attn_c", "attn_f", "in_c", "in_f", "out_c", "out_f"):
        copies[name].wait_recv()
    for name in plan:
        copies[name].wait_send()


def finish(
    plane_sum,
    last_grads,
    sum_in,
    sum_out,
    dh_other,
    dh_own,
    dx_mid,
    tokens,
    pack,
    dgain_one,
    dgain_two,
    drouter,
    ddist,
    n_fsdp,
    n_experts,
    n_heads,
    hidden,
):
    n_rows, width = tokens.shape
    part_attn = plane_sum.shape[1]
    split = last_grads.shape[1:]
    part_in = sum_in.shape[1]
    anywhere = pl.BlockSpec(memory_space=pl.ANY)
    inside = pl.BlockSpec(memory_space=pltpu.VMEM)
    dma = lambda n: pltpu.SemaphoreType.DMA((n,))
    return pl.pallas_call(
        functools.partial(finish_kernel, n_fsdp, n_experts, n_heads),
        out_shape=[
            jax.ShapeDtypeStruct((4, part_attn, width), bf16),
            jax.ShapeDtypeStruct((n_experts, part_in, hidden), bf16),
            jax.ShapeDtypeStruct((n_experts,) + sum_out.shape, bf16),
            jax.ShapeDtypeStruct((n_rows, width), bf16),
            jax.ShapeDtypeStruct((8, width), f32),
        ],
        in_specs=[anywhere] * 3 + [inside] * 2 + [anywhere] * 3 + [inside] * 5,
        out_specs=[anywhere] * 3 + [inside] * 2,
        scratch_shapes=[
            pltpu.VMEM((3,) + plane_sum.shape[1:], bf16),
            pltpu.VMEM((2,) + split, bf16),
            pltpu.VMEM((2,) + split, bf16),
            pltpu.VMEM((3, n_fsdp) + split[2:], bf16),
            pltpu.VMEM((n_fsdp,) + split[2:], bf16),
            pltpu.VMEM((3,) + split[2:], bf16),
            pltpu.VMEM((part_attn, width), bf16),
            pltpu.VMEM((n_rows, width), bf16),
            pltpu.VMEM((8, 8, width), f32),
            pltpu.VMEM((n_fsdp, 8, width), f32),
            pltpu.VMEM(sum_in.shape[1:], bf16),
            pltpu.VMEM(sum_out.shape, bf16),
            pltpu.VMEM((n_rows, width), f32),
            pltpu.VMEM((n_rows, width), f32),
            pltpu.VMEM((n_rows, width), bf16),
            dma(40),
            dma(40),
            dma(14),
        ],
        compiler_params=pltpu.CompilerParams(
            vmem_limit_bytes=VMEM_LIMIT, collective_id=5, has_side_effects=True
        ),
        name="finish_gradients",
    )(
        sum_in,
        sum_out,
        dh_other,
        plane_sum,
        last_grads,
        dh_own,
        dx_mid,
        tokens,
        pack,
        dgain_one,
        dgain_two,
        drouter,
        ddist,
    )


def widen_kernel(
    n_experts,
    n_heads,
    n_buckets,
    out_rows,
    tokens,
    attn,
    grad_in,
    grad_out,
    small,
    out_rows_copy,
    tokens_copy,
    q,
    k,
    v,
    o,
    win,
    wout,
    *rest,
):
    step = pl.program_id(0)
    out_rows_copy[...] = out_rows[...]
    tokens_copy[...] = tokens[...]
    for i, target in enumerate((q, k, v, o)):

        @pl.when(step == i)
        def _():
            target[...] = attn[...].astype(f32)

    win[...] = grad_in[...].astype(f32)
    wout[...] = grad_out[...].astype(f32)
    gain_one, gain_two, table, router = rest

    @pl.when(step == 0)
    def _():
        gain_one[...] = small[0, :]
        gain_two[...] = small[1, :]
        router[...] = small[2 : 2 + n_experts, :]
        for head in range(n_heads):
            at = head % 6 * LANES
            table[head : head + 1, :] = small[
                6 + head // 6 : 7 + head // 6, at : at + n_buckets
            ]


def widen(out_rows, tokens, attn, grad_in, grad_out, small, n_heads, n_buckets):
    n_experts = grad_in.shape[0]
    rows = pl.BlockSpec((tokens.shape[0] // n_experts, tokens.shape[1]), lambda i: (i, 0))
    width = small.shape[1]
    own = lambda a: pl.BlockSpec((None,) + a.shape[1:], lambda i: (i, 0, 0))
    whole = lambda shape: pl.BlockSpec(shape, lambda i: (0,) * len(shape))
    small_shapes = [(width,), (width,), (n_heads, n_buckets), (n_experts, width)]
    wide = [attn.shape[1:]] * 4
    return pl.pallas_call(
        functools.partial(widen_kernel, n_experts, n_heads, n_buckets),
        out_shape=[jax.ShapeDtypeStruct(tokens.shape, bf16)] * 2
        + [jax.ShapeDtypeStruct(shape, f32) for shape in wide]
        + [jax.ShapeDtypeStruct(a.shape, f32) for a in (grad_in, grad_out)]
        + [jax.ShapeDtypeStruct(shape, f32) for shape in small_shapes],
        grid=(n_experts,),
        in_specs=[rows, rows, own(attn), own(grad_in), own(grad_out), whole(small.shape)],
        out_specs=[rows, rows]
        + [whole(shape) for shape in wide]
        + [own(grad_in), own(grad_out)]
        + [whole(shape) for shape in small_shapes],
        compiler_params=pltpu.CompilerParams(vmem_limit_bytes=VMEM_LIMIT),
        name="widen",
    )(out_rows, tokens, attn, grad_in, grad_out, small)


def per_device(
    tokens,
    piece_starts,
    routes,
    buckets,
    attn_q,
    attn_k,
    attn_v,
    attn_o,
    expert_in,
    expert_out,
    gain_attn,
    gain_ffn,
    rel_table,
    router,
    cotangent,
):
    n_rep, n_fsdp, n_seq = (lax.axis_size(a) for a in ("rep", "fsdp", "seq"))
    rep = lax.axis_index("rep")
    seq = lax.axis_index("seq")
    plane = ("rep", "seq")
    n_rows, width = tokens.shape
    n_buckets, n_heads = rel_table.shape
    head_dim = width // n_heads
    n_experts, part_in, hidden = expert_in.shape
    part_out = expert_out.shape[1]
    part_attn = attn_q.shape[0]
    length = n_rows * n_seq
    assert n_experts == n_rep == 4 and n_seq == 2 and 2 * head_dim == LANES
    pairs = n_heads // 2

    place = piece_starts[0]
    near = n_fsdp == 4 and part_attn % 16 == 0
    pick = lambda array: lax.dynamic_index_in_dim(array, rep, 0, keepdims=False)
    span = -(-buckets.shape[0] // LANES) * LANES
    if near:
        weights, x_all, w_in, w_out, pack = gather(
            (attn_q, attn_k, attn_v, attn_o),
            tokens,
            expert_in,
            expert_out,
            n_fsdp,
            (router.T, gain_attn, gain_ffn, buckets, rel_table.T, routes.T),
            span,
        )
    else:
        attn_own = pick(jnp.stack([attn_q, attn_k, attn_v, attn_o]))
        attn_line = lax.all_gather(attn_own, "fsdp", axis=0, tiled=False)
        attn_all = lax.all_gather(attn_line, plane, axis=0, tiled=False)
        attn_all = attn_all.reshape(n_rep, n_seq, n_fsdp, part_attn, width)
        weights = attn_all.transpose(0, 2, 1, 3, 4).reshape(n_rep, width, width)
        x_all = lax.all_gather(tokens, "seq", axis=0, tiled=True)
        in_own = pick(expert_in).reshape(part_in, n_fsdp, n_seq, part_out)
        in_own = in_own.transpose(2, 0, 1, 3).reshape(n_seq, part_in, n_fsdp * part_out)
        in_pair = lax.all_to_all(in_own, "seq", split_axis=0, concat_axis=0, tiled=True)
        in_pair = in_pair.reshape(n_seq * part_in, n_fsdp * part_out)
        w_in = lax.all_gather(in_pair, "fsdp", axis=0, tiled=True)
        w_out = lax.all_gather(pick(expert_out), "fsdp", axis=0, tiled=True)
        dy_all = lax.all_gather(cotangent, plane, axis=0, tiled=True)
        pack = pack_small(router, gain_attn, gain_ffn, buckets, rel_table, routes, span)

    q, k, v, o, p, x_mid, message, probs, h_all, *gathered = attention_forward(
        place,
        x_all,
        weights,
        pack,
        n_rows,
        n_experts,
        head_dim,
        Background(n_fsdp) if near else None,
        (cotangent, w_in) if near else (),
    )
    behind = ()
    if near:
        dy_all, w_in = gathered
        w_in = w_in.reshape(width, n_fsdp * part_out)
        message_all, act, slope, dw_out, w_out = experts_up(
            message, dy_all, w_in, expert_out, w_out, n_experts, n_fsdp
        )
        back, out_half, dw_in, sum_out = experts_down(
            message_all,
            dy_all,
            act,
            slope,
            w_in,
            w_out.reshape(n_fsdp * part_out, width),
            dw_out.reshape(n_fsdp, part_out, width),
            n_experts,
            n_fsdp,
        )
        behind = (out_half, dw_in.reshape(n_fsdp, n_seq * part_in, n_fsdp * part_out))
    else:
        message_all = lax.all_gather(message, plane, axis=0, tiled=True)
        out_part, back_part, dw_in, dw_out = experts(
            rep[None].astype(jnp.int32), message_all, dy_all, w_in, w_out, n_experts, n_rows
        )
        back = lax.psum_scatter(back_part, plane, scatter_dimension=0, tiled=True)
        out_sum = lax.psum_scatter(out_part, plane, scatter_dimension=0, tiled=True)
        out_rows = (x_mid + out_sum.astype(f32)).astype(bf16)

    grads = attention_backward(
        back,
        cotangent,
        x_mid,
        message,
        probs,
        pack,
        h_all,
        weights,
        q,
        k,
        v,
        o,
        p,
        x_all,
        n_experts,
        head_dim,
        BackgroundBack(n_fsdp) if near else None,
        behind,
    )
    if near:
        dh_own, dh_other, dx_mid, dgain_two, drouter, ddist, dgain_one = grads[:7]
        out_rows, sum_in, plane_sum, last_grads = grads[7:]
        attn_sum, grad_in, grad_out, grad_tokens, small = finish(
            plane_sum,
            last_grads,
            sum_in.reshape(n_seq, part_in, n_fsdp * part_out),
            sum_out,
            dh_other,
            dh_own,
            dx_mid,
            tokens,
            pack,
            dgain_one,
            dgain_two,
            drouter,
            ddist,
            n_fsdp,
            n_experts,
            n_heads,
            hidden,
        )
        out_rows, grad_tokens, *wide, grad_one, grad_two, grad_table, grad_router = widen(
            out_rows, grad_tokens, attn_sum, grad_in, grad_out, small, n_heads, n_buckets
        )
        return (
            out_rows,
            grad_tokens,
            *wide,
            grad_one,
            grad_two,
            grad_table.T,
            grad_router.T,
        )
    dwq, dwk, dwv, dwo, dh_own, dh_other, dx_mid, dgain_two, drouter, ddist, dgain_one = grads
    sum_out = lax.psum_scatter(dw_out, "fsdp", scatter_dimension=0, tiled=True)
    sum_in = lax.psum_scatter(dw_in, "fsdp", scatter_dimension=0, tiled=True)
    sum_in = sum_in.reshape(n_seq, part_in, n_fsdp * part_out)
    sum_in = lax.all_to_all(sum_in, "seq", split_axis=0, concat_axis=0, tiled=True)
    sum_in = sum_in.reshape(n_seq, part_in, n_fsdp, part_out).transpose(1, 2, 0, 3)
    sum_in = sum_in.reshape(part_in, hidden)
    grad_out = lax.all_gather(sum_out, "rep", axis=0, tiled=False)
    grad_in = lax.all_gather(sum_in, "rep", axis=0, tiled=False)
    swap = [(0, 1), (1, 0)]
    dh_one = dh_own + lax.ppermute(dh_other, "seq", swap).astype(f32)
    dx, _ = norm_back(tokens.astype(f32), gain_attn[None, :], dh_one)
    grad_tokens = (dx_mid + dx).astype(bf16)
    attn_grads = jnp.stack([dwq, dwk, dwv, dwo])
    attn_grads = attn_grads.reshape(n_rep, n_fsdp, n_seq, part_attn, width)
    attn_grads = attn_grads.transpose(0, 2, 1, 3, 4)
    attn_grads = attn_grads.reshape(n_rep * n_seq * n_fsdp * part_attn, width)
    attn_sum = lax.psum_scatter(attn_grads, plane, scatter_dimension=0, tiled=True)
    attn_sum = lax.psum_scatter(attn_sum, "fsdp", scatter_dimension=0, tiled=True)
    attn_sum = lax.all_gather(attn_sum, "rep", axis=0, tiled=False)
    ddist = ddist[:n_heads, : buckets.shape[0]]
    match = (buckets[:, None] == jnp.arange(n_buckets)[None, :]).astype(f32)
    table = lax.dot_general(
        match,
        ddist,
        (((0,), (1,)), ((), ())),
        precision=highest,
        preferred_element_type=f32,
    )
    grad_one, grad_two, grad_table, grad_router = lax.psum(
        (dgain_one[0], dgain_two[0], table, drouter[:n_experts].T), ("rep", "fsdp", "seq")
    )
    attn_sum = attn_sum.astype(f32)
    return (
        out_rows,
        grad_tokens,
        attn_sum[0],
        attn_sum[1],
        attn_sum[2],
        attn_sum[3],
        grad_in.astype(f32),
        grad_out.astype(f32),
        grad_one,
        grad_two,
        grad_table,
        grad_router,
    )


def solution(mesh):
    rows = P(("rep", "fsdp", "seq"), None)
    owned = P(("fsdp", "seq"), None)
    expert = P(None, ("fsdp", "seq"), None)
    in_specs = (
        rows,
        P(("rep", "fsdp"), None),
        rows,
        P(),
        owned,
        owned,
        owned,
        owned,
        expert,
        expert,
        P(),
        P(),
        P(),
        P(),
        rows,
    )
    out_specs = (
        rows,
        rows,
        owned,
        owned,
        owned,
        owned,
        expert,
        expert,
        P(),
        P(),
        P(),
        P(),
    )
    return jax.shard_map(
        per_device, mesh=mesh, in_specs=in_specs, out_specs=out_specs, check_vma=False
    )
```
